32 devices in a mesh: fsdp: 4 (over z), ctx: 4 (over x, core), tp: 2 (over y).
Axes of the slice: x: 2, y: 2, z: 4, core: 2. Of those that a mesh axis runs over, the one named last changes fastest.
Arguments:
- tokens: bfloat16 [8, 4096, 1024], P('fsdp', ('ctx', 'tp')), may hold values from -6 to 6
- time_embed: float32 [8, 256], P('fsdp'), may hold values from -6 to 6
- segment_ids: int32 [8, 4096], P('fsdp'), may hold values from 0 to 15, as said below
- block_pairs: int32 [8, 4, 15, 2], P('fsdp', 'ctx'), may hold values from 0 to 7, as said below
- pair_counts: int32 [8, 4], P('fsdp', 'ctx'), may hold values from 2 to 15, as said below
- w_time: float32 [256, 2048], P(('fsdp', 'ctx')), may hold values from -0.1875 to 0.1875
- w_qkv: float32 [1024, 3072], P(('fsdp', 'ctx'), 'tp'), may hold values from -0.1875 to 0.1875
- w_out: float32 [1024, 1024], P(('fsdp', 'ctx'), 'tp'), may hold values from -1.5 to 1.5
- w_up: float32 [1024, 4096], P(('fsdp', 'ctx'), 'tp'), may hold values from -0.1875 to 0.1875
- w_down: float32 [1024, 4096], P(('fsdp', 'ctx'), 'tp'), may hold values from -0.09375 to 0.09375
- cotangent: bfloat16 [8, 4096, 1024], P('fsdp', ('ctx', 'tp')), may hold values from -6 to 6
Outputs:
- layer_out: bfloat16 [8, 4096, 1024], P('fsdp', ('ctx', 'tp'))
- grad_tokens: bfloat16 [8, 4096, 1024], P('fsdp', ('ctx', 'tp'))
- grad_time: float32 [256, 2048], P(('fsdp', 'ctx'))
- grad_qkv: float32 [1024, 3072], P(('fsdp', 'ctx'), 'tp')
- grad_proj: float32 [1024, 1024], P(('fsdp', 'ctx'), 'tp')
- grad_up: float32 [1024, 4096], P(('fsdp', 'ctx'), 'tp')
- grad_down: float32 [1024, 4096], P(('fsdp', 'ctx'), 'tp')
The draws below stay inside these ranges and needn't reach their ends.
Inputs may be any that keep to these rules, and one draw needn't show every extreme that they name: `segment_ids`: in each row the ids start at 0 and never fall; a new document starts at a position with probability 1 / 512; row 0 holds one document; in the last row a document also starts at every multiple of 256 until the id reaches 15; ids stop rising at 15, so the last documents of a row may merge. `block_pairs`: for row r and ctx index c, slots p < pair_counts[r, c] list in increasing order of (local query block, key block) exactly the pairs of a local query block (0 to 1) and a key block of the row that share a document with the key not after the query; other slots hold 0. `pair_counts`: the number of listed pairs; the last ctx index of row 0 reaches 15.
All inputs are finite; a program needn't handle non-finite values.
Results may differ from the reference program's by a relative error of at most 0.02.
Values may be sent and summed in bfloat16 or wider, within the bound.
No kernel may reach another device: no remote copies, remote signals or barrier semaphores. Data moves between devices by JAX's collectives and lax.ppermute only.
A program may use at most 256 MiB of HBM per device.

```python
import jax
import jax.numpy as jnp
from jax import lax

D = 1024
HEADS = 16
HEAD_DIM = 64
FF = 4096
TEMB = 256
BLK = 512
ROWS = 8
LEN = 4096
QBD = 2
KB = 8
MAXPAIRS = 15
N_CTX = 4


def packing(key):
    starts = (jax.random.randint(jax.random.fold_in(key, 7), (ROWS, LEN), 0, BLK) == 0).astype(jnp.int32)
    column = jnp.arange(LEN, dtype=jnp.int32)[None, :]
    row_number = jnp.arange(ROWS, dtype=jnp.int32)[:, None]
    forced = (row_number == ROWS - 1) & (column % (BLK // 2) == 0)
    starts = jnp.where(forced, 1, starts)
    starts = jnp.where((column == 0) | (row_number == 0), 0, starts)
    counted = jnp.cumsum(starts, axis=1).astype(jnp.int32)
    return jnp.minimum(counted, 2 * KB - 1).astype(jnp.int32)


def pair_table(key):
    seg_all = packing(key)
    block_start = seg_all[:, ::BLK]
    block_end = seg_all[:, BLK - 1::BLK]
    query_global = jnp.arange(N_CTX, dtype=jnp.int32)[:, None] * QBD + jnp.arange(QBD, dtype=jnp.int32)[None, :]
    start_query = block_start[:, query_global]
    key_ids = jnp.arange(KB, dtype=jnp.int32)
    flagged = (key_ids[None, None, None, :] <= query_global[None, :, :, None]) & (block_end[:, None, None, :] >= start_query[:, :, :, None])
    flagged = flagged.reshape(ROWS, N_CTX, QBD * KB).astype(jnp.int32)
    slot_ids = jnp.arange(QBD * KB, dtype=jnp.int32)
    ranking = (1 - flagged) * (QBD * KB) + slot_ids
    ordered = jnp.argsort(ranking, axis=-1)[:, :, :MAXPAIRS].astype(jnp.int32)
    counted = jnp.sum(flagged, axis=-1).astype(jnp.int32)
    live_slot = jnp.arange(MAXPAIRS, dtype=jnp.int32)[None, None, :] < counted[:, :, None]
    first_part = jnp.where(live_slot, ordered // KB, 0)
    second_part = jnp.where(live_slot, ordered % KB, 0)
    return (jnp.stack([first_part, second_part], axis=-1).astype(jnp.int32), counted)


def draw_segment_ids(key, part):
    return packing(key)


def draw_block_pairs(key, part):
    return pair_table(key)[0]


def draw_pair_counts(key, part):
    return pair_table(key)[1]


def level_of(own_key, dims, cuts, smallest, high):
    loudness = 1.0
    for axis_at, parts in cuts:
        steps = jax.random.uniform(jax.random.fold_in(jax.random.fold_in(own_key, 6), axis_at), (parts,), jnp.float32, smallest / len(cuts), high / len(cuts))
        loudness = loudness * jnp.repeat(jnp.exp(steps), dims[axis_at] // parts).reshape((-1,) + (1,) * (len(dims) - 1 - axis_at))
    return loudness


def gaussian(rng, extent, scale, limit, shards=(), held_as=jnp.bfloat16):
    array = scale * jax.random.normal(rng, extent, jnp.float32)
    if shards:
        array = array * level_of(rng, extent, shards, -0.22, 0.18)
    return jnp.clip(array, -limit, limit).astype(held_as)


def setup_inputs(seed: int = 0) -> dict:
    seeds = jax.random.split(jax.random.key(seed), 12)
    return {
        "tokens": gaussian(seeds[0], (ROWS, LEN, D), 1.0, 6.0, ((0, 4), (1, 8))),
        "time_embed": gaussian(seeds[1], (ROWS, TEMB), 1.0, 6.0, ((0, 4),), jnp.float32),
        "segment_ids": draw_segment_ids(jax.random.fold_in(seeds[11], 71), 0),
        "block_pairs": draw_block_pairs(jax.random.fold_in(seeds[11], 71), 0),
        "pair_counts": draw_pair_counts(jax.random.fold_in(seeds[11], 71), 0),
        "w_time": gaussian(seeds[5], (TEMB, 2 * D), (4 * TEMB) ** -0.5, 0.1875, ((0, 16),), jnp.float32),
        "w_qkv": gaussian(seeds[6], (D, 3 * D), D ** -0.5, 0.1875, ((0, 16), (1, 2)), jnp.float32),
        "w_out": gaussian(seeds[7], (D, D), (max(D // 64, 1)) ** -0.5, 1.5, ((0, 16), (1, 2)), jnp.float32),
        "w_up": gaussian(seeds[8], (D, FF), D ** -0.5, 0.1875, ((0, 16), (1, 2)), jnp.float32),
        "w_down": gaussian(seeds[9], (D, FF), FF ** -0.5, 0.09375, ((0, 16), (1, 2)), jnp.float32),
        "cotangent": gaussian(seeds[10], (ROWS, LEN, D), 1.0, 6.0, ((0, 4), (1, 8))),
    }


@jax.custom_vjp
def low(v):
    return lax.optimization_barrier(v.astype(jnp.bfloat16)).astype(jnp.float32)

@jax.custom_vjp
def low_back(v):
    return v

def low_keep(v):
    return (low(v), None)

def low_pass(kept, grad):
    return (grad,)

def back_keep(v):
    return (v, None)

def back_low(kept, grad):
    return (low(grad),)
low.defvjp(low_keep, low_pass)
low_back.defvjp(back_keep, back_low)
epsilon = 1e-05
highest = lax.Precision.HIGHEST
masked_out = -1e+30

def product(left_side, right_side):
    return jnp.dot(left_side, right_side, precision=highest, preferred_element_type=jnp.float32)

def normalize(values):
    mean_value = lax.optimization_barrier(jnp.mean(values, axis=-1, keepdims=True))
    centred = values - mean_value
    variance = lax.optimization_barrier(jnp.mean(centred * centred, axis=-1, keepdims=True))
    return centred * lax.rsqrt(variance + epsilon)

def listed_blocks(pair_rows, pair_total):
    live_slot = jnp.arange(MAXPAIRS, dtype=jnp.int32)[None, :] < pair_total[:, None]
    query_block = jnp.arange(N_CTX, dtype=jnp.int32)[:, None] * QBD + pair_rows[:, :, 0]
    block_ids = jnp.arange(KB, dtype=jnp.int32)
    block_hits = live_slot[:, :, None, None] & (query_block[:, :, None, None] == block_ids[:, None]) & (pair_rows[:, :, 1][:, :, None, None] == block_ids[None, :])
    return jnp.any(block_hits, axis=(0, 1))

def attend_block(query_block, key_rows, value_rows, seg_query, seg_keys, pos_query, pos_keys, block_okay):
    scores = jnp.einsum('qhe,khe->hqk', query_block, key_rows, precision=highest) * HEAD_DIM ** (-0.5)
    scores = low_back(scores)
    allowed = (seg_query[:, None] == seg_keys[None, :]) & (pos_keys[None, :] <= pos_query[:, None]) & block_okay[None, :]
    scores = jnp.where(allowed[None], scores, masked_out)
    row_max = lax.optimization_barrier(jnp.max(scores, axis=-1, keepdims=True))
    weights = jnp.exp(scores - row_max)
    probabilities = low(weights / lax.optimization_barrier(jnp.sum(weights, axis=-1, keepdims=True)))
    return jnp.einsum('hqk,khe->qhe', probabilities, value_rows, precision=highest)

def row_forward(x_row, time_row, seg_row, pair_rows, pair_total, w_time, w_qkv, w_out, w_up, w_down):
    scales = 1.0 + product(time_row[None, :], low(w_time))[0]
    normed = low(normalize(x_row) * scales[:D])
    projected = low(low_back(product(normed, low(w_qkv)))).reshape(LEN, HEADS, 3, HEAD_DIM)
    query_all = projected[:, :, 0]
    key_all = projected[:, :, 1]
    value_all = projected[:, :, 2]
    blocks_okay = listed_blocks(pair_rows, pair_total)
    positions = jnp.arange(LEN, dtype=jnp.int32)
    pieces = []
    for block_index in range(KB):
        lower_end = block_index * BLK
        upper_end = (block_index + 1) * BLK
        pieces.append(jax.checkpoint(attend_block)(query_all[lower_end:upper_end], key_all[:upper_end], value_all[:upper_end], seg_row[lower_end:upper_end], seg_row[:upper_end], positions[lower_end:upper_end], positions[:upper_end], jnp.repeat(blocks_okay[block_index, :block_index + 1], BLK)))
    mixed_heads = low(low_back(jnp.concatenate(pieces, axis=0))).reshape(LEN, D)
    attention = low_back(product(mixed_heads, low(w_out).T))
    hidden = x_row + attention
    normed_mlp = low(normalize(hidden) * scales[D:])
    pre_act = low_back(product(normed_mlp, low(w_up)))
    activated = low(jax.nn.gelu(pre_act, approximate=True))
    return hidden + low_back(product(activated, low(w_down).T))

def reference(tokens, time_embed, segment_ids, block_pairs, pair_counts, w_time, w_qkv, w_out, w_up, w_down, cotangent):

    def forward(inputs, weight_time, weight_qkv, weight_out, weight_up, weight_down):

        def one_row(carried, row_items):
            x_row, time_row, seg_row, pair_rows, pair_total = row_items
            result = jax.checkpoint(row_forward)(x_row, time_row, seg_row, pair_rows, pair_total, weight_time, weight_qkv, weight_out, weight_up, weight_down)
            return (carried, result)
        _, outputs = lax.scan(one_row, jnp.zeros((), jnp.float32), (inputs, time_embed, segment_ids, block_pairs, pair_counts))
        return outputs
    outputs, pullback = jax.vjp(forward, tokens.astype(jnp.float32), w_time, w_qkv, w_out, w_up, w_down)
    gradients = pullback(cotangent.astype(jnp.float32))
    return (outputs.astype(jnp.bfloat16), gradients[0].astype(jnp.bfloat16), gradients[1], gradients[2], gradients[3], gradients[4], gradients[5])
```

```python
import functools

import jax
import jax.numpy as jnp
from jax import lax
from jax.experimental import pallas as pl
from jax.experimental.pallas import tpu as pltpu
from jax.sharding import PartitionSpec as P

HEAD_DIM = 64
BLK = 512


epsilon = 1e-05
highest = lax.Precision.HIGHEST
masked_out = -1e30


def normalize(values):
    mean_value = jnp.mean(values, axis=-1, keepdims=True)
    centred = values - mean_value
    variance = jnp.mean(centred * centred, axis=-1, keepdims=True)
    inverse = lax.rsqrt(variance + epsilon)
    return (centred * inverse, inverse)


def normalize_back(grad_hat, normal_hat, inverse):
    first_mean = jnp.mean(grad_hat, axis=-1, keepdims=True)
    second_mean = jnp.mean(grad_hat * normal_hat, axis=-1, keepdims=True)
    return inverse * (grad_hat - first_mean - normal_hat * second_mean)


def smooth_gate(values):
    return jax.nn.gelu(values, approximate=True)


def block_scores(pair_entry, query_rows, key_rows, seg_row, offset):
    query_start = pair_entry[0] * BLK
    key_start = pair_entry[1] * BLK
    query_block = lax.dynamic_slice_in_dim(query_rows, query_start, BLK, 0)
    key_block = lax.dynamic_slice_in_dim(key_rows, key_start, BLK, 0)
    seg_query = lax.dynamic_slice_in_dim(seg_row, offset + query_start, BLK, 0)
    seg_keys = lax.dynamic_slice_in_dim(seg_row, key_start, BLK, 0)
    steps_in = jnp.arange(BLK, dtype=jnp.int32)
    allowed = (seg_query[:, None] == seg_keys[None, :]) & (
        key_start + steps_in[None, :] <= offset + query_start + steps_in[:, None]
    )
    scores = jnp.einsum(
        "qhe,khe->hqk", query_block, key_block, preferred_element_type=jnp.float32
    ) * HEAD_DIM ** (-0.5)
    return (query_block, key_block, query_start, key_start, allowed, scores)


def attend_forward(query_rows, key_rows, value_rows, seg_row, pair_rows, pair_total, offset):
    length_here, head_count, _ = query_rows.shape

    def statistic_step(pair_index, carried):
        running_max, running_sum = carried
        _, _, query_start, _, allowed, scores = block_scores(
            pair_rows[pair_index], query_rows, key_rows, seg_row, offset
        )
        scores = jnp.where(allowed[None], scores, masked_out)
        old_max = lax.dynamic_slice_in_dim(running_max, query_start, BLK, 1)
        old_sum = lax.dynamic_slice_in_dim(running_sum, query_start, BLK, 1)
        new_max = jnp.maximum(old_max, jnp.max(scores, axis=-1))
        weights = jnp.where(allowed[None], jnp.exp(scores - new_max[:, :, None]), 0.0)
        new_sum = old_sum * jnp.exp(old_max - new_max) + jnp.sum(weights, axis=-1)
        return (
            lax.dynamic_update_slice_in_dim(running_max, new_max, query_start, 1),
            lax.dynamic_update_slice_in_dim(running_sum, new_sum, query_start, 1),
        )

    start_max = jnp.full((head_count, length_here), masked_out, jnp.float32)
    start_sum = jnp.zeros((head_count, length_here), jnp.float32)
    running_max, running_sum = lax.fori_loop(0, pair_total, statistic_step, (start_max, start_sum))
    log_total = running_max + jnp.log(running_sum)

    def output_step(pair_index, accumulated):
        _, _, query_start, key_start, allowed, scores = block_scores(
            pair_rows[pair_index], query_rows, key_rows, seg_row, offset
        )
        block_log = lax.dynamic_slice_in_dim(log_total, query_start, BLK, 1)
        probabilities = jnp.where(
            allowed[None], jnp.exp(scores - block_log[:, :, None]), 0.0
        ).astype(jnp.bfloat16)
        value_block = lax.dynamic_slice_in_dim(value_rows, key_start, BLK, 0)
        addition = jnp.einsum(
            "hqk,khe->qhe", probabilities, value_block, preferred_element_type=jnp.float32
        )
        previous = lax.dynamic_slice_in_dim(accumulated, query_start, BLK, 0)
        return lax.dynamic_update_slice_in_dim(accumulated, previous + addition, query_start, 0)

    mixed_rows = lax.fori_loop(0, pair_total, output_step, jnp.zeros(query_rows.shape, jnp.float32))
    return (mixed_rows, log_total)


def attend_backward(
    query_rows,
    key_rows,
    value_rows,
    seg_row,
    pair_rows,
    pair_total,
    offset,
    log_total,
    grad_mixed,
    inner_sums,
):
    scale_factor = HEAD_DIM ** (-0.5)

    def add_block(whole, start_at, addition):
        previous = lax.dynamic_slice_in_dim(whole, start_at, BLK, 0)
        return lax.dynamic_update_slice_in_dim(whole, previous + addition, start_at, 0)

    def gradient_step(pair_index, carried):
        grad_query, grad_keys, grad_values = carried
        query_block, key_block, query_start, key_start, allowed, scores = block_scores(
            pair_rows[pair_index], query_rows, key_rows, seg_row, offset
        )
        block_log = lax.dynamic_slice_in_dim(log_total, query_start, BLK, 1)
        probabilities = jnp.where(allowed[None], jnp.exp(scores - block_log[:, :, None]), 0.0)
        grad_block = lax.dynamic_slice_in_dim(grad_mixed, query_start, BLK, 0)
        value_block = lax.dynamic_slice_in_dim(value_rows, key_start, BLK, 0)
        grad_probs = jnp.einsum(
            "qhe,khe->hqk", grad_block, value_block, preferred_element_type=jnp.float32
        )
        inner_block = lax.dynamic_slice_in_dim(inner_sums, query_start, BLK, 1)
        grad_scores = (probabilities * (grad_probs - inner_block[:, :, None])).astype(jnp.bfloat16)
        query_add = (
            jnp.einsum("hqk,khe->qhe", grad_scores, key_block, preferred_element_type=jnp.float32)
            * scale_factor
        )
        key_add = (
            jnp.einsum("hqk,qhe->khe", grad_scores, query_block, preferred_element_type=jnp.float32)
            * scale_factor
        )
        value_add = jnp.einsum(
            "hqk,qhe->khe",
            probabilities.astype(jnp.bfloat16),
            grad_block,
            preferred_element_type=jnp.float32,
        )
        return (
            add_block(grad_query, query_start, query_add),
            add_block(grad_keys, key_start, key_add),
            add_block(grad_values, key_start, value_add),
        )

    start_state = (
        jnp.zeros(query_rows.shape, jnp.float32),
        jnp.zeros(key_rows.shape, jnp.float32),
        jnp.zeros(value_rows.shape, jnp.float32),
    )
    return lax.fori_loop(0, pair_total, gradient_step, start_state)


def body(
    tokens,
    time_embed,
    segment_ids,
    block_pairs,
    pair_counts,
    w_time,
    w_qkv,
    w_out,
    w_up,
    w_down,
    cotangent,
):
    row_count, local_len, model_width = tokens.shape
    time_all, qkv_all, out_all, up_all, down_all = (
        lax.all_gather(w_time.astype(jnp.bfloat16), ("fsdp", "ctx"), axis=0, tiled=True),
        lax.all_gather(w_qkv.astype(jnp.bfloat16), ("fsdp", "ctx"), axis=0, tiled=True),
        lax.all_gather(w_out.astype(jnp.bfloat16), ("fsdp", "ctx"), axis=0, tiled=True),
        lax.all_gather(w_up.astype(jnp.bfloat16), ("fsdp", "ctx"), axis=0, tiled=True),
        lax.all_gather(w_down.astype(jnp.bfloat16), ("fsdp", "ctx"), axis=0, tiled=True),
    )
    scales = 1.0 + jnp.dot(time_embed, time_all.astype(jnp.float32), precision=highest)
    scale_attn = scales[:, None, :model_width]
    scale_mlp = scales[:, None, model_width:]
    x_input = tokens.astype(jnp.float32)
    hat_attn, inverse_attn = normalize(x_input)
    normed = (hat_attn * scale_attn).astype(jnp.bfloat16)
    normed_all = lax.all_gather(normed, "tp", axis=1, tiled=True)
    ctx_len = normed_all.shape[1]
    head_count = qkv_all.shape[1] // (3 * HEAD_DIM)
    projected = jnp.einsum("rtd,dc->rtc", normed_all, qkv_all, preferred_element_type=jnp.float32)
    projected = projected.astype(jnp.bfloat16).reshape(row_count, ctx_len, head_count, 3, HEAD_DIM)
    query_all = projected[:, :, :, 0]
    key_part = projected[:, :, :, 1]
    value_part = projected[:, :, :, 2]
    key_all, value_all = (
        lax.all_gather(key_part, "ctx", axis=1, tiled=True),
        lax.all_gather(value_part, "ctx", axis=1, tiled=True),
    )
    offset = lax.axis_index("ctx") * ctx_len
    mixed_list = []
    log_list = []
    for row_index in range(row_count):
        mixed_rows, log_total = attend_forward(
            query_all[row_index],
            key_all[row_index],
            value_all[row_index],
            segment_ids[row_index],
            block_pairs[row_index, 0],
            pair_counts[row_index, 0],
            offset,
        )
        mixed_list.append(mixed_rows)
        log_list.append(log_total)
    mixed_exact = jnp.stack(mixed_list)
    mixed_heads = mixed_exact.astype(jnp.bfloat16).reshape(
        row_count, ctx_len, head_count * HEAD_DIM
    )
    attn_part = jnp.einsum("rtc,dc->rtd", mixed_heads, out_all, preferred_element_type=jnp.float32)
    attn_local = lax.psum_scatter(
        attn_part.astype(jnp.bfloat16), "tp", scatter_dimension=1, tiled=True
    ).astype(jnp.float32)
    hidden = x_input + attn_local
    hat_mlp, inverse_mlp = normalize(hidden)
    normed_mlp = (hat_mlp * scale_mlp).astype(jnp.bfloat16)
    mlp_all = lax.all_gather(normed_mlp, "tp", axis=1, tiled=True)
    pre_act = jnp.einsum("rtd,df->rtf", mlp_all, up_all, preferred_element_type=jnp.float32)
    activated = smooth_gate(pre_act).astype(jnp.bfloat16)
    mlp_part = jnp.einsum("rtf,df->rtd", activated, down_all, preferred_element_type=jnp.float32)
    mlp_local = lax.psum_scatter(
        mlp_part.astype(jnp.bfloat16), "tp", scatter_dimension=1, tiled=True
    ).astype(jnp.float32)
    grad_all = lax.all_gather(cotangent, "tp", axis=1, tiled=True)
    grad_act = jnp.einsum("rtd,df->rtf", grad_all, down_all, preferred_element_type=jnp.float32)
    _, gate_back = jax.vjp(smooth_gate, pre_act)
    grad_pre = gate_back(grad_act)[0].astype(jnp.bfloat16)
    grad_down = jnp.einsum("rtd,rtf->df", grad_all, activated, preferred_element_type=jnp.float32)
    grad_up = jnp.einsum("rtd,rtf->df", mlp_all, grad_pre, preferred_element_type=jnp.float32)
    norm_part = jnp.einsum("rtf,df->rtd", grad_pre, up_all, preferred_element_type=jnp.float32)
    grad_normed_mlp = lax.psum_scatter(
        norm_part.astype(jnp.bfloat16), "tp", scatter_dimension=1, tiled=True
    ).astype(jnp.float32)
    layer_out = (hidden + mlp_local).astype(jnp.bfloat16)
    grad_output = cotangent.astype(jnp.float32)
    grad_scale_mlp = jnp.sum(grad_normed_mlp * hat_mlp, axis=1)
    grad_hidden = grad_output + normalize_back(grad_normed_mlp * scale_mlp, hat_mlp, inverse_mlp)
    grad_attn_all = lax.all_gather(grad_hidden.astype(jnp.bfloat16), "tp", axis=1, tiled=True)
    grad_mixed = jnp.einsum(
        "rtd,dc->rtc", grad_attn_all, out_all, preferred_element_type=jnp.float32
    ).astype(jnp.bfloat16)
    grad_proj = jnp.einsum(
        "rtd,rtc->dc", grad_attn_all, mixed_heads, preferred_element_type=jnp.float32
    )
    grad_mixed = grad_mixed.reshape(row_count, ctx_len, head_count, HEAD_DIM)
    inner_sums = jnp.einsum("rqhe,rqhe->rhq", grad_mixed.astype(jnp.float32), mixed_exact)
    query_grads = []
    key_grads = []
    value_grads = []
    for row_index in range(row_count):
        grad_query, grad_keys, grad_values = attend_backward(
            query_all[row_index],
            key_all[row_index],
            value_all[row_index],
            segment_ids[row_index],
            block_pairs[row_index, 0],
            pair_counts[row_index, 0],
            offset,
            log_list[row_index],
            grad_mixed[row_index],
            inner_sums[row_index],
        )
        query_grads.append(grad_query)
        key_grads.append(grad_keys)
        value_grads.append(grad_values)
    key_local, value_local = (
        lax.psum_scatter(
            jnp.stack(key_grads).astype(jnp.bfloat16), "ctx", scatter_dimension=1, tiled=True
        ).astype(jnp.float32),
        lax.psum_scatter(
            jnp.stack(value_grads).astype(jnp.bfloat16), "ctx", scatter_dimension=1, tiled=True
        ).astype(jnp.float32),
    )
    grad_projected = jnp.stack(
        [
            jnp.stack(query_grads).astype(jnp.bfloat16),
            key_local.astype(jnp.bfloat16),
            value_local.astype(jnp.bfloat16),
        ],
        axis=3,
    )
    grad_projected = grad_projected.reshape(row_count, ctx_len, head_count * 3 * HEAD_DIM)
    grad_qkv = jnp.einsum(
        "rtd,rtc->dc", normed_all, grad_projected, preferred_element_type=jnp.float32
    )
    first_part = jnp.einsum(
        "rtc,dc->rtd", grad_projected, qkv_all, preferred_element_type=jnp.float32
    )
    grad_normed = lax.psum_scatter(
        first_part.astype(jnp.bfloat16), "tp", scatter_dimension=1, tiled=True
    ).astype(jnp.float32)
    grad_scale_attn = jnp.sum(grad_normed * hat_attn, axis=1)
    grad_tokens = grad_hidden + normalize_back(grad_normed * scale_attn, hat_attn, inverse_attn)
    grad_scales = lax.psum(jnp.concatenate([grad_scale_attn, grad_scale_mlp], axis=1), "tp")
    grad_time = jnp.dot(time_embed.T, grad_scales, precision=highest)
    shared = (
        lax.psum_scatter(
            grad_time.astype(jnp.bfloat16), ("fsdp", "ctx"), scatter_dimension=0, tiled=True
        ).astype(jnp.float32),
        lax.psum_scatter(
            grad_qkv.astype(jnp.bfloat16), ("fsdp", "ctx"), scatter_dimension=0, tiled=True
        ).astype(jnp.float32),
        lax.psum_scatter(
            grad_proj.astype(jnp.bfloat16), ("fsdp", "ctx"), scatter_dimension=0, tiled=True
        ).astype(jnp.float32),
        lax.psum_scatter(
            grad_up.astype(jnp.bfloat16), ("fsdp", "ctx"), scatter_dimension=0, tiled=True
        ).astype(jnp.float32),
        lax.psum_scatter(
            grad_down.astype(jnp.bfloat16), ("fsdp", "ctx"), scatter_dimension=0, tiled=True
        ).astype(jnp.float32),
    )
    return (
        layer_out,
        grad_tokens.astype(jnp.bfloat16),
        shared[0],
        shared[1],
        shared[2],
        shared[3],
        shared[4],
    )


def params(limit=58):
    return pltpu.CompilerParams(vmem_limit_bytes=limit * 1024 * 1024)


def whole(shape):
    zeros = (0,) * len(shape)
    return pl.BlockSpec(shape, lambda *_: zeros, pipeline_mode=pl.Buffered(1))


def cost(flops, nbytes, exps=0):
    return pl.CostEstimate(flops=int(flops), bytes_accessed=int(nbytes), transcendentals=int(exps))


def dot_nn(left, right):
    return jnp.dot(left, right, preferred_element_type=jnp.float32)


def dot_nt(left, right):
    return lax.dot_general(left, right, (((1,), (1,)), ((), ())), preferred_element_type=jnp.float32)


def transposed(values):
    return values.astype(jnp.float32).T.astype(values.dtype)


def turned_apart(into_ref, values, chunk_at, chunks):
    turned = values.astype(jnp.float32).T.astype(values.dtype)
    high = turned.shape[0] // chunks
    bits = chunks.bit_length() - 1
    for chunk in range(chunks):
        apart = chunk ^ chunk_at
        place = 0
        for bit in range(bits):
            place += ((apart >> bit) & 1) << (bits - 1 - bit)
        into_ref[pl.ds(pl.multiple_of(place * high, high), high), :] = turned[
            chunk * high : (chunk + 1) * high, :
        ]


def low_lanes(shape):
    return lax.broadcasted_iota(jnp.int32, shape, 1) < HEAD_DIM


def pair_apart(stored):
    first, second, third = stored[:, :128], stored[:, 128:256], stored[:, 256:]
    low = low_lanes(first.shape)
    keys = pltpu.roll(jnp.where(low, third, first), HEAD_DIM, 1)
    return jnp.concatenate(
        [jnp.where(low, first, second), keys, jnp.where(low, second, third)], axis=1
    )


def pair_together(query, keys, values):
    low = low_lanes(query.shape)
    turned = pltpu.roll(keys, HEAD_DIM, 1)
    return jnp.concatenate(
        [jnp.where(low, query, turned), jnp.where(low, values, query), jnp.where(low, turned, values)],
        axis=1,
    )


def project_kernel(te_ref, tok_ref, w_ref, qkv_ref, normed_ref, scales_ref, *, tiles, k_rows, q_cols, t_cols):
    step = pl.program_id(0)
    chunks, halves = w_ref.shape[0], w_ref.shape[1]

    @pl.when(step == 0)
    def _():
        exact = te_ref[...]
        high = exact.astype(jnp.bfloat16)
        rest = exact - high.astype(jnp.float32)
        middle = rest.astype(jnp.bfloat16)
        last = (rest - middle.astype(jnp.float32)).astype(jnp.bfloat16)
        folds = w_ref.shape[2] // k_rows
        for half in range(halves):
            for fold in range(folds):
                weights = w_ref[:, half, fold * k_rows : (fold + 1) * k_rows, q_cols : q_cols + t_cols]
                weights = weights.reshape(chunks * k_rows, t_cols)
                total = dot_nn(last, weights) + dot_nn(middle, weights) + dot_nn(high, weights)
                at = (half * folds + fold) * t_cols
                scales_ref[:, at : at + t_cols] = 1.0 + total

    row = step // tiles
    values = tok_ref[0].astype(jnp.float32)
    width = values.shape[1]
    hat, _ = normalize(values)
    normed = (hat * scales_ref[pl.ds(row, 1), :width]).astype(jnp.bfloat16)
    normed_ref[0] = normed
    pair = 6 * HEAD_DIM
    for half in range(halves):
        weights = w_ref[:, half, :, :q_cols].reshape(width, q_cols)
        out = dot_nn(normed, weights)
        for group in range(q_cols // pair):
            qkv_ref[half * (q_cols // pair) + group, 0] = pair_apart(
                out[:, group * pair : (group + 1) * pair]
            ).astype(jnp.bfloat16)


def project(time_embed, tokens, w_all, k_rows, q_cols, t_cols):
    rows, length, width = tokens.shape
    chunks, halves = w_all.shape[:2]
    groups = halves * q_cols // (6 * HEAD_DIM)
    tile = 256
    tiles = length // tile
    return pl.pallas_call(
        functools.partial(project_kernel, tiles=tiles, k_rows=k_rows, q_cols=q_cols, t_cols=t_cols),
        grid=(rows * tiles,),
        in_specs=[
            whole(time_embed.shape),
            pl.BlockSpec((1, tile, width), lambda i: (i // tiles, i % tiles, 0)),
            whole(w_all.shape),
        ],
        out_specs=[
            pl.BlockSpec((groups, 1, tile, 6 * HEAD_DIM), lambda i: (0, i // tiles, i % tiles, 0)),
            pl.BlockSpec((1, tile, width), lambda i: (i // tiles, i % tiles, 0)),
            whole((rows, 2 * width)),
        ],
        out_shape=[
            jax.ShapeDtypeStruct((groups, rows, length, 6 * HEAD_DIM), jnp.bfloat16),
            jax.ShapeDtypeStruct(tokens.shape, jnp.bfloat16),
            jax.ShapeDtypeStruct((rows, 2 * width), jnp.float32),
        ],
        compiler_params=params(),
        cost_estimate=cost(2 * rows * length * width * halves * q_cols, 2 * w_all.size + 10 * tokens.size),
        name="project",
    )(time_embed, tokens, w_all)


def tile_mask(segc_ref, segr_ref, key_block, query_block):
    key_at = pl.multiple_of(key_block * BLK, BLK)
    query_at = pl.multiple_of(query_block * BLK, BLK)
    same = segc_ref[0, pl.ds(key_at, BLK), :] == segr_ref[0, :, pl.ds(query_at, BLK)]
    key_pos = key_at + lax.broadcasted_iota(jnp.int32, (BLK, BLK), 0)
    query_pos = query_at + lax.broadcasted_iota(jnp.int32, (BLK, BLK), 1)
    return same & (key_pos <= query_pos)


def split_heads(values):
    low = low_lanes(values.shape)
    zero = jnp.zeros_like(values)
    return jnp.concatenate([jnp.where(low, values, zero), jnp.where(low, zero, values)], axis=0)


def is_full(edge_ref, row, blocks, key_block, query_block):
    same = edge_ref[row, key_block] == edge_ref[row, blocks + query_block]
    return same & (key_block < query_block)


def attend_kernel(listed_ref, edge_ref, qkv_ref, segc_ref, segr_ref, mixed_ref, lse_ref, vt_ref, qz_ref, acc_ref, stat_ref):
    row = pl.program_id(0)
    blocks = qkv_ref.shape[0]

    def turn(block, carried):
        at = pl.multiple_of(block * BLK, BLK)
        vt_ref[:, pl.ds(at, BLK)] = transposed(qkv_ref[block, 0, :, 256:384])
        return carried

    lax.fori_loop(0, blocks, turn, 0)

    def one_query(query_block, carried):
        query = qkv_ref[query_block, 0, :, :128].astype(jnp.float32) * HEAD_DIM ** (-0.5)
        qz_ref[...] = split_heads(query.astype(jnp.bfloat16))
        stat_ref[0:1, :] = jnp.full((1, 2 * BLK), masked_out, jnp.float32)
        stat_ref[1:2, :] = jnp.zeros((1, 2 * BLK), jnp.float32)
        acc_ref[...] = jnp.zeros(acc_ref.shape, jnp.float32)

        def update(key_block, mask):
            scores = dot_nt(qkv_ref[key_block, 0, :, 128:256], qz_ref[...])
            if mask is not None:
                scores = jnp.concatenate(
                    [
                        jnp.where(mask, scores[:, :BLK], masked_out),
                        jnp.where(mask, scores[:, BLK:], masked_out),
                    ],
                    axis=1,
                )
            old_max = stat_ref[0:1, :]
            new_max = jnp.maximum(old_max, jnp.max(scores, axis=0, keepdims=True))
            weights = jnp.exp(scores - new_max)
            shrink = jnp.exp(old_max - new_max)
            stat_ref[0:1, :] = new_max
            stat_ref[1:2, :] = stat_ref[1:2, :] * shrink + jnp.sum(weights, axis=0, keepdims=True)
            rounded = weights.astype(jnp.bfloat16)
            at = pl.multiple_of(key_block * BLK, BLK)
            for head in range(2):
                part = slice(head * BLK, (head + 1) * BLK)
                value = vt_ref[head * HEAD_DIM : (head + 1) * HEAD_DIM, pl.ds(at, BLK)]
                acc_ref[:, part] = acc_ref[:, part] * shrink[:, part] + dot_nn(value, rounded[:, part])

        def one_key(key_block, carried):
            listed = listed_ref[row, query_block * blocks + key_block] != 0
            full = is_full(edge_ref, row, blocks, key_block, query_block)

            @pl.when(listed & full)
            def _():
                update(key_block, None)

            @pl.when(listed & jnp.logical_not(full))
            def _():
                update(key_block, tile_mask(segc_ref, segr_ref, key_block, query_block))

            return carried

        lax.fori_loop(0, query_block + 1, one_key, 0)
        total = stat_ref[1:2, :]
        mixed = acc_ref[...] / total
        mixed = jnp.concatenate([mixed[:, :BLK], mixed[:, BLK:]], axis=0).T
        mixed_ref[query_block, 0] = mixed.astype(jnp.bfloat16)
        log_total = stat_ref[0:1, :] + jnp.log(total)
        at = pl.multiple_of(query_block * BLK, BLK)
        lse_ref[0, 0:1, pl.ds(at, BLK)] = log_total[:, :BLK]
        lse_ref[0, 1:2, pl.ds(at, BLK)] = log_total[:, BLK:]
        return carried

    lax.fori_loop(0, blocks, one_query, 0)


def attend(listed, edges, qkv, segc, segr):
    blocks, rows, blk, width = qkv.shape
    length = blocks * blk
    pair = 2 * HEAD_DIM
    return pl.pallas_call(
        attend_kernel,
        grid_spec=pltpu.PrefetchScalarGridSpec(
            num_scalar_prefetch=2,
            grid=(rows,),
            in_specs=[
                pl.BlockSpec((blocks, 1, blk, width), lambda r, *_: (0, r, 0, 0)),
                pl.BlockSpec((1, length, 1), lambda r, *_: (r, 0, 0)),
                pl.BlockSpec((1, 1, length), lambda r, *_: (r, 0, 0)),
            ],
            out_specs=[
                pl.BlockSpec((blocks, 1, blk, pair), lambda r, *_: (0, r, 0, 0)),
                pl.BlockSpec((1, 2, length), lambda r, *_: (r, 0, 0)),
            ],
            scratch_shapes=[
                pltpu.VMEM((pair, length), jnp.bfloat16),
                pltpu.VMEM((2 * blk, pair), jnp.bfloat16),
                pltpu.VMEM((HEAD_DIM, 2 * blk), jnp.float32),
                pltpu.VMEM((2, 2 * blk), jnp.float32),
            ],
        ),
        out_shape=[
            jax.ShapeDtypeStruct((blocks, rows, blk, pair), jnp.bfloat16),
            jax.ShapeDtypeStruct((rows, 2, length), jnp.float32),
        ],
        compiler_params=params(),
        cost_estimate=cost(30e9, 12e6, 40e6),
        name="attend",
    )(listed, edges, qkv, segc, segr)


def attend_back_kernel(
    listed_ref, edge_ref, qkv_ref, grad_ref, mixed_ref, lse_ref, segc_ref, segr_ref, out_ref,
    kt_ref, qz_ref, gz_ref, inner_ref, dq_ref, dk_ref, dv_ref,
):
    row = pl.program_id(0)
    blocks = qkv_ref.shape[0]
    scale = HEAD_DIM ** (-0.5)

    def prepare(block, carried):
        at = pl.multiple_of(block * BLK, BLK)
        kt_ref[:, pl.ds(at, BLK)] = transposed(qkv_ref[block, 0, :, 128:256])
        query = qkv_ref[block, 0, :, :128].astype(jnp.float32) * scale
        qz_ref[block] = split_heads(query.astype(jnp.bfloat16))
        grad = grad_ref[block, 0]
        gz_ref[block] = split_heads(grad)
        product = (grad.astype(jnp.float32) * mixed_ref[block, 0].astype(jnp.float32)).T
        for head in range(2):
            part = product[head * HEAD_DIM : (head + 1) * HEAD_DIM, :]
            inner_ref[head : head + 1, pl.ds(at, BLK)] = jnp.sum(part, axis=0, keepdims=True)
        return carried

    lax.fori_loop(0, blocks, prepare, 0)
    dq_ref[...] = jnp.zeros(dq_ref.shape, jnp.float32)

    def one_key(key_block, carried):
        dk_ref[...] = jnp.zeros(dk_ref.shape, jnp.float32)
        dv_ref[...] = jnp.zeros(dv_ref.shape, jnp.float32)
        key_at = pl.multiple_of(key_block * BLK, BLK)

        def update(query_block, mask):
            query_at = pl.multiple_of(query_block * BLK, BLK)
            keys = qkv_ref[key_block, 0, :, 128:256]
            values = qkv_ref[key_block, 0, :, 256:384]
            for head in range(2):
                part = slice(head * BLK, (head + 1) * BLK)
                query = qz_ref[query_block, part, :]
                grad = gz_ref[query_block, part, :]
                scores = dot_nt(keys, query)
                probs = jnp.exp(scores - lse_ref[0, head : head + 1, pl.ds(query_at, BLK)])
                if mask is not None:
                    probs = jnp.where(mask, probs, 0.0)
                grad_probs = dot_nt(values, grad)
                grad_scores = probs * (grad_probs - inner_ref[head : head + 1, pl.ds(query_at, BLK)])
                probs = probs.astype(jnp.bfloat16)
                grad_scores = grad_scores.astype(jnp.bfloat16)
                dv_ref[...] += dot_nn(probs, grad)
                dk_ref[...] += dot_nn(grad_scores, query)
                lanes = slice(head * HEAD_DIM, (head + 1) * HEAD_DIM)
                dq_ref[lanes, pl.ds(query_at, BLK)] += dot_nn(
                    kt_ref[lanes, pl.ds(key_at, BLK)], grad_scores
                )

        def one_query(query_block, carried):
            listed = listed_ref[row, query_block * blocks + key_block] != 0
            full = is_full(edge_ref, row, blocks, key_block, query_block)

            @pl.when(listed & full)
            def _():
                update(query_block, None)

            @pl.when(listed & jnp.logical_not(full))
            def _():
                update(query_block, tile_mask(segc_ref, segr_ref, key_block, query_block))

            return carried

        lax.fori_loop(key_block, blocks, one_query, 0)
        grad_query = dq_ref[:, pl.ds(key_at, BLK)].T * scale
        out_ref[key_block, 0] = pair_together(grad_query, dk_ref[...], dv_ref[...]).astype(jnp.bfloat16)
        return carried

    lax.fori_loop(0, blocks, one_key, 0)


def attend_back(listed, edges, qkv, grad, mixed, lse, segc, segr):
    blocks, rows, blk, width = qkv.shape
    length = blocks * blk
    pair = 2 * HEAD_DIM
    wide = pl.BlockSpec((blocks, 1, blk, width), lambda r, *_: (0, r, 0, 0))
    narrow = pl.BlockSpec((blocks, 1, blk, pair), lambda r, *_: (0, r, 0, 0))
    return pl.pallas_call(
        attend_back_kernel,
        grid_spec=pltpu.PrefetchScalarGridSpec(
            num_scalar_prefetch=2,
            grid=(rows,),
            in_specs=[
                wide,
                narrow,
                narrow,
                pl.BlockSpec((1, 2, length), lambda r, *_: (r, 0, 0)),
                pl.BlockSpec((1, length, 1), lambda r, *_: (r, 0, 0)),
                pl.BlockSpec((1, 1, length), lambda r, *_: (r, 0, 0)),
            ],
            out_specs=wide,
            scratch_shapes=[
                pltpu.VMEM((pair, length), jnp.bfloat16),
                pltpu.VMEM((blocks, 2 * blk, pair), jnp.bfloat16),
                pltpu.VMEM((blocks, 2 * blk, pair), jnp.bfloat16),
                pltpu.VMEM((2, length), jnp.float32),
                pltpu.VMEM((pair, length), jnp.float32),
                pltpu.VMEM((blk, pair), jnp.float32),
                pltpu.VMEM((blk, pair), jnp.float32),
            ],
        ),
        out_shape=jax.ShapeDtypeStruct(qkv.shape, jnp.bfloat16),
        compiler_params=params(),
        cost_estimate=cost(70e9, 20e6, 40e6),
        name="attend_back",
    )(listed, edges, qkv, grad, mixed, lse, segc, segr)


def joined(ref, first, count):
    return jnp.concatenate([ref[first + i, 0] for i in range(count)], axis=1)


def outward_kernel(mixed_ref, tok_ref, w_ref, scales_ref, hidden_ref, normed_ref, *, tiles):
    row = pl.program_id(0) // tiles
    halves = w_ref.shape[1]
    per_half = mixed_ref.shape[0] // halves
    hidden = tok_ref[0].astype(jnp.float32)
    width = hidden.shape[1]
    for half in range(halves):
        hidden += dot_nt(joined(mixed_ref, half * per_half, per_half), w_ref[:, half].reshape(width, -1))
    hidden_ref[0] = hidden
    hat, _ = normalize(hidden)
    normed_ref[0] = (hat * scales_ref[pl.ds(row, 1), width:]).astype(jnp.bfloat16)


def outward(mixed, tokens, w_all, scales, columns):
    rows, length, width = tokens.shape
    groups, _, _, pair = mixed.shape
    chunks, halves, high, _ = w_all.shape
    tile = 256
    tiles = length // tile
    one = pl.BlockSpec((1, tile, width), lambda i: (i // tiles, i % tiles, 0))
    return pl.pallas_call(
        functools.partial(outward_kernel, tiles=tiles),
        grid=(rows * tiles,),
        in_specs=[
            pl.BlockSpec((groups, 1, tile, pair), lambda i: (0, i // tiles, i % tiles, 0)),
            one,
            whole((chunks, halves, high, columns)),
            whole(scales.shape),
        ],
        out_specs=[one, one],
        out_shape=[
            jax.ShapeDtypeStruct(tokens.shape, jnp.float32),
            jax.ShapeDtypeStruct(tokens.shape, jnp.bfloat16),
        ],
        compiler_params=params(),
        cost_estimate=cost(2 * rows * length * width * width, 12 * tokens.size),
        name="outward",
    )(mixed, tokens, w_all, scales)


def mlp_kernel(
    me_ref, nm_ref, cot_ref, hidden_ref, scales_ref, up_ref, down_ref,
    up_keep_ref, up_send_ref, down_keep_ref, down_send_ref,
    layer_ref, grad_hidden_ref, grad_attn_ref, gscale_ref,
    nmt_ref, cott_ref, out_ref, gn_ref, act_ref, gpre_ref,
):
    tile = pl.program_id(0)
    phase = pl.program_id(1)
    count, width = nm_ref.shape
    chunk = 256
    root = 0.7978845608028654
    cube = 0.044715

    @pl.when((tile == 0) & (phase == 0))
    def _():
        turned_apart(nmt_ref, nm_ref[...], me_ref[0], up_ref.shape[0])
        turned_apart(cott_ref, cot_ref[...], me_ref[0], up_ref.shape[0])
        out_ref[...] = jnp.zeros(out_ref.shape, jnp.float32)
        gn_ref[...] = jnp.zeros(gn_ref.shape, jnp.float32)

    @pl.when(phase == 0)
    def _():
        up = up_ref[:, 0].reshape(width, -1)
        down = down_ref[:, 0].reshape(width, -1)
        for at in range(0, count, chunk):
            part = slice(at, at + chunk)
            pre = dot_nn(nm_ref[part, :], up)
            grad_act = dot_nn(cot_ref[part, :], down)
            square = pre * pre
            bent = jnp.tanh(root * (pre + cube * pre * square))
            half = 0.5 * (1.0 + bent)
            act_ref[part, :] = (pre * half).astype(jnp.bfloat16)
            slope = half + (0.5 * root) * pre * (1.0 - bent * bent) * (1.0 + (3.0 * cube) * square)
            gpre_ref[part, :] = (grad_act * slope).astype(jnp.bfloat16)
        grad = dot_nn(nmt_ref[...], gpre_ref[...]).astype(jnp.bfloat16)
        shape = up_keep_ref.shape[1:]
        up_keep_ref[0] = grad[: width // 2].reshape(shape)
        up_send_ref[0] = grad[width // 2 :].reshape(shape)

    @pl.when(phase == 1)
    def _():
        up = up_ref[:, 0].reshape(width, -1)
        down = down_ref[:, 0].reshape(width, -1)
        out_ref[...] += dot_nt(act_ref[...], down)
        gn_ref[...] += dot_nt(gpre_ref[...], up)
        grad = dot_nn(cott_ref[...], act_ref[...]).astype(jnp.bfloat16)
        shape = (down_keep_ref.shape[0],) + down_keep_ref.shape[2:]
        down_keep_ref[:, 0] = grad[: width // 2].reshape(shape)
        down_send_ref[:, 0] = grad[width // 2 :].reshape(shape)

    @pl.when((tile == pl.num_programs(0) - 1) & (phase == 1))
    def _():
        rows = scales_ref.shape[0]
        per_row = count // rows
        for row in range(rows):
            scale = scales_ref[row : row + 1, width:]
            total = jnp.zeros((1, width), jnp.float32)
            for at in range(row * per_row, (row + 1) * per_row, chunk):
                part = slice(at, at + chunk)
                hidden = hidden_ref[part, :]
                layer_ref[part, :] = (hidden + out_ref[part, :]).astype(jnp.bfloat16)
                hat, inverse = normalize(hidden)
                grad = gn_ref[part, :]
                total += jnp.sum(grad * hat, axis=0, keepdims=True)
                back = cot_ref[part, :].astype(jnp.float32) + normalize_back(grad * scale, hat, inverse)
                grad_hidden_ref[part, :] = back
                grad_attn_ref[part, :] = back.astype(jnp.bfloat16)
            gscale_ref[row : row + 1, :] = total


def mlp(me, normed, cotangent, hidden, scales, w_all, skip, hidden_cols):
    rows, length, width = hidden.shape
    count = rows * length
    chunks, halves, high, columns = w_all.shape
    tile = 512
    per_half = hidden_cols // tile
    first = skip // tile
    quarter = chunks // 4
    flat = (count, width)
    up_at = lambda f, s, me: (0, f // per_half, 0, first + f % per_half)
    down_at = lambda f, s, me: (0, f // per_half, 0, first + per_half + f % per_half)
    up_out = pl.BlockSpec(
        (1, 2, quarter, high, tile), lambda f, s, me: ((f // per_half) ^ me[1], 0, 0, 0, f % per_half)
    )
    down_out = pl.BlockSpec(
        (2, 1, quarter, high, tile), lambda f, s, me: (0, (f // per_half) ^ me[1], 0, 0, f % per_half)
    )
    grads = jax.ShapeDtypeStruct((2, 2, quarter, high, hidden_cols), jnp.bfloat16)
    return pl.pallas_call(
        mlp_kernel,
        grid_spec=pltpu.PrefetchScalarGridSpec(
            num_scalar_prefetch=1,
            grid=(halves * per_half, 2),
            in_specs=[
                whole(flat),
                whole(flat),
                whole(flat),
                whole(scales.shape),
                pl.BlockSpec((chunks, 1, high, tile), up_at),
                pl.BlockSpec((chunks, 1, high, tile), down_at),
            ],
            out_specs=[up_out, up_out, down_out, down_out]
            + [whole(flat), whole(flat), whole(flat), whole((rows, width))],
            scratch_shapes=[
                pltpu.VMEM((width, count), jnp.bfloat16),
                pltpu.VMEM((width, count), jnp.bfloat16),
                pltpu.VMEM(flat, jnp.float32),
                pltpu.VMEM(flat, jnp.float32),
                pltpu.VMEM((count, tile), jnp.bfloat16),
                pltpu.VMEM((count, tile), jnp.bfloat16),
            ],
        ),
        out_shape=[grads] * 4
        + [
            jax.ShapeDtypeStruct(flat, jnp.bfloat16),
            jax.ShapeDtypeStruct(flat, jnp.float32),
            jax.ShapeDtypeStruct(flat, jnp.bfloat16),
            jax.ShapeDtypeStruct((rows, width), jnp.float32),
        ],
        compiler_params=params(60),
        cost_estimate=cost(12 * count * width * halves * hidden_cols, 4 * w_all.size + 16 * count * width),
        name="mlp",
    )(me, normed.reshape(flat), cotangent.reshape(flat), hidden.reshape(flat), scales, w_all, w_all)


def grad_mixed_kernel(grad_ref, w_ref, out_ref):
    halves = w_ref.shape[1]
    per_half = out_ref.shape[0] // halves
    grad = grad_ref[...]
    pair = out_ref.shape[3]
    for half in range(halves):
        out = dot_nn(grad, w_ref[:, half].reshape(grad.shape[1], -1)).astype(jnp.bfloat16)
        for group in range(per_half):
            out_ref[half * per_half + group, 0] = out[:, group * pair : (group + 1) * pair]


def grad_mixed_of(grad_attn, w_all, mixed_shape, columns):
    groups, rows, length, pair = mixed_shape
    chunks, halves, high, _ = w_all.shape
    width = grad_attn.shape[1]
    tile = 256
    tiles = length // tile
    return pl.pallas_call(
        grad_mixed_kernel,
        grid=(rows * tiles,),
        in_specs=[
            pl.BlockSpec((tile, width), lambda i: (i, 0)),
            whole((chunks, halves, high, columns)),
        ],
        out_specs=pl.BlockSpec((groups, 1, tile, pair), lambda i: (0, i // tiles, i % tiles, 0)),
        out_shape=jax.ShapeDtypeStruct(mixed_shape, jnp.bfloat16),
        compiler_params=params(),
        cost_estimate=cost(2 * rows * length * width * width, 8 * rows * length * width),
        name="grad_mixed",
    )(grad_attn, w_all)


def grad_proj_kernel(me_ref, grad_ref, mixed_ref, keep_ref, send_ref, turned_ref):
    count, width = grad_ref.shape

    @pl.when(pl.program_id(0) == 0)
    def _():
        turned_apart(turned_ref, grad_ref[...], me_ref[0], 4 * keep_ref.shape[2])

    pair = mixed_ref.shape[3]
    mixed = jnp.concatenate(
        [mixed_ref[i].reshape(count, pair) for i in range(mixed_ref.shape[0])], axis=1
    )
    grad = dot_nn(turned_ref[...], mixed).astype(jnp.bfloat16)
    shape = keep_ref.shape[1:]
    keep_ref[0] = grad[: width // 2].reshape(shape)
    send_ref[0] = grad[width // 2 :].reshape(shape)


def grad_proj_of(me, grad_attn, mixed, chunks, halves, columns):
    groups, rows, length, pair = mixed.shape
    count, width = grad_attn.shape
    high = width // chunks
    shape = (halves, 2, chunks // 4, high, columns)
    one = pl.BlockSpec((1,) + shape[1:], lambda h, me: (h ^ me[1], 0, 0, 0, 0))
    return pl.pallas_call(
        grad_proj_kernel,
        grid_spec=pltpu.PrefetchScalarGridSpec(
            num_scalar_prefetch=1,
            grid=(halves,),
            in_specs=[
                whole(grad_attn.shape),
                pl.BlockSpec((groups // halves, rows, length, pair), lambda h, me: (h, 0, 0, 0)),
            ],
            out_specs=[one, one],
            scratch_shapes=[pltpu.VMEM((width, count), jnp.bfloat16)],
        ),
        out_shape=[jax.ShapeDtypeStruct(shape, jnp.bfloat16)] * 2,
        compiler_params=params(),
        cost_estimate=cost(2 * count * width * width, 6 * count * width),
        name="grad_proj",
    )(me, grad_attn, mixed)


def first_norm_kernel(gq_ref, tok_ref, grad_hidden_ref, w_ref, scales_ref, out_ref, gscale_ref, *, tiles, q_cols):
    step = pl.program_id(0)
    row = step // tiles
    halves = w_ref.shape[1]
    per_half = gq_ref.shape[0] // halves
    values = tok_ref[0].astype(jnp.float32)
    width = values.shape[1]
    grad = jnp.zeros(values.shape, jnp.float32)
    for half in range(halves):
        weights = w_ref[:, half, :, :q_cols].reshape(width, q_cols)
        grad += dot_nt(joined(gq_ref, half * per_half, per_half), weights)
    hat, inverse = normalize(values)
    total = jnp.sum(grad * hat, axis=0, keepdims=True)

    @pl.when(step % tiles == 0)
    def _():
        gscale_ref[pl.ds(row, 1), :] = total

    @pl.when(step % tiles != 0)
    def _():
        gscale_ref[pl.ds(row, 1), :] += total

    back = normalize_back(grad * scales_ref[pl.ds(row, 1), :width], hat, inverse)
    out_ref[0] = (grad_hidden_ref[0] + back).astype(jnp.bfloat16)


def first_norm_back(grad_qkv, tokens, grad_hidden, w_all, scales, q_cols):
    rows, length, width = tokens.shape
    groups, _, _, pair = grad_qkv.shape
    tile = 256
    tiles = length // tile
    one = pl.BlockSpec((1, tile, width), lambda i: (i // tiles, i % tiles, 0))
    return pl.pallas_call(
        functools.partial(first_norm_kernel, tiles=tiles, q_cols=q_cols),
        grid=(rows * tiles,),
        in_specs=[
            pl.BlockSpec((groups, 1, tile, pair), lambda i: (0, i // tiles, i % tiles, 0)),
            one,
            one,
            whole(w_all.shape),
            whole(scales.shape),
        ],
        out_specs=[one, whole((rows, width))],
        out_shape=[
            jax.ShapeDtypeStruct(tokens.shape, jnp.bfloat16),
            jax.ShapeDtypeStruct((rows, width), jnp.float32),
        ],
        compiler_params=params(),
        cost_estimate=cost(2 * rows * length * width * groups * pair, 2 * w_all.size + 20 * tokens.size),
        name="first_norm_back",
    )(grad_qkv, tokens, grad_hidden, w_all, scales)


def grad_qkv_kernel(
    me_ref, normed_ref, gq_ref, tet_ref, gs_ref,
    a_keep_ref, a_send_ref, b_keep_ref, b_send_ref, t_keep_ref, t_send_ref,
    turned_ref, tet_apart_ref, *, pairs, chunks, folds, t_cols,
):
    half = pl.program_id(0)
    part = pl.program_id(1)
    count, width = normed_ref.shape

    @pl.when((half == 0) & (part == 0))
    def _():
        turned_apart(turned_ref, normed_ref[...], me_ref[0], chunks)
        bits = chunks.bit_length() - 1
        high = tet_ref.shape[0] // chunks
        for chunk in range(chunks):
            apart = chunk ^ me_ref[0]
            place = 0
            for bit in range(bits):
                place += ((apart >> bit) & 1) << (bits - 1 - bit)
            tet_apart_ref[pl.ds(pl.multiple_of(place * high, high), high), :] = tet_ref[
                chunk * high : (chunk + 1) * high, :
            ]

    def grad():
        return dot_nn(turned_ref[...], gq_ref[0].reshape(count, -1)).astype(jnp.bfloat16)

    @pl.when(part < pairs // 2)
    def _():
        found = grad()
        shape = a_keep_ref.shape[1:]
        a_keep_ref[0] = found[: width // 2].reshape(shape)
        a_send_ref[0] = found[width // 2 :].reshape(shape)

    @pl.when((part >= pairs // 2) & (part < pairs))
    def _():
        found = grad()
        shape = (b_keep_ref.shape[0],) + b_keep_ref.shape[2:]
        b_keep_ref[:, 0] = found[: width // 2].reshape(shape)
        b_send_ref[:, 0] = found[width // 2 :].reshape(shape)

    @pl.when(part == pairs)
    def _():
        k_rows = tet_ref.shape[0] // chunks
        shape = t_keep_ref.shape[1:3] + (k_rows, t_cols)
        for fold in range(folds):
            at = pl.multiple_of((half * folds + fold) * t_cols, t_cols)
            total = jnp.zeros((chunks * k_rows, t_cols), jnp.float32)
            for row in range(gs_ref.shape[0]):
                total += tet_apart_ref[:, row : row + 1] * gs_ref[row : row + 1, pl.ds(at, t_cols)]
            total = total.astype(jnp.bfloat16)
            middle = chunks * k_rows // 2
            t_keep_ref[0, :, :, fold * k_rows : (fold + 1) * k_rows, :] = total[:middle].reshape(shape)
            t_send_ref[0, :, :, fold * k_rows : (fold + 1) * k_rows, :] = total[middle:].reshape(shape)


def grad_qkv_of(me, normed, grad_qkv, time_embed, grad_scales, chunks, halves, k_rows, t_cols):
    rows, length, width = normed.shape
    groups, _, _, pair = grad_qkv.shape
    pairs = groups // halves
    high = width // chunks
    count = rows * length
    quarter = chunks // 4
    some = pairs // 2
    turned = time_embed.T
    a_out = pl.BlockSpec(
        (1, 2, quarter, high, pair), lambda h, j, me: (h ^ me[1], 0, 0, 0, jnp.minimum(j, some - 1))
    )
    b_out = pl.BlockSpec(
        (2, 1, quarter, high, pair),
        lambda h, j, me: (0, h ^ me[1], 0, 0, jnp.clip(j - some, 0, some - 1)),
    )
    t_out = pl.BlockSpec((1, 2, quarter, high, t_cols), lambda h, j, me: (h ^ me[1], 0, 0, 0, 0))
    wide = jax.ShapeDtypeStruct((halves, 2, quarter, high, some * pair), jnp.bfloat16)
    thin = jax.ShapeDtypeStruct((halves, 2, quarter, high, t_cols), jnp.bfloat16)
    return pl.pallas_call(
        functools.partial(
            grad_qkv_kernel, pairs=pairs, chunks=chunks, folds=high // k_rows, t_cols=t_cols
        ),
        grid_spec=pltpu.PrefetchScalarGridSpec(
            num_scalar_prefetch=1,
            grid=(halves, pairs + 1),
            in_specs=[
                whole((count, width)),
                pl.BlockSpec(
                    (1, rows, length, pair),
                    lambda h, j, me: (h * pairs + jnp.minimum(j, pairs - 1), 0, 0, 0),
                ),
                whole(turned.shape),
                whole(grad_scales.shape),
            ],
            out_specs=[a_out, a_out, b_out, b_out, t_out, t_out],
            scratch_shapes=[
                pltpu.VMEM((width, count), jnp.bfloat16),
                pltpu.VMEM(turned.shape, jnp.float32),
            ],
        ),
        out_shape=[wide] * 4 + [thin] * 2,
        compiler_params=params(),
        cost_estimate=cost(2 * count * width * groups * pair, 6 * count * width),
        name="grad_qkv",
    )(me, normed.reshape(count, width), grad_qkv, turned, grad_scales)


def across(values, axis, apart):
    size = lax.axis_size(axis)
    return lax.ppermute(values, axis, [(i, i ^ apart) for i in range(size)])


def summed(parts, index):
    total = parts[0][index].astype(jnp.float32)
    for part in parts[1:]:
        total += part[index].astype(jnp.float32)
    return total


STAGES = {"x": ("ctx", 2), "y": ("tp", 1)}


def scatter_sum(keep, send, order):
    parts = [keep, across(send, "ctx", 1)]
    for name in order:
        axis, apart = STAGES[name]
        given = across(summed(parts, 1).astype(jnp.bfloat16), axis, apart)
        parts = [part[0] for part in parts] + [given]
    given = across(summed(parts, slice(2, 4)).astype(jnp.bfloat16), "fsdp", 1)
    parts = [part[:2] for part in parts] + [given]
    given = across(summed(parts, 1).astype(jnp.bfloat16), "fsdp", 2)
    parts = [part[0] for part in parts] + [given]
    return summed(parts, slice(None))


def listed_table(block_pairs, pair_counts, row_blocks, ctx_size):
    rows, _, slots, _ = block_pairs.shape
    packed = jnp.concatenate([block_pairs.reshape(rows, 1, slots * 2), pair_counts[:, :, None]], axis=2)
    packed = jnp.concatenate(
        [packed] + [across(packed, "ctx", apart) for apart in range(1, ctx_size)], axis=1
    )
    pairs = packed[:, :, : slots * 2].reshape(rows, ctx_size, slots, 2)
    live = jnp.arange(slots, dtype=jnp.int32)[None, None, :] < packed[:, :, slots * 2 :]
    owner = lax.axis_index("ctx") ^ jnp.arange(ctx_size, dtype=jnp.int32)[None, :, None]
    base = owner * (row_blocks // ctx_size)
    code = jnp.where(live, (base + pairs[..., 0]) * row_blocks + pairs[..., 1], -1)
    code = code.reshape(rows, ctx_size * slots)
    cells = jnp.arange(row_blocks * row_blocks, dtype=jnp.int32)
    return jnp.any(code[:, :, None] == cells[None, None, :], axis=1).astype(jnp.int32)


EVERY = ("fsdp", "ctx", "tp")
GROUP = ("ctx", "tp")


def spread_body(
    tokens, time_embed, segment_ids, block_pairs, pair_counts,
    w_time, w_qkv, w_out, w_up, w_down, cotangent,
):
    rows, length, width = tokens.shape
    chunks = width // w_qkv.shape[0]
    halves = lax.axis_size("tp")
    high = w_qkv.shape[0]
    q_cols, o_cols, f_cols = w_qkv.shape[1], w_out.shape[1], w_up.shape[1]
    k_rows = w_time.shape[0]
    t_all = w_time.shape[1] // halves
    folds = high // k_rows
    t_cols = t_all // folds
    mine = lax.axis_index("tp")
    me = jnp.stack([lax.axis_index("fsdp") * lax.axis_size("ctx") + lax.axis_index("ctx"), mine])
    time_part = lax.dynamic_slice_in_dim(w_time, mine * t_all, t_all, 1)
    time_part = time_part.reshape(k_rows, folds, t_cols).transpose(1, 0, 2).reshape(high, t_cols)
    first = jnp.concatenate([w_qkv, time_part], axis=1).astype(jnp.bfloat16)
    second = jnp.concatenate([w_out, w_up, w_down], axis=1).astype(jnp.bfloat16)
    first = lax.all_gather(first, EVERY, axis=0, tiled=True).reshape(chunks, halves, high, -1)
    second = lax.all_gather(second, EVERY, axis=0, tiled=True).reshape(chunks, halves, high, -1)

    row_blocks = segment_ids.shape[1] // BLK
    listed = listed_table(block_pairs, pair_counts, row_blocks, lax.axis_size("ctx"))
    edges = jnp.concatenate([segment_ids[:, ::BLK], segment_ids[:, BLK - 1 :: BLK]], axis=1)
    segc = segment_ids[:, :, None]
    segr = segment_ids[:, None, :]

    qkv, normed, scales = project(time_embed, tokens, first, k_rows, q_cols, t_cols)
    qkv = lax.all_to_all(qkv, GROUP, 0, 0, tiled=True)
    mixed_own, lse = attend(listed, edges, qkv, segc, segr)
    mixed = lax.all_to_all(mixed_own, GROUP, 0, 0, tiled=True)
    hidden, normed_mlp = outward(mixed, tokens, second, scales, o_cols)
    up_keep, up_send, down_keep, down_send, layer_out, grad_hidden, grad_attn, gscale_mlp = mlp(
        me, normed_mlp, cotangent, hidden, scales, second, o_cols, f_cols
    )
    grad_mixed = grad_mixed_of(grad_attn, second, mixed.shape, o_cols)
    grad_mixed = lax.all_to_all(grad_mixed, GROUP, 0, 0, tiled=True)
    out_keep, out_send = grad_proj_of(me, grad_attn, mixed, chunks, halves, o_cols)
    grad_down = scatter_sum(down_keep, down_send, "xy")
    grad_up = scatter_sum(up_keep, up_send, "yx")
    grad_mixed, out_keep, out_send = lax.optimization_barrier((grad_mixed, out_keep, out_send))
    grad_out = scatter_sum(out_keep, out_send, "yx")
    grad_qkv = attend_back(listed, edges, qkv, grad_mixed, mixed_own, lse, segc, segr)
    grad_qkv = lax.all_to_all(grad_qkv, GROUP, 0, 0, tiled=True)
    grad_tokens, gscale_attn = first_norm_back(
        grad_qkv, tokens, grad_hidden.reshape(tokens.shape), first, scales, q_cols
    )
    grad_scales = jnp.concatenate([gscale_attn, gscale_mlp], axis=1)
    a_keep, a_send, b_keep, b_send, t_keep, t_send = grad_qkv_of(
        me, normed, grad_qkv, time_embed, grad_scales, chunks, halves, k_rows, t_cols
    )
    grad_time = scatter_sum(t_keep, t_send, "yx").reshape(folds, k_rows, t_cols)
    grad_time = grad_time.transpose(1, 0, 2).reshape(k_rows, t_all)
    other = across(grad_time.astype(jnp.bfloat16), "tp", 1).astype(jnp.float32)
    grad_time = jnp.concatenate(
        [jnp.where(mine == 0, grad_time, other), jnp.where(mine == 0, other, grad_time)], axis=1
    )
    grad_w_qkv = jnp.concatenate(
        [scatter_sum(a_keep, a_send, "yx"), scatter_sum(b_keep, b_send, "xy")], axis=1
    )
    return (
        layer_out.reshape(tokens.shape),
        grad_tokens,
        grad_time,
        grad_w_qkv,
        grad_out,
        grad_up,
        grad_down,
    )


def choose(*args):
    tokens, w_qkv, w_out, w_up = args[0], args[6], args[7], args[8]
    group = lax.axis_size("ctx") * lax.axis_size("tp")
    heads_pair = 6 * HEAD_DIM
    fits = (
        (lax.axis_size("fsdp"), lax.axis_size("ctx"), lax.axis_size("tp")) == (4, 4, 2)
        and tokens.shape[1] == BLK
        and group * BLK == args[2].shape[1]
        and w_qkv.shape[1] * lax.axis_size("tp") == group * heads_pair
        and w_out.shape[1] % 512 == 0
        and w_up.shape[1] % 512 == 0
        and w_qkv.shape[0] % args[5].shape[0] == 0
    )
    return spread_body(*args) if fits else body(*args)


def solution(mesh):
    placed = (
        P("fsdp", ("ctx", "tp"), None),
        P("fsdp", None),
        P("fsdp", None),
        P("fsdp", "ctx", None, None),
        P("fsdp", "ctx"),
        P(("fsdp", "ctx"), None),
        P(("fsdp", "ctx"), "tp"),
        P(("fsdp", "ctx"), "tp"),
        P(("fsdp", "ctx"), "tp"),
        P(("fsdp", "ctx"), "tp"),
        P("fsdp", ("ctx", "tp"), None),
    )
    return jax.shard_map(
        choose,
        mesh=mesh,
        in_specs=placed,
        out_specs=(
            P("fsdp", ("ctx", "tp"), None),
            P("fsdp", ("ctx", "tp"), None),
            P(("fsdp", "ctx"), None),
            P(("fsdp", "ctx"), "tp"),
            P(("fsdp", "ctx"), "tp"),
            P(("fsdp", "ctx"), "tp"),
            P(("fsdp", "ctx"), "tp"),
        ),
        check_vma=False,
    )
```

```python
import functools

import jax
import jax.numpy as jnp
from jax import lax
from jax.experimental import pallas as pl
from jax.experimental.pallas import tpu as pltpu
from jax.sharding import PartitionSpec as P

HEAD_DIM = 64
BLK = 512


epsilon = 1e-05
highest = lax.Precision.HIGHEST
masked_out = -1e30


def normalize(values):
    mean_value = jnp.mean(values, axis=-1, keepdims=True)
    centred = values - mean_value
    variance = jnp.mean(centred * centred, axis=-1, keepdims=True)
    inverse = lax.rsqrt(variance + epsilon)
    return (centred * inverse, inverse)


def normalize_back(grad_hat, normal_hat, inverse):
    first_mean = jnp.mean(grad_hat, axis=-1, keepdims=True)
    second_mean = jnp.mean(grad_hat * normal_hat, axis=-1, keepdims=True)
    return inverse * (grad_hat - first_mean - normal_hat * second_mean)


def smooth_gate(values):
    return jax.nn.gelu(values, approximate=True)


def block_scores(pair_entry, query_rows, key_rows, seg_row, offset):
    query_start = pair_entry[0] * BLK
    key_start = pair_entry[1] * BLK
    query_block = lax.dynamic_slice_in_dim(query_rows, query_start, BLK, 0)
    key_block = lax.dynamic_slice_in_dim(key_rows, key_start, BLK, 0)
    seg_query = lax.dynamic_slice_in_dim(seg_row, offset + query_start, BLK, 0)
    seg_keys = lax.dynamic_slice_in_dim(seg_row, key_start, BLK, 0)
    steps_in = jnp.arange(BLK, dtype=jnp.int32)
    allowed = (seg_query[:, None] == seg_keys[None, :]) & (
        key_start + steps_in[None, :] <= offset + query_start + steps_in[:, None]
    )
    scores = jnp.einsum(
        "qhe,khe->hqk", query_block, key_block, preferred_element_type=jnp.float32
    ) * HEAD_DIM ** (-0.5)
    return (query_block, key_block, query_start, key_start, allowed, scores)


def attend_forward(query_rows, key_rows, value_rows, seg_row, pair_rows, pair_total, offset):
    length_here, head_count, _ = query_rows.shape

    def statistic_step(pair_index, carried):
        running_max, running_sum = carried
        _, _, query_start, _, allowed, scores = block_scores(
            pair_rows[pair_index], query_rows, key_rows, seg_row, offset
        )
        scores = jnp.where(allowed[None], scores, masked_out)
        old_max = lax.dynamic_slice_in_dim(running_max, query_start, BLK, 1)
        old_sum = lax.dynamic_slice_in_dim(running_sum, query_start, BLK, 1)
        new_max = jnp.maximum(old_max, jnp.max(scores, axis=-1))
        weights = jnp.where(allowed[None], jnp.exp(scores - new_max[:, :, None]), 0.0)
        new_sum = old_sum * jnp.exp(old_max - new_max) + jnp.sum(weights, axis=-1)
        return (
            lax.dynamic_update_slice_in_dim(running_max, new_max, query_start, 1),
            lax.dynamic_update_slice_in_dim(running_sum, new_sum, query_start, 1),
        )

    start_max = jnp.full((head_count, length_here), masked_out, jnp.float32)
    start_sum = jnp.zeros((head_count, length_here), jnp.float32)
    running_max, running_sum = lax.fori_loop(0, pair_total, statistic_step, (start_max, start_sum))
    log_total = running_max + jnp.log(running_sum)

    def output_step(pair_index, accumulated):
        _, _, query_start, key_start, allowed, scores = block_scores(
            pair_rows[pair_index], query_rows, key_rows, seg_row, offset
        )
        block_log = lax.dynamic_slice_in_dim(log_total, query_start, BLK, 1)
        probabilities = jnp.where(
            allowed[None], jnp.exp(scores - block_log[:, :, None]), 0.0
        ).astype(jnp.bfloat16)
        value_block = lax.dynamic_slice_in_dim(value_rows, key_start, BLK, 0)
        addition = jnp.einsum(
            "hqk,khe->qhe", probabilities, value_block, preferred_element_type=jnp.float32
        )
        previous = lax.dynamic_slice_in_dim(accumulated, query_start, BLK, 0)
        return lax.dynamic_update_slice_in_dim(accumulated, previous + addition, query_start, 0)

    mixed_rows = lax.fori_loop(0, pair_total, output_step, jnp.zeros(query_rows.shape, jnp.float32))
    return (mixed_rows, log_total)


def attend_backward(
    query_rows,
    key_rows,
    value_rows,
    seg_row,
    pair_rows,
    pair_total,
    offset,
    log_total,
    grad_mixed,
    inner_sums,
):
    scale_factor = HEAD_DIM ** (-0.5)

    def add_block(whole, start_at, addition):
        previous = lax.dynamic_slice_in_dim(whole, start_at, BLK, 0)
        return lax.dynamic_update_slice_in_dim(whole, previous + addition, start_at, 0)

    def gradient_step(pair_index, carried):
        grad_query, grad_keys, grad_values = carried
        query_block, key_block, query_start, key_start, allowed, scores = block_scores(
            pair_rows[pair_index], query_rows, key_rows, seg_row, offset
        )
        block_log = lax.dynamic_slice_in_dim(log_total, query_start, BLK, 1)
        probabilities = jnp.where(allowed[None], jnp.exp(scores - block_log[:, :, None]), 0.0)
        grad_block = lax.dynamic_slice_in_dim(grad_mixed, query_start, BLK, 0)
        value_block = lax.dynamic_slice_in_dim(value_rows, key_start, BLK, 0)
        grad_probs = jnp.einsum(
            "qhe,khe->hqk", grad_block, value_block, preferred_element_type=jnp.float32
        )
        inner_block = lax.dynamic_slice_in_dim(inner_sums, query_start, BLK, 1)
        grad_scores = (probabilities * (grad_probs - inner_block[:, :, None])).astype(jnp.bfloat16)
        query_add = (
            jnp.einsum("hqk,khe->qhe", grad_scores, key_block, preferred_element_type=jnp.float32)
            * scale_factor
        )
        key_add = (
            jnp.einsum("hqk,qhe->khe", grad_scores, query_block, preferred_element_type=jnp.float32)
            * scale_factor
        )
        value_add = jnp.einsum(
            "hqk,qhe->khe",
            probabilities.astype(jnp.bfloat16),
            grad_block,
            preferred_element_type=jnp.float32,
        )
        return (
            add_block(grad_query, query_start, query_add),
            add_block(grad_keys, key_start, key_add),
            add_block(grad_values, key_start, value_add),
        )

    start_state = (
        jnp.zeros(query_rows.shape, jnp.float32),
        jnp.zeros(key_rows.shape, jnp.float32),
        jnp.zeros(value_rows.shape, jnp.float32),
    )
    return lax.fori_loop(0, pair_total, gradient_step, start_state)


def body(
    tokens,
    time_embed,
    segment_ids,
    block_pairs,
    pair_counts,
    w_time,
    w_qkv,
    w_out,
    w_up,
    w_down,
    cotangent,
):
    row_count, local_len, model_width = tokens.shape
    time_all, qkv_all, out_all, up_all, down_all = (
        lax.all_gather(w_time.astype(jnp.bfloat16), ("fsdp", "ctx"), axis=0, tiled=True),
        lax.all_gather(w_qkv.astype(jnp.bfloat16), ("fsdp", "ctx"), axis=0, tiled=True),
        lax.all_gather(w_out.astype(jnp.bfloat16), ("fsdp", "ctx"), axis=0, tiled=True),
        lax.all_gather(w_up.astype(jnp.bfloat16), ("fsdp", "ctx"), axis=0, tiled=True),
        lax.all_gather(w_down.astype(jnp.bfloat16), ("fsdp", "ctx"), axis=0, tiled=True),
    )
    scales = 1.0 + jnp.dot(time_embed, time_all.astype(jnp.float32), precision=highest)
    scale_attn = scales[:, None, :model_width]
    scale_mlp = scales[:, None, model_width:]
    x_input = tokens.astype(jnp.float32)
    hat_attn, inverse_attn = normalize(x_input)
    normed = (hat_attn * scale_attn).astype(jnp.bfloat16)
    normed_all = lax.all_gather(normed, "tp", axis=1, tiled=True)
    ctx_len = normed_all.shape[1]
    head_count = qkv_all.shape[1] // (3 * HEAD_DIM)
    projected = jnp.einsum("rtd,dc->rtc", normed_all, qkv_all, preferred_element_type=jnp.float32)
    projected = projected.astype(jnp.bfloat16).reshape(row_count, ctx_len, head_count, 3, HEAD_DIM)
    query_all = projected[:, :, :, 0]
    key_part = projected[:, :, :, 1]
    value_part = projected[:, :, :, 2]
    key_all, value_all = (
        lax.all_gather(key_part, "ctx", axis=1, tiled=True),
        lax.all_gather(value_part, "ctx", axis=1, tiled=True),
    )
    offset = lax.axis_index("ctx") * ctx_len
    mixed_list = []
    log_list = []
    for row_index in range(row_count):
        mixed_rows, log_total = attend_forward(
            query_all[row_index],
            key_all[row_index],
            value_all[row_index],
            segment_ids[row_index],
            block_pairs[row_index, 0],
            pair_counts[row_index, 0],
            offset,
        )
        mixed_list.append(mixed_rows)
        log_list.append(log_total)
    mixed_exact = jnp.stack(mixed_list)
    mixed_heads = mixed_exact.astype(jnp.bfloat16).reshape(
        row_count, ctx_len, head_count * HEAD_DIM
    )
    attn_part = jnp.einsum("rtc,dc->rtd", mixed_heads, out_all, preferred_element_type=jnp.float32)
    attn_local = lax.psum_scatter(
        attn_part.astype(jnp.bfloat16), "tp", scatter_dimension=1, tiled=True
    ).astype(jnp.float32)
    hidden = x_input + attn_local
    hat_mlp, inverse_mlp = normalize(hidden)
    normed_mlp = (hat_mlp * scale_mlp).astype(jnp.bfloat16)
    mlp_all = lax.all_gather(normed_mlp, "tp", axis=1, tiled=True)
    pre_act = jnp.einsum("rtd,df->rtf", mlp_all, up_all, preferred_element_type=jnp.float32)
    activated = smooth_gate(pre_act).astype(jnp.bfloat16)
    mlp_part = jnp.einsum("rtf,df->rtd", activated, down_all, preferred_element_type=jnp.float32)
    mlp_local = lax.psum_scatter(
        mlp_part.astype(jnp.bfloat16), "tp", scatter_dimension=1, tiled=True
    ).astype(jnp.float32)
    grad_all = lax.all_gather(cotangent, "tp", axis=1, tiled=True)
    grad_act = jnp.einsum("rtd,df->rtf", grad_all, down_all, preferred_element_type=jnp.float32)
    _, gate_back = jax.vjp(smooth_gate, pre_act)
    grad_pre = gate_back(grad_act)[0].astype(jnp.bfloat16)
    grad_down = jnp.einsum("rtd,rtf->df", grad_all, activated, preferred_element_type=jnp.float32)
    grad_up = jnp.einsum("rtd,rtf->df", mlp_all, grad_pre, preferred_element_type=jnp.float32)
    norm_part = jnp.einsum("rtf,df->rtd", grad_pre, up_all, preferred_element_type=jnp.float32)
    grad_normed_mlp = lax.psum_scatter(
        norm_part.astype(jnp.bfloat16), "tp", scatter_dimension=1, tiled=True
    ).astype(jnp.float32)
    layer_out = (hidden + mlp_local).astype(jnp.bfloat16)
    grad_output = cotangent.astype(jnp.float32)
    grad_scale_mlp = jnp.sum(grad_normed_mlp * hat_mlp, axis=1)
    grad_hidden = grad_output + normalize_back(grad_normed_mlp * scale_mlp, hat_mlp, inverse_mlp)
    grad_attn_all = lax.all_gather(grad_hidden.astype(jnp.bfloat16), "tp", axis=1, tiled=True)
    grad_mixed = jnp.einsum(
        "rtd,dc->rtc", grad_attn_all, out_all, preferred_element_type=jnp.float32
    ).astype(jnp.bfloat16)
    grad_proj = jnp.einsum(
        "rtd,rtc->dc", grad_attn_all, mixed_heads, preferred_element_type=jnp.float32
    )
    grad_mixed = grad_mixed.reshape(row_count, ctx_len, head_count, HEAD_DIM)
    inner_sums = jnp.einsum("rqhe,rqhe->rhq", grad_mixed.astype(jnp.float32), mixed_exact)
    query_grads = []
    key_grads = []
    value_grads = []
    for row_index in range(row_count):
        grad_query, grad_keys, grad_values = attend_backward(
            query_all[row_index],
            key_all[row_index],
            value_all[row_index],
            segment_ids[row_index],
            block_pairs[row_index, 0],
            pair_counts[row_index, 0],
            offset,
            log_list[row_index],
            grad_mixed[row_index],
            inner_sums[row_index],
        )
        query_grads.append(grad_query)
        key_grads.append(grad_keys)
        value_grads.append(grad_values)
    key_local, value_local = (
        lax.psum_scatter(
            jnp.stack(key_grads).astype(jnp.bfloat16), "ctx", scatter_dimension=1, tiled=True
        ).astype(jnp.float32),
        lax.psum_scatter(
            jnp.stack(value_grads).astype(jnp.bfloat16), "ctx", scatter_dimension=1, tiled=True
        ).astype(jnp.float32),
    )
    grad_projected = jnp.stack(
        [
            jnp.stack(query_grads).astype(jnp.bfloat16),
            key_local.astype(jnp.bfloat16),
            value_local.astype(jnp.bfloat16),
        ],
        axis=3,
    )
    grad_projected = grad_projected.reshape(row_count, ctx_len, head_count * 3 * HEAD_DIM)
    grad_qkv = jnp.einsum(
        "rtd,rtc->dc", normed_all, grad_projected, preferred_element_type=jnp.float32
    )
    first_part = jnp.einsum(
        "rtc,dc->rtd", grad_projected, qkv_all, preferred_element_type=jnp.float32
    )
    grad_normed = lax.psum_scatter(
        first_part.astype(jnp.bfloat16), "tp", scatter_dimension=1, tiled=True
    ).astype(jnp.float32)
    grad_scale_attn = jnp.sum(grad_normed * hat_attn, axis=1)
    grad_tokens = grad_hidden + normalize_back(grad_normed * scale_attn, hat_attn, inverse_attn)
    grad_scales = lax.psum(jnp.concatenate([grad_scale_attn, grad_scale_mlp], axis=1), "tp")
    grad_time = jnp.dot(time_embed.T, grad_scales, precision=highest)
    shared = (
        lax.psum_scatter(
            grad_time.astype(jnp.bfloat16), ("fsdp", "ctx"), scatter_dimension=0, tiled=True
        ).astype(jnp.float32),
        lax.psum_scatter(
            grad_qkv.astype(jnp.bfloat16), ("fsdp", "ctx"), scatter_dimension=0, tiled=True
        ).astype(jnp.float32),
        lax.psum_scatter(
            grad_proj.astype(jnp.bfloat16), ("fsdp", "ctx"), scatter_dimension=0, tiled=True
        ).astype(jnp.float32),
        lax.psum_scatter(
            grad_up.astype(jnp.bfloat16), ("fsdp", "ctx"), scatter_dimension=0, tiled=True
        ).astype(jnp.float32),
        lax.psum_scatter(
            grad_down.astype(jnp.bfloat16), ("fsdp", "ctx"), scatter_dimension=0, tiled=True
        ).astype(jnp.float32),
    )
    return (
        layer_out,
        grad_tokens.astype(jnp.bfloat16),
        shared[0],
        shared[1],
        shared[2],
        shared[3],
        shared[4],
    )


def params(limit=58):
    return pltpu.CompilerParams(vmem_limit_bytes=limit * 1024 * 1024)


def whole(shape):
    zeros = (0,) * len(shape)
    return pl.BlockSpec(shape, lambda *_: zeros, pipeline_mode=pl.Buffered(1))


def cost(flops, nbytes, exps=0):
    return pl.CostEstimate(flops=int(flops), bytes_accessed=int(nbytes), transcendentals=int(exps))


def dot_nn(left, right):
    return jnp.dot(left, right, preferred_element_type=jnp.float32)


def dot_nt(left, right):
    return lax.dot_general(left, right, (((1,), (1,)), ((), ())), preferred_element_type=jnp.float32)


def transposed(values):
    return values.astype(jnp.float32).T.astype(values.dtype)


def turned_apart(into_ref, values, chunk_at, chunks):
    turned = values.astype(jnp.float32).T.astype(values.dtype)
    high = turned.shape[0] // chunks
    bits = chunks.bit_length() - 1
    for chunk in range(chunks):
        apart = chunk ^ chunk_at
        place = 0
        for bit in range(bits):
            place += ((apart >> bit) & 1) << (bits - 1 - bit)
        into_ref[pl.ds(pl.multiple_of(place * high, high), high), :] = turned[
            chunk * high : (chunk + 1) * high, :
        ]


def low_lanes(shape):
    return lax.broadcasted_iota(jnp.int32, shape, 1) < HEAD_DIM


def pair_apart(stored):
    first, second, third = stored[:, :128], stored[:, 128:256], stored[:, 256:]
    low = low_lanes(first.shape)
    keys = pltpu.roll(jnp.where(low, third, first), HEAD_DIM, 1)
    return jnp.concatenate(
        [jnp.where(low, first, second), keys, jnp.where(low, second, third)], axis=1
    )


def pair_together(query, keys, values):
    low = low_lanes(query.shape)
    turned = pltpu.roll(keys, HEAD_DIM, 1)
    return jnp.concatenate(
        [jnp.where(low, query, turned), jnp.where(low, values, query), jnp.where(low, turned, values)],
        axis=1,
    )


def time_scales(te_ref, w_ref, scales_ref, k_rows, q_cols, t_cols):
    exact = te_ref[...]
    high = exact.astype(jnp.bfloat16)
    rest = exact - high.astype(jnp.float32)
    middle = rest.astype(jnp.bfloat16)
    last = (rest - middle.astype(jnp.float32)).astype(jnp.bfloat16)
    chunks, halves, tall, _ = w_ref.shape
    folds = tall // k_rows
    for half in range(halves):
        for fold in range(folds):
            weights = w_ref[:, half, fold * k_rows : (fold + 1) * k_rows, q_cols : q_cols + t_cols]
            weights = weights.reshape(chunks * k_rows, t_cols)
            total = dot_nn(last, weights) + dot_nn(middle, weights) + dot_nn(high, weights)
            at = (half * folds + fold) * t_cols
            scales_ref[:, at : at + t_cols] = 1.0 + total


def project_kernel(te_ref, tok_ref, w_ref, qkv_ref, normed_ref, scales_ref, *, row, k_rows, q_cols, t_cols):
    @pl.when(pl.program_id(0) == 0)
    def _():
        time_scales(te_ref, w_ref, scales_ref, k_rows, q_cols, t_cols)

    halves = w_ref.shape[1]
    values = tok_ref[0].astype(jnp.float32)
    width = values.shape[1]
    hat, _ = normalize(values)
    normed = (hat * scales_ref[row : row + 1, :width]).astype(jnp.bfloat16)
    normed_ref[...] = normed
    pair = 6 * HEAD_DIM
    for half in range(halves):
        weights = w_ref[:, half, :, :q_cols].reshape(width, q_cols)
        out = dot_nn(normed, weights)
        for group in range(q_cols // pair):
            qkv_ref[half * (q_cols // pair) + group] = pair_apart(
                out[:, group * pair : (group + 1) * pair]
            ).astype(jnp.bfloat16)


def project(row, time_embed, tokens, w_all, k_rows, q_cols, t_cols):
    rows, length, width = tokens.shape
    chunks, halves = w_all.shape[:2]
    pair = 6 * HEAD_DIM
    groups = halves * q_cols // pair
    tile = 256
    return pl.pallas_call(
        functools.partial(project_kernel, row=row, k_rows=k_rows, q_cols=q_cols, t_cols=t_cols),
        grid=(length // tile,),
        in_specs=[
            whole(time_embed.shape),
            pl.BlockSpec((1, tile, width), lambda i: (row, i, 0)),
            whole(w_all.shape),
        ],
        out_specs=[
            pl.BlockSpec((groups, tile, pair), lambda i: (0, i, 0)),
            pl.BlockSpec((tile, width), lambda i: (i, 0)),
            whole((rows, 2 * width)),
        ],
        out_shape=[
            jax.ShapeDtypeStruct((groups, length, pair), jnp.bfloat16),
            jax.ShapeDtypeStruct((length, width), jnp.bfloat16),
            jax.ShapeDtypeStruct((rows, 2 * width), jnp.float32),
        ],
        compiler_params=params(),
        cost_estimate=cost(2 * length * width * halves * q_cols, 2 * w_all.size + 10 * length * width),
        name="project",
    )(time_embed, tokens, w_all)


def tile_mask(segc_ref, segr_ref, key_block, query_block):
    key_at = pl.multiple_of(key_block * BLK, BLK)
    query_at = pl.multiple_of(query_block * BLK, BLK)
    same = segc_ref[0, pl.ds(key_at, BLK), :] == segr_ref[0, :, pl.ds(query_at, BLK)]
    key_pos = key_at + lax.broadcasted_iota(jnp.int32, (BLK, BLK), 0)
    query_pos = query_at + lax.broadcasted_iota(jnp.int32, (BLK, BLK), 1)
    return same & (key_pos <= query_pos)


def split_heads(values):
    low = low_lanes(values.shape)
    zero = jnp.zeros_like(values)
    return jnp.concatenate([jnp.where(low, values, zero), jnp.where(low, zero, values)], axis=0)


def is_full(edge_ref, row, blocks, key_block, query_block):
    same = edge_ref[row, key_block] == edge_ref[row, blocks + query_block]
    return same & (key_block < query_block)


def attend_kernel(
    listed_ref, edge_ref, qkv_ref, segc_ref, segr_ref, mixed_ref, lse_ref,
    vt_ref, qz_ref, acc_ref, stat_ref, *, row,
):
    blocks = qkv_ref.shape[0]

    def turn(block, carried):
        at = pl.multiple_of(block * BLK, BLK)
        vt_ref[:, pl.ds(at, BLK)] = transposed(qkv_ref[block, :, 256:384])
        return carried

    lax.fori_loop(0, blocks, turn, 0)

    def one_query(query_block, carried):
        query = qkv_ref[query_block, :, :128].astype(jnp.float32) * HEAD_DIM ** (-0.5)
        qz_ref[...] = split_heads(query.astype(jnp.bfloat16))
        stat_ref[0:1, :] = jnp.full((1, 2 * BLK), masked_out, jnp.float32)
        stat_ref[1:2, :] = jnp.zeros((1, 2 * BLK), jnp.float32)
        acc_ref[...] = jnp.zeros(acc_ref.shape, jnp.float32)

        def update(key_block, mask):
            keys = qkv_ref[key_block, :, 128:256]
            at = pl.multiple_of(key_block * BLK, BLK)
            parts = [slice(head * BLK, (head + 1) * BLK) for head in range(2)]
            values = [vt_ref[h * HEAD_DIM : (h + 1) * HEAD_DIM, pl.ds(at, BLK)] for h in range(2)]
            old_max = [stat_ref[0:1, part] for part in parts]
            old_sum = [stat_ref[1:2, part] for part in parts]
            old_acc = [acc_ref[:, part] for part in parts]
            scores = [dot_nt(keys, qz_ref[part, :]) for part in parts]
            if mask is not None:
                scores = [jnp.where(mask, one, masked_out) for one in scores]
            new_max, new_sum, new_acc = [], [], []
            for head in range(2):
                top = jnp.maximum(old_max[head], jnp.max(scores[head], axis=0, keepdims=True))
                weights = jnp.exp(scores[head] - top)
                shrink = jnp.exp(old_max[head] - top)
                new_max.append(top)
                new_sum.append(old_sum[head] * shrink + jnp.sum(weights, axis=0, keepdims=True))
                new_acc.append(old_acc[head] * shrink + dot_nn(values[head], weights.astype(jnp.bfloat16)))
            for head, part in enumerate(parts):
                stat_ref[0:1, part] = new_max[head]
                stat_ref[1:2, part] = new_sum[head]
                acc_ref[:, part] = new_acc[head]

        def one_key(key_block, carried):
            listed = listed_ref[row, query_block * blocks + key_block] != 0
            full = is_full(edge_ref, row, blocks, key_block, query_block)

            @pl.when(listed & full)
            def _():
                update(key_block, None)

            @pl.when(listed & jnp.logical_not(full))
            def _():
                update(key_block, tile_mask(segc_ref, segr_ref, key_block, query_block))

            return carried

        lax.fori_loop(0, query_block + 1, one_key, 0)
        total = stat_ref[1:2, :]
        mixed = acc_ref[...] / total
        mixed = jnp.concatenate([mixed[:, :BLK], mixed[:, BLK:]], axis=0).T
        mixed_ref[query_block] = mixed.astype(jnp.bfloat16)
        log_total = stat_ref[0:1, :] + jnp.log(total)
        at = pl.multiple_of(query_block * BLK, BLK)
        lse_ref[0:1, pl.ds(at, BLK)] = log_total[:, :BLK]
        lse_ref[1:2, pl.ds(at, BLK)] = log_total[:, BLK:]
        return carried

    lax.fori_loop(0, blocks, one_query, 0)


def attend(row, listed, edges, qkv, segc, segr):
    blocks, blk, width = qkv.shape
    length = blocks * blk
    pair = 2 * HEAD_DIM
    return pl.pallas_call(
        functools.partial(attend_kernel, row=row),
        grid_spec=pltpu.PrefetchScalarGridSpec(
            num_scalar_prefetch=2,
            grid=(1,),
            in_specs=[
                whole(qkv.shape),
                pl.BlockSpec((1, length, 1), lambda i, *_: (row, 0, 0)),
                pl.BlockSpec((1, 1, length), lambda i, *_: (row, 0, 0)),
            ],
            out_specs=[whole((blocks, blk, pair)), whole((2, length))],
            scratch_shapes=[
                pltpu.VMEM((pair, length), jnp.bfloat16),
                pltpu.VMEM((2 * blk, pair), jnp.bfloat16),
                pltpu.VMEM((HEAD_DIM, 2 * blk), jnp.float32),
                pltpu.VMEM((2, 2 * blk), jnp.float32),
            ],
        ),
        out_shape=[
            jax.ShapeDtypeStruct((blocks, blk, pair), jnp.bfloat16),
            jax.ShapeDtypeStruct((2, length), jnp.float32),
        ],
        compiler_params=params(),
        cost_estimate=cost(20e9, 6e6, 20e6),
        name="attend",
    )(listed, edges, qkv, segc, segr)


def attend_back_kernel(
    listed_ref, edge_ref, qkv_ref, grad_ref, mixed_ref, lse_ref, segc_ref, segr_ref, out_ref,
    kt_ref, qz_ref, gz_ref, inner_ref, dq_ref, dk_ref, dv_ref, *, row,
):
    blocks = qkv_ref.shape[0]
    scale = HEAD_DIM ** (-0.5)

    def prepare(block, carried):
        at = pl.multiple_of(block * BLK, BLK)
        kt_ref[:, pl.ds(at, BLK)] = transposed(qkv_ref[block, :, 128:256])
        query = qkv_ref[block, :, :128].astype(jnp.float32) * scale
        qz_ref[block] = split_heads(query.astype(jnp.bfloat16))
        grad = grad_ref[block]
        gz_ref[block] = split_heads(grad)
        product = (grad.astype(jnp.float32) * mixed_ref[block].astype(jnp.float32)).T
        for head in range(2):
            part = product[head * HEAD_DIM : (head + 1) * HEAD_DIM, :]
            inner_ref[head : head + 1, pl.ds(at, BLK)] = jnp.sum(part, axis=0, keepdims=True)
        return carried

    lax.fori_loop(0, blocks, prepare, 0)
    dq_ref[...] = jnp.zeros(dq_ref.shape, jnp.float32)

    def one_key(key_block, carried):
        dk_ref[...] = jnp.zeros(dk_ref.shape, jnp.float32)
        dv_ref[...] = jnp.zeros(dv_ref.shape, jnp.float32)
        key_at = pl.multiple_of(key_block * BLK, BLK)

        def update(query_block, mask):
            query_at = pl.multiple_of(query_block * BLK, BLK)
            keys = qkv_ref[key_block, :, 128:256]
            values = qkv_ref[key_block, :, 256:384]
            for head in range(2):
                part = slice(head * BLK, (head + 1) * BLK)
                query = qz_ref[query_block, part, :]
                grad = gz_ref[query_block, part, :]
                scores = dot_nt(keys, query)
                probs = jnp.exp(scores - lse_ref[head : head + 1, pl.ds(query_at, BLK)])
                if mask is not None:
                    probs = jnp.where(mask, probs, 0.0)
                grad_probs = dot_nt(values, grad)
                grad_scores = probs * (grad_probs - inner_ref[head : head + 1, pl.ds(query_at, BLK)])
                probs = probs.astype(jnp.bfloat16)
                grad_scores = grad_scores.astype(jnp.bfloat16)
                dv_ref[...] += dot_nn(probs, grad)
                dk_ref[...] += dot_nn(grad_scores, query)
                lanes = slice(head * HEAD_DIM, (head + 1) * HEAD_DIM)
                dq_ref[lanes, pl.ds(query_at, BLK)] += dot_nn(
                    kt_ref[lanes, pl.ds(key_at, BLK)], grad_scores
                )

        def one_query(query_block, carried):
            listed = listed_ref[row, query_block * blocks + key_block] != 0
            full = is_full(edge_ref, row, blocks, key_block, query_block)

            @pl.when(listed & full)
            def _():
                update(query_block, None)

            @pl.when(listed & jnp.logical_not(full))
            def _():
                update(query_block, tile_mask(segc_ref, segr_ref, key_block, query_block))

            return carried

        lax.fori_loop(key_block, blocks, one_query, 0)
        grad_query = dq_ref[:, pl.ds(key_at, BLK)].T * scale
        out_ref[key_block] = pair_together(grad_query, dk_ref[...], dv_ref[...]).astype(jnp.bfloat16)
        return carried

    lax.fori_loop(0, blocks, one_key, 0)


def attend_back(row, listed, edges, qkv, grad, mixed, lse, segc, segr):
    blocks, blk, width = qkv.shape
    length = blocks * blk
    pair = 2 * HEAD_DIM
    return pl.pallas_call(
        functools.partial(attend_back_kernel, row=row),
        grid_spec=pltpu.PrefetchScalarGridSpec(
            num_scalar_prefetch=2,
            grid=(1,),
            in_specs=[
                whole(qkv.shape),
                whole(grad.shape),
                whole(mixed.shape),
                whole(lse.shape),
                pl.BlockSpec((1, length, 1), lambda i, *_: (row, 0, 0)),
                pl.BlockSpec((1, 1, length), lambda i, *_: (row, 0, 0)),
            ],
            out_specs=whole(qkv.shape),
            scratch_shapes=[
                pltpu.VMEM((pair, length), jnp.bfloat16),
                pltpu.VMEM((blocks, 2 * blk, pair), jnp.bfloat16),
                pltpu.VMEM((blocks, 2 * blk, pair), jnp.bfloat16),
                pltpu.VMEM((2, length), jnp.float32),
                pltpu.VMEM((pair, length), jnp.float32),
                pltpu.VMEM((blk, pair), jnp.float32),
                pltpu.VMEM((blk, pair), jnp.float32),
            ],
        ),
        out_shape=jax.ShapeDtypeStruct(qkv.shape, jnp.bfloat16),
        compiler_params=params(),
        cost_estimate=cost(50e9, 10e6, 20e6),
        name="attend_back",
    )(listed, edges, qkv, grad, mixed, lse, segc, segr)


def joined(ref, first, count):
    return jnp.concatenate([ref[first + i] for i in range(count)], axis=1)


def outward_kernel(mixed_ref, tok_ref, w_ref, scales_ref, hidden_ref, normed_ref, *, row):
    halves = w_ref.shape[1]
    per_half = mixed_ref.shape[0] // halves
    hidden = tok_ref[0].astype(jnp.float32)
    width = hidden.shape[1]
    for half in range(halves):
        hidden += dot_nt(joined(mixed_ref, half * per_half, per_half), w_ref[:, half].reshape(width, -1))
    hidden_ref[...] = hidden
    hat, _ = normalize(hidden)
    normed_ref[...] = (hat * scales_ref[row : row + 1, width:]).astype(jnp.bfloat16)


def outward(row, mixed, tokens, w_all, scales, columns):
    rows, length, width = tokens.shape
    groups, _, pair = mixed.shape
    chunks, halves, high, _ = w_all.shape
    tile = 256
    one = pl.BlockSpec((tile, width), lambda i: (i, 0))
    return pl.pallas_call(
        functools.partial(outward_kernel, row=row),
        grid=(length // tile,),
        in_specs=[
            pl.BlockSpec((groups, tile, pair), lambda i: (0, i, 0)),
            pl.BlockSpec((1, tile, width), lambda i: (row, i, 0)),
            whole((chunks, halves, high, columns)),
            whole(scales.shape),
        ],
        out_specs=[one, one],
        out_shape=[
            jax.ShapeDtypeStruct((length, width), jnp.float32),
            jax.ShapeDtypeStruct((length, width), jnp.bfloat16),
        ],
        compiler_params=params(),
        cost_estimate=cost(2 * length * width * width, 12 * length * width),
        name="outward",
    )(mixed, tokens, w_all, scales)


def mlp_kernel(
    me_ref, nm0_ref, nm1_ref, cot_ref, hidden0_ref, hidden1_ref, scales_ref, up_ref, down_ref,
    up_keep_ref, up_send_ref, down_keep_ref, down_send_ref,
    layer_ref, grad_hidden_ref, grad_attn_ref, gscale_ref,
    nmt_ref, cott_ref, out_ref, gn_ref, act_ref, gpre_ref,
):
    tile = pl.program_id(0)
    phase = pl.program_id(1)
    length, width = nm0_ref.shape
    count = 2 * length
    root = 0.7978845608028654
    cube = 0.044715

    @pl.when((tile == 0) & (phase == 0))
    def _():
        chunks = up_ref.shape[0]
        turned_apart(nmt_ref.at[:, :length], nm0_ref[...], me_ref[0], chunks)
        turned_apart(nmt_ref.at[:, length:], nm1_ref[...], me_ref[0], chunks)
        turned_apart(cott_ref, cot_ref[...], me_ref[0], chunks)
        out_ref[...] = jnp.zeros(out_ref.shape, jnp.float32)
        gn_ref[...] = jnp.zeros(gn_ref.shape, jnp.float32)

    @pl.when(phase == 0)
    def _():
        up = up_ref[:, 0].reshape(width, -1)
        down = down_ref[:, 0].reshape(width, -1)
        for row, nm_ref in enumerate((nm0_ref, nm1_ref)):
            part = slice(row * length, (row + 1) * length)
            pre = dot_nn(nm_ref[...], up)
            grad_act = dot_nn(cot_ref[part, :], down)
            square = pre * pre
            bent = jnp.tanh(root * (pre + cube * pre * square))
            half = 0.5 * (1.0 + bent)
            act_ref[part, :] = (pre * half).astype(jnp.bfloat16)
            slope = half + (0.5 * root) * pre * (1.0 - bent * bent) * (1.0 + (3.0 * cube) * square)
            gpre_ref[part, :] = (grad_act * slope).astype(jnp.bfloat16)
        grad = dot_nn(nmt_ref[...], gpre_ref[...]).astype(jnp.bfloat16)
        shape = up_keep_ref.shape[1:]
        up_keep_ref[0] = grad[: width // 2].reshape(shape)
        up_send_ref[0] = grad[width // 2 :].reshape(shape)

    @pl.when(phase == 1)
    def _():
        up = up_ref[:, 0].reshape(width, -1)
        down = down_ref[:, 0].reshape(width, -1)
        out_ref[...] += dot_nt(act_ref[...], down)
        gn_ref[...] += dot_nt(gpre_ref[...], up)
        grad = dot_nn(cott_ref[...], act_ref[...]).astype(jnp.bfloat16)
        shape = (down_keep_ref.shape[0],) + down_keep_ref.shape[2:]
        down_keep_ref[:, 0] = grad[: width // 2].reshape(shape)
        down_send_ref[:, 0] = grad[width // 2 :].reshape(shape)

    @pl.when((tile == pl.num_programs(0) - 1) & (phase == 1))
    def _():
        chunk = 256
        for row, hidden_ref in enumerate((hidden0_ref, hidden1_ref)):
            scale = scales_ref[row : row + 1, width:]
            total = jnp.zeros((1, width), jnp.float32)
            for at in range(0, length, chunk):
                part = slice(row * length + at, row * length + at + chunk)
                hidden = hidden_ref[at : at + chunk, :]
                layer_ref[part, :] = (hidden + out_ref[part, :]).astype(jnp.bfloat16)
                hat, inverse = normalize(hidden)
                grad = gn_ref[part, :]
                total += jnp.sum(grad * hat, axis=0, keepdims=True)
                back = cot_ref[part, :].astype(jnp.float32) + normalize_back(grad * scale, hat, inverse)
                grad_hidden_ref[part, :] = back
                grad_attn_ref[part, :] = back.astype(jnp.bfloat16)
            gscale_ref[row : row + 1, :] = total


def mlp(me, normed, cotangent, hidden, scales, w_all, skip, hidden_cols):
    rows, length, width = cotangent.shape
    count = rows * length
    chunks, halves, high, columns = w_all.shape
    tile = 512
    per_half = hidden_cols // tile
    first = skip // tile
    quarter = chunks // 4
    flat = (count, width)
    up_at = lambda f, s, me: (0, f // per_half, 0, first + f % per_half)
    down_at = lambda f, s, me: (0, f // per_half, 0, first + per_half + f % per_half)
    up_out = pl.BlockSpec(
        (1, 2, quarter, high, tile), lambda f, s, me: ((f // per_half) ^ me[1], 0, 0, 0, f % per_half)
    )
    down_out = pl.BlockSpec(
        (2, 1, quarter, high, tile), lambda f, s, me: (0, (f // per_half) ^ me[1], 0, 0, f % per_half)
    )
    grads = jax.ShapeDtypeStruct((2, 2, quarter, high, hidden_cols), jnp.bfloat16)
    return pl.pallas_call(
        mlp_kernel,
        grid_spec=pltpu.PrefetchScalarGridSpec(
            num_scalar_prefetch=1,
            grid=(halves * per_half, 2),
            in_specs=[
                whole((length, width)),
                whole((length, width)),
                whole(flat),
                whole((length, width)),
                whole((length, width)),
                whole(scales.shape),
                pl.BlockSpec((chunks, 1, high, tile), up_at),
                pl.BlockSpec((chunks, 1, high, tile), down_at),
            ],
            out_specs=[up_out, up_out, down_out, down_out]
            + [whole(flat), whole(flat), whole(flat), whole((rows, width))],
            scratch_shapes=[
                pltpu.VMEM((width, count), jnp.bfloat16),
                pltpu.VMEM((width, count), jnp.bfloat16),
                pltpu.VMEM(flat, jnp.float32),
                pltpu.VMEM(flat, jnp.float32),
                pltpu.VMEM((count, tile), jnp.bfloat16),
                pltpu.VMEM((count, tile), jnp.bfloat16),
            ],
        ),
        out_shape=[grads] * 4
        + [
            jax.ShapeDtypeStruct(flat, jnp.bfloat16),
            jax.ShapeDtypeStruct(flat, jnp.float32),
            jax.ShapeDtypeStruct(flat, jnp.bfloat16),
            jax.ShapeDtypeStruct((rows, width), jnp.float32),
        ],
        compiler_params=params(60),
        cost_estimate=cost(12 * count * width * halves * hidden_cols, 4 * w_all.size + 16 * count * width),
        name="mlp",
    )(me, *normed, cotangent.reshape(flat), *hidden, scales, w_all, w_all)


def grad_mixed_kernel(grad_ref, w_ref, out_ref):
    halves = w_ref.shape[1]
    per_half = out_ref.shape[0] // halves
    grad = grad_ref[...]
    pair = out_ref.shape[2]
    for half in range(halves):
        out = dot_nn(grad, w_ref[:, half].reshape(grad.shape[1], -1)).astype(jnp.bfloat16)
        for group in range(per_half):
            out_ref[half * per_half + group] = out[:, group * pair : (group + 1) * pair]


def grad_mixed_of(row, grad_attn, w_all, mixed_shape, columns):
    groups, length, pair = mixed_shape
    chunks, halves, high, _ = w_all.shape
    width = grad_attn.shape[1]
    tile = 256
    tiles = length // tile
    return pl.pallas_call(
        grad_mixed_kernel,
        grid=(tiles,),
        in_specs=[
            pl.BlockSpec((tile, width), lambda i: (row * tiles + i, 0)),
            whole((chunks, halves, high, columns)),
        ],
        out_specs=pl.BlockSpec((groups, tile, pair), lambda i: (0, i, 0)),
        out_shape=jax.ShapeDtypeStruct(mixed_shape, jnp.bfloat16),
        compiler_params=params(),
        cost_estimate=cost(2 * length * width * width, 8 * length * width),
        name="grad_mixed",
    )(grad_attn, w_all)


def grad_proj_kernel(me_ref, grad_ref, *refs):
    mixed_refs, (keep_ref, send_ref, turned_ref) = refs[:-3], refs[-3:]
    width = grad_ref.shape[1]

    @pl.when(pl.program_id(0) == 0)
    def _():
        turned_apart(turned_ref, grad_ref[...], me_ref[0], 4 * keep_ref.shape[2])

    grad = 0.0
    for row, mixed_ref in enumerate(mixed_refs):
        length = mixed_ref.shape[1]
        part = slice(row * length, (row + 1) * length)
        grad += dot_nn(turned_ref[:, part], joined(mixed_ref, 0, mixed_ref.shape[0]))
    grad = grad.astype(jnp.bfloat16)
    shape = keep_ref.shape[1:]
    keep_ref[0] = grad[: width // 2].reshape(shape)
    send_ref[0] = grad[width // 2 :].reshape(shape)


def grad_proj_of(me, grad_attn, mixed, chunks, halves, columns):
    groups, length, pair = mixed[0].shape
    count, width = grad_attn.shape
    high = width // chunks
    shape = (halves, 2, chunks // 4, high, columns)
    one = pl.BlockSpec((1,) + shape[1:], lambda h, me: (h ^ me[1], 0, 0, 0, 0))
    given = pl.BlockSpec((groups // halves, length, pair), lambda h, me: (h, 0, 0))
    return pl.pallas_call(
        grad_proj_kernel,
        grid_spec=pltpu.PrefetchScalarGridSpec(
            num_scalar_prefetch=1,
            grid=(halves,),
            in_specs=[whole(grad_attn.shape)] + [given] * len(mixed),
            out_specs=[one, one],
            scratch_shapes=[pltpu.VMEM((width, count), jnp.bfloat16)],
        ),
        out_shape=[jax.ShapeDtypeStruct(shape, jnp.bfloat16)] * 2,
        compiler_params=params(),
        cost_estimate=cost(2 * count * width * width, 6 * count * width),
        name="grad_proj",
    )(me, grad_attn, *mixed)


def first_norm_kernel(gq_ref, tok_ref, grad_hidden_ref, w_ref, scales_ref, out_ref, gscale_ref, *, row, q_cols):
    step = pl.program_id(0)
    halves = w_ref.shape[1]
    per_half = gq_ref.shape[0] // halves
    values = tok_ref[0].astype(jnp.float32)
    width = values.shape[1]
    grad = jnp.zeros(values.shape, jnp.float32)
    for half in range(halves):
        weights = w_ref[:, half, :, :q_cols].reshape(width, q_cols)
        grad += dot_nt(joined(gq_ref, half * per_half, per_half), weights)
    hat, inverse = normalize(values)
    total = jnp.sum(grad * hat, axis=0, keepdims=True)

    @pl.when(step == 0)
    def _():
        gscale_ref[...] = total

    @pl.when(step != 0)
    def _():
        gscale_ref[...] += total

    back = normalize_back(grad * scales_ref[row : row + 1, :width], hat, inverse)
    out_ref[...] = (grad_hidden_ref[...] + back).astype(jnp.bfloat16)


def first_norm_back(row, grad_qkv, tokens, grad_hidden, w_all, scales, q_cols):
    rows, length, width = tokens.shape
    groups, _, pair = grad_qkv.shape
    tile = 256
    tiles = length // tile
    return pl.pallas_call(
        functools.partial(first_norm_kernel, row=row, q_cols=q_cols),
        grid=(tiles,),
        in_specs=[
            pl.BlockSpec((groups, tile, pair), lambda i: (0, i, 0)),
            pl.BlockSpec((1, tile, width), lambda i: (row, i, 0)),
            pl.BlockSpec((tile, width), lambda i: (row * tiles + i, 0)),
            whole(w_all.shape),
            whole(scales.shape),
        ],
        out_specs=[pl.BlockSpec((tile, width), lambda i: (i, 0)), whole((1, width))],
        out_shape=[
            jax.ShapeDtypeStruct((length, width), jnp.bfloat16),
            jax.ShapeDtypeStruct((1, width), jnp.float32),
        ],
        compiler_params=params(),
        cost_estimate=cost(2 * length * width * groups * pair, 2 * w_all.size + 20 * length * width),
        name="first_norm_back",
    )(grad_qkv, tokens, grad_hidden, w_all, scales)


def grad_qkv_kernel(me_ref, *refs, chunks, at_front):
    rows = (len(refs) - 3) // 2
    normed_refs, gq_refs, (keep_ref, send_ref, turned_ref) = refs[:rows], refs[rows:-3], refs[-3:]
    length, width = normed_refs[0].shape

    @pl.when((pl.program_id(0) == 0) & (pl.program_id(1) == 0))
    def _():
        for row in range(rows):
            part = slice(row * length, (row + 1) * length)
            turned_apart(turned_ref.at[:, part], normed_refs[row][...], me_ref[0], chunks)

    found = 0.0
    for row in range(rows):
        found += dot_nn(turned_ref[:, row * length : (row + 1) * length], gq_refs[row][0])
    found = found.astype(jnp.bfloat16)
    if at_front:
        shape = keep_ref.shape[1:]
        keep_ref[0] = found[: width // 2].reshape(shape)
        send_ref[0] = found[width // 2 :].reshape(shape)
    else:
        shape = (keep_ref.shape[0],) + keep_ref.shape[2:]
        keep_ref[:, 0] = found[: width // 2].reshape(shape)
        send_ref[:, 0] = found[width // 2 :].reshape(shape)


def grad_qkv_of(me, normed, grad_qkv, chunks, halves, first, some, at_front):
    length, width = normed[0].shape
    rows = len(normed)
    groups, _, pair = grad_qkv[0].shape
    pairs = groups // halves
    high = width // chunks
    quarter = chunks // 4
    if at_front:
        out = pl.BlockSpec((1, 2, quarter, high, pair), lambda h, j, me: (h ^ me[1], 0, 0, 0, j))
    else:
        out = pl.BlockSpec((2, 1, quarter, high, pair), lambda h, j, me: (0, h ^ me[1], 0, 0, j))
    wide = jax.ShapeDtypeStruct((halves, 2, quarter, high, some * pair), jnp.bfloat16)
    given = pl.BlockSpec((1, length, pair), lambda h, j, me: (h * pairs + first + j, 0, 0))
    return pl.pallas_call(
        functools.partial(grad_qkv_kernel, chunks=chunks, at_front=at_front),
        grid_spec=pltpu.PrefetchScalarGridSpec(
            num_scalar_prefetch=1,
            grid=(halves, some),
            in_specs=[whole((length, width))] * rows + [given] * rows,
            out_specs=[out, out],
            scratch_shapes=[pltpu.VMEM((width, rows * length), jnp.bfloat16)],
        ),
        out_shape=[wide] * 2,
        compiler_params=params(),
        cost_estimate=cost(2 * rows * length * width * halves * some * pair, 6 * rows * length * width),
        name="grad_qkv",
    )(me, *normed, *grad_qkv)


def grad_time_kernel(me_ref, tet_ref, gs_ref, keep_ref, send_ref, apart_ref, *, chunks, folds, t_cols):
    bits = chunks.bit_length() - 1
    k_rows = tet_ref.shape[0] // chunks
    for chunk in range(chunks):
        apart = chunk ^ me_ref[0]
        place = 0
        for bit in range(bits):
            place += ((apart >> bit) & 1) << (bits - 1 - bit)
        apart_ref[pl.ds(pl.multiple_of(place * k_rows, k_rows), k_rows), :] = tet_ref[
            chunk * k_rows : (chunk + 1) * k_rows, :
        ]
    half = pl.program_id(0)
    shape = keep_ref.shape[1:3] + (k_rows, t_cols)
    middle = chunks * k_rows // 2
    for fold in range(folds):
        at = pl.multiple_of((half * folds + fold) * t_cols, t_cols)
        total = jnp.zeros((chunks * k_rows, t_cols), jnp.float32)
        for row in range(gs_ref.shape[0]):
            total += apart_ref[:, row : row + 1] * gs_ref[row : row + 1, pl.ds(at, t_cols)]
        total = total.astype(jnp.bfloat16)
        rows = slice(fold * k_rows, (fold + 1) * k_rows)
        keep_ref[0, :, :, rows, :] = total[:middle].reshape(shape)
        send_ref[0, :, :, rows, :] = total[middle:].reshape(shape)


def grad_time_of(me, time_embed, grad_scales, chunks, halves, high, k_rows, t_cols):
    turned = time_embed.T
    quarter = chunks // 4
    thin = jax.ShapeDtypeStruct((halves, 2, quarter, high, t_cols), jnp.bfloat16)
    out = pl.BlockSpec((1, 2, quarter, high, t_cols), lambda h, me: (h ^ me[1], 0, 0, 0, 0))
    return pl.pallas_call(
        functools.partial(grad_time_kernel, chunks=chunks, folds=high // k_rows, t_cols=t_cols),
        grid_spec=pltpu.PrefetchScalarGridSpec(
            num_scalar_prefetch=1,
            grid=(halves,),
            in_specs=[whole(turned.shape), whole(grad_scales.shape)],
            out_specs=[out, out],
            scratch_shapes=[pltpu.VMEM(turned.shape, jnp.float32)],
        ),
        out_shape=[thin] * 2,
        compiler_params=params(),
        cost_estimate=cost(4 * turned.shape[0] * grad_scales.size, 4 * grad_scales.size),
        name="grad_time",
    )(me, turned, grad_scales)


def across(values, axis, apart):
    size = lax.axis_size(axis)
    return lax.ppermute(values, axis, [(i, i ^ apart) for i in range(size)])


def summed(parts, index):
    total = parts[0][index].astype(jnp.float32)
    for part in parts[1:]:
        total += part[index].astype(jnp.float32)
    return total


HOPS = {"x": ("ctx", 2), "y": ("tp", 1), "near": ("fsdp", 1), "far": ("fsdp", 2)}


class TreeSum:
    def __init__(self, keep, send, order):
        self.parts = [keep, across(send, "ctx", 1)]
        self.left = list(order) + ["near", "far"]

    def ready(self):
        upper = slice(2, 4) if self.left[0] == "near" else 1
        self.given = summed(self.parts, upper).astype(jnp.bfloat16)
        return self.given

    def go(self):
        name = self.left.pop(0)
        lower = slice(0, 2) if name == "near" else 0
        self.parts = [part[lower] for part in self.parts] + [across(self.given, *HOPS[name])]

    def finish(self):
        while self.left:
            self.ready()
            self.go()
        return summed(self.parts, slice(None))


def together(value, trees):
    given = [tree.ready() for tree in trees]
    value, *given = lax.optimization_barrier((value, *given))
    for tree, one in zip(trees, given):
        tree.given = one
        tree.go()
    return value


def listed_table(block_pairs, pair_counts, row_blocks, ctx_size):
    rows, _, slots, _ = block_pairs.shape
    packed = jnp.concatenate([block_pairs.reshape(rows, 1, slots * 2), pair_counts[:, :, None]], axis=2)
    packed = jnp.concatenate(
        [packed] + [across(packed, "ctx", apart) for apart in range(1, ctx_size)], axis=1
    )
    pairs = packed[:, :, : slots * 2].reshape(rows, ctx_size, slots, 2)
    live = jnp.arange(slots, dtype=jnp.int32)[None, None, :] < packed[:, :, slots * 2 :]
    owner = lax.axis_index("ctx") ^ jnp.arange(ctx_size, dtype=jnp.int32)[None, :, None]
    base = owner * (row_blocks // ctx_size)
    code = jnp.where(live, (base + pairs[..., 0]) * row_blocks + pairs[..., 1], -1)
    code = code.reshape(rows, ctx_size * slots)
    cells = jnp.arange(row_blocks * row_blocks, dtype=jnp.int32)
    return jnp.any(code[:, :, None] == cells[None, None, :], axis=1).astype(jnp.int32)


EVERY = ("fsdp", "ctx", "tp")
GROUP = ("ctx", "tp")


def spread_body(
    tokens, time_embed, segment_ids, block_pairs, pair_counts,
    w_time, w_qkv, w_out, w_up, w_down, cotangent,
):
    rows, length, width = tokens.shape
    chunks = width // w_qkv.shape[0]
    halves = lax.axis_size("tp")
    high = w_qkv.shape[0]
    q_cols, o_cols, f_cols = w_qkv.shape[1], w_out.shape[1], w_up.shape[1]
    k_rows = w_time.shape[0]
    t_all = w_time.shape[1] // halves
    folds = high // k_rows
    t_cols = t_all // folds
    mine = lax.axis_index("tp")
    me = jnp.stack([lax.axis_index("fsdp") * lax.axis_size("ctx") + lax.axis_index("ctx"), mine])
    time_part = lax.dynamic_slice_in_dim(w_time, mine * t_all, t_all, 1)
    time_part = time_part.reshape(k_rows, folds, t_cols).transpose(1, 0, 2).reshape(high, t_cols)
    first = jnp.concatenate([w_qkv, time_part], axis=1).astype(jnp.bfloat16)
    second = jnp.concatenate([w_out, w_up, w_down], axis=1).astype(jnp.bfloat16)
    first = lax.all_gather(first, EVERY, axis=0, tiled=True).reshape(chunks, halves, high, -1)
    second = lax.all_gather(second, EVERY, axis=0, tiled=True).reshape(chunks, halves, high, -1)

    row_blocks = segment_ids.shape[1] // BLK
    listed = listed_table(block_pairs, pair_counts, row_blocks, lax.axis_size("ctx"))
    edges = jnp.concatenate([segment_ids[:, ::BLK], segment_ids[:, BLK - 1 :: BLK]], axis=1)
    segc = segment_ids[:, :, None]
    segr = segment_ids[:, None, :]

    qkv, normed = [], []
    for row in range(rows):
        out, one, scales = project(row, time_embed, tokens, first, k_rows, q_cols, t_cols)
        qkv.append(lax.all_to_all(out, GROUP, 0, 0, tiled=True))
        normed.append(one)
    mixed_own, lse, mixed = [], [], []
    for row in range(rows):
        out, one = attend(row, listed, edges, qkv[row], segc, segr)
        mixed_own.append(out)
        lse.append(one)
        mixed.append(lax.all_to_all(out, GROUP, 0, 0, tiled=True))
    hidden, normed_mlp = [], []
    for row in range(rows):
        out, one = outward(row, mixed[row], tokens, second, scales, o_cols)
        hidden.append(out)
        normed_mlp.append(one)
    up_keep, up_send, down_keep, down_send, layer_out, grad_hidden, grad_attn, gscale_mlp = mlp(
        me, normed_mlp, cotangent, hidden, scales, second, o_cols, f_cols
    )
    down_tree = TreeSum(down_keep, down_send, "xy")
    up_tree = TreeSum(up_keep, up_send, "yx")
    grad_mixed = []
    for row in range(rows):
        out = grad_mixed_of(row, grad_attn, second, mixed[row].shape, o_cols)
        grad_mixed.append(lax.all_to_all(out, GROUP, 0, 0, tiled=True))
    out_keep, out_send = grad_proj_of(me, grad_attn, mixed, chunks, halves, o_cols)
    out_tree = TreeSum(out_keep, out_send, "yx")
    trees = [down_tree, up_tree, out_tree]
    grad_qkv = []
    for row in range(rows):
        grad_mixed[row] = together(grad_mixed[row], trees)
        out = attend_back(row, listed, edges, qkv[row], grad_mixed[row], mixed_own[row], lse[row], segc, segr)
        grad_qkv.append(lax.all_to_all(out, GROUP, 0, 0, tiled=True))
    grad_tokens, gscale_attn = [], []
    for row in range(rows - 1):
        out, one = first_norm_back(row, grad_qkv[row], tokens, grad_hidden, first, scales, q_cols)
        grad_tokens.append(out)
        gscale_attn.append(one)
    some = q_cols // (6 * HEAD_DIM) // 2
    a_keep, a_send = grad_qkv_of(me, normed, grad_qkv, chunks, halves, 0, some, True)
    b_keep, b_send = grad_qkv_of(me, normed, grad_qkv, chunks, halves, some, some, False)
    last, a_keep, b_keep = lax.optimization_barrier((grad_qkv[-1], a_keep, b_keep))
    out, one = first_norm_back(rows - 1, last, tokens, grad_hidden, first, scales, q_cols)
    grad_tokens.append(out)
    gscale_attn.append(one)
    grad_scales = jnp.concatenate([jnp.concatenate(gscale_attn, axis=0), gscale_mlp], axis=1)
    t_keep, t_send = grad_time_of(me, time_embed, grad_scales, chunks, halves, high, k_rows, t_cols)
    grad_time = TreeSum(t_keep, t_send, "yx").finish().reshape(folds, k_rows, t_cols)
    grad_time = grad_time.transpose(1, 0, 2).reshape(k_rows, t_all)
    other = across(grad_time.astype(jnp.bfloat16), "tp", 1).astype(jnp.float32)
    grad_time = jnp.concatenate(
        [jnp.where(mine == 0, grad_time, other), jnp.where(mine == 0, other, grad_time)], axis=1
    )
    grad_w_qkv = jnp.concatenate(
        [TreeSum(a_keep, a_send, "yx").finish(), TreeSum(b_keep, b_send, "xy").finish()], axis=1
    )
    return (
        layer_out.reshape(tokens.shape),
        jnp.stack(grad_tokens),
        grad_time,
        grad_w_qkv,
        out_tree.finish(),
        up_tree.finish(),
        down_tree.finish(),
    )


def choose(*args):
    tokens, w_qkv, w_out, w_up = args[0], args[6], args[7], args[8]
    group = lax.axis_size("ctx") * lax.axis_size("tp")
    heads_pair = 6 * HEAD_DIM
    fits = (
        (lax.axis_size("fsdp"), lax.axis_size("ctx"), lax.axis_size("tp")) == (4, 4, 2)
        and tokens.shape[1] == BLK
        and group * BLK == args[2].shape[1]
        and w_qkv.shape[1] * lax.axis_size("tp") == group * heads_pair
        and w_out.shape[1] % 512 == 0
        and w_up.shape[1] % 512 == 0
        and w_qkv.shape[0] % args[5].shape[0] == 0
    )
    return spread_body(*args) if fits else body(*args)


def solution(mesh):
    placed = (
        P("fsdp", ("ctx", "tp"), None),
        P("fsdp", None),
        P("fsdp", None),
        P("fsdp", "ctx", None, None),
        P("fsdp", "ctx"),
        P(("fsdp", "ctx"), None),
        P(("fsdp", "ctx"), "tp"),
        P(("fsdp", "ctx"), "tp"),
        P(("fsdp", "ctx"), "tp"),
        P(("fsdp", "ctx"), "tp"),
        P("fsdp", ("ctx", "tp"), None),
    )
    return jax.shard_map(
        choose,
        mesh=mesh,
        in_specs=placed,
        out_specs=(
            P("fsdp", ("ctx", "tp"), None),
            P("fsdp", ("ctx", "tp"), None),
            P(("fsdp", "ctx"), None),
            P(("fsdp", "ctx"), "tp"),
            P(("fsdp", "ctx"), "tp"),
            P(("fsdp", "ctx"), "tp"),
            P(("fsdp", "ctx"), "tp"),
        ),
        check_vma=False,
    )
```

```python
import functools
import math

import jax
import jax.numpy as jnp
from jax import lax
from jax.experimental import pallas as pl
from jax.experimental.pallas import tpu as pltpu
from jax.sharding import PartitionSpec as P

HEAD_DIM = 64
BLK = 512


epsilon = 1e-05
highest = lax.Precision.HIGHEST
masked_out = -1e30


def normalize(values):
    mean_value = jnp.mean(values, axis=-1, keepdims=True)
    centred = values - mean_value
    variance = jnp.mean(centred * centred, axis=-1, keepdims=True)
    inverse = lax.rsqrt(variance + epsilon)
    return (centred * inverse, inverse)


def normalize_back(grad_hat, normal_hat, inverse):
    first_mean = jnp.mean(grad_hat, axis=-1, keepdims=True)
    second_mean = jnp.mean(grad_hat * normal_hat, axis=-1, keepdims=True)
    return inverse * (grad_hat - first_mean - normal_hat * second_mean)


def smooth_gate(values):
    return jax.nn.gelu(values, approximate=True)


def block_scores(pair_entry, query_rows, key_rows, seg_row, offset):
    query_start = pair_entry[0] * BLK
    key_start = pair_entry[1] * BLK
    query_block = lax.dynamic_slice_in_dim(query_rows, query_start, BLK, 0)
    key_block = lax.dynamic_slice_in_dim(key_rows, key_start, BLK, 0)
    seg_query = lax.dynamic_slice_in_dim(seg_row, offset + query_start, BLK, 0)
    seg_keys = lax.dynamic_slice_in_dim(seg_row, key_start, BLK, 0)
    steps_in = jnp.arange(BLK, dtype=jnp.int32)
    allowed = (seg_query[:, None] == seg_keys[None, :]) & (
        key_start + steps_in[None, :] <= offset + query_start + steps_in[:, None]
    )
    scores = jnp.einsum(
        "qhe,khe->hqk", query_block, key_block, preferred_element_type=jnp.float32
    ) * HEAD_DIM ** (-0.5)
    return (query_block, key_block, query_start, key_start, allowed, scores)


def attend_forward(query_rows, key_rows, value_rows, seg_row, pair_rows, pair_total, offset):
    length_here, head_count, _ = query_rows.shape

    def statistic_step(pair_index, carried):
        running_max, running_sum = carried
        _, _, query_start, _, allowed, scores = block_scores(
            pair_rows[pair_index], query_rows, key_rows, seg_row, offset
        )
        scores = jnp.where(allowed[None], scores, masked_out)
        old_max = lax.dynamic_slice_in_dim(running_max, query_start, BLK, 1)
        old_sum = lax.dynamic_slice_in_dim(running_sum, query_start, BLK, 1)
        new_max = jnp.maximum(old_max, jnp.max(scores, axis=-1))
        weights = jnp.where(allowed[None], jnp.exp(scores - new_max[:, :, None]), 0.0)
        new_sum = old_sum * jnp.exp(old_max - new_max) + jnp.sum(weights, axis=-1)
        return (
            lax.dynamic_update_slice_in_dim(running_max, new_max, query_start, 1),
            lax.dynamic_update_slice_in_dim(running_sum, new_sum, query_start, 1),
        )

    start_max = jnp.full((head_count, length_here), masked_out, jnp.float32)
    start_sum = jnp.zeros((head_count, length_here), jnp.float32)
    running_max, running_sum = lax.fori_loop(0, pair_total, statistic_step, (start_max, start_sum))
    log_total = running_max + jnp.log(running_sum)

    def output_step(pair_index, accumulated):
        _, _, query_start, key_start, allowed, scores = block_scores(
            pair_rows[pair_index], query_rows, key_rows, seg_row, offset
        )
        block_log = lax.dynamic_slice_in_dim(log_total, query_start, BLK, 1)
        probabilities = jnp.where(
            allowed[None], jnp.exp(scores - block_log[:, :, None]), 0.0
        ).astype(jnp.bfloat16)
        value_block = lax.dynamic_slice_in_dim(value_rows, key_start, BLK, 0)
        addition = jnp.einsum(
            "hqk,khe->qhe", probabilities, value_block, preferred_element_type=jnp.float32
        )
        previous = lax.dynamic_slice_in_dim(accumulated, query_start, BLK, 0)
        return lax.dynamic_update_slice_in_dim(accumulated, previous + addition, query_start, 0)

    mixed_rows = lax.fori_loop(0, pair_total, output_step, jnp.zeros(query_rows.shape, jnp.float32))
    return (mixed_rows, log_total)


def attend_backward(
    query_rows,
    key_rows,
    value_rows,
    seg_row,
    pair_rows,
    pair_total,
    offset,
    log_total,
    grad_mixed,
    inner_sums,
):
    scale_factor = HEAD_DIM ** (-0.5)

    def add_block(whole, start_at, addition):
        previous = lax.dynamic_slice_in_dim(whole, start_at, BLK, 0)
        return lax.dynamic_update_slice_in_dim(whole, previous + addition, start_at, 0)

    def gradient_step(pair_index, carried):
        grad_query, grad_keys, grad_values = carried
        query_block, key_block, query_start, key_start, allowed, scores = block_scores(
            pair_rows[pair_index], query_rows, key_rows, seg_row, offset
        )
        block_log = lax.dynamic_slice_in_dim(log_total, query_start, BLK, 1)
        probabilities = jnp.where(allowed[None], jnp.exp(scores - block_log[:, :, None]), 0.0)
        grad_block = lax.dynamic_slice_in_dim(grad_mixed, query_start, BLK, 0)
        value_block = lax.dynamic_slice_in_dim(value_rows, key_start, BLK, 0)
        grad_probs = jnp.einsum(
            "qhe,khe->hqk", grad_block, value_block, preferred_element_type=jnp.float32
        )
        inner_block = lax.dynamic_slice_in_dim(inner_sums, query_start, BLK, 1)
        grad_scores = (probabilities * (grad_probs - inner_block[:, :, None])).astype(jnp.bfloat16)
        query_add = (
            jnp.einsum("hqk,khe->qhe", grad_scores, key_block, preferred_element_type=jnp.float32)
            * scale_factor
        )
        key_add = (
            jnp.einsum("hqk,qhe->khe", grad_scores, query_block, preferred_element_type=jnp.float32)
            * scale_factor
        )
        value_add = jnp.einsum(
            "hqk,qhe->khe",
            probabilities.astype(jnp.bfloat16),
            grad_block,
            preferred_element_type=jnp.float32,
        )
        return (
            add_block(grad_query, query_start, query_add),
            add_block(grad_keys, key_start, key_add),
            add_block(grad_values, key_start, value_add),
        )

    start_state = (
        jnp.zeros(query_rows.shape, jnp.float32),
        jnp.zeros(key_rows.shape, jnp.float32),
        jnp.zeros(value_rows.shape, jnp.float32),
    )
    return lax.fori_loop(0, pair_total, gradient_step, start_state)


def body(
    tokens,
    time_embed,
    segment_ids,
    block_pairs,
    pair_counts,
    w_time,
    w_qkv,
    w_out,
    w_up,
    w_down,
    cotangent,
):
    row_count, local_len, model_width = tokens.shape
    time_all, qkv_all, out_all, up_all, down_all = (
        lax.all_gather(w_time.astype(jnp.bfloat16), ("fsdp", "ctx"), axis=0, tiled=True),
        lax.all_gather(w_qkv.astype(jnp.bfloat16), ("fsdp", "ctx"), axis=0, tiled=True),
        lax.all_gather(w_out.astype(jnp.bfloat16), ("fsdp", "ctx"), axis=0, tiled=True),
        lax.all_gather(w_up.astype(jnp.bfloat16), ("fsdp", "ctx"), axis=0, tiled=True),
        lax.all_gather(w_down.astype(jnp.bfloat16), ("fsdp", "ctx"), axis=0, tiled=True),
    )
    scales = 1.0 + jnp.dot(time_embed, time_all.astype(jnp.float32), precision=highest)
    scale_attn = scales[:, None, :model_width]
    scale_mlp = scales[:, None, model_width:]
    x_input = tokens.astype(jnp.float32)
    hat_attn, inverse_attn = normalize(x_input)
    normed = (hat_attn * scale_attn).astype(jnp.bfloat16)
    normed_all = lax.all_gather(normed, "tp", axis=1, tiled=True)
    ctx_len = normed_all.shape[1]
    head_count = qkv_all.shape[1] // (3 * HEAD_DIM)
    projected = jnp.einsum("rtd,dc->rtc", normed_all, qkv_all, preferred_element_type=jnp.float32)
    projected = projected.astype(jnp.bfloat16).reshape(row_count, ctx_len, head_count, 3, HEAD_DIM)
    query_all = projected[:, :, :, 0]
    key_part = projected[:, :, :, 1]
    value_part = projected[:, :, :, 2]
    key_all, value_all = (
        lax.all_gather(key_part, "ctx", axis=1, tiled=True),
        lax.all_gather(value_part, "ctx", axis=1, tiled=True),
    )
    offset = lax.axis_index("ctx") * ctx_len
    mixed_list = []
    log_list = []
    for row_index in range(row_count):
        mixed_rows, log_total = attend_forward(
            query_all[row_index],
            key_all[row_index],
            value_all[row_index],
            segment_ids[row_index],
            block_pairs[row_index, 0],
            pair_counts[row_index, 0],
            offset,
        )
        mixed_list.append(mixed_rows)
        log_list.append(log_total)
    mixed_exact = jnp.stack(mixed_list)
    mixed_heads = mixed_exact.astype(jnp.bfloat16).reshape(
        row_count, ctx_len, head_count * HEAD_DIM
    )
    attn_part = jnp.einsum("rtc,dc->rtd", mixed_heads, out_all, preferred_element_type=jnp.float32)
    attn_local = lax.psum_scatter(
        attn_part.astype(jnp.bfloat16), "tp", scatter_dimension=1, tiled=True
    ).astype(jnp.float32)
    hidden = x_input + attn_local
    hat_mlp, inverse_mlp = normalize(hidden)
    normed_mlp = (hat_mlp * scale_mlp).astype(jnp.bfloat16)
    mlp_all = lax.all_gather(normed_mlp, "tp", axis=1, tiled=True)
    pre_act = jnp.einsum("rtd,df->rtf", mlp_all, up_all, preferred_element_type=jnp.float32)
    activated = smooth_gate(pre_act).astype(jnp.bfloat16)
    mlp_part = jnp.einsum("rtf,df->rtd", activated, down_all, preferred_element_type=jnp.float32)
    mlp_local = lax.psum_scatter(
        mlp_part.astype(jnp.bfloat16), "tp", scatter_dimension=1, tiled=True
    ).astype(jnp.float32)
    grad_all = lax.all_gather(cotangent, "tp", axis=1, tiled=True)
    grad_act = jnp.einsum("rtd,df->rtf", grad_all, down_all, preferred_element_type=jnp.float32)
    _, gate_back = jax.vjp(smooth_gate, pre_act)
    grad_pre = gate_back(grad_act)[0].astype(jnp.bfloat16)
    grad_down = jnp.einsum("rtd,rtf->df", grad_all, activated, preferred_element_type=jnp.float32)
    grad_up = jnp.einsum("rtd,rtf->df", mlp_all, grad_pre, preferred_element_type=jnp.float32)
    norm_part = jnp.einsum("rtf,df->rtd", grad_pre, up_all, preferred_element_type=jnp.float32)
    grad_normed_mlp = lax.psum_scatter(
        norm_part.astype(jnp.bfloat16), "tp", scatter_dimension=1, tiled=True
    ).astype(jnp.float32)
    layer_out = (hidden + mlp_local).astype(jnp.bfloat16)
    grad_output = cotangent.astype(jnp.float32)
    grad_scale_mlp = jnp.sum(grad_normed_mlp * hat_mlp, axis=1)
    grad_hidden = grad_output + normalize_back(grad_normed_mlp * scale_mlp, hat_mlp, inverse_mlp)
    grad_attn_all = lax.all_gather(grad_hidden.astype(jnp.bfloat16), "tp", axis=1, tiled=True)
    grad_mixed = jnp.einsum(
        "rtd,dc->rtc", grad_attn_all, out_all, preferred_element_type=jnp.float32
    ).astype(jnp.bfloat16)
    grad_proj = jnp.einsum(
        "rtd,rtc->dc", grad_attn_all, mixed_heads, preferred_element_type=jnp.float32
    )
    grad_mixed = grad_mixed.reshape(row_count, ctx_len, head_count, HEAD_DIM)
    inner_sums = jnp.einsum("rqhe,rqhe->rhq", grad_mixed.astype(jnp.float32), mixed_exact)
    query_grads = []
    key_grads = []
    value_grads = []
    for row_index in range(row_count):
        grad_query, grad_keys, grad_values = attend_backward(
            query_all[row_index],
            key_all[row_index],
            value_all[row_index],
            segment_ids[row_index],
            block_pairs[row_index, 0],
            pair_counts[row_index, 0],
            offset,
            log_list[row_index],
            grad_mixed[row_index],
            inner_sums[row_index],
        )
        query_grads.append(grad_query)
        key_grads.append(grad_keys)
        value_grads.append(grad_values)
    key_local, value_local = (
        lax.psum_scatter(
            jnp.stack(key_grads).astype(jnp.bfloat16), "ctx", scatter_dimension=1, tiled=True
        ).astype(jnp.float32),
        lax.psum_scatter(
            jnp.stack(value_grads).astype(jnp.bfloat16), "ctx", scatter_dimension=1, tiled=True
        ).astype(jnp.float32),
    )
    grad_projected = jnp.stack(
        [
            jnp.stack(query_grads).astype(jnp.bfloat16),
            key_local.astype(jnp.bfloat16),
            value_local.astype(jnp.bfloat16),
        ],
        axis=3,
    )
    grad_projected = grad_projected.reshape(row_count, ctx_len, head_count * 3 * HEAD_DIM)
    grad_qkv = jnp.einsum(
        "rtd,rtc->dc", normed_all, grad_projected, preferred_element_type=jnp.float32
    )
    first_part = jnp.einsum(
        "rtc,dc->rtd", grad_projected, qkv_all, preferred_element_type=jnp.float32
    )
    grad_normed = lax.psum_scatter(
        first_part.astype(jnp.bfloat16), "tp", scatter_dimension=1, tiled=True
    ).astype(jnp.float32)
    grad_scale_attn = jnp.sum(grad_normed * hat_attn, axis=1)
    grad_tokens = grad_hidden + normalize_back(grad_normed * scale_attn, hat_attn, inverse_attn)
    grad_scales = lax.psum(jnp.concatenate([grad_scale_attn, grad_scale_mlp], axis=1), "tp")
    grad_time = jnp.dot(time_embed.T, grad_scales, precision=highest)
    shared = (
        lax.psum_scatter(
            grad_time.astype(jnp.bfloat16), ("fsdp", "ctx"), scatter_dimension=0, tiled=True
        ).astype(jnp.float32),
        lax.psum_scatter(
            grad_qkv.astype(jnp.bfloat16), ("fsdp", "ctx"), scatter_dimension=0, tiled=True
        ).astype(jnp.float32),
        lax.psum_scatter(
            grad_proj.astype(jnp.bfloat16), ("fsdp", "ctx"), scatter_dimension=0, tiled=True
        ).astype(jnp.float32),
        lax.psum_scatter(
            grad_up.astype(jnp.bfloat16), ("fsdp", "ctx"), scatter_dimension=0, tiled=True
        ).astype(jnp.float32),
        lax.psum_scatter(
            grad_down.astype(jnp.bfloat16), ("fsdp", "ctx"), scatter_dimension=0, tiled=True
        ).astype(jnp.float32),
    )
    return (
        layer_out,
        grad_tokens.astype(jnp.bfloat16),
        shared[0],
        shared[1],
        shared[2],
        shared[3],
        shared[4],
    )


def params(limit=58):
    return pltpu.CompilerParams(vmem_limit_bytes=limit * 1024 * 1024)


def whole(shape):
    zeros = (0,) * len(shape)
    return pl.BlockSpec(shape, lambda *_: zeros, pipeline_mode=pl.Buffered(1))


def cost(flops, nbytes, exps=0):
    return pl.CostEstimate(flops=int(flops), bytes_accessed=int(nbytes), transcendentals=int(exps))


def dot_nn(left, right):
    return jnp.dot(left, right, preferred_element_type=jnp.float32)


def dot_nt(left, right):
    return lax.dot_general(left, right, (((1,), (1,)), ((), ())), preferred_element_type=jnp.float32)


def transposed(values):
    return values.astype(jnp.float32).T.astype(values.dtype)


def turned_apart(into_ref, values, chunk_at, chunks):
    turned = values.astype(jnp.float32).T.astype(values.dtype)
    high = turned.shape[0] // chunks
    bits = chunks.bit_length() - 1
    for chunk in range(chunks):
        apart = chunk ^ chunk_at
        place = 0
        for bit in range(bits):
            place += ((apart >> bit) & 1) << (bits - 1 - bit)
        into_ref[pl.ds(pl.multiple_of(place * high, high), high), :] = turned[
            chunk * high : (chunk + 1) * high, :
        ]


def low_lanes(shape):
    return lax.broadcasted_iota(jnp.int32, shape, 1) < HEAD_DIM


def pair_apart(stored):
    first, second, third = stored[:, :128], stored[:, 128:256], stored[:, 256:]
    low = low_lanes(first.shape)
    keys = pltpu.roll(jnp.where(low, third, first), HEAD_DIM, 1)
    return jnp.concatenate(
        [jnp.where(low, first, second), keys, jnp.where(low, second, third)], axis=1
    )


def pair_together(query, keys, values):
    low = low_lanes(query.shape)
    turned = pltpu.roll(keys, HEAD_DIM, 1)
    return jnp.concatenate(
        [jnp.where(low, query, turned), jnp.where(low, values, query), jnp.where(low, turned, values)],
        axis=1,
    )


def time_scales(te_ref, w_ref, scales_ref, k_rows, q_cols, t_cols):
    exact = te_ref[...]
    high = exact.astype(jnp.bfloat16)
    rest = exact - high.astype(jnp.float32)
    middle = rest.astype(jnp.bfloat16)
    last = (rest - middle.astype(jnp.float32)).astype(jnp.bfloat16)
    chunks, halves, tall, _ = w_ref.shape
    folds = tall // k_rows
    for half in range(halves):
        for fold in range(folds):
            weights = w_ref[:, half, fold * k_rows : (fold + 1) * k_rows, q_cols : q_cols + t_cols]
            weights = weights.reshape(chunks * k_rows, t_cols)
            total = dot_nn(last, weights) + dot_nn(middle, weights) + dot_nn(high, weights)
            at = (half * folds + fold) * t_cols
            scales_ref[:, at : at + t_cols] = 1.0 + total


def project_kernel(te_ref, tok_ref, w_ref, qkv_ref, normed_ref, scales_ref, *, row, k_rows, q_cols, t_cols):
    @pl.when(pl.program_id(0) == 0)
    def _():
        time_scales(te_ref, w_ref, scales_ref, k_rows, q_cols, t_cols)

    halves = w_ref.shape[1]
    values = tok_ref[0].astype(jnp.float32)
    width = values.shape[1]
    hat, _ = normalize(values)
    normed = (hat * scales_ref[row : row + 1, :width]).astype(jnp.bfloat16)
    normed_ref[...] = normed
    pair = 6 * HEAD_DIM
    for half in range(halves):
        weights = w_ref[:, half, :, :q_cols].reshape(width, q_cols)
        out = dot_nn(normed, weights)
        for group in range(q_cols // pair):
            qkv_ref[half * (q_cols // pair) + group] = pair_apart(
                out[:, group * pair : (group + 1) * pair]
            ).astype(jnp.bfloat16)


def project(row, time_embed, tokens, w_all, k_rows, q_cols, t_cols):
    rows, length, width = tokens.shape
    chunks, halves = w_all.shape[:2]
    pair = 6 * HEAD_DIM
    groups = halves * q_cols // pair
    tile = 256
    return pl.pallas_call(
        functools.partial(project_kernel, row=row, k_rows=k_rows, q_cols=q_cols, t_cols=t_cols),
        grid=(length // tile,),
        in_specs=[
            whole(time_embed.shape),
            pl.BlockSpec((1, tile, width), lambda i: (row, i, 0)),
            whole(w_all.shape),
        ],
        out_specs=[
            pl.BlockSpec((groups, tile, pair), lambda i: (0, i, 0)),
            pl.BlockSpec((tile, width), lambda i: (i, 0)),
            whole((rows, 2 * width)),
        ],
        out_shape=[
            jax.ShapeDtypeStruct((groups, length, pair), jnp.bfloat16),
            jax.ShapeDtypeStruct((length, width), jnp.bfloat16),
            jax.ShapeDtypeStruct((rows, 2 * width), jnp.float32),
        ],
        compiler_params=params(),
        cost_estimate=cost(2 * length * width * halves * q_cols, 2 * w_all.size + 10 * length * width),
        name="project",
    )(time_embed, tokens, w_all)


HALF = BLK // 2


def tile_mask(segc_ref, segr_ref, key_at, query_at, size):
    key_at, query_at = pl.multiple_of(key_at, size), pl.multiple_of(query_at, size)
    same = segc_ref[0, pl.ds(key_at, size), :] == segr_ref[0, :, pl.ds(query_at, size)]
    key_pos = key_at + lax.broadcasted_iota(jnp.int32, (size, size), 0)
    query_pos = query_at + lax.broadcasted_iota(jnp.int32, (size, size), 1)
    return same & (key_pos <= query_pos)


def split_heads(values):
    low = low_lanes(values.shape)
    zero = jnp.zeros_like(values)
    return jnp.concatenate([jnp.where(low, values, zero), jnp.where(low, zero, values)], axis=0)


def is_full(edge_ref, row, key_block, query_block):
    ends = edge_ref.shape[1] // 2
    same = edge_ref[row, 2 * key_block] == edge_ref[row, ends + 2 * query_block + 1]
    return same & (key_block < query_block)


def over_quarters(edge_ref, row, key_block, query_block, update):
    ends = edge_ref.shape[1] // 2

    def quarter(number, carried):
        key_half = 2 * key_block + number % 2
        query_half = 2 * query_block + number // 2
        shared = edge_ref[row, ends + key_half] >= edge_ref[row, query_half]

        @pl.when(shared & (key_half <= query_half))
        def _():
            update(pl.multiple_of(key_half * HALF, HALF), pl.multiple_of(query_half * HALF, HALF))

        return carried

    lax.fori_loop(0, 4, quarter, 0)


def largest(values, head):
    part = jnp.where(low_lanes(values.shape) == (head == 0), values, 0.0)
    return jnp.max(jnp.sum(part * part, axis=1, keepdims=True))


def attend_kernel(
    listed_ref, edge_ref, qkv_ref, segc_ref, segr_ref, mixed_ref, lse_ref,
    vt_ref, qz_ref, acc_ref, stat_ref, *, row,
):
    blocks = qkv_ref.shape[0]
    tall = HEAD_DIM + 16

    def turn(block, tops):
        at = pl.multiple_of(block * BLK, BLK)
        turned = transposed(qkv_ref[block, :, 256:384])
        ones = jnp.ones((16, BLK), jnp.bfloat16)
        for head in range(2):
            vt_ref[head * tall : head * tall + HEAD_DIM, pl.ds(at, BLK)] = turned[
                head * HEAD_DIM : (head + 1) * HEAD_DIM
            ]
            vt_ref[head * tall + HEAD_DIM : (head + 1) * tall, pl.ds(at, BLK)] = ones
        keys = qkv_ref[block, :, 128:256].astype(jnp.float32)
        return tuple(jnp.maximum(tops[head], largest(keys, head)) for head in range(2))

    key_tops = lax.fori_loop(0, blocks, turn, (0.0, 0.0))

    def one_query(query_block, carried):
        query = qkv_ref[query_block, :, :128].astype(jnp.float32) * HEAD_DIM ** (-0.5)
        qz_ref[...] = split_heads(query.astype(jnp.bfloat16))
        acc_ref[...] = jnp.zeros(acc_ref.shape, jnp.float32)
        shift = []
        for head in range(2):
            both = jnp.full((1, BLK), largest(query, head) * key_tops[head], jnp.float32)
            shift.append(jnp.sqrt(both) * 1.01)
        small = (jnp.max(shift[0]) < 40.0) & (jnp.max(shift[1]) < 40.0)

        def over_keys(full_update, part_update):
            def one_key(key_block, carried):
                listed = listed_ref[row, query_block * blocks + key_block] != 0
                full = is_full(edge_ref, row, key_block, query_block)

                @pl.when(listed & full)
                def _():
                    full_update(key_block)

                @pl.when(listed & jnp.logical_not(full))
                def _():
                    part_update(key_block)

                return carried

            lax.fori_loop(0, query_block + 1, one_key, 0)

        @pl.when(small)
        def _():
            def update(key_block, mask):
                at = pl.multiple_of(key_block * BLK, BLK)
                keys = qkv_ref[key_block, :, 128:256]
                parts = [slice(head * BLK, (head + 1) * BLK) for head in range(2)]
                scores = [dot_nt(keys, qz_ref[part, :]) for part in parts]
                for head, part in enumerate(parts):
                    one = scores[head] - shift[head]
                    if mask is not None:
                        one = jnp.where(mask, one, masked_out)
                    value = vt_ref[head * tall : (head + 1) * tall, pl.ds(at, BLK)]
                    acc_ref[:, part] += dot_nn(value, jnp.exp(one).astype(jnp.bfloat16))

            def part_update(key_block):
                update(key_block, tile_mask(segc_ref, segr_ref, key_block * BLK, query_block * BLK, BLK))

            def full_update(key_block):
                update(key_block, None)

            over_keys(full_update, part_update)
            stat_ref[0:1, :] = jnp.concatenate(shift, axis=1)

        @pl.when(jnp.logical_not(small))
        def _():
            stat_ref[0:1, :] = jnp.full((1, 2 * BLK), masked_out, jnp.float32)

            def part_update(key_at, query_at):
                keys = qkv_ref[key_at // BLK, pl.ds(pl.multiple_of(key_at % BLK, HALF), HALF), 128:256]
                mask = tile_mask(segc_ref, segr_ref, key_at, query_at, HALF)
                for head in range(2):
                    part = pl.ds(pl.multiple_of(head * BLK + query_at % BLK, HALF), HALF)
                    scores = jnp.where(mask, dot_nt(keys, qz_ref[part, :]), masked_out)
                    old_max = stat_ref[0:1, part]
                    new_max = jnp.maximum(old_max, jnp.max(scores, axis=0, keepdims=True))
                    weights = jnp.where(mask, jnp.exp(scores - new_max), 0.0)
                    value = vt_ref[head * tall : (head + 1) * tall, pl.ds(key_at, HALF)]
                    shrink = jnp.exp(old_max - new_max)
                    acc_ref[:, part] = acc_ref[:, part] * shrink + dot_nn(value, weights.astype(jnp.bfloat16))
                    stat_ref[0:1, part] = new_max

            def full_update(key_block):
                over_quarters(edge_ref, row, key_block, query_block, part_update)

            over_keys(full_update, full_update)

        total = acc_ref[HEAD_DIM : HEAD_DIM + 1, :]
        mixed = acc_ref[:HEAD_DIM, :] / total
        mixed = jnp.concatenate([mixed[:, :BLK], mixed[:, BLK:]], axis=0).T
        mixed_ref[query_block] = mixed.astype(jnp.bfloat16)
        log_total = stat_ref[0:1, :] + jnp.log(total)
        at = pl.multiple_of(query_block * BLK, BLK)
        lse_ref[0:1, pl.ds(at, BLK)] = log_total[:, :BLK]
        lse_ref[1:2, pl.ds(at, BLK)] = log_total[:, BLK:]
        return carried

    lax.fori_loop(0, blocks, one_query, 0)


def attend(row, listed, edges, qkv, segc, segr):
    blocks, blk, width = qkv.shape
    length = blocks * blk
    pair = 2 * HEAD_DIM
    return pl.pallas_call(
        functools.partial(attend_kernel, row=row),
        grid_spec=pltpu.PrefetchScalarGridSpec(
            num_scalar_prefetch=2,
            grid=(1,),
            in_specs=[
                whole(qkv.shape),
                pl.BlockSpec((1, length, 1), lambda i, *_: (row, 0, 0)),
                pl.BlockSpec((1, 1, length), lambda i, *_: (row, 0, 0)),
            ],
            out_specs=[whole((blocks, blk, pair)), whole((2, length))],
            scratch_shapes=[
                pltpu.VMEM((pair + 32, length), jnp.bfloat16),
                pltpu.VMEM((2 * blk, pair), jnp.bfloat16),
                pltpu.VMEM((HEAD_DIM + 16, 2 * blk), jnp.float32),
                pltpu.VMEM((1, 2 * blk), jnp.float32),
            ],
        ),
        out_shape=[
            jax.ShapeDtypeStruct((blocks, blk, pair), jnp.bfloat16),
            jax.ShapeDtypeStruct((2, length), jnp.float32),
        ],
        compiler_params=params(),
        cost_estimate=cost(20e9, 6e6, 20e6),
        name="attend",
    )(listed, edges, qkv, segc, segr)


def attend_back_kernel(
    listed_ref, edge_ref, qkv_ref, grad_ref, mixed_ref, lse_ref, segc_ref, segr_ref, out_ref,
    kt_ref, qz_ref, gz_ref, inner_ref, dq_ref, dk_ref, dv_ref, *, row,
):
    blocks = qkv_ref.shape[0]
    scale = HEAD_DIM ** (-0.5)

    def prepare(block, carried):
        at = pl.multiple_of(block * BLK, BLK)
        kt_ref[:, pl.ds(at, BLK)] = transposed(qkv_ref[block, :, 128:256])
        query = qkv_ref[block, :, :128].astype(jnp.float32) * scale
        qz_ref[block] = split_heads(query.astype(jnp.bfloat16))
        grad = grad_ref[block]
        gz_ref[block] = split_heads(grad)
        product = (grad.astype(jnp.float32) * mixed_ref[block].astype(jnp.float32)).T
        for head in range(2):
            part = product[head * HEAD_DIM : (head + 1) * HEAD_DIM, :]
            inner_ref[head : head + 1, pl.ds(at, BLK)] = jnp.sum(part, axis=0, keepdims=True)
        return carried

    lax.fori_loop(0, blocks, prepare, 0)
    dq_ref[...] = jnp.zeros(dq_ref.shape, jnp.float32)

    def one_key(key_block, carried):
        dk_ref[...] = jnp.zeros(dk_ref.shape, jnp.float32)
        dv_ref[...] = jnp.zeros(dv_ref.shape, jnp.float32)
        key_at = pl.multiple_of(key_block * BLK, BLK)

        def accumulate(head, key_at, query_at, keys, values, query, grad, mask):
            keys_here = pl.ds(pl.multiple_of(key_at % BLK, HALF), keys.shape[0])
            queries_here = pl.ds(query_at, query.shape[0])
            scores = dot_nt(keys, query)
            probs = jnp.exp(scores - lse_ref[head : head + 1, queries_here])
            if mask is not None:
                probs = jnp.where(mask, probs, 0.0)
            grad_probs = dot_nt(values, grad)
            grad_scores = probs * (grad_probs - inner_ref[head : head + 1, queries_here])
            probs = probs.astype(jnp.bfloat16)
            grad_scores = grad_scores.astype(jnp.bfloat16)
            dv_ref[keys_here, :] += dot_nn(probs, grad)
            dk_ref[keys_here, :] += dot_nn(grad_scores, query)
            lanes = slice(head * HEAD_DIM, (head + 1) * HEAD_DIM)
            dq_ref[lanes, queries_here] += dot_nn(
                kt_ref[lanes, pl.ds(key_at, keys.shape[0])], grad_scores
            )

        def full_update(query_block, mask):
            query_at = pl.multiple_of(query_block * BLK, BLK)
            keys = qkv_ref[key_block, :, 128:256]
            values = qkv_ref[key_block, :, 256:384]
            for head in range(2):
                part = slice(head * BLK, (head + 1) * BLK)
                query, grad = qz_ref[query_block, part, :], gz_ref[query_block, part, :]
                accumulate(head, key_at, query_at, keys, values, query, grad, mask)

        def one_query(query_block, carried):
            listed = listed_ref[row, query_block * blocks + key_block] != 0
            full = is_full(edge_ref, row, key_block, query_block)

            @pl.when(listed & full)
            def _():
                full_update(query_block, None)

            @pl.when(listed & jnp.logical_not(full))
            def _():
                full_update(query_block, tile_mask(segc_ref, segr_ref, key_block * BLK, query_block * BLK, BLK))

            return carried

        lax.fori_loop(key_block, blocks, one_query, 0)
        grad_query = dq_ref[:, pl.ds(key_at, BLK)].T * scale
        out_ref[key_block] = pair_together(grad_query, dk_ref[...], dv_ref[...]).astype(jnp.bfloat16)
        return carried

    lax.fori_loop(0, blocks, one_key, 0)


def attend_back(row, listed, edges, qkv, grad, mixed, lse, segc, segr):
    blocks, blk, width = qkv.shape
    length = blocks * blk
    pair = 2 * HEAD_DIM
    return pl.pallas_call(
        functools.partial(attend_back_kernel, row=row),
        grid_spec=pltpu.PrefetchScalarGridSpec(
            num_scalar_prefetch=2,
            grid=(1,),
            in_specs=[
                whole(qkv.shape),
                whole(grad.shape),
                whole(mixed.shape),
                whole(lse.shape),
                pl.BlockSpec((1, length, 1), lambda i, *_: (row, 0, 0)),
                pl.BlockSpec((1, 1, length), lambda i, *_: (row, 0, 0)),
            ],
            out_specs=whole(qkv.shape),
            scratch_shapes=[
                pltpu.VMEM((pair, length), jnp.bfloat16),
                pltpu.VMEM((blocks, 2 * blk, pair), jnp.bfloat16),
                pltpu.VMEM((blocks, 2 * blk, pair), jnp.bfloat16),
                pltpu.VMEM((2, length), jnp.float32),
                pltpu.VMEM((pair, length), jnp.float32),
                pltpu.VMEM((blk, pair), jnp.float32),
                pltpu.VMEM((blk, pair), jnp.float32),
            ],
        ),
        out_shape=jax.ShapeDtypeStruct(qkv.shape, jnp.bfloat16),
        compiler_params=params(),
        cost_estimate=cost(50e9, 10e6, 20e6),
        name="attend_back",
    )(listed, edges, qkv, grad, mixed, lse, segc, segr)


def joined(ref, first, count):
    return jnp.concatenate([ref[first + i] for i in range(count)], axis=1)


def outward_kernel(mixed_ref, tok_ref, w_ref, scales_ref, hidden_ref, normed_ref, *, row):
    halves = w_ref.shape[1]
    per_half = mixed_ref.shape[0] // halves
    hidden = tok_ref[0].astype(jnp.float32)
    width = hidden.shape[1]
    for half in range(halves):
        hidden += dot_nt(joined(mixed_ref, half * per_half, per_half), w_ref[:, half].reshape(width, -1))
    hidden_ref[...] = hidden
    hat, _ = normalize(hidden)
    normed_ref[...] = (hat * scales_ref[row : row + 1, width:]).astype(jnp.bfloat16)


def outward(row, mixed, tokens, w_all, scales, columns):
    rows, length, width = tokens.shape
    groups, _, pair = mixed.shape
    chunks, halves, high, _ = w_all.shape
    tile = 256
    one = pl.BlockSpec((tile, width), lambda i: (i, 0))
    return pl.pallas_call(
        functools.partial(outward_kernel, row=row),
        grid=(length // tile,),
        in_specs=[
            pl.BlockSpec((groups, tile, pair), lambda i: (0, i, 0)),
            pl.BlockSpec((1, tile, width), lambda i: (row, i, 0)),
            whole((chunks, halves, high, columns)),
            whole(scales.shape),
        ],
        out_specs=[one, one],
        out_shape=[
            jax.ShapeDtypeStruct((length, width), jnp.float32),
            jax.ShapeDtypeStruct((length, width), jnp.bfloat16),
        ],
        compiler_params=params(),
        cost_estimate=cost(2 * length * width * width, 12 * length * width),
        name="outward",
    )(mixed, tokens, w_all, scales)


def mlp_kernel(
    nm0_ref, nm1_ref, cot_ref, hidden0_ref, hidden1_ref, scales_ref, up_ref, down_ref,
    grads_ref, layer_ref, grad_hidden_ref, grad_attn_ref, gscale_ref,
    nmt_ref, cott_ref, out_ref, gn_ref, act_ref, gpre_ref,
):
    tile = pl.program_id(0)
    phase = pl.program_id(1)
    length, width = nm0_ref.shape
    count = 2 * length
    root = 0.7978845608028654
    cube = 0.044715

    @pl.when((tile == 0) & (phase == 0))
    def _():
        nmt_ref[:, :length] = transposed(nm0_ref[...])
        nmt_ref[:, length:] = transposed(nm1_ref[...])
        cott_ref[...] = transposed(cot_ref[...])
        out_ref[...] = jnp.zeros(out_ref.shape, jnp.float32)
        gn_ref[...] = jnp.zeros(gn_ref.shape, jnp.float32)

    @pl.when(phase == 0)
    def _():
        up = up_ref[:, 0].reshape(width, -1)
        down = down_ref[:, 0].reshape(width, -1)
        for row, nm_ref in enumerate((nm0_ref, nm1_ref)):
            part = slice(row * length, (row + 1) * length)
            pre = dot_nn(nm_ref[...], up)
            grad_act = dot_nn(cot_ref[part, :], down)
            square = pre * pre
            bent = jnp.tanh(root * (pre + cube * pre * square))
            half = 0.5 * (1.0 + bent)
            act_ref[part, :] = (pre * half).astype(jnp.bfloat16)
            slope = half + (0.5 * root) * pre * (1.0 - bent * bent) * (1.0 + (3.0 * cube) * square)
            gpre_ref[part, :] = (grad_act * slope).astype(jnp.bfloat16)
        grad = dot_nn(nmt_ref[...], gpre_ref[...]).astype(jnp.bfloat16)
        grads_ref[:, 0] = grad.reshape(grads_ref.shape[0], grads_ref.shape[2], -1)

    @pl.when(phase == 1)
    def _():
        up = up_ref[:, 0].reshape(width, -1)
        down = down_ref[:, 0].reshape(width, -1)
        out_ref[...] += dot_nt(act_ref[...], down)
        gn_ref[...] += dot_nt(gpre_ref[...], up)
        grad = dot_nn(cott_ref[...], act_ref[...]).astype(jnp.bfloat16)
        grads_ref[:, 0] = grad.reshape(grads_ref.shape[0], grads_ref.shape[2], -1)

    @pl.when((tile == pl.num_programs(0) - 1) & (phase == 1))
    def _():
        chunk = 256
        for row, hidden_ref in enumerate((hidden0_ref, hidden1_ref)):
            scale = scales_ref[row : row + 1, width:]
            total = jnp.zeros((1, width), jnp.float32)
            for at in range(0, length, chunk):
                part = slice(row * length + at, row * length + at + chunk)
                hidden = hidden_ref[at : at + chunk, :]
                layer_ref[part, :] = (hidden + out_ref[part, :]).astype(jnp.bfloat16)
                hat, inverse = normalize(hidden)
                grad = gn_ref[part, :]
                total += jnp.sum(grad * hat, axis=0, keepdims=True)
                back = cot_ref[part, :].astype(jnp.float32) + normalize_back(grad * scale, hat, inverse)
                grad_hidden_ref[part, :] = back
                grad_attn_ref[part, :] = back.astype(jnp.bfloat16)
            gscale_ref[row : row + 1, :] = total


def mlp(normed, cotangent, hidden, scales, w_all, skip, hidden_cols):
    rows, length, width = cotangent.shape
    count = rows * length
    chunks, halves, high, columns = w_all.shape
    tile = 512
    per_half = hidden_cols // tile
    first = skip // tile
    flat = (count, width)
    one = (length, width)
    block = (chunks, 1, high, tile)
    return pl.pallas_call(
        mlp_kernel,
        grid=(halves * per_half, 2),
        in_specs=[
            whole(one),
            whole(one),
            whole(flat),
            whole(one),
            whole(one),
            whole(scales.shape),
            pl.BlockSpec(block, lambda f, s: (0, f // per_half, 0, first + f % per_half)),
            pl.BlockSpec(block, lambda f, s: (0, f // per_half, 0, first + per_half + f % per_half)),
        ],
        out_specs=[
            pl.BlockSpec(block, lambda f, s: (0, f // per_half, 0, first + s * per_half + f % per_half)),
            whole(flat),
            whole(flat),
            whole(flat),
            whole((rows, width)),
        ],
        out_shape=[
            jax.ShapeDtypeStruct(w_all.shape, jnp.bfloat16),
            jax.ShapeDtypeStruct(flat, jnp.bfloat16),
            jax.ShapeDtypeStruct(flat, jnp.float32),
            jax.ShapeDtypeStruct(flat, jnp.bfloat16),
            jax.ShapeDtypeStruct((rows, width), jnp.float32),
        ],
        scratch_shapes=[
            pltpu.VMEM((width, count), jnp.bfloat16),
            pltpu.VMEM((width, count), jnp.bfloat16),
            pltpu.VMEM(flat, jnp.float32),
            pltpu.VMEM(flat, jnp.float32),
            pltpu.VMEM((count, tile), jnp.bfloat16),
            pltpu.VMEM((count, tile), jnp.bfloat16),
        ],
        compiler_params=params(60),
        cost_estimate=cost(12 * count * width * halves * hidden_cols, 4 * w_all.size + 16 * count * width),
        name="mlp",
    )(*normed, cotangent.reshape(flat), *hidden, scales, w_all, w_all)


def grad_mixed_kernel(grad_ref, w_ref, out_ref):
    halves = w_ref.shape[1]
    per_half = out_ref.shape[0] // halves
    grad = grad_ref[...]
    pair = out_ref.shape[2]
    for half in range(halves):
        out = dot_nn(grad, w_ref[:, half].reshape(grad.shape[1], -1)).astype(jnp.bfloat16)
        for group in range(per_half):
            out_ref[half * per_half + group] = out[:, group * pair : (group + 1) * pair]


def grad_mixed_of(row, grad_attn, w_all, mixed_shape, columns):
    groups, length, pair = mixed_shape
    chunks, halves, high, _ = w_all.shape
    width = grad_attn.shape[1]
    tile = 256
    tiles = length // tile
    return pl.pallas_call(
        grad_mixed_kernel,
        grid=(tiles,),
        in_specs=[
            pl.BlockSpec((tile, width), lambda i: (row * tiles + i, 0)),
            whole((chunks, halves, high, columns)),
        ],
        out_specs=pl.BlockSpec((groups, tile, pair), lambda i: (0, i, 0)),
        out_shape=jax.ShapeDtypeStruct(mixed_shape, jnp.bfloat16),
        compiler_params=params(),
        cost_estimate=cost(2 * length * width * width, 8 * length * width),
        name="grad_mixed",
    )(grad_attn, w_all)


def grad_proj_kernel(grad_ref, mixed0_ref, mixed1_ref, into_ref, out_ref, turned_ref):
    @pl.when(pl.program_id(0) == 0)
    def _():
        turned_ref[...] = transposed(grad_ref[...])

    groups, length, _ = mixed0_ref.shape
    grad = dot_nn(turned_ref[:, :length], joined(mixed0_ref, 0, groups))
    grad += dot_nn(turned_ref[:, length:], joined(mixed1_ref, 0, groups))
    out_ref[:, 0] = grad.astype(jnp.bfloat16).reshape(out_ref.shape[0], out_ref.shape[2], -1)


def grad_proj_into(grads, grad_attn, mixed, columns):
    groups, length, pair = mixed[0].shape
    chunks, halves, high, _ = grads.shape
    count, width = grad_attn.shape
    given = pl.BlockSpec((groups // halves, length, pair), lambda h: (h, 0, 0))
    return pl.pallas_call(
        grad_proj_kernel,
        grid=(halves,),
        in_specs=[whole(grad_attn.shape), given, given, pl.BlockSpec(memory_space=pl.ANY)],
        out_specs=pl.BlockSpec((chunks, 1, high, columns), lambda h: (0, h, 0, 0)),
        out_shape=jax.ShapeDtypeStruct(grads.shape, jnp.bfloat16),
        scratch_shapes=[pltpu.VMEM((width, count), jnp.bfloat16)],
        input_output_aliases={3: 0},
        compiler_params=params(),
        cost_estimate=cost(2 * count * width * width, 6 * count * width),
        name="grad_proj",
    )(grad_attn, *mixed, grads)


def first_norm_kernel(gq_ref, tok_ref, grad_hidden_ref, w_ref, scales_ref, out_ref, gscale_ref, *, row, q_cols):
    step = pl.program_id(0)
    halves = w_ref.shape[1]
    per_half = gq_ref.shape[0] // halves
    values = tok_ref[0].astype(jnp.float32)
    width = values.shape[1]
    grad = jnp.zeros(values.shape, jnp.float32)
    for half in range(halves):
        weights = w_ref[:, half, :, :q_cols].reshape(width, q_cols)
        grad += dot_nt(joined(gq_ref, half * per_half, per_half), weights)
    hat, inverse = normalize(values)
    total = jnp.sum(grad * hat, axis=0, keepdims=True)

    @pl.when(step == 0)
    def _():
        gscale_ref[...] = total

    @pl.when(step != 0)
    def _():
        gscale_ref[...] += total

    back = normalize_back(grad * scales_ref[row : row + 1, :width], hat, inverse)
    out_ref[...] = (grad_hidden_ref[...] + back).astype(jnp.bfloat16)


def first_norm_back(row, grad_qkv, tokens, grad_hidden, w_all, scales, q_cols):
    rows, length, width = tokens.shape
    groups, _, pair = grad_qkv.shape
    tile = 256
    tiles = length // tile
    return pl.pallas_call(
        functools.partial(first_norm_kernel, row=row, q_cols=q_cols),
        grid=(tiles,),
        in_specs=[
            pl.BlockSpec((groups, tile, pair), lambda i: (0, i, 0)),
            pl.BlockSpec((1, tile, width), lambda i: (row, i, 0)),
            pl.BlockSpec((tile, width), lambda i: (row * tiles + i, 0)),
            whole(w_all.shape),
            whole(scales.shape),
        ],
        out_specs=[pl.BlockSpec((tile, width), lambda i: (i, 0)), whole((1, width))],
        out_shape=[
            jax.ShapeDtypeStruct((length, width), jnp.bfloat16),
            jax.ShapeDtypeStruct((1, width), jnp.float32),
        ],
        compiler_params=params(),
        cost_estimate=cost(2 * length * width * groups * pair, 2 * w_all.size + 20 * length * width),
        name="first_norm_back",
    )(grad_qkv, tokens, grad_hidden, w_all, scales)


def grad_qkv_kernel(me_ref, normed_ref, gq_ref, *refs, chunks):
    *base_refs, keep_ref, send_ref, turned_ref = refs
    width = normed_ref.shape[1]

    @pl.when(pl.program_id(0) == 0)
    def _():
        turned_apart(turned_ref, normed_ref[...], me_ref[0], chunks)

    pair = gq_ref.shape[2]
    for one in range(gq_ref.shape[0]):
        found = dot_nn(turned_ref[...], gq_ref[one])
        lanes = slice(one * pair, (one + 1) * pair)
        if keep_ref.shape[0] == 1:
            at = (0, slice(None), slice(None), slice(None), lanes)
        else:
            at = (slice(None), 0, slice(None), slice(None), lanes)
        for number, out_ref in enumerate((keep_ref, send_ref)):
            part = found[number * width // 2 : (number + 1) * width // 2]
            part = part.reshape(2, chunks // 4, width // chunks, pair)
            for base_ref in base_refs[number : number + 1]:
                part += base_ref[at]
            out_ref[at] = part.astype(out_ref.dtype)


def grad_qkv_of(me, normed, grad_qkv, chunks, halves, first, some, at_front, base=()):
    length, width = normed.shape
    groups, _, pair = grad_qkv.shape
    pairs = groups // halves
    high = width // chunks
    quarter = chunks // 4
    columns = some * pair
    if at_front:
        out = pl.BlockSpec((1, 2, quarter, high, columns), lambda h, me: (h ^ me[1], 0, 0, 0, 0))
    else:
        out = pl.BlockSpec((2, 1, quarter, high, columns), lambda h, me: (0, h ^ me[1], 0, 0, 0))
    dtype = jnp.bfloat16 if base else jnp.float32
    wide = jax.ShapeDtypeStruct((halves, 2, quarter, high, columns), dtype)
    given = pl.BlockSpec((some, length, pair), lambda h, me: ((h * pairs + first) // some, 0, 0))
    return pl.pallas_call(
        functools.partial(grad_qkv_kernel, chunks=chunks),
        grid_spec=pltpu.PrefetchScalarGridSpec(
            num_scalar_prefetch=1,
            grid=(halves,),
            in_specs=[whole((length, width)), given] + [out] * len(base),
            out_specs=[out, out],
            scratch_shapes=[pltpu.VMEM((width, length), jnp.bfloat16)],
        ),
        out_shape=[wide] * 2,
        compiler_params=params(),
        cost_estimate=cost(2 * length * width * halves * some * pair, 6 * length * width),
        name="grad_qkv",
    )(me, normed, grad_qkv, *base)


def grad_time_kernel(me_ref, tet_ref, gs_ref, keep_ref, send_ref, apart_ref, *, chunks, folds, t_cols):
    bits = chunks.bit_length() - 1
    k_rows = tet_ref.shape[0] // chunks
    for chunk in range(chunks):
        apart = chunk ^ me_ref[0]
        place = 0
        for bit in range(bits):
            place += ((apart >> bit) & 1) << (bits - 1 - bit)
        apart_ref[pl.ds(pl.multiple_of(place * k_rows, k_rows), k_rows), :] = tet_ref[
            chunk * k_rows : (chunk + 1) * k_rows, :
        ]
    half = pl.program_id(0)
    shape = keep_ref.shape[1:3] + (k_rows, t_cols)
    middle = chunks * k_rows // 2
    for fold in range(folds):
        at = pl.multiple_of((half * folds + fold) * t_cols, t_cols)
        total = jnp.zeros((chunks * k_rows, t_cols), jnp.float32)
        for row in range(gs_ref.shape[0]):
            total += apart_ref[:, row : row + 1] * gs_ref[row : row + 1, pl.ds(at, t_cols)]
        total = total.astype(jnp.bfloat16)
        rows = slice(fold * k_rows, (fold + 1) * k_rows)
        keep_ref[0, :, :, rows, :] = total[:middle].reshape(shape)
        send_ref[0, :, :, rows, :] = total[middle:].reshape(shape)


def grad_time_of(me, time_embed, grad_scales, chunks, halves, high, k_rows, t_cols):
    turned = time_embed.T
    quarter = chunks // 4
    thin = jax.ShapeDtypeStruct((halves, 2, quarter, high, t_cols), jnp.bfloat16)
    out = pl.BlockSpec((1, 2, quarter, high, t_cols), lambda h, me: (h ^ me[1], 0, 0, 0, 0))
    return pl.pallas_call(
        functools.partial(grad_time_kernel, chunks=chunks, folds=high // k_rows, t_cols=t_cols),
        grid_spec=pltpu.PrefetchScalarGridSpec(
            num_scalar_prefetch=1,
            grid=(halves,),
            in_specs=[whole(turned.shape), whole(grad_scales.shape)],
            out_specs=[out, out],
            scratch_shapes=[pltpu.VMEM(turned.shape, jnp.float32)],
        ),
        out_shape=[thin] * 2,
        compiler_params=params(),
        cost_estimate=cost(4 * turned.shape[0] * grad_scales.size, 4 * grad_scales.size),
        name="grad_time",
    )(me, turned, grad_scales)


def across(values, axis, apart):
    size = math.prod(lax.axis_size(name) for name in ([axis] if isinstance(axis, str) else axis))
    return lax.ppermute(values, axis, [(i, i ^ apart) for i in range(size)])


def summed(parts, index):
    total = parts[0][index].astype(jnp.float32)
    for part in parts[1:]:
        total += part[index].astype(jnp.float32)
    return total


HOPS = {"x": ("ctx", 2), "y": ("tp", 1)}


class TreeSum:
    def __init__(self, keep, send, order, stages):
        self.parts = [keep, across(send, "ctx", 1)]
        self.order = order
        self.left = list(stages)

    def ready(self):
        name = self.left[0]
        if name in HOPS:
            places = {1: HOPS[name]}
        elif name == "xy":
            first, second = HOPS[self.order[0]], HOPS[self.order[1]]
            both = (GROUP, 2 * lax.axis_size("tp") + 1)
            places = {(1, 1): both, (1, 0): first, (0, 1): second}
        else:
            places = {3: ("fsdp", 3), 1: ("fsdp", 2), 2: ("fsdp", 1)}
        self.hops = list(places.values())
        self.given = [summed(self.parts, place).astype(jnp.bfloat16) for place in places]
        return self.given

    def go(self):
        lower = (0, 0) if self.left.pop(0) == "xy" else 0
        got = [across(one, *hop) for one, hop in zip(self.given, self.hops)]
        self.parts = [part[lower] for part in self.parts] + got

    def finish(self):
        while self.left:
            self.ready()
            self.go()
        return summed(self.parts, slice(None))


def together(value, trees):
    given = [tree.ready() for tree in trees]
    value, given = lax.optimization_barrier((value, given))
    for tree, some in zip(trees, given):
        tree.given = some
        tree.go()
    return value


def after(value, tree):
    value, tree.parts = lax.optimization_barrier((value, tree.parts))
    return value


def listed_table(block_pairs, pair_counts, row_blocks, ctx_size):
    rows, _, slots, _ = block_pairs.shape
    packed = jnp.concatenate([block_pairs.reshape(rows, 1, slots * 2), pair_counts[:, :, None]], axis=2)
    packed = jnp.concatenate(
        [packed] + [across(packed, "ctx", apart) for apart in range(1, ctx_size)], axis=1
    )
    pairs = packed[:, :, : slots * 2].reshape(rows, ctx_size, slots, 2)
    live = jnp.arange(slots, dtype=jnp.int32)[None, None, :] < packed[:, :, slots * 2 :]
    owner = lax.axis_index("ctx") ^ jnp.arange(ctx_size, dtype=jnp.int32)[None, :, None]
    base = owner * (row_blocks // ctx_size)
    code = jnp.where(live, (base + pairs[..., 0]) * row_blocks + pairs[..., 1], -1)
    code = code.reshape(rows, ctx_size * slots)
    cells = jnp.arange(row_blocks * row_blocks, dtype=jnp.int32)
    return jnp.any(code[:, :, None] == cells[None, None, :], axis=1).astype(jnp.int32)


EVERY = ("fsdp", "ctx", "tp")
GROUP = ("ctx", "tp")


def spread_body(
    tokens, time_embed, segment_ids, block_pairs, pair_counts,
    w_time, w_qkv, w_out, w_up, w_down, cotangent,
):
    rows, length, width = tokens.shape
    chunks = width // w_qkv.shape[0]
    halves = lax.axis_size("tp")
    high = w_qkv.shape[0]
    q_cols, o_cols, f_cols = w_qkv.shape[1], w_out.shape[1], w_up.shape[1]
    k_rows = w_time.shape[0]
    t_all = w_time.shape[1] // halves
    folds = high // k_rows
    t_cols = t_all // folds
    mine = lax.axis_index("tp")
    me = jnp.stack([lax.axis_index("fsdp") * lax.axis_size("ctx") + lax.axis_index("ctx"), mine])
    time_part = lax.dynamic_slice_in_dim(w_time, mine * t_all, t_all, 1)
    time_part = time_part.reshape(k_rows, folds, t_cols).transpose(1, 0, 2).reshape(high, t_cols)
    first = jnp.concatenate([w_qkv, time_part], axis=1).astype(jnp.bfloat16)
    second = jnp.concatenate([w_out, w_up, w_down], axis=1).astype(jnp.bfloat16)
    first = lax.all_gather(first, EVERY, axis=0, tiled=True).reshape(chunks, halves, high, -1)
    second = lax.all_gather(second, EVERY, axis=0, tiled=True).reshape(chunks, halves, high, -1)

    row_blocks = segment_ids.shape[1] // BLK
    listed = listed_table(block_pairs, pair_counts, row_blocks, lax.axis_size("ctx"))
    edges = jnp.concatenate([segment_ids[:, ::HALF], segment_ids[:, HALF - 1 :: HALF]], axis=1)
    segc = segment_ids[:, :, None]
    segr = segment_ids[:, None, :]

    time_embed, listed, edges, segc, segr = lax.optimization_barrier(
        (time_embed, listed, edges, segc, segr)
    )
    qkv, normed = [], []
    for row in range(rows):
        out, one, scales = project(row, time_embed, tokens, first, k_rows, q_cols, t_cols)
        qkv.append(lax.all_to_all(out, GROUP, 0, 0, tiled=True))
        normed.append(one)
    mixed_own, lse, mixed = [], [], []
    for row in range(rows):
        out, one = attend(row, listed, edges, qkv[row], segc, segr)
        mixed_own.append(out)
        lse.append(one)
        mixed.append(lax.all_to_all(out, GROUP, 0, 0, tiled=True))
    hidden, normed_mlp = [], []
    for row in range(rows):
        out, one = outward(row, mixed[row], tokens, second, scales, o_cols)
        hidden.append(out)
        normed_mlp.append(one)
    grads, layer_out, grad_hidden, grad_attn, gscale_mlp = mlp(
        normed_mlp, cotangent, hidden, scales, second, o_cols, f_cols
    )
    grad_mixed = {}
    for row in reversed(range(rows)):
        out = grad_mixed_of(row, grad_attn, second, mixed[row].shape, o_cols)
        grad_mixed[row] = lax.all_to_all(out, GROUP, 0, 0, tiled=True)
    grads = grad_proj_into(grads, grad_attn, mixed, o_cols)
    last = rows - 1
    grad_mixed[last], grads = lax.optimization_barrier((grad_mixed[last], grads))
    grads = lax.psum_scatter(grads.reshape(-1, grads.shape[3]), EVERY, scatter_dimension=0, tiled=True)
    grad_qkv = {}
    for row in reversed(range(rows)):
        out = attend_back(row, listed, edges, qkv[row], grad_mixed[row], mixed_own[row], lse[row], segc, segr)
        grad_qkv[row] = lax.all_to_all(out, GROUP, 0, 0, tiled=True)
    some = q_cols // (6 * HEAD_DIM) // 2
    held, _ = lax.optimization_barrier((grad_qkv[last], out))
    a_base = grad_qkv_of(me, normed[last], held, chunks, halves, 0, some, True)
    b_base = grad_qkv_of(me, normed[last], held, chunks, halves, some, some, False)
    grad_tokens, gscale_attn = {}, {}
    grad_tokens[last], gscale_attn[last] = first_norm_back(
        last, held, tokens, grad_hidden, first, scales, q_cols
    )
    held, gscale_attn[last], a_base, b_base = lax.optimization_barrier(
        (grad_qkv[0], gscale_attn[last], a_base, b_base)
    )
    a_keep, a_send = grad_qkv_of(me, normed[0], held, chunks, halves, 0, some, True, a_base)
    a_tree = TreeSum(a_keep, a_send, "yx", ["xy", "z"])
    held, a_keep = lax.optimization_barrier((held, a_keep))
    b_keep, b_send = grad_qkv_of(me, normed[0], held, chunks, halves, some, some, False, b_base)
    b_tree = TreeSum(b_keep, b_send, "xy", ["xy", "z"])
    held, b_keep = lax.optimization_barrier((held, b_keep))
    held = together(held, [a_tree])
    grad_tokens[0], gscale_attn[0] = first_norm_back(0, held, tokens, grad_hidden, first, scales, q_cols)
    gscale_attn = jnp.concatenate([gscale_attn[row] for row in range(rows)], axis=0)
    grad_scales = jnp.concatenate([gscale_attn, gscale_mlp], axis=1)
    grad_scales = together(grad_scales, [b_tree])
    t_keep, t_send = grad_time_of(me, time_embed, grad_scales, chunks, halves, high, k_rows, t_cols)
    t_tree = TreeSum(t_keep, t_send, "yx", ["xy", "z"])
    t_tree.parts = together(t_tree.parts, [a_tree])
    b_tree.parts = together(b_tree.parts, [t_tree])
    a_sum = a_tree.finish()
    t_tree.parts = together(t_tree.parts, [b_tree])
    grad_time = t_tree.finish().reshape(folds, k_rows, t_cols)
    grad_time = grad_time.transpose(1, 0, 2).reshape(k_rows, t_all)
    other = across(grad_time.astype(jnp.bfloat16), "tp", 1).astype(jnp.float32)
    b_sum = b_tree.finish()
    grad_time = jnp.concatenate(
        [jnp.where(mine == 0, grad_time, other), jnp.where(mine == 0, other, grad_time)], axis=1
    )
    f32 = jnp.float32
    return (
        layer_out.reshape(tokens.shape),
        jnp.stack([grad_tokens[row] for row in range(rows)]),
        grad_time,
        jnp.concatenate([a_sum, b_sum], axis=1),
        grads[:, :o_cols].astype(f32),
        grads[:, o_cols : o_cols + f_cols].astype(f32),
        grads[:, o_cols + f_cols :].astype(f32),
    )


def choose(*args):
    tokens, w_qkv, w_out, w_up = args[0], args[6], args[7], args[8]
    group = lax.axis_size("ctx") * lax.axis_size("tp")
    heads_pair = 6 * HEAD_DIM
    fits = (
        (lax.axis_size("fsdp"), lax.axis_size("ctx"), lax.axis_size("tp")) == (4, 4, 2)
        and tokens.shape[1] == BLK
        and group * BLK == args[2].shape[1]
        and w_qkv.shape[1] * lax.axis_size("tp") == group * heads_pair
        and w_out.shape[1] % 512 == 0
        and w_up.shape[1] % 512 == 0
        and w_qkv.shape[0] % args[5].shape[0] == 0
    )
    return spread_body(*args) if fits else body(*args)


def solution(mesh):
    placed = (
        P("fsdp", ("ctx", "tp"), None),
        P("fsdp", None),
        P("fsdp", None),
        P("fsdp", "ctx", None, None),
        P("fsdp", "ctx"),
        P(("fsdp", "ctx"), None),
        P(("fsdp", "ctx"), "tp"),
        P(("fsdp", "ctx"), "tp"),
        P(("fsdp", "ctx"), "tp"),
        P(("fsdp", "ctx"), "tp"),
        P("fsdp", ("ctx", "tp"), None),
    )
    return jax.shard_map(
        choose,
        mesh=mesh,
        in_specs=placed,
        out_specs=(
            P("fsdp", ("ctx", "tp"), None),
            P("fsdp", ("ctx", "tp"), None),
            P(("fsdp", "ctx"), None),
            P(("fsdp", "ctx"), "tp"),
            P(("fsdp", "ctx"), "tp"),
            P(("fsdp", "ctx"), "tp"),
            P(("fsdp", "ctx"), "tp"),
        ),
        check_vma=False,
    )
```

```python
import functools

import jax
import jax.numpy as jnp
from jax import lax
from jax.experimental import pallas as pl
from jax.experimental.pallas import tpu as pltpu
from jax.sharding import Mesh
from jax.sharding import PartitionSpec as P

HEAD_DIM = 64
BLK = 512


epsilon = 1e-05
highest = lax.Precision.HIGHEST
masked_out = -1e30


def normalize(values):
    mean_value = jnp.mean(values, axis=-1, keepdims=True)
    centred = values - mean_value
    variance = jnp.mean(centred * centred, axis=-1, keepdims=True)
    inverse = lax.rsqrt(variance + epsilon)
    return (centred * inverse, inverse)


def normalize_back(grad_hat, normal_hat, inverse):
    first_mean = jnp.mean(grad_hat, axis=-1, keepdims=True)
    second_mean = jnp.mean(grad_hat * normal_hat, axis=-1, keepdims=True)
    return inverse * (grad_hat - first_mean - normal_hat * second_mean)


def smooth_gate(values):
    return jax.nn.gelu(values, approximate=True)


def block_scores(pair_entry, query_rows, key_rows, seg_row, offset):
    query_start = pair_entry[0] * BLK
    key_start = pair_entry[1] * BLK
    query_block = lax.dynamic_slice_in_dim(query_rows, query_start, BLK, 0)
    key_block = lax.dynamic_slice_in_dim(key_rows, key_start, BLK, 0)
    seg_query = lax.dynamic_slice_in_dim(seg_row, offset + query_start, BLK, 0)
    seg_keys = lax.dynamic_slice_in_dim(seg_row, key_start, BLK, 0)
    steps_in = jnp.arange(BLK, dtype=jnp.int32)
    allowed = (seg_query[:, None] == seg_keys[None, :]) & (
        key_start + steps_in[None, :] <= offset + query_start + steps_in[:, None]
    )
    scores = jnp.einsum(
        "qhe,khe->hqk", query_block, key_block, preferred_element_type=jnp.float32
    ) * HEAD_DIM ** (-0.5)
    return (query_block, key_block, query_start, key_start, allowed, scores)


def attend_forward(query_rows, key_rows, value_rows, seg_row, pair_rows, pair_total, offset):
    length_here, head_count, _ = query_rows.shape

    def statistic_step(pair_index, carried):
        running_max, running_sum = carried
        _, _, query_start, _, allowed, scores = block_scores(
            pair_rows[pair_index], query_rows, key_rows, seg_row, offset
        )
        scores = jnp.where(allowed[None], scores, masked_out)
        old_max = lax.dynamic_slice_in_dim(running_max, query_start, BLK, 1)
        old_sum = lax.dynamic_slice_in_dim(running_sum, query_start, BLK, 1)
        new_max = jnp.maximum(old_max, jnp.max(scores, axis=-1))
        weights = jnp.where(allowed[None], jnp.exp(scores - new_max[:, :, None]), 0.0)
        new_sum = old_sum * jnp.exp(old_max - new_max) + jnp.sum(weights, axis=-1)
        return (
            lax.dynamic_update_slice_in_dim(running_max, new_max, query_start, 1),
            lax.dynamic_update_slice_in_dim(running_sum, new_sum, query_start, 1),
        )

    start_max = jnp.full((head_count, length_here), masked_out, jnp.float32)
    start_sum = jnp.zeros((head_count, length_here), jnp.float32)
    running_max, running_sum = lax.fori_loop(0, pair_total, statistic_step, (start_max, start_sum))
    log_total = running_max + jnp.log(running_sum)

    def output_step(pair_index, accumulated):
        _, _, query_start, key_start, allowed, scores = block_scores(
            pair_rows[pair_index], query_rows, key_rows, seg_row, offset
        )
        block_log = lax.dynamic_slice_in_dim(log_total, query_start, BLK, 1)
        probabilities = jnp.where(
            allowed[None], jnp.exp(scores - block_log[:, :, None]), 0.0
        ).astype(jnp.bfloat16)
        value_block = lax.dynamic_slice_in_dim(value_rows, key_start, BLK, 0)
        addition = jnp.einsum(
            "hqk,khe->qhe", probabilities, value_block, preferred_element_type=jnp.float32
        )
        previous = lax.dynamic_slice_in_dim(accumulated, query_start, BLK, 0)
        return lax.dynamic_update_slice_in_dim(accumulated, previous + addition, query_start, 0)

    mixed_rows = lax.fori_loop(0, pair_total, output_step, jnp.zeros(query_rows.shape, jnp.float32))
    return (mixed_rows, log_total)


def attend_backward(
    query_rows,
    key_rows,
    value_rows,
    seg_row,
    pair_rows,
    pair_total,
    offset,
    log_total,
    grad_mixed,
    inner_sums,
):
    scale_factor = HEAD_DIM ** (-0.5)

    def add_block(whole, start_at, addition):
        previous = lax.dynamic_slice_in_dim(whole, start_at, BLK, 0)
        return lax.dynamic_update_slice_in_dim(whole, previous + addition, start_at, 0)

    def gradient_step(pair_index, carried):
        grad_query, grad_keys, grad_values = carried
        query_block, key_block, query_start, key_start, allowed, scores = block_scores(
            pair_rows[pair_index], query_rows, key_rows, seg_row, offset
        )
        block_log = lax.dynamic_slice_in_dim(log_total, query_start, BLK, 1)
        probabilities = jnp.where(allowed[None], jnp.exp(scores - block_log[:, :, None]), 0.0)
        grad_block = lax.dynamic_slice_in_dim(grad_mixed, query_start, BLK, 0)
        value_block = lax.dynamic_slice_in_dim(value_rows, key_start, BLK, 0)
        grad_probs = jnp.einsum(
            "qhe,khe->hqk", grad_block, value_block, preferred_element_type=jnp.float32
        )
        inner_block = lax.dynamic_slice_in_dim(inner_sums, query_start, BLK, 1)
        grad_scores = (probabilities * (grad_probs - inner_block[:, :, None])).astype(jnp.bfloat16)
        query_add = (
            jnp.einsum("hqk,khe->qhe", grad_scores, key_block, preferred_element_type=jnp.float32)
            * scale_factor
        )
        key_add = (
            jnp.einsum("hqk,qhe->khe", grad_scores, query_block, preferred_element_type=jnp.float32)
            * scale_factor
        )
        value_add = jnp.einsum(
            "hqk,qhe->khe",
            probabilities.astype(jnp.bfloat16),
            grad_block,
            preferred_element_type=jnp.float32,
        )
        return (
            add_block(grad_query, query_start, query_add),
            add_block(grad_keys, key_start, key_add),
            add_block(grad_values, key_start, value_add),
        )

    start_state = (
        jnp.zeros(query_rows.shape, jnp.float32),
        jnp.zeros(key_rows.shape, jnp.float32),
        jnp.zeros(value_rows.shape, jnp.float32),
    )
    return lax.fori_loop(0, pair_total, gradient_step, start_state)


def body(
    tokens,
    time_embed,
    segment_ids,
    block_pairs,
    pair_counts,
    w_time,
    w_qkv,
    w_out,
    w_up,
    w_down,
    cotangent,
):
    row_count, local_len, model_width = tokens.shape
    time_all, qkv_all, out_all, up_all, down_all = (
        lax.all_gather(w_time.astype(jnp.bfloat16), ("fsdp", "ctx"), axis=0, tiled=True),
        lax.all_gather(w_qkv.astype(jnp.bfloat16), ("fsdp", "ctx"), axis=0, tiled=True),
        lax.all_gather(w_out.astype(jnp.bfloat16), ("fsdp", "ctx"), axis=0, tiled=True),
        lax.all_gather(w_up.astype(jnp.bfloat16), ("fsdp", "ctx"), axis=0, tiled=True),
        lax.all_gather(w_down.astype(jnp.bfloat16), ("fsdp", "ctx"), axis=0, tiled=True),
    )
    scales = 1.0 + jnp.dot(time_embed, time_all.astype(jnp.float32), precision=highest)
    scale_attn = scales[:, None, :model_width]
    scale_mlp = scales[:, None, model_width:]
    x_input = tokens.astype(jnp.float32)
    hat_attn, inverse_attn = normalize(x_input)
    normed = (hat_attn * scale_attn).astype(jnp.bfloat16)
    normed_all = lax.all_gather(normed, "tp", axis=1, tiled=True)
    ctx_len = normed_all.shape[1]
    head_count = qkv_all.shape[1] // (3 * HEAD_DIM)
    projected = jnp.einsum("rtd,dc->rtc", normed_all, qkv_all, preferred_element_type=jnp.float32)
    projected = projected.astype(jnp.bfloat16).reshape(row_count, ctx_len, head_count, 3, HEAD_DIM)
    query_all = projected[:, :, :, 0]
    key_part = projected[:, :, :, 1]
    value_part = projected[:, :, :, 2]
    key_all, value_all = (
        lax.all_gather(key_part, "ctx", axis=1, tiled=True),
        lax.all_gather(value_part, "ctx", axis=1, tiled=True),
    )
    offset = lax.axis_index("ctx") * ctx_len
    mixed_list = []
    log_list = []
    for row_index in range(row_count):
        mixed_rows, log_total = attend_forward(
            query_all[row_index],
            key_all[row_index],
            value_all[row_index],
            segment_ids[row_index],
            block_pairs[row_index, 0],
            pair_counts[row_index, 0],
            offset,
        )
        mixed_list.append(mixed_rows)
        log_list.append(log_total)
    mixed_exact = jnp.stack(mixed_list)
    mixed_heads = mixed_exact.astype(jnp.bfloat16).reshape(
        row_count, ctx_len, head_count * HEAD_DIM
    )
    attn_part = jnp.einsum("rtc,dc->rtd", mixed_heads, out_all, preferred_element_type=jnp.float32)
    attn_local = lax.psum_scatter(
        attn_part.astype(jnp.bfloat16), "tp", scatter_dimension=1, tiled=True
    ).astype(jnp.float32)
    hidden = x_input + attn_local
    hat_mlp, inverse_mlp = normalize(hidden)
    normed_mlp = (hat_mlp * scale_mlp).astype(jnp.bfloat16)
    mlp_all = lax.all_gather(normed_mlp, "tp", axis=1, tiled=True)
    pre_act = jnp.einsum("rtd,df->rtf", mlp_all, up_all, preferred_element_type=jnp.float32)
    activated = smooth_gate(pre_act).astype(jnp.bfloat16)
    mlp_part = jnp.einsum("rtf,df->rtd", activated, down_all, preferred_element_type=jnp.float32)
    mlp_local = lax.psum_scatter(
        mlp_part.astype(jnp.bfloat16), "tp", scatter_dimension=1, tiled=True
    ).astype(jnp.float32)
    grad_all = lax.all_gather(cotangent, "tp", axis=1, tiled=True)
    grad_act = jnp.einsum("rtd,df->rtf", grad_all, down_all, preferred_element_type=jnp.float32)
    _, gate_back = jax.vjp(smooth_gate, pre_act)
    grad_pre = gate_back(grad_act)[0].astype(jnp.bfloat16)
    grad_down = jnp.einsum("rtd,rtf->df", grad_all, activated, preferred_element_type=jnp.float32)
    grad_up = jnp.einsum("rtd,rtf->df", mlp_all, grad_pre, preferred_element_type=jnp.float32)
    norm_part = jnp.einsum("rtf,df->rtd", grad_pre, up_all, preferred_element_type=jnp.float32)
    grad_normed_mlp = lax.psum_scatter(
        norm_part.astype(jnp.bfloat16), "tp", scatter_dimension=1, tiled=True
    ).astype(jnp.float32)
    layer_out = (hidden + mlp_local).astype(jnp.bfloat16)
    grad_output = cotangent.astype(jnp.float32)
    grad_scale_mlp = jnp.sum(grad_normed_mlp * hat_mlp, axis=1)
    grad_hidden = grad_output + normalize_back(grad_normed_mlp * scale_mlp, hat_mlp, inverse_mlp)
    grad_attn_all = lax.all_gather(grad_hidden.astype(jnp.bfloat16), "tp", axis=1, tiled=True)
    grad_mixed = jnp.einsum(
        "rtd,dc->rtc", grad_attn_all, out_all, preferred_element_type=jnp.float32
    ).astype(jnp.bfloat16)
    grad_proj = jnp.einsum(
        "rtd,rtc->dc", grad_attn_all, mixed_heads, preferred_element_type=jnp.float32
    )
    grad_mixed = grad_mixed.reshape(row_count, ctx_len, head_count, HEAD_DIM)
    inner_sums = jnp.einsum("rqhe,rqhe->rhq", grad_mixed.astype(jnp.float32), mixed_exact)
    query_grads = []
    key_grads = []
    value_grads = []
    for row_index in range(row_count):
        grad_query, grad_keys, grad_values = attend_backward(
            query_all[row_index],
            key_all[row_index],
            value_all[row_index],
            segment_ids[row_index],
            block_pairs[row_index, 0],
            pair_counts[row_index, 0],
            offset,
            log_list[row_index],
            grad_mixed[row_index],
            inner_sums[row_index],
        )
        query_grads.append(grad_query)
        key_grads.append(grad_keys)
        value_grads.append(grad_values)
    key_local, value_local = (
        lax.psum_scatter(
            jnp.stack(key_grads).astype(jnp.bfloat16), "ctx", scatter_dimension=1, tiled=True
        ).astype(jnp.float32),
        lax.psum_scatter(
            jnp.stack(value_grads).astype(jnp.bfloat16), "ctx", scatter_dimension=1, tiled=True
        ).astype(jnp.float32),
    )
    grad_projected = jnp.stack(
        [
            jnp.stack(query_grads).astype(jnp.bfloat16),
            key_local.astype(jnp.bfloat16),
            value_local.astype(jnp.bfloat16),
        ],
        axis=3,
    )
    grad_projected = grad_projected.reshape(row_count, ctx_len, head_count * 3 * HEAD_DIM)
    grad_qkv = jnp.einsum(
        "rtd,rtc->dc", normed_all, grad_projected, preferred_element_type=jnp.float32
    )
    first_part = jnp.einsum(
        "rtc,dc->rtd", grad_projected, qkv_all, preferred_element_type=jnp.float32
    )
    grad_normed = lax.psum_scatter(
        first_part.astype(jnp.bfloat16), "tp", scatter_dimension=1, tiled=True
    ).astype(jnp.float32)
    grad_scale_attn = jnp.sum(grad_normed * hat_attn, axis=1)
    grad_tokens = grad_hidden + normalize_back(grad_normed * scale_attn, hat_attn, inverse_attn)
    grad_scales = lax.psum(jnp.concatenate([grad_scale_attn, grad_scale_mlp], axis=1), "tp")
    grad_time = jnp.dot(time_embed.T, grad_scales, precision=highest)
    shared = (
        lax.psum_scatter(
            grad_time.astype(jnp.bfloat16), ("fsdp", "ctx"), scatter_dimension=0, tiled=True
        ).astype(jnp.float32),
        lax.psum_scatter(
            grad_qkv.astype(jnp.bfloat16), ("fsdp", "ctx"), scatter_dimension=0, tiled=True
        ).astype(jnp.float32),
        lax.psum_scatter(
            grad_proj.astype(jnp.bfloat16), ("fsdp", "ctx"), scatter_dimension=0, tiled=True
        ).astype(jnp.float32),
        lax.psum_scatter(
            grad_up.astype(jnp.bfloat16), ("fsdp", "ctx"), scatter_dimension=0, tiled=True
        ).astype(jnp.float32),
        lax.psum_scatter(
            grad_down.astype(jnp.bfloat16), ("fsdp", "ctx"), scatter_dimension=0, tiled=True
        ).astype(jnp.float32),
    )
    return (
        layer_out,
        grad_tokens.astype(jnp.bfloat16),
        shared[0],
        shared[1],
        shared[2],
        shared[3],
        shared[4],
    )


def params(limit=58):
    return pltpu.CompilerParams(vmem_limit_bytes=limit * 1024 * 1024)


def whole(shape):
    zeros = (0,) * len(shape)
    return pl.BlockSpec(shape, lambda *_: zeros, pipeline_mode=pl.Buffered(1))


def cost(flops, nbytes, exps=0):
    return pl.CostEstimate(flops=int(flops), bytes_accessed=int(nbytes), transcendentals=int(exps))


def dot_nn(left, right):
    return jnp.dot(left, right, preferred_element_type=jnp.float32)


def dot_nt(left, right):
    return lax.dot_general(left, right, (((1,), (1,)), ((), ())), preferred_element_type=jnp.float32)


def transposed(values):
    return values.astype(jnp.float32).T.astype(values.dtype)


def turned_apart(into_ref, values, core, chunks):
    turned = transposed(values)
    high = turned.shape[0] // chunks
    for chunk in range(chunks):
        inner = (chunk // 2 % 2) * (chunks // 4) + chunk // 4
        at = ((chunk % 2) ^ core) * (chunks // 2) + inner
        into_ref[pl.ds(pl.multiple_of(at * high, high), high), :] = turned[chunk * high : (chunk + 1) * high]


def put_apart(keep_ref, send_ref, grad):
    middle = grad.shape[0] // 2
    shape = (keep_ref.shape[0],) + keep_ref.shape[2:]
    keep_ref[:, 0] = grad[:middle].reshape(shape)
    send_ref[:, 0] = grad[middle:].reshape(shape)


def low_lanes(shape):
    return lax.broadcasted_iota(jnp.int32, shape, 1) < HEAD_DIM


def pair_apart(stored):
    first, second, third = stored[:, :128], stored[:, 128:256], stored[:, 256:]
    low = low_lanes(first.shape)
    keys = pltpu.roll(jnp.where(low, third, first), HEAD_DIM, 1)
    return jnp.concatenate(
        [jnp.where(low, first, second), keys, jnp.where(low, second, third)], axis=1
    )


def pair_together(query, keys, values):
    low = low_lanes(query.shape)
    turned = pltpu.roll(keys, HEAD_DIM, 1)
    return jnp.concatenate(
        [jnp.where(low, query, turned), jnp.where(low, values, query), jnp.where(low, turned, values)],
        axis=1,
    )


def project_kernel(place_ref, scales_ref, *refs, row, pieces, parts):
    weight_refs, token_refs = refs[:parts], refs[parts : parts + pieces]
    qkv_ref, normed_ref, held_ref, w_ref, sem_ref = refs[parts + pieces :]
    step = pl.program_id(0)

    def fetch(piece):
        source = token_refs[piece]
        source = source.at[row] if len(source.shape) == 3 else source
        return pltpu.make_async_copy(source, held_ref.at[piece], sem_ref.at[piece])

    @pl.when(step == 0)
    def _():
        for piece in range(pieces):
            fetch(piece).start()
        tall = weight_refs[0].shape[0]
        for apart, weight_ref in enumerate(weight_refs):
            at = pl.multiple_of((apart ^ place_ref[1]) * tall, tall)
            w_ref[pl.ds(at, tall), :] = pair_apart(weight_ref[...].astype(jnp.float32)).astype(jnp.bfloat16)
    pltpu.make_async_copy(held_ref.at[step], held_ref.at[step], sem_ref.at[step]).wait()
    values = held_ref[step].astype(jnp.float32)
    width = values.shape[1]
    hat, _ = normalize(values)
    normed = (hat * scales_ref[row : row + 1, :width]).astype(jnp.bfloat16)
    normed_ref[0] = normed
    qkv_ref[0] = dot_nn(normed, w_ref[...]).astype(jnp.bfloat16)


def project(row, place, scales, weights, tokens, others):
    _, length, width = tokens.shape
    pair = weights[0].shape[1]
    pieces = 1 + len(others)
    anywhere = pl.BlockSpec(memory_space=pl.ANY)
    return pl.pallas_call(
        functools.partial(project_kernel, row=row, pieces=pieces, parts=len(weights)),
        grid_spec=pltpu.PrefetchScalarGridSpec(
            num_scalar_prefetch=1,
            grid=(pieces,),
            in_specs=[whole(scales.shape)]
            + [whole(one.shape) for one in weights]
            + [anywhere] * pieces,
            out_specs=[
                pl.BlockSpec((1, length, pair), lambda i, place: (i ^ place[0], 0, 0)),
                pl.BlockSpec((1, length, width), lambda i, place: (i ^ place[0], 0, 0)),
            ],
            scratch_shapes=[
                pltpu.VMEM((pieces, length, width), jnp.bfloat16),
                pltpu.VMEM((width, pair), jnp.bfloat16),
                pltpu.SemaphoreType.DMA((pieces,)),
            ],
        ),
        out_shape=[
            jax.ShapeDtypeStruct((pieces, length, pair), jnp.bfloat16),
            jax.ShapeDtypeStruct((pieces, length, width), jnp.bfloat16),
        ],
        compiler_params=params(),
        cost_estimate=cost(2 * pieces * length * width * pair, 5 * pieces * length * width),
        name="project",
    )(place, scales, *weights, tokens, *others)


HALF = BLK // 2


def tile_mask(segc_ref, segr_ref, key_at, query_at, size):
    key_at, query_at = pl.multiple_of(key_at, size), pl.multiple_of(query_at, size)
    same = segc_ref[0, pl.ds(key_at, size), :] == segr_ref[0, :, pl.ds(query_at, size)]
    key_pos = key_at + lax.broadcasted_iota(jnp.int32, (size, size), 0)
    query_pos = query_at + lax.broadcasted_iota(jnp.int32, (size, size), 1)
    return same & (key_pos <= query_pos)


def split_heads(values):
    low = low_lanes(values.shape)
    zero = jnp.zeros_like(values)
    return jnp.concatenate([jnp.where(low, values, zero), jnp.where(low, zero, values)], axis=0)


def is_full(edge_ref, row, key_block, query_block):
    ends = edge_ref.shape[1] // 2
    same = edge_ref[row, 2 * key_block] == edge_ref[row, ends + 2 * query_block + 1]
    return same & (key_block < query_block)


def over_quarters(edge_ref, row, key_block, query_block, update):
    ends = edge_ref.shape[1] // 2

    def quarter(number, carried):
        key_half = 2 * key_block + number % 2
        query_half = 2 * query_block + number // 2
        shared = edge_ref[row, ends + key_half] >= edge_ref[row, query_half]

        @pl.when(shared & (key_half <= query_half))
        def _():
            update(pl.multiple_of(key_half * HALF, HALF), pl.multiple_of(query_half * HALF, HALF))

        return carried

    lax.fori_loop(0, 4, quarter, 0)


def largest(values, head):
    part = jnp.where(low_lanes(values.shape) == (head == 0), values, 0.0)
    return jnp.max(jnp.sum(part * part, axis=1, keepdims=True))


def attend_kernel(
    listed_ref, edge_ref, qkv_ref, segc_ref, segr_ref, mixed_ref, lse_ref,
    vt_ref, qz_ref, acc_ref, stat_ref, *, row,
):
    blocks = qkv_ref.shape[0]
    tall = HEAD_DIM + 16

    def turn(block, tops):
        at = pl.multiple_of(block * BLK, BLK)
        turned = transposed(qkv_ref[block, :, 256:384])
        ones = jnp.ones((16, BLK), jnp.bfloat16)
        for head in range(2):
            vt_ref[head * tall : head * tall + HEAD_DIM, pl.ds(at, BLK)] = turned[
                head * HEAD_DIM : (head + 1) * HEAD_DIM
            ]
            vt_ref[head * tall + HEAD_DIM : (head + 1) * tall, pl.ds(at, BLK)] = ones
        keys = qkv_ref[block, :, 128:256].astype(jnp.float32)
        return tuple(jnp.maximum(tops[head], largest(keys, head)) for head in range(2))

    key_tops = lax.fori_loop(0, blocks, turn, (0.0, 0.0))

    def one_query(query_block, carried):
        query = qkv_ref[query_block, :, :128].astype(jnp.float32) * HEAD_DIM ** (-0.5)
        qz_ref[...] = split_heads(query.astype(jnp.bfloat16))
        acc_ref[...] = jnp.zeros(acc_ref.shape, jnp.float32)
        shift = []
        for head in range(2):
            both = jnp.full((1, BLK), largest(query, head) * key_tops[head], jnp.float32)
            shift.append(jnp.sqrt(both) * 1.01)
        small = (jnp.max(shift[0]) < 40.0) & (jnp.max(shift[1]) < 40.0)

        def over_keys(full_update, part_update):
            def one_key(key_block, carried):
                listed = listed_ref[row, query_block * blocks + key_block] != 0
                full = is_full(edge_ref, row, key_block, query_block)

                @pl.when(listed & full)
                def _():
                    full_update(key_block)

                @pl.when(listed & jnp.logical_not(full))
                def _():
                    part_update(key_block)

                return carried

            lax.fori_loop(0, query_block + 1, one_key, 0)

        @pl.when(small)
        def _():
            def update(key_block, mask):
                at = pl.multiple_of(key_block * BLK, BLK)
                keys = qkv_ref[key_block, :, 128:256]
                parts = [slice(head * BLK, (head + 1) * BLK) for head in range(2)]
                scores = [dot_nt(keys, qz_ref[part, :]) for part in parts]
                for head, part in enumerate(parts):
                    one = scores[head] - shift[head]
                    if mask is not None:
                        one = jnp.where(mask, one, masked_out)
                    value = vt_ref[head * tall : (head + 1) * tall, pl.ds(at, BLK)]
                    acc_ref[:, part] += dot_nn(value, jnp.exp(one).astype(jnp.bfloat16))

            def part_update(key_block):
                update(key_block, tile_mask(segc_ref, segr_ref, key_block * BLK, query_block * BLK, BLK))

            def full_update(key_block):
                update(key_block, None)

            over_keys(full_update, part_update)
            stat_ref[0:1, :] = jnp.concatenate(shift, axis=1)

        @pl.when(jnp.logical_not(small))
        def _():
            stat_ref[0:1, :] = jnp.full((1, 2 * BLK), masked_out, jnp.float32)

            def part_update(key_at, query_at):
                keys = qkv_ref[key_at // BLK, pl.ds(pl.multiple_of(key_at % BLK, HALF), HALF), 128:256]
                mask = tile_mask(segc_ref, segr_ref, key_at, query_at, HALF)
                for head in range(2):
                    part = pl.ds(pl.multiple_of(head * BLK + query_at % BLK, HALF), HALF)
                    scores = jnp.where(mask, dot_nt(keys, qz_ref[part, :]), masked_out)
                    old_max = stat_ref[0:1, part]
                    new_max = jnp.maximum(old_max, jnp.max(scores, axis=0, keepdims=True))
                    weights = jnp.where(mask, jnp.exp(scores - new_max), 0.0)
                    value = vt_ref[head * tall : (head + 1) * tall, pl.ds(key_at, HALF)]
                    shrink = jnp.exp(old_max - new_max)
                    acc_ref[:, part] = acc_ref[:, part] * shrink + dot_nn(value, weights.astype(jnp.bfloat16))
                    stat_ref[0:1, part] = new_max

            def full_update(key_block):
                over_quarters(edge_ref, row, key_block, query_block, part_update)

            over_keys(full_update, full_update)

        total = acc_ref[HEAD_DIM : HEAD_DIM + 1, :]
        mixed = acc_ref[:HEAD_DIM, :] / total
        mixed = jnp.concatenate([mixed[:, :BLK], mixed[:, BLK:]], axis=0).T
        mixed_ref[query_block] = mixed.astype(jnp.bfloat16)
        log_total = stat_ref[0:1, :] + jnp.log(total)
        at = pl.multiple_of(query_block * BLK, BLK)
        lse_ref[0:1, pl.ds(at, BLK)] = log_total[:, :BLK]
        lse_ref[1:2, pl.ds(at, BLK)] = log_total[:, BLK:]
        return carried

    lax.fori_loop(0, blocks, one_query, 0)


def attend(row, listed, edges, qkv, segc, segr):
    blocks, blk, width = qkv.shape
    length = blocks * blk
    pair = 2 * HEAD_DIM
    return pl.pallas_call(
        functools.partial(attend_kernel, row=row),
        grid_spec=pltpu.PrefetchScalarGridSpec(
            num_scalar_prefetch=2,
            grid=(1,),
            in_specs=[
                whole(qkv.shape),
                pl.BlockSpec((1, length, 1), lambda i, *_: (row, 0, 0)),
                pl.BlockSpec((1, 1, length), lambda i, *_: (row, 0, 0)),
            ],
            out_specs=[whole((blocks, blk, pair)), whole((2, length))],
            scratch_shapes=[
                pltpu.VMEM((pair + 32, length), jnp.bfloat16),
                pltpu.VMEM((2 * blk, pair), jnp.bfloat16),
                pltpu.VMEM((HEAD_DIM + 16, 2 * blk), jnp.float32),
                pltpu.VMEM((1, 2 * blk), jnp.float32),
            ],
        ),
        out_shape=[
            jax.ShapeDtypeStruct((blocks, blk, pair), jnp.bfloat16),
            jax.ShapeDtypeStruct((2, length), jnp.float32),
        ],
        compiler_params=params(),
        cost_estimate=cost(20e9, 6e6, 20e6),
        name="attend",
    )(listed, edges, qkv, segc, segr)


def attend_back_kernel(
    listed_ref, edge_ref, qkv_ref, grad_ref, mixed_ref, lse_ref, segc_ref, segr_ref, out_ref,
    kt_ref, qz_ref, gz_ref, inner_ref, dq_ref, dk_ref, dv_ref, *, row,
):
    blocks = qkv_ref.shape[0]
    scale = HEAD_DIM ** (-0.5)

    def prepare(block, carried):
        at = pl.multiple_of(block * BLK, BLK)
        kt_ref[:, pl.ds(at, BLK)] = transposed(qkv_ref[block, :, 128:256])
        query = qkv_ref[block, :, :128].astype(jnp.float32) * scale
        qz_ref[block] = split_heads(query.astype(jnp.bfloat16))
        grad = grad_ref[block]
        gz_ref[block] = split_heads(grad)
        product = (grad.astype(jnp.float32) * mixed_ref[block].astype(jnp.float32)).T
        for head in range(2):
            part = product[head * HEAD_DIM : (head + 1) * HEAD_DIM, :]
            inner_ref[head : head + 1, pl.ds(at, BLK)] = jnp.sum(part, axis=0, keepdims=True)
        return carried

    lax.fori_loop(0, blocks, prepare, 0)
    dq_ref[...] = jnp.zeros(dq_ref.shape, jnp.float32)

    def one_key(key_block, carried):
        dk_ref[...] = jnp.zeros(dk_ref.shape, jnp.float32)
        dv_ref[...] = jnp.zeros(dv_ref.shape, jnp.float32)
        key_at = pl.multiple_of(key_block * BLK, BLK)

        def accumulate(head, key_at, query_at, keys, values, query, grad, mask):
            keys_here = pl.ds(pl.multiple_of(key_at % BLK, HALF), keys.shape[0])
            queries_here = pl.ds(query_at, query.shape[0])
            scores = dot_nt(keys, query)
            probs = jnp.exp(scores - lse_ref[head : head + 1, queries_here])
            if mask is not None:
                probs = jnp.where(mask, probs, 0.0)
            grad_probs = dot_nt(values, grad)
            grad_scores = probs * (grad_probs - inner_ref[head : head + 1, queries_here])
            probs = probs.astype(jnp.bfloat16)
            grad_scores = grad_scores.astype(jnp.bfloat16)
            dv_ref[keys_here, :] += dot_nn(probs, grad)
            dk_ref[keys_here, :] += dot_nn(grad_scores, query)
            lanes = slice(head * HEAD_DIM, (head + 1) * HEAD_DIM)
            dq_ref[lanes, queries_here] += dot_nn(
                kt_ref[lanes, pl.ds(key_at, keys.shape[0])], grad_scores
            )

        def full_update(query_block, mask):
            query_at = pl.multiple_of(query_block * BLK, BLK)
            keys = qkv_ref[key_block, :, 128:256]
            values = qkv_ref[key_block, :, 256:384]
            for head in range(2):
                part = slice(head * BLK, (head + 1) * BLK)
                query, grad = qz_ref[query_block, part, :], gz_ref[query_block, part, :]
                accumulate(head, key_at, query_at, keys, values, query, grad, mask)

        def one_query(query_block, carried):
            listed = listed_ref[row, query_block * blocks + key_block] != 0
            full = is_full(edge_ref, row, key_block, query_block)

            @pl.when(listed & full)
            def _():
                full_update(query_block, None)

            @pl.when(listed & jnp.logical_not(full))
            def _():
                full_update(query_block, tile_mask(segc_ref, segr_ref, key_block * BLK, query_block * BLK, BLK))

            return carried

        lax.fori_loop(key_block, blocks, one_query, 0)
        grad_query = dq_ref[:, pl.ds(key_at, BLK)].T * scale
        out_ref[key_block] = pair_together(grad_query, dk_ref[...], dv_ref[...]).astype(jnp.bfloat16)
        return carried

    lax.fori_loop(0, blocks, one_key, 0)


def attend_back(row, listed, edges, qkv, grad, mixed, lse, segc, segr):
    blocks, blk, width = qkv.shape
    length = blocks * blk
    pair = 2 * HEAD_DIM
    return pl.pallas_call(
        functools.partial(attend_back_kernel, row=row),
        grid_spec=pltpu.PrefetchScalarGridSpec(
            num_scalar_prefetch=2,
            grid=(1,),
            in_specs=[
                whole(qkv.shape),
                whole(grad.shape),
                whole(mixed.shape),
                whole(lse.shape),
                pl.BlockSpec((1, length, 1), lambda i, *_: (row, 0, 0)),
                pl.BlockSpec((1, 1, length), lambda i, *_: (row, 0, 0)),
            ],
            out_specs=whole(qkv.shape),
            scratch_shapes=[
                pltpu.VMEM((pair, length), jnp.bfloat16),
                pltpu.VMEM((blocks, 2 * blk, pair), jnp.bfloat16),
                pltpu.VMEM((blocks, 2 * blk, pair), jnp.bfloat16),
                pltpu.VMEM((2, length), jnp.float32),
                pltpu.VMEM((pair, length), jnp.float32),
                pltpu.VMEM((blk, pair), jnp.float32),
                pltpu.VMEM((blk, pair), jnp.float32),
            ],
        ),
        out_shape=jax.ShapeDtypeStruct(qkv.shape, jnp.bfloat16),
        compiler_params=params(),
        cost_estimate=cost(50e9, 10e6, 20e6),
        name="attend_back",
    )(listed, edges, qkv, grad, mixed, lse, segc, segr)


def joined(ref, half, halves):
    return jnp.concatenate([ref[i * halves + half] for i in range(ref.shape[0] // halves)], axis=1)


def outward_kernel(mixed_ref, tok_ref, w_ref, scales_ref, hidden_ref, normed_ref, *, row):
    halves = w_ref.shape[1]
    hidden = tok_ref[0].astype(jnp.float32)
    width = hidden.shape[1]
    for half in range(halves):
        hidden += dot_nt(joined(mixed_ref, half, halves), w_ref[:, half].reshape(width, -1))
    hidden_ref[...] = hidden
    hat, _ = normalize(hidden)
    normed_ref[...] = (hat * scales_ref[row : row + 1, width:]).astype(jnp.bfloat16)


def outward(row, mixed, tokens, w_all, scales, columns):
    rows, length, width = tokens.shape
    groups, _, pair = mixed.shape
    chunks, halves, high, _ = w_all.shape
    tile = 256
    one = pl.BlockSpec((tile, width), lambda i: (i, 0))
    return pl.pallas_call(
        functools.partial(outward_kernel, row=row),
        grid=(length // tile,),
        in_specs=[
            pl.BlockSpec((groups, tile, pair), lambda i: (0, i, 0)),
            pl.BlockSpec((1, tile, width), lambda i: (row, i, 0)),
            whole((chunks, halves, high, columns)),
            whole(scales.shape),
        ],
        out_specs=[one, one],
        out_shape=[
            jax.ShapeDtypeStruct((length, width), jnp.float32),
            jax.ShapeDtypeStruct((length, width), jnp.bfloat16),
        ],
        compiler_params=params(),
        cost_estimate=cost(2 * length * width * width, 12 * length * width),
        name="outward",
    )(mixed, tokens, w_all, scales)


def mlp_kernel(
    place_ref, nm0_ref, nm1_ref, cot_ref, hidden0_ref, hidden1_ref, scales_ref, up_ref, down_ref,
    keep_ref, send_ref, layer_ref, grad_hidden_ref, grad_attn_ref, gscale_ref,
    nmt_ref, cott_ref, out_ref, gn_ref, act_ref, gpre_ref,
):
    tile = pl.program_id(0)
    phase = pl.program_id(1)
    length, width = nm0_ref.shape
    count = 2 * length
    root = 0.7978845608028654
    cube = 0.044715

    @pl.when((tile == 0) & (phase == 0))
    def _():
        chunks = up_ref.shape[0]
        turned_apart(nmt_ref.at[:, :length], nm0_ref[...], place_ref[2], chunks)
        turned_apart(nmt_ref.at[:, length:], nm1_ref[...], place_ref[2], chunks)
        turned_apart(cott_ref, cot_ref[...], place_ref[2], chunks)
        out_ref[...] = jnp.zeros(out_ref.shape, jnp.float32)
        gn_ref[...] = jnp.zeros(gn_ref.shape, jnp.float32)

    @pl.when(phase == 0)
    def _():
        up = up_ref[:, 0].reshape(width, -1)
        down = down_ref[:, 0].reshape(width, -1)
        for row, nm_ref in enumerate((nm0_ref, nm1_ref)):
            part = slice(row * length, (row + 1) * length)
            pre = dot_nn(nm_ref[...], up)
            grad_act = dot_nn(cot_ref[part, :], down)
            square = pre * pre
            bent = jnp.tanh(root * (pre + cube * pre * square))
            half = 0.5 * (1.0 + bent)
            act_ref[part, :] = (pre * half).astype(jnp.bfloat16)
            slope = half + (0.5 * root) * pre * (1.0 - bent * bent) * (1.0 + (3.0 * cube) * square)
            gpre_ref[part, :] = (grad_act * slope).astype(jnp.bfloat16)
        put_apart(keep_ref, send_ref, dot_nn(nmt_ref[...], gpre_ref[...]).astype(jnp.bfloat16))

    @pl.when(phase == 1)
    def _():
        up = up_ref[:, 0].reshape(width, -1)
        down = down_ref[:, 0].reshape(width, -1)
        out_ref[...] += dot_nt(act_ref[...], down)
        gn_ref[...] += dot_nt(gpre_ref[...], up)
        put_apart(keep_ref, send_ref, dot_nn(cott_ref[...], act_ref[...]).astype(jnp.bfloat16))

    @pl.when((tile == pl.num_programs(0) - 1) & (phase == 1))
    def _():
        chunk = 256
        for row, hidden_ref in enumerate((hidden0_ref, hidden1_ref)):
            scale = scales_ref[row : row + 1, width:]
            total = jnp.zeros((1, width), jnp.float32)
            for at in range(0, length, chunk):
                part = slice(row * length + at, row * length + at + chunk)
                hidden = hidden_ref[at : at + chunk, :]
                layer_ref[part, :] = (hidden + out_ref[part, :]).astype(jnp.bfloat16)
                hat, inverse = normalize(hidden)
                grad = gn_ref[part, :]
                total += jnp.sum(grad * hat, axis=0, keepdims=True)
                back = cot_ref[part, :].astype(jnp.float32) + normalize_back(grad * scale, hat, inverse)
                grad_hidden_ref[part, :] = back
                grad_attn_ref[part, :] = back.astype(jnp.bfloat16)
            gscale_ref[row : row + 1, :] = total


def mlp(place, normed, cotangent, hidden, scales, w_all, room):
    rows, length, width = cotangent.shape
    count = rows * length
    chunks, halves, high, columns = w_all.shape
    tile = 512
    hidden_cols = columns // 2
    per_half = hidden_cols // tile
    flat = (count, width)
    one = (length, width)
    block = (chunks, 1, high, tile)
    apart = pl.BlockSpec(
        (2, 1, chunks // 4, high, tile),
        lambda f, s, at: (0, f // per_half, 0, 0, room // tile + s * per_half + f % per_half),
    )
    grads = jax.ShapeDtypeStruct((2, halves, chunks // 4, high, room + columns), jnp.bfloat16)
    return pl.pallas_call(
        mlp_kernel,
        grid_spec=pltpu.PrefetchScalarGridSpec(
            num_scalar_prefetch=1,
            grid=(halves * per_half, 2),
            in_specs=[
                whole(one),
                whole(one),
                whole(flat),
                whole(one),
                whole(one),
                whole(scales.shape),
                pl.BlockSpec(block, lambda f, s, at: (0, f // per_half, 0, f % per_half)),
                pl.BlockSpec(block, lambda f, s, at: (0, f // per_half, 0, per_half + f % per_half)),
            ],
            out_specs=[
                apart,
                apart,
                whole(flat),
                whole(flat),
                whole(flat),
                whole((rows, width)),
            ],
            scratch_shapes=[
                pltpu.VMEM((width, count), jnp.bfloat16),
                pltpu.VMEM((width, count), jnp.bfloat16),
                pltpu.VMEM(flat, jnp.float32),
                pltpu.VMEM(flat, jnp.float32),
                pltpu.VMEM((count, tile), jnp.bfloat16),
                pltpu.VMEM((count, tile), jnp.bfloat16),
            ],
        ),
        out_shape=[
            grads,
            grads,
            jax.ShapeDtypeStruct(flat, jnp.bfloat16),
            jax.ShapeDtypeStruct(flat, jnp.float32),
            jax.ShapeDtypeStruct(flat, jnp.bfloat16),
            jax.ShapeDtypeStruct((rows, width), jnp.float32),
        ],
        compiler_params=params(60),
        cost_estimate=cost(12 * count * width * halves * hidden_cols, 4 * w_all.size + 16 * count * width),
        name="mlp",
    )(place, *normed, cotangent.reshape(flat), *hidden, scales, w_all, w_all)


def grad_mixed_kernel(grad_ref, w_ref, out_ref):
    halves = w_ref.shape[1]
    per_half = out_ref.shape[0] // halves
    grad = grad_ref[...]
    pair = out_ref.shape[2]
    for half in range(halves):
        out = dot_nn(grad, w_ref[:, half].reshape(grad.shape[1], -1)).astype(jnp.bfloat16)
        for group in range(per_half):
            out_ref[group * halves + half] = out[:, group * pair : (group + 1) * pair]


def grad_mixed_of(row, grad_attn, w_all, mixed_shape, columns):
    groups, length, pair = mixed_shape
    chunks, halves, high, _ = w_all.shape
    width = grad_attn.shape[1]
    tile = 256
    tiles = length // tile
    return pl.pallas_call(
        grad_mixed_kernel,
        grid=(tiles,),
        in_specs=[
            pl.BlockSpec((tile, width), lambda i: (row * tiles + i, 0)),
            whole((chunks, halves, high, columns)),
        ],
        out_specs=pl.BlockSpec((groups, tile, pair), lambda i: (0, i, 0)),
        out_shape=jax.ShapeDtypeStruct(mixed_shape, jnp.bfloat16),
        compiler_params=params(),
        cost_estimate=cost(2 * length * width * width, 8 * length * width),
        name="grad_mixed",
    )(grad_attn, w_all)


def grad_proj_kernel(place_ref, grad_ref, mixed0_ref, mixed1_ref, _k, _s, keep_ref, send_ref, turned_ref):
    half = pl.program_id(0)
    halves = pl.num_programs(0)

    @pl.when(half == 0)
    def _():
        turned_apart(turned_ref, grad_ref[...], place_ref[2], 4 * keep_ref.shape[2])

    groups, length, pair = mixed0_ref.shape
    count = keep_ref.shape[4] // pair
    grad = 0.0
    for row, mixed_ref in enumerate((mixed0_ref, mixed1_ref)):
        mixed = jnp.concatenate([mixed_ref[i * halves + half] for i in range(count)], axis=1)
        grad += dot_nn(turned_ref[:, row * length : (row + 1) * length], mixed)
    put_apart(keep_ref, send_ref, grad.astype(jnp.bfloat16))


def grad_proj_into(place, keep, send, grad_attn, mixed, columns):
    count, width = grad_attn.shape
    given = whole(mixed[0].shape)
    anywhere = pl.BlockSpec(memory_space=pl.ANY)
    out = pl.BlockSpec((2, 1) + keep.shape[2:4] + (columns,), lambda h, at: (0, h, 0, 0, 0))
    return pl.pallas_call(
        grad_proj_kernel,
        grid_spec=pltpu.PrefetchScalarGridSpec(
            num_scalar_prefetch=1,
            grid=(keep.shape[1],),
            in_specs=[whole(grad_attn.shape), given, given, anywhere, anywhere],
            out_specs=[out, out],
            scratch_shapes=[pltpu.VMEM((width, count), jnp.bfloat16)],
        ),
        out_shape=[jax.ShapeDtypeStruct(keep.shape, jnp.bfloat16)] * 2,
        input_output_aliases={4: 0, 5: 1},
        compiler_params=params(),
        cost_estimate=cost(2 * count * width * width, 6 * count * width),
        name="grad_proj",
    )(place, grad_attn, *mixed, keep, send)


def first_norm_kernel(gq_ref, tok_ref, grad_hidden_ref, w_ref, scales_ref, out_ref, gscale_ref, *, row, q_cols):
    step = pl.program_id(0)
    halves = w_ref.shape[1]
    values = tok_ref[0].astype(jnp.float32)
    width = values.shape[1]
    grad = jnp.zeros(values.shape, jnp.float32)
    for half in range(halves):
        weights = w_ref[:, half, :, :q_cols].reshape(width, q_cols)
        grad += dot_nt(joined(gq_ref, half, halves), weights)
    hat, inverse = normalize(values)
    total = jnp.sum(grad * hat, axis=0, keepdims=True)

    @pl.when(step == 0)
    def _():
        gscale_ref[...] = total

    @pl.when(step != 0)
    def _():
        gscale_ref[...] += total

    back = normalize_back(grad * scales_ref[row : row + 1, :width], hat, inverse)
    out_ref[...] = (grad_hidden_ref[...] + back).astype(jnp.bfloat16)


def first_norm_back(row, grad_qkv, tokens, grad_hidden, w_all, scales, q_cols):
    rows, length, width = tokens.shape
    groups, _, pair = grad_qkv.shape
    tile = 256
    tiles = length // tile
    return pl.pallas_call(
        functools.partial(first_norm_kernel, row=row, q_cols=q_cols),
        grid=(tiles,),
        in_specs=[
            pl.BlockSpec((groups, tile, pair), lambda i: (0, i, 0)),
            pl.BlockSpec((1, tile, width), lambda i: (row, i, 0)),
            pl.BlockSpec((tile, width), lambda i: (row * tiles + i, 0)),
            whole(w_all.shape),
            whole(scales.shape),
        ],
        out_specs=[pl.BlockSpec((tile, width), lambda i: (i, 0)), whole((1, width))],
        out_shape=[
            jax.ShapeDtypeStruct((length, width), jnp.bfloat16),
            jax.ShapeDtypeStruct((1, width), jnp.float32),
        ],
        compiler_params=params(),
        cost_estimate=cost(2 * length * width * groups * pair, 2 * w_all.size + 20 * length * width),
        name="first_norm_back",
    )(grad_qkv, tokens, grad_hidden, w_all, scales)


def grad_qkv_kernel(place_ref, normed_ref, gq_ref, *refs):
    step = pl.program_id(0)
    base_refs, out_refs, total_ref = refs[:-2], refs[-2:-1], refs[-1]
    if len(refs) > 3:
        base_refs, out_refs, (total_ref, turned_ref) = refs[:1], refs[1:-2], refs[-2:]

    @pl.when(step == 0)
    def _():
        total_ref[...] = base_refs[0][...] if base_refs else jnp.zeros(total_ref.shape, jnp.float32)

    total_ref[...] += dot_nn(transposed(gq_ref[0]), normed_ref[0])

    @pl.when(step == pl.num_programs(0) - 1)
    def _():
        if base_refs:
            turned_ref[...] = total_ref[...].T
            tall = out_refs[0].shape[0]
            for apart, out_ref in enumerate(out_refs):
                at = pl.multiple_of((apart ^ place_ref[1]) * tall, tall)
                out_ref[...] = turned_ref[pl.ds(at, tall), :].astype(jnp.bfloat16)
        else:
            out_refs[0][...] = total_ref[...]


def grad_qkv_of(place, normed, grad_qkv, parts, base=()):
    blocks, length, width = normed.shape
    pair = grad_qkv.shape[2]
    turned = (pair, width)
    if base:
        shapes = [jax.ShapeDtypeStruct((width // parts, pair), jnp.bfloat16)] * parts
    else:
        shapes = [jax.ShapeDtypeStruct(turned, jnp.float32)]
    return pl.pallas_call(
        grad_qkv_kernel,
        grid_spec=pltpu.PrefetchScalarGridSpec(
            num_scalar_prefetch=1,
            grid=(blocks,),
            in_specs=[
                pl.BlockSpec((1, length, width), lambda i, place: (i, 0, 0)),
                pl.BlockSpec((1, length, pair), lambda i, place: (i, 0, 0)),
            ]
            + [whole(turned)] * len(base),
            out_specs=[whole(one.shape) for one in shapes],
            scratch_shapes=[pltpu.VMEM(turned, jnp.float32)]
            + [pltpu.VMEM((width, pair), jnp.float32)] * len(base),
        ),
        out_shape=shapes,
        compiler_params=params(),
        cost_estimate=cost(2 * blocks * length * width * pair, 3 * blocks * length * width),
        name="grad_qkv",
    )(place, normed, grad_qkv, *base)


CTX = ("x", "core")
GROUP = ("x", "core", "tp")
EVERY = ("fsdp", "x", "core", "tp")


def size_of(axis):
    names = (axis,) if isinstance(axis, str) else axis
    return functools.reduce(lambda size, name: size * lax.axis_size(name), names, 1)


def across(values, axis, apart):
    size = size_of(axis)
    return lax.ppermute(values, axis, [(i, i ^ apart) for i in range(size)])


def summed(parts):
    return sum(part.astype(jnp.float32) for part in parts)


def exchange(values, axes):
    return lax.all_to_all(values, axes, 0, 0, tiled=True)


HOPS = {1: "tp", 2: "core", 4: "x"}


def widened(found, apart):
    return {**found, **{held ^ apart: across(one, HOPS[apart], 1) for held, one in found.items()}}


def listed_table(block_pairs, pair_counts, row_blocks, ctx_size):
    rows, _, slots, _ = block_pairs.shape
    packed = jnp.concatenate([block_pairs.reshape(rows, 1, slots * 2), pair_counts[:, :, None]], axis=2)
    packed = jnp.concatenate(
        [packed] + [across(packed, CTX, apart) for apart in range(1, ctx_size)], axis=1
    )
    pairs = packed[:, :, : slots * 2].reshape(rows, ctx_size, slots, 2)
    live = jnp.arange(slots, dtype=jnp.int32)[None, None, :] < packed[:, :, slots * 2 :]
    owner = lax.axis_index(CTX) ^ jnp.arange(ctx_size, dtype=jnp.int32)[None, :, None]
    base = owner * (row_blocks // ctx_size)
    code = jnp.where(live, (base + pairs[..., 0]) * row_blocks + pairs[..., 1], -1)
    code = code.reshape(rows, ctx_size * slots)
    cells = jnp.arange(row_blocks * row_blocks, dtype=jnp.int32)
    return jnp.any(code[:, :, None] == cells[None, None, :], axis=1).astype(jnp.int32)


def spread_body(
    tokens, time_embed, segment_ids, block_pairs, pair_counts,
    w_time, w_qkv, w_out, w_up, w_down, cotangent,
):
    rows, length, width = tokens.shape
    chunks = width // w_qkv.shape[0]
    halves = lax.axis_size("tp")
    high = w_qkv.shape[0]
    q_cols, o_cols, f_cols = w_qkv.shape[1], w_out.shape[1], w_up.shape[1]
    k_rows = w_time.shape[0]
    mine = lax.axis_index("tp")
    ctx, fsdp = lax.axis_index(CTX), lax.axis_index("fsdp")
    n_ctx, n_fsdp = size_of(CTX), lax.axis_size("fsdp")
    bf16, f32 = jnp.bfloat16, jnp.float32
    chunk = fsdp * n_ctx + ctx
    place = jnp.stack([ctx * halves + mine, fsdp, lax.axis_index("core")])

    w_out = lax.all_gather(w_out.astype(bf16), EVERY, axis=0, tiled=True).reshape(chunks, halves, high, -1)

    found = [{0: tokens[row]} for row in range(rows)]
    orders = [(4, 1, 2) if row % 2 == 0 else (1, 4, 2) for row in range(rows)]
    found = [widened(one, order[0]) for one, order in zip(found, orders)]
    w_qkv = w_qkv.astype(bf16)
    columns = exchange(w_qkv.reshape(high, n_ctx, -1).transpose(1, 0, 2), CTX).reshape(n_ctx * high, -1)
    columns = [columns] + [across(columns, "fsdp", apart) for apart in range(1, n_fsdp)]
    embeds = [time_embed] + [across(time_embed, "fsdp", apart) for apart in range(1, n_fsdp)]
    mine_of = [lax.dynamic_slice_in_dim(one, chunk * k_rows, k_rows, 1) for one in embeds]
    given = jnp.dot(jnp.concatenate(mine_of, axis=0), w_time.astype(bf16).astype(f32), precision=highest)
    given = given.reshape(n_fsdp, rows, -1)
    scales = given[0]
    for apart in range(1, n_fsdp):
        scales += across(given[apart], "fsdp", apart)
    scales = 1.0 + scales + sum(across(scales, CTX, apart) for apart in range(1, n_ctx))

    row_blocks = segment_ids.shape[1] // BLK
    listed = listed_table(block_pairs, pair_counts, row_blocks, n_ctx)
    edges = jnp.concatenate([segment_ids[:, ::HALF], segment_ids[:, HALF - 1 :: HALF]], axis=1)
    segc = segment_ids[:, :, None]
    segr = segment_ids[:, None, :]
    found, scales, columns, listed, edges, segc, segr = lax.optimization_barrier(
        (found, scales, columns, listed, edges, segc, segr)
    )
    found = [widened(one, order[1]) for one, order in zip(found, orders)]
    second = jnp.concatenate([w_up, w_down], axis=1).astype(bf16)
    found, second = lax.optimization_barrier((found, second))
    second = lax.all_gather(second, EVERY, axis=0, tiled=True)
    found = [widened(one, order[2]) for one, order in zip(found, orders)]
    others = [[one[apart] for apart in range(1, len(one))] for one in found]

    qkv, normed = [], []
    for row in range(rows):
        out, one = project(row, place, scales, columns, tokens, others[row])
        qkv.append(out)
        normed.append(one)
    mixed_own, lse, mixed = [], [], []
    for row in range(rows):
        out, one = attend(row, listed, edges, qkv[row], segc, segr)
        mixed_own.append(out)
        lse.append(one)
        mixed.append(exchange(out, GROUP))
    mixed[0], mixed_own = lax.optimization_barrier((mixed[0], mixed_own))
    second = second.reshape(chunks, halves, high, -1)
    hidden, normed_mlp = [], []
    for row in range(rows):
        if row:
            mixed[row], hidden[row - 1] = lax.optimization_barrier((mixed[row], hidden[row - 1]))
        out, one = outward(row, mixed[row], tokens, w_out, scales, o_cols)
        hidden.append(out)
        normed_mlp.append(one)
    w_qkv, normed_mlp = lax.optimization_barrier((w_qkv, normed_mlp))
    third = lax.all_gather(w_qkv, EVERY, axis=0, tiled=True).reshape(chunks, halves, high, -1)
    keep, send, layer_out, grad_hidden, grad_attn, gscale_mlp = mlp(
        place, normed_mlp, cotangent, hidden, scales, second, o_cols
    )
    keep, send = grad_proj_into(place, keep, send, grad_attn, mixed, o_cols)
    grad_attn, keep, send, third = lax.optimization_barrier((grad_attn, keep, send, third))
    sent = across(send, "core", 1)
    grad_mixed = {}
    for row in reversed(range(rows)):
        out = grad_mixed_of(row, grad_attn, w_out, mixed[row].shape, o_cols)
        grad_mixed[row] = exchange(out, GROUP)
    last = rows - 1
    grads = summed([keep, sent]).astype(bf16)
    grad_mixed[last], grads = lax.optimization_barrier((grad_mixed[last], grads))
    grads = lax.psum_scatter(
        grads.reshape(-1, grads.shape[4]), ("x", "tp"), scatter_dimension=0, tiled=True
    )
    own, grad_qkv = {}, {}
    for row in reversed(range(rows)):
        if row < last:
            grad_mixed[row], own[row + 1] = lax.optimization_barrier((grad_mixed[row], own[row + 1]))
        own[row] = attend_back(row, listed, edges, qkv[row], grad_mixed[row], mixed_own[row], lse[row], segc, segr)
        if row < last:
            grad_qkv[row + 1] = exchange(own[row + 1], GROUP)
    grad_qkv[0] = exchange(own[0], GROUP)
    held, _ = lax.optimization_barrier((own[last], own[0]))
    base = grad_qkv_of(place, normed[last], held, n_fsdp)
    cut = list(grad_qkv_of(place, normed[0], own[0], n_fsdp, base))
    grad_tokens, gscale_attn = {}, {}
    held, _ = lax.optimization_barrier((grad_qkv[last], cut[0]))
    grad_tokens[last], gscale_attn[last] = first_norm_back(
        last, held, tokens, grad_hidden, third, scales, q_cols
    )
    cut[0], gscale_attn[last] = lax.optimization_barrier((cut[0], gscale_attn[last]))
    total = summed([cut[0]] + [across(cut[apart], "fsdp", apart) for apart in range(1, n_fsdp)])
    grads, gscale_attn[last], total = lax.optimization_barrier(
        (grads, gscale_attn[last], total.astype(bf16))
    )
    grads = lax.psum_scatter(grads, "fsdp", scatter_dimension=0, tiled=True)
    total = exchange(total.reshape(n_ctx, high, -1), CTX)
    grad_tokens[0], gscale_attn[0] = first_norm_back(
        0, grad_qkv[0], tokens, grad_hidden, third, scales, q_cols
    )
    devices = n_fsdp * n_ctx * halves
    both = jnp.concatenate([gscale_mlp, gscale_attn[last], gscale_attn[0]], axis=0)
    both = exchange(jnp.broadcast_to(both[None], (devices,) + both.shape), EVERY)
    both, total = lax.optimization_barrier((both, total))
    grad_w_qkv = total.transpose(1, 0, 2).reshape(high, q_cols).astype(f32)
    both = jnp.sum(both.reshape(n_fsdp, n_ctx * halves, 2 * rows, width), axis=1)
    both = jnp.concatenate([both[:, 3], both[:, 0], both[:, 2], both[:, 1]], axis=1)
    both = both.reshape(n_fsdp * rows, 2 * width)
    mine_of = [lax.dynamic_index_in_dim(jnp.stack(mine_of), i ^ fsdp, 0, False) for i in range(n_fsdp)]
    grad_time = jnp.dot(jnp.concatenate(mine_of, axis=0).T, both, precision=highest)
    return (
        layer_out.reshape(tokens.shape),
        jnp.stack([grad_tokens[row] for row in range(rows)]),
        grad_time,
        grad_w_qkv,
        grads[:, :o_cols].astype(f32),
        grads[:, o_cols : o_cols + f_cols].astype(f32),
        grads[:, o_cols + f_cols :].astype(f32),
    )


def specs_of(ctx):
    flat = ctx if isinstance(ctx, tuple) else (ctx,)
    tokens, weights = P("fsdp", (*flat, "tp"), None), P(("fsdp", *flat), "tp")
    placed = (tokens, P("fsdp", None), P("fsdp", None), P("fsdp", ctx, None, None), P("fsdp", ctx))
    placed += (P(("fsdp", *flat), None), weights, weights, weights, weights, tokens)
    return placed, (tokens, tokens, P(("fsdp", *flat), None), weights, weights, weights, weights)


def solution(mesh):
    sizes = tuple(mesh.shape[name] for name in ("fsdp", "ctx", "tp"))

    def run(*args):
        tokens, w_qkv, w_out, w_up = args[0], args[6], args[7], args[8]
        group = sizes[1] * sizes[2]
        fits = (
            sizes == (4, 4, 2)
            and tokens.shape[:2] == (8, group * BLK)
            and w_qkv.shape[1] == group * 6 * HEAD_DIM
            and w_out.shape[1] % (512 * sizes[2]) == 0
            and w_up.shape[1] % (512 * sizes[2]) == 0
        )
        if fits:
            devices = mesh.devices.reshape(sizes[0], 2, 2, sizes[2])
            parted = Mesh(devices, ("fsdp", "x", "core", "tp"))
            placed, given = specs_of(CTX)
            return jax.shard_map(
                spread_body, mesh=parted, in_specs=placed, out_specs=given, check_vma=False
            )(*args)
        placed, given = specs_of("ctx")
        return jax.shard_map(body, mesh=mesh, in_specs=placed, out_specs=given, check_vma=False)(*args)

    return run
```

```python
import functools

import jax
import jax.numpy as jnp
from jax import lax
from jax.experimental import pallas as pl
from jax.experimental.pallas import tpu as pltpu
from jax.sharding import Mesh
from jax.sharding import PartitionSpec as P

HEAD_DIM = 64
BLK = 512


epsilon = 1e-05
highest = lax.Precision.HIGHEST
masked_out = -1e30


def normalize(values):
    mean_value = jnp.mean(values, axis=-1, keepdims=True)
    centred = values - mean_value
    variance = jnp.mean(centred * centred, axis=-1, keepdims=True)
    inverse = lax.rsqrt(variance + epsilon)
    return (centred * inverse, inverse)


def normalize_back(grad_hat, normal_hat, inverse):
    first_mean = jnp.mean(grad_hat, axis=-1, keepdims=True)
    second_mean = jnp.mean(grad_hat * normal_hat, axis=-1, keepdims=True)
    return inverse * (grad_hat - first_mean - normal_hat * second_mean)


def smooth_gate(values):
    return jax.nn.gelu(values, approximate=True)


def block_scores(pair_entry, query_rows, key_rows, seg_row, offset):
    query_start = pair_entry[0] * BLK
    key_start = pair_entry[1] * BLK
    query_block = lax.dynamic_slice_in_dim(query_rows, query_start, BLK, 0)
    key_block = lax.dynamic_slice_in_dim(key_rows, key_start, BLK, 0)
    seg_query = lax.dynamic_slice_in_dim(seg_row, offset + query_start, BLK, 0)
    seg_keys = lax.dynamic_slice_in_dim(seg_row, key_start, BLK, 0)
    steps_in = jnp.arange(BLK, dtype=jnp.int32)
    allowed = (seg_query[:, None] == seg_keys[None, :]) & (
        key_start + steps_in[None, :] <= offset + query_start + steps_in[:, None]
    )
    scores = jnp.einsum(
        "qhe,khe->hqk", query_block, key_block, preferred_element_type=jnp.float32
    ) * HEAD_DIM ** (-0.5)
    return (query_block, key_block, query_start, key_start, allowed, scores)


def attend_forward(query_rows, key_rows, value_rows, seg_row, pair_rows, pair_total, offset):
    length_here, head_count, _ = query_rows.shape

    def statistic_step(pair_index, carried):
        running_max, running_sum = carried
        _, _, query_start, _, allowed, scores = block_scores(
            pair_rows[pair_index], query_rows, key_rows, seg_row, offset
        )
        scores = jnp.where(allowed[None], scores, masked_out)
        old_max = lax.dynamic_slice_in_dim(running_max, query_start, BLK, 1)
        old_sum = lax.dynamic_slice_in_dim(running_sum, query_start, BLK, 1)
        new_max = jnp.maximum(old_max, jnp.max(scores, axis=-1))
        weights = jnp.where(allowed[None], jnp.exp(scores - new_max[:, :, None]), 0.0)
        new_sum = old_sum * jnp.exp(old_max - new_max) + jnp.sum(weights, axis=-1)
        return (
            lax.dynamic_update_slice_in_dim(running_max, new_max, query_start, 1),
            lax.dynamic_update_slice_in_dim(running_sum, new_sum, query_start, 1),
        )

    start_max = jnp.full((head_count, length_here), masked_out, jnp.float32)
    start_sum = jnp.zeros((head_count, length_here), jnp.float32)
    running_max, running_sum = lax.fori_loop(0, pair_total, statistic_step, (start_max, start_sum))
    log_total = running_max + jnp.log(running_sum)

    def output_step(pair_index, accumulated):
        _, _, query_start, key_start, allowed, scores = block_scores(
            pair_rows[pair_index], query_rows, key_rows, seg_row, offset
        )
        block_log = lax.dynamic_slice_in_dim(log_total, query_start, BLK, 1)
        probabilities = jnp.where(
            allowed[None], jnp.exp(scores - block_log[:, :, None]), 0.0
        ).astype(jnp.bfloat16)
        value_block = lax.dynamic_slice_in_dim(value_rows, key_start, BLK, 0)
        addition = jnp.einsum(
            "hqk,khe->qhe", probabilities, value_block, preferred_element_type=jnp.float32
        )
        previous = lax.dynamic_slice_in_dim(accumulated, query_start, BLK, 0)
        return lax.dynamic_update_slice_in_dim(accumulated, previous + addition, query_start, 0)

    mixed_rows = lax.fori_loop(0, pair_total, output_step, jnp.zeros(query_rows.shape, jnp.float32))
    return (mixed_rows, log_total)


def attend_backward(
    query_rows,
    key_rows,
    value_rows,
    seg_row,
    pair_rows,
    pair_total,
    offset,
    log_total,
    grad_mixed,
    inner_sums,
):
    scale_factor = HEAD_DIM ** (-0.5)

    def add_block(whole, start_at, addition):
        previous = lax.dynamic_slice_in_dim(whole, start_at, BLK, 0)
        return lax.dynamic_update_slice_in_dim(whole, previous + addition, start_at, 0)

    def gradient_step(pair_index, carried):
        grad_query, grad_keys, grad_values = carried
        query_block, key_block, query_start, key_start, allowed, scores = block_scores(
            pair_rows[pair_index], query_rows, key_rows, seg_row, offset
        )
        block_log = lax.dynamic_slice_in_dim(log_total, query_start, BLK, 1)
        probabilities = jnp.where(allowed[None], jnp.exp(scores - block_log[:, :, None]), 0.0)
        grad_block = lax.dynamic_slice_in_dim(grad_mixed, query_start, BLK, 0)
        value_block = lax.dynamic_slice_in_dim(value_rows, key_start, BLK, 0)
        grad_probs = jnp.einsum(
            "qhe,khe->hqk", grad_block, value_block, preferred_element_type=jnp.float32
        )
        inner_block = lax.dynamic_slice_in_dim(inner_sums, query_start, BLK, 1)
        grad_scores = (probabilities * (grad_probs - inner_block[:, :, None])).astype(jnp.bfloat16)
        query_add = (
            jnp.einsum("hqk,khe->qhe", grad_scores, key_block, preferred_element_type=jnp.float32)
            * scale_factor
        )
        key_add = (
            jnp.einsum("hqk,qhe->khe", grad_scores, query_block, preferred_element_type=jnp.float32)
            * scale_factor
        )
        value_add = jnp.einsum(
            "hqk,qhe->khe",
            probabilities.astype(jnp.bfloat16),
            grad_block,
            preferred_element_type=jnp.float32,
        )
        return (
            add_block(grad_query, query_start, query_add),
            add_block(grad_keys, key_start, key_add),
            add_block(grad_values, key_start, value_add),
        )

    start_state = (
        jnp.zeros(query_rows.shape, jnp.float32),
        jnp.zeros(key_rows.shape, jnp.float32),
        jnp.zeros(value_rows.shape, jnp.float32),
    )
    return lax.fori_loop(0, pair_total, gradient_step, start_state)


def body(
    tokens,
    time_embed,
    segment_ids,
    block_pairs,
    pair_counts,
    w_time,
    w_qkv,
    w_out,
    w_up,
    w_down,
    cotangent,
):
    row_count, local_len, model_width = tokens.shape
    time_all, qkv_all, out_all, up_all, down_all = (
        lax.all_gather(w_time.astype(jnp.bfloat16), ("fsdp", "ctx"), axis=0, tiled=True),
        lax.all_gather(w_qkv.astype(jnp.bfloat16), ("fsdp", "ctx"), axis=0, tiled=True),
        lax.all_gather(w_out.astype(jnp.bfloat16), ("fsdp", "ctx"), axis=0, tiled=True),
        lax.all_gather(w_up.astype(jnp.bfloat16), ("fsdp", "ctx"), axis=0, tiled=True),
        lax.all_gather(w_down.astype(jnp.bfloat16), ("fsdp", "ctx"), axis=0, tiled=True),
    )
    scales = 1.0 + jnp.dot(time_embed, time_all.astype(jnp.float32), precision=highest)
    scale_attn = scales[:, None, :model_width]
    scale_mlp = scales[:, None, model_width:]
    x_input = tokens.astype(jnp.float32)
    hat_attn, inverse_attn = normalize(x_input)
    normed = (hat_attn * scale_attn).astype(jnp.bfloat16)
    normed_all = lax.all_gather(normed, "tp", axis=1, tiled=True)
    ctx_len = normed_all.shape[1]
    head_count = qkv_all.shape[1] // (3 * HEAD_DIM)
    projected = jnp.einsum("rtd,dc->rtc", normed_all, qkv_all, preferred_element_type=jnp.float32)
    projected = projected.astype(jnp.bfloat16).reshape(row_count, ctx_len, head_count, 3, HEAD_DIM)
    query_all = projected[:, :, :, 0]
    key_part = projected[:, :, :, 1]
    value_part = projected[:, :, :, 2]
    key_all, value_all = (
        lax.all_gather(key_part, "ctx", axis=1, tiled=True),
        lax.all_gather(value_part, "ctx", axis=1, tiled=True),
    )
    offset = lax.axis_index("ctx") * ctx_len
    mixed_list = []
    log_list = []
    for row_index in range(row_count):
        mixed_rows, log_total = attend_forward(
            query_all[row_index],
            key_all[row_index],
            value_all[row_index],
            segment_ids[row_index],
            block_pairs[row_index, 0],
            pair_counts[row_index, 0],
            offset,
        )
        mixed_list.append(mixed_rows)
        log_list.append(log_total)
    mixed_exact = jnp.stack(mixed_list)
    mixed_heads = mixed_exact.astype(jnp.bfloat16).reshape(
        row_count, ctx_len, head_count * HEAD_DIM
    )
    attn_part = jnp.einsum("rtc,dc->rtd", mixed_heads, out_all, preferred_element_type=jnp.float32)
    attn_local = lax.psum_scatter(
        attn_part.astype(jnp.bfloat16), "tp", scatter_dimension=1, tiled=True
    ).astype(jnp.float32)
    hidden = x_input + attn_local
    hat_mlp, inverse_mlp = normalize(hidden)
    normed_mlp = (hat_mlp * scale_mlp).astype(jnp.bfloat16)
    mlp_all = lax.all_gather(normed_mlp, "tp", axis=1, tiled=True)
    pre_act = jnp.einsum("rtd,df->rtf", mlp_all, up_all, preferred_element_type=jnp.float32)
    activated = smooth_gate(pre_act).astype(jnp.bfloat16)
    mlp_part = jnp.einsum("rtf,df->rtd", activated, down_all, preferred_element_type=jnp.float32)
    mlp_local = lax.psum_scatter(
        mlp_part.astype(jnp.bfloat16), "tp", scatter_dimension=1, tiled=True
    ).astype(jnp.float32)
    grad_all = lax.all_gather(cotangent, "tp", axis=1, tiled=True)
    grad_act = jnp.einsum("rtd,df->rtf", grad_all, down_all, preferred_element_type=jnp.float32)
    _, gate_back = jax.vjp(smooth_gate, pre_act)
    grad_pre = gate_back(grad_act)[0].astype(jnp.bfloat16)
    grad_down = jnp.einsum("rtd,rtf->df", grad_all, activated, preferred_element_type=jnp.float32)
    grad_up = jnp.einsum("rtd,rtf->df", mlp_all, grad_pre, preferred_element_type=jnp.float32)
    norm_part = jnp.einsum("rtf,df->rtd", grad_pre, up_all, preferred_element_type=jnp.float32)
    grad_normed_mlp = lax.psum_scatter(
        norm_part.astype(jnp.bfloat16), "tp", scatter_dimension=1, tiled=True
    ).astype(jnp.float32)
    layer_out = (hidden + mlp_local).astype(jnp.bfloat16)
    grad_output = cotangent.astype(jnp.float32)
    grad_scale_mlp = jnp.sum(grad_normed_mlp * hat_mlp, axis=1)
    grad_hidden = grad_output + normalize_back(grad_normed_mlp * scale_mlp, hat_mlp, inverse_mlp)
    grad_attn_all = lax.all_gather(grad_hidden.astype(jnp.bfloat16), "tp", axis=1, tiled=True)
    grad_mixed = jnp.einsum(
        "rtd,dc->rtc", grad_attn_all, out_all, preferred_element_type=jnp.float32
    ).astype(jnp.bfloat16)
    grad_proj = jnp.einsum(
        "rtd,rtc->dc", grad_attn_all, mixed_heads, preferred_element_type=jnp.float32
    )
    grad_mixed = grad_mixed.reshape(row_count, ctx_len, head_count, HEAD_DIM)
    inner_sums = jnp.einsum("rqhe,rqhe->rhq", grad_mixed.astype(jnp.float32), mixed_exact)
    query_grads = []
    key_grads = []
    value_grads = []
    for row_index in range(row_count):
        grad_query, grad_keys, grad_values = attend_backward(
            query_all[row_index],
            key_all[row_index],
            value_all[row_index],
            segment_ids[row_index],
            block_pairs[row_index, 0],
            pair_counts[row_index, 0],
            offset,
            log_list[row_index],
            grad_mixed[row_index],
            inner_sums[row_index],
        )
        query_grads.append(grad_query)
        key_grads.append(grad_keys)
        value_grads.append(grad_values)
    key_local, value_local = (
        lax.psum_scatter(
            jnp.stack(key_grads).astype(jnp.bfloat16), "ctx", scatter_dimension=1, tiled=True
        ).astype(jnp.float32),
        lax.psum_scatter(
            jnp.stack(value_grads).astype(jnp.bfloat16), "ctx", scatter_dimension=1, tiled=True
        ).astype(jnp.float32),
    )
    grad_projected = jnp.stack(
        [
            jnp.stack(query_grads).astype(jnp.bfloat16),
            key_local.astype(jnp.bfloat16),
            value_local.astype(jnp.bfloat16),
        ],
        axis=3,
    )
    grad_projected = grad_projected.reshape(row_count, ctx_len, head_count * 3 * HEAD_DIM)
    grad_qkv = jnp.einsum(
        "rtd,rtc->dc", normed_all, grad_projected, preferred_element_type=jnp.float32
    )
    first_part = jnp.einsum(
        "rtc,dc->rtd", grad_projected, qkv_all, preferred_element_type=jnp.float32
    )
    grad_normed = lax.psum_scatter(
        first_part.astype(jnp.bfloat16), "tp", scatter_dimension=1, tiled=True
    ).astype(jnp.float32)
    grad_scale_attn = jnp.sum(grad_normed * hat_attn, axis=1)
    grad_tokens = grad_hidden + normalize_back(grad_normed * scale_attn, hat_attn, inverse_attn)
    grad_scales = lax.psum(jnp.concatenate([grad_scale_attn, grad_scale_mlp], axis=1), "tp")
    grad_time = jnp.dot(time_embed.T, grad_scales, precision=highest)
    shared = (
        lax.psum_scatter(
            grad_time.astype(jnp.bfloat16), ("fsdp", "ctx"), scatter_dimension=0, tiled=True
        ).astype(jnp.float32),
        lax.psum_scatter(
            grad_qkv.astype(jnp.bfloat16), ("fsdp", "ctx"), scatter_dimension=0, tiled=True
        ).astype(jnp.float32),
        lax.psum_scatter(
            grad_proj.astype(jnp.bfloat16), ("fsdp", "ctx"), scatter_dimension=0, tiled=True
        ).astype(jnp.float32),
        lax.psum_scatter(
            grad_up.astype(jnp.bfloat16), ("fsdp", "ctx"), scatter_dimension=0, tiled=True
        ).astype(jnp.float32),
        lax.psum_scatter(
            grad_down.astype(jnp.bfloat16), ("fsdp", "ctx"), scatter_dimension=0, tiled=True
        ).astype(jnp.float32),
    )
    return (
        layer_out,
        grad_tokens.astype(jnp.bfloat16),
        shared[0],
        shared[1],
        shared[2],
        shared[3],
        shared[4],
    )


def params(limit=58):
    return pltpu.CompilerParams(vmem_limit_bytes=limit * 1024 * 1024)


def whole(shape):
    zeros = (0,) * len(shape)
    return pl.BlockSpec(shape, lambda *_: zeros, pipeline_mode=pl.Buffered(1))


def cost(flops, nbytes, exps=0):
    return pl.CostEstimate(flops=int(flops), bytes_accessed=int(nbytes), transcendentals=int(exps))


def dot_nn(left, right):
    return jnp.dot(left, right, preferred_element_type=jnp.float32)


def dot_nt(left, right):
    return lax.dot_general(left, right, (((1,), (1,)), ((), ())), preferred_element_type=jnp.float32)


def transposed(values):
    return values.astype(jnp.float32).T.astype(values.dtype)


def turned_apart(into_ref, values, core, chunks):
    turned = transposed(values)
    high = turned.shape[0] // chunks
    for chunk in range(chunks):
        inner = (chunk // 2 % 2) * (chunks // 4) + chunk // 4
        at = ((chunk % 2) ^ core) * (chunks // 2) + inner
        into_ref[pl.ds(pl.multiple_of(at * high, high), high), :] = turned[chunk * high : (chunk + 1) * high]


def put_apart(keep_ref, send_ref, grad):
    middle = grad.shape[0] // 2
    shape = (keep_ref.shape[0],) + keep_ref.shape[2:]
    keep_ref[:, 0] = grad[:middle].reshape(shape)
    send_ref[:, 0] = grad[middle:].reshape(shape)


def low_lanes(shape):
    return lax.broadcasted_iota(jnp.int32, shape, 1) < HEAD_DIM


def pair_apart(stored):
    first, second, third = stored[:, :128], stored[:, 128:256], stored[:, 256:]
    low = low_lanes(first.shape)
    keys = pltpu.roll(jnp.where(low, third, first), HEAD_DIM, 1)
    return jnp.concatenate(
        [jnp.where(low, first, second), keys, jnp.where(low, second, third)], axis=1
    )


def pair_together(query, keys, values):
    low = low_lanes(query.shape)
    turned = pltpu.roll(keys, HEAD_DIM, 1)
    return jnp.concatenate(
        [jnp.where(low, query, turned), jnp.where(low, values, query), jnp.where(low, turned, values)],
        axis=1,
    )


def project_kernel(place_ref, scales_ref, *refs, row, pieces, parts):
    weight_refs, token_refs = refs[:parts], refs[parts : parts + pieces]
    qkv_ref, normed_ref, held_ref, w_ref, sem_ref = refs[parts + pieces :]
    step = pl.program_id(0)

    def fetch(piece):
        source = token_refs[piece]
        source = source.at[row] if len(source.shape) == 3 else source
        return pltpu.make_async_copy(source, held_ref.at[piece], sem_ref.at[piece])

    @pl.when(step == 0)
    def _():
        for piece in range(pieces):
            fetch(piece).start()
        tall = weight_refs[0].shape[0]
        for apart, weight_ref in enumerate(weight_refs):
            at = pl.multiple_of((apart ^ place_ref[1]) * tall, tall)
            w_ref[pl.ds(at, tall), :] = pair_apart(weight_ref[...].astype(jnp.float32)).astype(jnp.bfloat16)
    pltpu.make_async_copy(held_ref.at[step], held_ref.at[step], sem_ref.at[step]).wait()
    values = held_ref[step].astype(jnp.float32)
    width = values.shape[1]
    hat, _ = normalize(values)
    normed = (hat * scales_ref[row : row + 1, :width]).astype(jnp.bfloat16)
    normed_ref[0] = normed
    qkv_ref[0] = dot_nn(normed, w_ref[...]).astype(jnp.bfloat16)


def project(row, place, scales, weights, tokens, others):
    _, length, width = tokens.shape
    pair = weights[0].shape[1]
    pieces = 1 + len(others)
    anywhere = pl.BlockSpec(memory_space=pl.ANY)
    return pl.pallas_call(
        functools.partial(project_kernel, row=row, pieces=pieces, parts=len(weights)),
        grid_spec=pltpu.PrefetchScalarGridSpec(
            num_scalar_prefetch=1,
            grid=(pieces,),
            in_specs=[whole(scales.shape)]
            + [whole(one.shape) for one in weights]
            + [anywhere] * pieces,
            out_specs=[
                pl.BlockSpec((1, length, pair), lambda i, place: (i ^ place[0], 0, 0)),
                pl.BlockSpec((1, length, width), lambda i, place: (i ^ place[0], 0, 0)),
            ],
            scratch_shapes=[
                pltpu.VMEM((pieces, length, width), jnp.bfloat16),
                pltpu.VMEM((width, pair), jnp.bfloat16),
                pltpu.SemaphoreType.DMA((pieces,)),
            ],
        ),
        out_shape=[
            jax.ShapeDtypeStruct((pieces, length, pair), jnp.bfloat16),
            jax.ShapeDtypeStruct((pieces, length, width), jnp.bfloat16),
        ],
        compiler_params=params(),
        cost_estimate=cost(2 * pieces * length * width * pair, 5 * pieces * length * width),
        name="project",
    )(place, scales, *weights, tokens, *others)


HALF = BLK // 2


def tile_mask(segc_ref, segr_ref, key_at, query_at, size):
    key_at, query_at = pl.multiple_of(key_at, size), pl.multiple_of(query_at, size)
    same = segc_ref[0, pl.ds(key_at, size), :] == segr_ref[0, :, pl.ds(query_at, size)]
    key_pos = key_at + lax.broadcasted_iota(jnp.int32, (size, size), 0)
    query_pos = query_at + lax.broadcasted_iota(jnp.int32, (size, size), 1)
    return same & (key_pos <= query_pos)


def split_heads(values):
    low = low_lanes(values.shape)
    zero = jnp.zeros_like(values)
    return jnp.concatenate([jnp.where(low, values, zero), jnp.where(low, zero, values)], axis=0)


def is_full(edge_ref, row, key_block, query_block):
    ends = edge_ref.shape[1] // 2
    same = edge_ref[row, 2 * key_block] == edge_ref[row, ends + 2 * query_block + 1]
    return same & (key_block < query_block)


def over_quarters(edge_ref, row, key_block, query_block, update):
    ends = edge_ref.shape[1] // 2

    def quarter(number, carried):
        key_half = 2 * key_block + number % 2
        query_half = 2 * query_block + number // 2
        shared = edge_ref[row, ends + key_half] >= edge_ref[row, query_half]

        @pl.when(shared & (key_half <= query_half))
        def _():
            update(pl.multiple_of(key_half * HALF, HALF), pl.multiple_of(query_half * HALF, HALF))

        return carried

    lax.fori_loop(0, 4, quarter, 0)


def largest(values, head):
    part = jnp.where(low_lanes(values.shape) == (head == 0), values, 0.0)
    return jnp.max(jnp.sum(part * part, axis=1, keepdims=True))


def attend_kernel(
    listed_ref, edge_ref, qkv_ref, segc_ref, segr_ref, mixed_ref, lse_ref,
    vt_ref, qz_ref, acc_ref, stat_ref, *, row,
):
    blocks = qkv_ref.shape[0]
    tall = HEAD_DIM + 16

    def turn(block, tops):
        at = pl.multiple_of(block * BLK, BLK)
        turned = transposed(qkv_ref[block, :, 256:384])
        ones = jnp.ones((16, BLK), jnp.bfloat16)
        for head in range(2):
            vt_ref[head * tall : head * tall + HEAD_DIM, pl.ds(at, BLK)] = turned[
                head * HEAD_DIM : (head + 1) * HEAD_DIM
            ]
            vt_ref[head * tall + HEAD_DIM : (head + 1) * tall, pl.ds(at, BLK)] = ones
        keys = qkv_ref[block, :, 128:256].astype(jnp.float32)
        return tuple(jnp.maximum(tops[head], largest(keys, head)) for head in range(2))

    key_tops = lax.fori_loop(0, blocks, turn, (0.0, 0.0))

    def one_query(query_block, carried):
        query = qkv_ref[query_block, :, :128].astype(jnp.float32) * HEAD_DIM ** (-0.5)
        qz_ref[...] = split_heads(query.astype(jnp.bfloat16))
        acc_ref[...] = jnp.zeros(acc_ref.shape, jnp.float32)
        shift = []
        for head in range(2):
            both = jnp.full((1, BLK), largest(query, head) * key_tops[head], jnp.float32)
            shift.append(jnp.sqrt(both) * 1.01)
        small = (jnp.max(shift[0]) < 40.0) & (jnp.max(shift[1]) < 40.0)

        def over_keys(full_update, part_update):
            def one_key(key_block, carried):
                listed = listed_ref[row, query_block * blocks + key_block] != 0
                full = is_full(edge_ref, row, key_block, query_block)

                @pl.when(listed & full)
                def _():
                    full_update(key_block)

                @pl.when(listed & jnp.logical_not(full))
                def _():
                    part_update(key_block)

                return carried

            lax.fori_loop(0, query_block + 1, one_key, 0)

        @pl.when(small)
        def _():
            def update(key_block, mask):
                at = pl.multiple_of(key_block * BLK, BLK)
                keys = qkv_ref[key_block, :, 128:256]
                parts = [slice(head * BLK, (head + 1) * BLK) for head in range(2)]
                scores = [dot_nt(keys, qz_ref[part, :]) for part in parts]
                for head, part in enumerate(parts):
                    one = scores[head] - shift[head]
                    if mask is not None:
                        one = jnp.where(mask, one, masked_out)
                    value = vt_ref[head * tall : (head + 1) * tall, pl.ds(at, BLK)]
                    acc_ref[:, part] += dot_nn(value, jnp.exp(one).astype(jnp.bfloat16))

            def part_update(key_block):
                update(key_block, tile_mask(segc_ref, segr_ref, key_block * BLK, query_block * BLK, BLK))

            def full_update(key_block):
                update(key_block, None)

            over_keys(full_update, part_update)
            stat_ref[0:1, :] = jnp.concatenate(shift, axis=1)

        @pl.when(jnp.logical_not(small))
        def _():
            stat_ref[0:1, :] = jnp.full((1, 2 * BLK), masked_out, jnp.float32)

            def part_update(key_at, query_at):
                keys = qkv_ref[key_at // BLK, pl.ds(pl.multiple_of(key_at % BLK, HALF), HALF), 128:256]
                mask = tile_mask(segc_ref, segr_ref, key_at, query_at, HALF)
                for head in range(2):
                    part = pl.ds(pl.multiple_of(head * BLK + query_at % BLK, HALF), HALF)
                    scores = jnp.where(mask, dot_nt(keys, qz_ref[part, :]), masked_out)
                    old_max = stat_ref[0:1, part]
                    new_max = jnp.maximum(old_max, jnp.max(scores, axis=0, keepdims=True))
                    weights = jnp.where(mask, jnp.exp(scores - new_max), 0.0)
                    value = vt_ref[head * tall : (head + 1) * tall, pl.ds(key_at, HALF)]
                    shrink = jnp.exp(old_max - new_max)
                    acc_ref[:, part] = acc_ref[:, part] * shrink + dot_nn(value, weights.astype(jnp.bfloat16))
                    stat_ref[0:1, part] = new_max

            def full_update(key_block):
                over_quarters(edge_ref, row, key_block, query_block, part_update)

            over_keys(full_update, full_update)

        total = acc_ref[HEAD_DIM : HEAD_DIM + 1, :]
        mixed = acc_ref[:HEAD_DIM, :] / total
        mixed = jnp.concatenate([mixed[:, :BLK], mixed[:, BLK:]], axis=0).T
        mixed_ref[query_block] = mixed.astype(jnp.bfloat16)
        log_total = stat_ref[0:1, :] + jnp.log(total)
        at = pl.multiple_of(query_block * BLK, BLK)
        lse_ref[0:1, pl.ds(at, BLK)] = log_total[:, :BLK]
        lse_ref[1:2, pl.ds(at, BLK)] = log_total[:, BLK:]
        return carried

    lax.fori_loop(0, blocks, one_query, 0)


def attend(row, listed, edges, qkv, segc, segr):
    blocks, blk, width = qkv.shape
    length = blocks * blk
    pair = 2 * HEAD_DIM
    return pl.pallas_call(
        functools.partial(attend_kernel, row=row),
        grid_spec=pltpu.PrefetchScalarGridSpec(
            num_scalar_prefetch=2,
            grid=(1,),
            in_specs=[
                whole(qkv.shape),
                pl.BlockSpec((1, length, 1), lambda i, *_: (row, 0, 0)),
                pl.BlockSpec((1, 1, length), lambda i, *_: (row, 0, 0)),
            ],
            out_specs=[whole((blocks, blk, pair)), whole((2, length))],
            scratch_shapes=[
                pltpu.VMEM((pair + 32, length), jnp.bfloat16),
                pltpu.VMEM((2 * blk, pair), jnp.bfloat16),
                pltpu.VMEM((HEAD_DIM + 16, 2 * blk), jnp.float32),
                pltpu.VMEM((1, 2 * blk), jnp.float32),
            ],
        ),
        out_shape=[
            jax.ShapeDtypeStruct((blocks, blk, pair), jnp.bfloat16),
            jax.ShapeDtypeStruct((2, length), jnp.float32),
        ],
        compiler_params=params(),
        cost_estimate=cost(20e9, 6e6, 20e6),
        name="attend",
    )(listed, edges, qkv, segc, segr)


def attend_back_kernel(
    listed_ref, edge_ref, qkv_ref, grad_ref, mixed_ref, lse_ref, segc_ref, segr_ref, out_ref,
    kt_ref, qz_ref, gz_ref, inner_ref, dq_ref, dk_ref, dv_ref, *, row,
):
    blocks = qkv_ref.shape[0]
    scale = HEAD_DIM ** (-0.5)

    def prepare(block, carried):
        at = pl.multiple_of(block * BLK, BLK)
        kt_ref[:, pl.ds(at, BLK)] = transposed(qkv_ref[block, :, 128:256])
        query = qkv_ref[block, :, :128].astype(jnp.float32) * scale
        qz_ref[block] = split_heads(query.astype(jnp.bfloat16))
        grad = grad_ref[block]
        gz_ref[block] = split_heads(grad)
        product = (grad.astype(jnp.float32) * mixed_ref[block].astype(jnp.float32)).T
        for head in range(2):
            part = product[head * HEAD_DIM : (head + 1) * HEAD_DIM, :]
            inner_ref[head : head + 1, pl.ds(at, BLK)] = jnp.sum(part, axis=0, keepdims=True)
        return carried

    lax.fori_loop(0, blocks, prepare, 0)
    dq_ref[...] = jnp.zeros(dq_ref.shape, jnp.float32)

    def one_key(key_block, carried):
        dk_ref[...] = jnp.zeros(dk_ref.shape, jnp.float32)
        dv_ref[...] = jnp.zeros(dv_ref.shape, jnp.float32)
        key_at = pl.multiple_of(key_block * BLK, BLK)

        def accumulate(head, key_at, query_at, keys, values, query, grad, mask):
            keys_here = pl.ds(pl.multiple_of(key_at % BLK, HALF), keys.shape[0])
            queries_here = pl.ds(query_at, query.shape[0])
            scores = dot_nt(keys, query)
            probs = jnp.exp(scores - lse_ref[head : head + 1, queries_here])
            if mask is not None:
                probs = jnp.where(mask, probs, 0.0)
            grad_probs = dot_nt(values, grad)
            grad_scores = probs * (grad_probs - inner_ref[head : head + 1, queries_here])
            probs = probs.astype(jnp.bfloat16)
            grad_scores = grad_scores.astype(jnp.bfloat16)
            dv_ref[keys_here, :] += dot_nn(probs, grad)
            dk_ref[keys_here, :] += dot_nn(grad_scores, query)
            lanes = slice(head * HEAD_DIM, (head + 1) * HEAD_DIM)
            dq_ref[lanes, queries_here] += dot_nn(
                kt_ref[lanes, pl.ds(key_at, keys.shape[0])], grad_scores
            )

        def full_update(query_block, mask):
            query_at = pl.multiple_of(query_block * BLK, BLK)
            keys = qkv_ref[key_block, :, 128:256]
            values = qkv_ref[key_block, :, 256:384]
            for head in range(2):
                part = slice(head * BLK, (head + 1) * BLK)
                query, grad = qz_ref[query_block, part, :], gz_ref[query_block, part, :]
                accumulate(head, key_at, query_at, keys, values, query, grad, mask)

        def one_query(query_block, carried):
            listed = listed_ref[row, query_block * blocks + key_block] != 0
            full = is_full(edge_ref, row, key_block, query_block)

            @pl.when(listed & full)
            def _():
                full_update(query_block, None)

            @pl.when(listed & jnp.logical_not(full))
            def _():
                full_update(query_block, tile_mask(segc_ref, segr_ref, key_block * BLK, query_block * BLK, BLK))

            return carried

        lax.fori_loop(key_block, blocks, one_query, 0)
        grad_query = dq_ref[:, pl.ds(key_at, BLK)].T * scale
        out_ref[key_block] = pair_together(grad_query, dk_ref[...], dv_ref[...]).astype(jnp.bfloat16)
        return carried

    lax.fori_loop(0, blocks, one_key, 0)


def attend_back(row, listed, edges, qkv, grad, mixed, lse, segc, segr):
    blocks, blk, width = qkv.shape
    length = blocks * blk
    pair = 2 * HEAD_DIM
    return pl.pallas_call(
        functools.partial(attend_back_kernel, row=row),
        grid_spec=pltpu.PrefetchScalarGridSpec(
            num_scalar_prefetch=2,
            grid=(1,),
            in_specs=[
                whole(qkv.shape),
                whole(grad.shape),
                whole(mixed.shape),
                whole(lse.shape),
                pl.BlockSpec((1, length, 1), lambda i, *_: (row, 0, 0)),
                pl.BlockSpec((1, 1, length), lambda i, *_: (row, 0, 0)),
            ],
            out_specs=whole(qkv.shape),
            scratch_shapes=[
                pltpu.VMEM((pair, length), jnp.bfloat16),
                pltpu.VMEM((blocks, 2 * blk, pair), jnp.bfloat16),
                pltpu.VMEM((blocks, 2 * blk, pair), jnp.bfloat16),
                pltpu.VMEM((2, length), jnp.float32),
                pltpu.VMEM((pair, length), jnp.float32),
                pltpu.VMEM((blk, pair), jnp.float32),
                pltpu.VMEM((blk, pair), jnp.float32),
            ],
        ),
        out_shape=jax.ShapeDtypeStruct(qkv.shape, jnp.bfloat16),
        compiler_params=params(),
        cost_estimate=cost(50e9, 10e6, 20e6),
        name="attend_back",
    )(listed, edges, qkv, grad, mixed, lse, segc, segr)


def joined(ref, half, halves):
    return jnp.concatenate([ref[i * halves + half] for i in range(ref.shape[0] // halves)], axis=1)


def outward_kernel(mixed_ref, tok_ref, w_ref, scales_ref, hidden_ref, normed_ref, *, row):
    halves = w_ref.shape[1]
    hidden = tok_ref[0].astype(jnp.float32)
    width = hidden.shape[1]
    for half in range(halves):
        hidden += dot_nt(joined(mixed_ref, half, halves), w_ref[:, half].reshape(width, -1))
    hidden_ref[...] = hidden
    hat, _ = normalize(hidden)
    normed_ref[...] = (hat * scales_ref[row : row + 1, width:]).astype(jnp.bfloat16)


def outward(row, mixed, tokens, w_all, scales, columns):
    rows, length, width = tokens.shape
    groups, _, pair = mixed.shape
    chunks, halves, high, _ = w_all.shape
    tile = 256
    one = pl.BlockSpec((tile, width), lambda i: (i, 0))
    return pl.pallas_call(
        functools.partial(outward_kernel, row=row),
        grid=(length // tile,),
        in_specs=[
            pl.BlockSpec((groups, tile, pair), lambda i: (0, i, 0)),
            pl.BlockSpec((1, tile, width), lambda i: (row, i, 0)),
            whole((chunks, halves, high, columns)),
            whole(scales.shape),
        ],
        out_specs=[one, one],
        out_shape=[
            jax.ShapeDtypeStruct((length, width), jnp.float32),
            jax.ShapeDtypeStruct((length, width), jnp.bfloat16),
        ],
        compiler_params=params(),
        cost_estimate=cost(2 * length * width * width, 12 * length * width),
        name="outward",
    )(mixed, tokens, w_all, scales)


def mlp_kernel(
    place_ref, nm0_ref, nm1_ref, cot_ref, hidden0_ref, hidden1_ref, scales_ref, up_ref, down_ref,
    keep_ref, send_ref, layer_ref, grad_hidden_ref, grad_attn_ref, gscale_ref,
    nmt_ref, cott_ref, out_ref, gn_ref, act_ref, gpre_ref,
):
    tile = pl.program_id(0)
    phase = pl.program_id(1)
    length, width = nm0_ref.shape
    count = 2 * length
    root = 0.7978845608028654
    cube = 0.044715

    @pl.when((tile == 0) & (phase == 0))
    def _():
        chunks = up_ref.shape[0]
        turned_apart(nmt_ref.at[:, :length], nm0_ref[...], place_ref[2], chunks)
        turned_apart(nmt_ref.at[:, length:], nm1_ref[...], place_ref[2], chunks)
        turned_apart(cott_ref, cot_ref[...], place_ref[2], chunks)
        out_ref[...] = jnp.zeros(out_ref.shape, jnp.float32)
        gn_ref[...] = jnp.zeros(gn_ref.shape, jnp.float32)

    @pl.when(phase == 0)
    def _():
        up = up_ref[:, 0].reshape(width, -1)
        down = down_ref[:, 0].reshape(width, -1)
        for row, nm_ref in enumerate((nm0_ref, nm1_ref)):
            part = slice(row * length, (row + 1) * length)
            pre = dot_nn(nm_ref[...], up)
            grad_act = dot_nn(cot_ref[part, :], down)
            square = pre * pre
            bent = jnp.tanh(root * (pre + cube * pre * square))
            half = 0.5 * (1.0 + bent)
            act_ref[part, :] = (pre * half).astype(jnp.bfloat16)
            slope = half + (0.5 * root) * pre * (1.0 - bent * bent) * (1.0 + (3.0 * cube) * square)
            gpre_ref[part, :] = (grad_act * slope).astype(jnp.bfloat16)
        put_apart(keep_ref, send_ref, dot_nn(nmt_ref[...], gpre_ref[...]).astype(jnp.bfloat16))

    @pl.when(phase == 1)
    def _():
        up = up_ref[:, 0].reshape(width, -1)
        down = down_ref[:, 0].reshape(width, -1)
        out_ref[...] += dot_nt(act_ref[...], down)
        gn_ref[...] += dot_nt(gpre_ref[...], up)
        put_apart(keep_ref, send_ref, dot_nn(cott_ref[...], act_ref[...]).astype(jnp.bfloat16))

    @pl.when((tile == pl.num_programs(0) - 1) & (phase == 1))
    def _():
        chunk = 256
        for row, hidden_ref in enumerate((hidden0_ref, hidden1_ref)):
            scale = scales_ref[row : row + 1, width:]
            total = jnp.zeros((1, width), jnp.float32)
            for at in range(0, length, chunk):
                part = slice(row * length + at, row * length + at + chunk)
                hidden = hidden_ref[at : at + chunk, :]
                layer_ref[part, :] = (hidden + out_ref[part, :]).astype(jnp.bfloat16)
                hat, inverse = normalize(hidden)
                grad = gn_ref[part, :]
                total += jnp.sum(grad * hat, axis=0, keepdims=True)
                back = cot_ref[part, :].astype(jnp.float32) + normalize_back(grad * scale, hat, inverse)
                grad_hidden_ref[part, :] = back
                grad_attn_ref[part, :] = back.astype(jnp.bfloat16)
            gscale_ref[row : row + 1, :] = total


def mlp(place, normed, cotangent, hidden, scales, w_all, room):
    rows, length, width = cotangent.shape
    count = rows * length
    chunks, halves, high, columns = w_all.shape
    tile = 512
    hidden_cols = (columns - room) // 2
    per_half = hidden_cols // tile
    first = room // tile
    flat = (count, width)
    one = (length, width)
    block = (chunks, 1, high, tile)
    apart = pl.BlockSpec(
        (2, 1, chunks // 4, high, tile),
        lambda f, s, at: (0, f // per_half, 0, 0, first + s * per_half + f % per_half),
    )
    grads = jax.ShapeDtypeStruct((2, halves, chunks // 4, high, columns), jnp.bfloat16)
    return pl.pallas_call(
        mlp_kernel,
        grid_spec=pltpu.PrefetchScalarGridSpec(
            num_scalar_prefetch=1,
            grid=(halves * per_half, 2),
            in_specs=[
                whole(one),
                whole(one),
                whole(flat),
                whole(one),
                whole(one),
                whole(scales.shape),
                pl.BlockSpec(block, lambda f, s, at: (0, f // per_half, 0, first + f % per_half)),
                pl.BlockSpec(block, lambda f, s, at: (0, f // per_half, 0, first + per_half + f % per_half)),
            ],
            out_specs=[
                apart,
                apart,
                whole(flat),
                whole(flat),
                whole(flat),
                whole((rows, width)),
            ],
            scratch_shapes=[
                pltpu.VMEM((width, count), jnp.bfloat16),
                pltpu.VMEM((width, count), jnp.bfloat16),
                pltpu.VMEM(flat, jnp.float32),
                pltpu.VMEM(flat, jnp.float32),
                pltpu.VMEM((count, tile), jnp.bfloat16),
                pltpu.VMEM((count, tile), jnp.bfloat16),
            ],
        ),
        out_shape=[
            grads,
            grads,
            jax.ShapeDtypeStruct(flat, jnp.bfloat16),
            jax.ShapeDtypeStruct(flat, jnp.float32),
            jax.ShapeDtypeStruct(flat, jnp.bfloat16),
            jax.ShapeDtypeStruct((rows, width), jnp.float32),
        ],
        compiler_params=params(60),
        cost_estimate=cost(12 * count * width * halves * hidden_cols, 4 * w_all.size + 16 * count * width),
        name="mlp",
    )(place, *normed, cotangent.reshape(flat), *hidden, scales, w_all, w_all)


def grad_mixed_kernel(grad_ref, w_ref, out_ref):
    halves = w_ref.shape[1]
    per_half = out_ref.shape[0] // halves
    grad = grad_ref[...]
    pair = out_ref.shape[2]
    for half in range(halves):
        out = dot_nn(grad, w_ref[:, half].reshape(grad.shape[1], -1)).astype(jnp.bfloat16)
        for group in range(per_half):
            out_ref[group * halves + half] = out[:, group * pair : (group + 1) * pair]


def grad_mixed_of(row, grad_attn, w_all, mixed_shape, columns):
    groups, length, pair = mixed_shape
    chunks, halves, high, _ = w_all.shape
    width = grad_attn.shape[1]
    tile = 256
    tiles = length // tile
    return pl.pallas_call(
        grad_mixed_kernel,
        grid=(tiles,),
        in_specs=[
            pl.BlockSpec((tile, width), lambda i: (row * tiles + i, 0)),
            whole((chunks, halves, high, columns)),
        ],
        out_specs=pl.BlockSpec((groups, tile, pair), lambda i: (0, i, 0)),
        out_shape=jax.ShapeDtypeStruct(mixed_shape, jnp.bfloat16),
        compiler_params=params(),
        cost_estimate=cost(2 * length * width * width, 8 * length * width),
        name="grad_mixed",
    )(grad_attn, w_all)


def grad_proj_kernel(place_ref, grad_ref, mixed0_ref, mixed1_ref, _k, _s, keep_ref, send_ref, turned_ref):
    half = pl.program_id(0)
    halves = pl.num_programs(0)

    @pl.when(half == 0)
    def _():
        turned_apart(turned_ref, grad_ref[...], place_ref[2], 4 * keep_ref.shape[2])

    groups, length, pair = mixed0_ref.shape
    count = keep_ref.shape[4] // pair
    grad = 0.0
    for row, mixed_ref in enumerate((mixed0_ref, mixed1_ref)):
        mixed = jnp.concatenate([mixed_ref[i * halves + half] for i in range(count)], axis=1)
        grad += dot_nn(turned_ref[:, row * length : (row + 1) * length], mixed)
    put_apart(keep_ref, send_ref, grad.astype(jnp.bfloat16))


def grad_proj_into(place, keep, send, grad_attn, mixed, columns):
    count, width = grad_attn.shape
    given = whole(mixed[0].shape)
    anywhere = pl.BlockSpec(memory_space=pl.ANY)
    out = pl.BlockSpec((2, 1) + keep.shape[2:4] + (columns,), lambda h, at: (0, h, 0, 0, 0))
    return pl.pallas_call(
        grad_proj_kernel,
        grid_spec=pltpu.PrefetchScalarGridSpec(
            num_scalar_prefetch=1,
            grid=(keep.shape[1],),
            in_specs=[whole(grad_attn.shape), given, given, anywhere, anywhere],
            out_specs=[out, out],
            scratch_shapes=[pltpu.VMEM((width, count), jnp.bfloat16)],
        ),
        out_shape=[jax.ShapeDtypeStruct(keep.shape, jnp.bfloat16)] * 2,
        input_output_aliases={4: 0, 5: 1},
        compiler_params=params(),
        cost_estimate=cost(2 * count * width * width, 6 * count * width),
        name="grad_proj",
    )(place, grad_attn, *mixed, keep, send)


def first_norm_kernel(gq_ref, tok_ref, grad_hidden_ref, w_ref, scales_ref, out_ref, gscale_ref, *, row, q_cols):
    step = pl.program_id(0)
    halves = w_ref.shape[1]
    values = tok_ref[0].astype(jnp.float32)
    width = values.shape[1]
    grad = jnp.zeros(values.shape, jnp.float32)
    for half in range(halves):
        weights = w_ref[:, half, :, :q_cols].reshape(width, q_cols)
        grad += dot_nt(joined(gq_ref, half, halves), weights)
    hat, inverse = normalize(values)
    total = jnp.sum(grad * hat, axis=0, keepdims=True)

    @pl.when(step == 0)
    def _():
        gscale_ref[...] = total

    @pl.when(step != 0)
    def _():
        gscale_ref[...] += total

    back = normalize_back(grad * scales_ref[row : row + 1, :width], hat, inverse)
    out_ref[...] = (grad_hidden_ref[...] + back).astype(jnp.bfloat16)


def first_norm_back(row, grad_qkv, tokens, grad_hidden, w_all, scales, q_cols):
    rows, length, width = tokens.shape
    groups, _, pair = grad_qkv.shape
    tile = 256
    tiles = length // tile
    return pl.pallas_call(
        functools.partial(first_norm_kernel, row=row, q_cols=q_cols),
        grid=(tiles,),
        in_specs=[
            pl.BlockSpec((groups, tile, pair), lambda i: (0, i, 0)),
            pl.BlockSpec((1, tile, width), lambda i: (row, i, 0)),
            pl.BlockSpec((tile, width), lambda i: (row * tiles + i, 0)),
            whole(w_all.shape),
            whole(scales.shape),
        ],
        out_specs=[pl.BlockSpec((tile, width), lambda i: (i, 0)), whole((1, width))],
        out_shape=[
            jax.ShapeDtypeStruct((length, width), jnp.bfloat16),
            jax.ShapeDtypeStruct((1, width), jnp.float32),
        ],
        compiler_params=params(),
        cost_estimate=cost(2 * length * width * groups * pair, 2 * w_all.size + 20 * length * width),
        name="first_norm_back",
    )(grad_qkv, tokens, grad_hidden, w_all, scales)


def grad_qkv_kernel(place_ref, normed_ref, gq_ref, *refs):
    step = pl.program_id(0)
    base_refs, out_refs, total_ref = refs[:-2], refs[-2:-1], refs[-1]
    if len(refs) > 3:
        base_refs, out_refs, (total_ref, turned_ref) = refs[:1], refs[1:-2], refs[-2:]

    @pl.when(step == 0)
    def _():
        total_ref[...] = base_refs[0][...] if base_refs else jnp.zeros(total_ref.shape, jnp.float32)

    total_ref[...] += dot_nn(transposed(gq_ref[0]), normed_ref[0])

    @pl.when(step == pl.num_programs(0) - 1)
    def _():
        if base_refs:
            turned_ref[...] = total_ref[...].T
            tall = out_refs[0].shape[0]
            for apart, out_ref in enumerate(out_refs):
                at = pl.multiple_of((apart ^ place_ref[1]) * tall, tall)
                out_ref[...] = turned_ref[pl.ds(at, tall), :].astype(jnp.bfloat16)
        else:
            out_refs[0][...] = total_ref[...]


def grad_qkv_of(place, normed, grad_qkv, parts, base=()):
    blocks, length, width = normed.shape
    pair = grad_qkv.shape[2]
    turned = (pair, width)
    if base:
        shapes = [jax.ShapeDtypeStruct((width // parts, pair), jnp.bfloat16)] * parts
    else:
        shapes = [jax.ShapeDtypeStruct(turned, jnp.float32)]
    return pl.pallas_call(
        grad_qkv_kernel,
        grid_spec=pltpu.PrefetchScalarGridSpec(
            num_scalar_prefetch=1,
            grid=(blocks,),
            in_specs=[
                pl.BlockSpec((1, length, width), lambda i, place: (i, 0, 0)),
                pl.BlockSpec((1, length, pair), lambda i, place: (i, 0, 0)),
            ]
            + [whole(turned)] * len(base),
            out_specs=[whole(one.shape) for one in shapes],
            scratch_shapes=[pltpu.VMEM(turned, jnp.float32)]
            + [pltpu.VMEM((width, pair), jnp.float32)] * len(base),
        ),
        out_shape=shapes,
        compiler_params=params(),
        cost_estimate=cost(2 * blocks * length * width * pair, 3 * blocks * length * width),
        name="grad_qkv",
    )(place, normed, grad_qkv, *base)


CTX = ("x", "core")
GROUP = ("x", "core", "tp")
EVERY = ("fsdp", "x", "core", "tp")


def size_of(axis):
    names = (axis,) if isinstance(axis, str) else axis
    return functools.reduce(lambda size, name: size * lax.axis_size(name), names, 1)


def across(values, axis, apart):
    size = size_of(axis)
    return lax.ppermute(values, axis, [(i, i ^ apart) for i in range(size)])


def summed(parts):
    return sum(part.astype(jnp.float32) for part in parts)


def exchange(values, axes):
    return lax.all_to_all(values, axes, 0, 0, tiled=True)


HOPS = {1: "tp", 2: "core", 4: "x"}


def widened(found, apart):
    return {**found, **{held ^ apart: across(one, HOPS[apart], 1) for held, one in found.items()}}


def listed_table(block_pairs, pair_counts, row_blocks, ctx_size):
    rows, _, slots, _ = block_pairs.shape
    packed = jnp.concatenate([block_pairs.reshape(rows, 1, slots * 2), pair_counts[:, :, None]], axis=2)
    packed = jnp.concatenate(
        [packed] + [across(packed, CTX, apart) for apart in range(1, ctx_size)], axis=1
    )
    pairs = packed[:, :, : slots * 2].reshape(rows, ctx_size, slots, 2)
    live = jnp.arange(slots, dtype=jnp.int32)[None, None, :] < packed[:, :, slots * 2 :]
    owner = lax.axis_index(CTX) ^ jnp.arange(ctx_size, dtype=jnp.int32)[None, :, None]
    base = owner * (row_blocks // ctx_size)
    code = jnp.where(live, (base + pairs[..., 0]) * row_blocks + pairs[..., 1], -1)
    code = code.reshape(rows, ctx_size * slots)
    cells = jnp.arange(row_blocks * row_blocks, dtype=jnp.int32)
    return jnp.any(code[:, :, None] == cells[None, None, :], axis=1).astype(jnp.int32)


def spread_body(
    tokens, time_embed, segment_ids, block_pairs, pair_counts,
    w_time, w_qkv, w_out, w_up, w_down, cotangent,
):
    rows, length, width = tokens.shape
    chunks = width // w_qkv.shape[0]
    halves = lax.axis_size("tp")
    high = w_qkv.shape[0]
    q_cols, o_cols, f_cols = w_qkv.shape[1], w_out.shape[1], w_up.shape[1]
    k_rows = w_time.shape[0]
    mine = lax.axis_index("tp")
    ctx, fsdp = lax.axis_index(CTX), lax.axis_index("fsdp")
    n_ctx, n_fsdp = size_of(CTX), lax.axis_size("fsdp")
    bf16, f32 = jnp.bfloat16, jnp.float32
    chunk = fsdp * n_ctx + ctx
    place = jnp.stack([ctx * halves + mine, fsdp, lax.axis_index("core")])

    found = [{0: tokens[row]} for row in range(rows)]
    orders = [(4, 1, 2) if row % 2 == 0 else (1, 4, 2) for row in range(rows)]
    found = [widened(one, order[0]) for one, order in zip(found, orders)]
    w_qkv = w_qkv.astype(bf16)
    columns = exchange(w_qkv.reshape(high, n_ctx, -1).transpose(1, 0, 2), CTX)
    embeds = [time_embed] + [across(time_embed, "fsdp", apart) for apart in range(1, n_fsdp)]
    w_time = w_time.astype(bf16)
    times = [w_time] + [across(w_time, CTX, apart) for apart in range(1, n_ctx)]
    row_blocks = segment_ids.shape[1] // BLK
    listed = listed_table(block_pairs, pair_counts, row_blocks, n_ctx)
    edges = jnp.concatenate([segment_ids[:, ::HALF], segment_ids[:, HALF - 1 :: HALF]], axis=1)
    segc = segment_ids[:, :, None]
    segr = segment_ids[:, None, :]
    second = jnp.concatenate([w_out, w_up, w_down], axis=1).astype(bf16)
    found, columns, embeds, times, second = lax.optimization_barrier((found, columns, embeds, times, second))
    second = lax.all_gather(second, EVERY, axis=0, tiled=True)
    found = [widened(one, order[1]) for one, order in zip(found, orders)]
    columns = columns.reshape(n_ctx * high, -1)
    columns = [columns] + [across(columns, "fsdp", apart) for apart in range(1, n_fsdp)]
    rows_of = [(chunk ^ apart) * k_rows for apart in range(n_ctx)]
    some = [
        jnp.concatenate([lax.dynamic_slice_in_dim(one, at, k_rows, 1) for at in rows_of], axis=1)
        for one in embeds
    ]
    mine_of = [one[:, :k_rows] for one in some]
    given = jnp.dot(jnp.concatenate(some, axis=0), jnp.concatenate(times, axis=0).astype(f32), precision=highest)
    given = given.reshape(n_fsdp, rows, -1)
    scales = 1.0 + given[0] + sum(across(given[apart], "fsdp", apart) for apart in range(1, n_fsdp))
    found, scales, columns, listed, edges, segc, segr = lax.optimization_barrier(
        (found, scales, columns, listed, edges, segc, segr)
    )
    found = [widened(one, order[2]) for one, order in zip(found, orders)]
    others = [[one[apart] for apart in range(1, len(one))] for one in found]

    qkv, normed = [], []
    for row in range(rows):
        out, one = project(row, place, scales, columns, tokens, others[row])
        qkv.append(out)
        normed.append(one)
    mixed_own, lse, mixed = [], [], []
    for row in range(rows):
        out, one = attend(row, listed, edges, qkv[row], segc, segr)
        mixed_own.append(out)
        lse.append(one)
        mixed.append(exchange(out, GROUP))
    mixed[0], mixed_own = lax.optimization_barrier((mixed[0], mixed_own))
    second = second.reshape(chunks, halves, high, -1)
    hidden, normed_mlp = [], []
    for row in range(rows):
        if row:
            mixed[row], hidden[row - 1] = lax.optimization_barrier((mixed[row], hidden[row - 1]))
        out, one = outward(row, mixed[row], tokens, second, scales, o_cols)
        hidden.append(out)
        normed_mlp.append(one)
    w_qkv, normed_mlp = lax.optimization_barrier((w_qkv, normed_mlp))
    third = lax.all_gather(w_qkv, EVERY, axis=0, tiled=True).reshape(chunks, halves, high, -1)
    keep, send, layer_out, grad_hidden, grad_attn, gscale_mlp = mlp(
        place, normed_mlp, cotangent, hidden, scales, second, o_cols
    )
    keep, send = grad_proj_into(place, keep, send, grad_attn, mixed, o_cols)
    grad_attn, keep, send, third = lax.optimization_barrier((grad_attn, keep, send, third))
    sent = across(send, "core", 1)
    grad_mixed = {}
    for row in reversed(range(rows)):
        out = grad_mixed_of(row, grad_attn, second, mixed[row].shape, o_cols)
        grad_mixed[row] = exchange(out, GROUP)
    last = rows - 1
    grads = summed([keep, sent]).astype(bf16)
    grad_mixed[last], grads = lax.optimization_barrier((grad_mixed[last], grads))
    grads = lax.psum_scatter(
        grads.reshape(-1, grads.shape[4]), ("x", "tp"), scatter_dimension=0, tiled=True
    )
    own, grad_qkv = {}, {}
    for row in reversed(range(rows)):
        if row < last:
            grad_mixed[row], own[row + 1] = lax.optimization_barrier((grad_mixed[row], own[row + 1]))
        own[row] = attend_back(row, listed, edges, qkv[row], grad_mixed[row], mixed_own[row], lse[row], segc, segr)
        if row < last:
            grad_qkv[row + 1] = exchange(own[row + 1], GROUP)
    grad_qkv[0] = exchange(own[0], GROUP)
    held, _ = lax.optimization_barrier((own[last], own[0]))
    base = grad_qkv_of(place, normed[last], held, n_fsdp)
    cut = list(grad_qkv_of(place, normed[0], own[0], n_fsdp, base))
    grad_tokens, gscale_attn = {}, {}
    held, _ = lax.optimization_barrier((grad_qkv[last], cut[0]))
    grad_tokens[last], gscale_attn[last] = first_norm_back(
        last, held, tokens, grad_hidden, third, scales, q_cols
    )
    cut[0], gscale_attn[last] = lax.optimization_barrier((cut[0], gscale_attn[last]))
    total = summed([cut[0]] + [across(cut[apart], "fsdp", apart) for apart in range(1, n_fsdp)])
    grads, gscale_attn[last], total = lax.optimization_barrier(
        (grads, gscale_attn[last], total.astype(bf16))
    )
    grads = lax.psum_scatter(grads, "fsdp", scatter_dimension=0, tiled=True)
    total = exchange(total.reshape(n_ctx, high, -1), CTX)
    grad_tokens[0], gscale_attn[0] = first_norm_back(
        0, grad_qkv[0], tokens, grad_hidden, third, scales, q_cols
    )
    devices = n_fsdp * n_ctx * halves
    both = jnp.concatenate([gscale_mlp, gscale_attn[last], gscale_attn[0]], axis=0)
    both = exchange(jnp.broadcast_to(both[None], (devices,) + both.shape), EVERY)
    both, total = lax.optimization_barrier((both, total))
    grad_w_qkv = total.transpose(1, 0, 2).reshape(high, q_cols).astype(f32)
    both = jnp.sum(both.reshape(n_fsdp, n_ctx * halves, 2 * rows, width), axis=1)
    both = jnp.concatenate([both[:, 3], both[:, 0], both[:, 2], both[:, 1]], axis=1)
    both = both.reshape(n_fsdp * rows, 2 * width)
    mine_of = [lax.dynamic_index_in_dim(jnp.stack(mine_of), i ^ fsdp, 0, False) for i in range(n_fsdp)]
    grad_time = jnp.dot(jnp.concatenate(mine_of, axis=0).T, both, precision=highest)
    return (
        layer_out.reshape(tokens.shape),
        jnp.stack([grad_tokens[row] for row in range(rows)]),
        grad_time,
        grad_w_qkv,
        grads[:, :o_cols].astype(f32),
        grads[:, o_cols : o_cols + f_cols].astype(f32),
        grads[:, o_cols + f_cols :].astype(f32),
    )


def specs_of(ctx):
    flat = ctx if isinstance(ctx, tuple) else (ctx,)
    tokens, weights = P("fsdp", (*flat, "tp"), None), P(("fsdp", *flat), "tp")
    placed = (tokens, P("fsdp", None), P("fsdp", None), P("fsdp", ctx, None, None), P("fsdp", ctx))
    placed += (P(("fsdp", *flat), None), weights, weights, weights, weights, tokens)
    return placed, (tokens, tokens, P(("fsdp", *flat), None), weights, weights, weights, weights)


def solution(mesh):
    sizes = tuple(mesh.shape[name] for name in ("fsdp", "ctx", "tp"))

    def run(*args):
        tokens, w_qkv, w_out, w_up = args[0], args[6], args[7], args[8]
        group = sizes[1] * sizes[2]
        fits = (
            sizes == (4, 4, 2)
            and tokens.shape[:2] == (8, group * BLK)
            and w_qkv.shape[1] == group * 6 * HEAD_DIM
            and w_out.shape[1] % (512 * sizes[2]) == 0
            and w_up.shape[1] % (512 * sizes[2]) == 0
        )
        if fits:
            devices = mesh.devices.reshape(sizes[0], 2, 2, sizes[2])
            parted = Mesh(devices, ("fsdp", "x", "core", "tp"))
            placed, given = specs_of(CTX)
            return jax.shard_map(
                spread_body, mesh=parted, in_specs=placed, out_specs=given, check_vma=False
            )(*args)
        placed, given = specs_of("ctx")
        return jax.shard_map(body, mesh=mesh, in_specs=placed, out_specs=given, check_vma=False)(*args)

    return run
```

```python
import functools

import jax
import jax.numpy as jnp
from jax import lax
from jax.experimental import pallas as pl
from jax.experimental.pallas import tpu as pltpu
from jax.sharding import Mesh
from jax.sharding import PartitionSpec as P

HEAD_DIM = 64
BLK = 512


epsilon = 1e-05
highest = lax.Precision.HIGHEST
masked_out = -1e30


def normalize(values):
    mean_value = jnp.mean(values, axis=-1, keepdims=True)
    centred = values - mean_value
    variance = jnp.mean(centred * centred, axis=-1, keepdims=True)
    inverse = lax.rsqrt(variance + epsilon)
    return (centred * inverse, inverse)


def normalize_back(grad_hat, normal_hat, inverse):
    first_mean = jnp.mean(grad_hat, axis=-1, keepdims=True)
    second_mean = jnp.mean(grad_hat * normal_hat, axis=-1, keepdims=True)
    return inverse * (grad_hat - first_mean - normal_hat * second_mean)


def smooth_gate(values):
    return jax.nn.gelu(values, approximate=True)


def block_scores(pair_entry, query_rows, key_rows, seg_row, offset):
    query_start = pair_entry[0] * BLK
    key_start = pair_entry[1] * BLK
    query_block = lax.dynamic_slice_in_dim(query_rows, query_start, BLK, 0)
    key_block = lax.dynamic_slice_in_dim(key_rows, key_start, BLK, 0)
    seg_query = lax.dynamic_slice_in_dim(seg_row, offset + query_start, BLK, 0)
    seg_keys = lax.dynamic_slice_in_dim(seg_row, key_start, BLK, 0)
    steps_in = jnp.arange(BLK, dtype=jnp.int32)
    allowed = (seg_query[:, None] == seg_keys[None, :]) & (
        key_start + steps_in[None, :] <= offset + query_start + steps_in[:, None]
    )
    scores = jnp.einsum(
        "qhe,khe->hqk", query_block, key_block, preferred_element_type=jnp.float32
    ) * HEAD_DIM ** (-0.5)
    return (query_block, key_block, query_start, key_start, allowed, scores)


def attend_forward(query_rows, key_rows, value_rows, seg_row, pair_rows, pair_total, offset):
    length_here, head_count, _ = query_rows.shape

    def statistic_step(pair_index, carried):
        running_max, running_sum = carried
        _, _, query_start, _, allowed, scores = block_scores(
            pair_rows[pair_index], query_rows, key_rows, seg_row, offset
        )
        scores = jnp.where(allowed[None], scores, masked_out)
        old_max = lax.dynamic_slice_in_dim(running_max, query_start, BLK, 1)
        old_sum = lax.dynamic_slice_in_dim(running_sum, query_start, BLK, 1)
        new_max = jnp.maximum(old_max, jnp.max(scores, axis=-1))
        weights = jnp.where(allowed[None], jnp.exp(scores - new_max[:, :, None]), 0.0)
        new_sum = old_sum * jnp.exp(old_max - new_max) + jnp.sum(weights, axis=-1)
        return (
            lax.dynamic_update_slice_in_dim(running_max, new_max, query_start, 1),
            lax.dynamic_update_slice_in_dim(running_sum, new_sum, query_start, 1),
        )

    start_max = jnp.full((head_count, length_here), masked_out, jnp.float32)
    start_sum = jnp.zeros((head_count, length_here), jnp.float32)
    running_max, running_sum = lax.fori_loop(0, pair_total, statistic_step, (start_max, start_sum))
    log_total = running_max + jnp.log(running_sum)

    def output_step(pair_index, accumulated):
        _, _, query_start, key_start, allowed, scores = block_scores(
            pair_rows[pair_index], query_rows, key_rows, seg_row, offset
        )
        block_log = lax.dynamic_slice_in_dim(log_total, query_start, BLK, 1)
        probabilities = jnp.where(
            allowed[None], jnp.exp(scores - block_log[:, :, None]), 0.0
        ).astype(jnp.bfloat16)
        value_block = lax.dynamic_slice_in_dim(value_rows, key_start, BLK, 0)
        addition = jnp.einsum(
            "hqk,khe->qhe", probabilities, value_block, preferred_element_type=jnp.float32
        )
        previous = lax.dynamic_slice_in_dim(accumulated, query_start, BLK, 0)
        return lax.dynamic_update_slice_in_dim(accumulated, previous + addition, query_start, 0)

    mixed_rows = lax.fori_loop(0, pair_total, output_step, jnp.zeros(query_rows.shape, jnp.float32))
    return (mixed_rows, log_total)


def attend_backward(
    query_rows,
    key_rows,
    value_rows,
    seg_row,
    pair_rows,
    pair_total,
    offset,
    log_total,
    grad_mixed,
    inner_sums,
):
    scale_factor = HEAD_DIM ** (-0.5)

    def add_block(whole, start_at, addition):
        previous = lax.dynamic_slice_in_dim(whole, start_at, BLK, 0)
        return lax.dynamic_update_slice_in_dim(whole, previous + addition, start_at, 0)

    def gradient_step(pair_index, carried):
        grad_query, grad_keys, grad_values = carried
        query_block, key_block, query_start, key_start, allowed, scores = block_scores(
            pair_rows[pair_index], query_rows, key_rows, seg_row, offset
        )
        block_log = lax.dynamic_slice_in_dim(log_total, query_start, BLK, 1)
        probabilities = jnp.where(allowed[None], jnp.exp(scores - block_log[:, :, None]), 0.0)
        grad_block = lax.dynamic_slice_in_dim(grad_mixed, query_start, BLK, 0)
        value_block = lax.dynamic_slice_in_dim(value_rows, key_start, BLK, 0)
        grad_probs = jnp.einsum(
            "qhe,khe->hqk", grad_block, value_block, preferred_element_type=jnp.float32
        )
        inner_block = lax.dynamic_slice_in_dim(inner_sums, query_start, BLK, 1)
        grad_scores = (probabilities * (grad_probs - inner_block[:, :, None])).astype(jnp.bfloat16)
        query_add = (
            jnp.einsum("hqk,khe->qhe", grad_scores, key_block, preferred_element_type=jnp.float32)
            * scale_factor
        )
        key_add = (
            jnp.einsum("hqk,qhe->khe", grad_scores, query_block, preferred_element_type=jnp.float32)
            * scale_factor
        )
        value_add = jnp.einsum(
            "hqk,qhe->khe",
            probabilities.astype(jnp.bfloat16),
            grad_block,
            preferred_element_type=jnp.float32,
        )
        return (
            add_block(grad_query, query_start, query_add),
            add_block(grad_keys, key_start, key_add),
            add_block(grad_values, key_start, value_add),
        )

    start_state = (
        jnp.zeros(query_rows.shape, jnp.float32),
        jnp.zeros(key_rows.shape, jnp.float32),
        jnp.zeros(value_rows.shape, jnp.float32),
    )
    return lax.fori_loop(0, pair_total, gradient_step, start_state)


def body(
    tokens,
    time_embed,
    segment_ids,
    block_pairs,
    pair_counts,
    w_time,
    w_qkv,
    w_out,
    w_up,
    w_down,
    cotangent,
):
    row_count, local_len, model_width = tokens.shape
    time_all, qkv_all, out_all, up_all, down_all = (
        lax.all_gather(w_time.astype(jnp.bfloat16), ("fsdp", "ctx"), axis=0, tiled=True),
        lax.all_gather(w_qkv.astype(jnp.bfloat16), ("fsdp", "ctx"), axis=0, tiled=True),
        lax.all_gather(w_out.astype(jnp.bfloat16), ("fsdp", "ctx"), axis=0, tiled=True),
        lax.all_gather(w_up.astype(jnp.bfloat16), ("fsdp", "ctx"), axis=0, tiled=True),
        lax.all_gather(w_down.astype(jnp.bfloat16), ("fsdp", "ctx"), axis=0, tiled=True),
    )
    scales = 1.0 + jnp.dot(time_embed, time_all.astype(jnp.float32), precision=highest)
    scale_attn = scales[:, None, :model_width]
    scale_mlp = scales[:, None, model_width:]
    x_input = tokens.astype(jnp.float32)
    hat_attn, inverse_attn = normalize(x_input)
    normed = (hat_attn * scale_attn).astype(jnp.bfloat16)
    normed_all = lax.all_gather(normed, "tp", axis=1, tiled=True)
    ctx_len = normed_all.shape[1]
    head_count = qkv_all.shape[1] // (3 * HEAD_DIM)
    projected = jnp.einsum("rtd,dc->rtc", normed_all, qkv_all, preferred_element_type=jnp.float32)
    projected = projected.astype(jnp.bfloat16).reshape(row_count, ctx_len, head_count, 3, HEAD_DIM)
    query_all = projected[:, :, :, 0]
    key_part = projected[:, :, :, 1]
    value_part = projected[:, :, :, 2]
    key_all, value_all = (
        lax.all_gather(key_part, "ctx", axis=1, tiled=True),
        lax.all_gather(value_part, "ctx", axis=1, tiled=True),
    )
    offset = lax.axis_index("ctx") * ctx_len
    mixed_list = []
    log_list = []
    for row_index in range(row_count):
        mixed_rows, log_total = attend_forward(
            query_all[row_index],
            key_all[row_index],
            value_all[row_index],
            segment_ids[row_index],
            block_pairs[row_index, 0],
            pair_counts[row_index, 0],
            offset,
        )
        mixed_list.append(mixed_rows)
        log_list.append(log_total)
    mixed_exact = jnp.stack(mixed_list)
    mixed_heads = mixed_exact.astype(jnp.bfloat16).reshape(
        row_count, ctx_len, head_count * HEAD_DIM
    )
    attn_part = jnp.einsum("rtc,dc->rtd", mixed_heads, out_all, preferred_element_type=jnp.float32)
    attn_local = lax.psum_scatter(
        attn_part.astype(jnp.bfloat16), "tp", scatter_dimension=1, tiled=True
    ).astype(jnp.float32)
    hidden = x_input + attn_local
    hat_mlp, inverse_mlp = normalize(hidden)
    normed_mlp = (hat_mlp * scale_mlp).astype(jnp.bfloat16)
    mlp_all = lax.all_gather(normed_mlp, "tp", axis=1, tiled=True)
    pre_act = jnp.einsum("rtd,df->rtf", mlp_all, up_all, preferred_element_type=jnp.float32)
    activated = smooth_gate(pre_act).astype(jnp.bfloat16)
    mlp_part = jnp.einsum("rtf,df->rtd", activated, down_all, preferred_element_type=jnp.float32)
    mlp_local = lax.psum_scatter(
        mlp_part.astype(jnp.bfloat16), "tp", scatter_dimension=1, tiled=True
    ).astype(jnp.float32)
    grad_all = lax.all_gather(cotangent, "tp", axis=1, tiled=True)
    grad_act = jnp.einsum("rtd,df->rtf", grad_all, down_all, preferred_element_type=jnp.float32)
    _, gate_back = jax.vjp(smooth_gate, pre_act)
    grad_pre = gate_back(grad_act)[0].astype(jnp.bfloat16)
    grad_down = jnp.einsum("rtd,rtf->df", grad_all, activated, preferred_element_type=jnp.float32)
    grad_up = jnp.einsum("rtd,rtf->df", mlp_all, grad_pre, preferred_element_type=jnp.float32)
    norm_part = jnp.einsum("rtf,df->rtd", grad_pre, up_all, preferred_element_type=jnp.float32)
    grad_normed_mlp = lax.psum_scatter(
        norm_part.astype(jnp.bfloat16), "tp", scatter_dimension=1, tiled=True
    ).astype(jnp.float32)
    layer_out = (hidden + mlp_local).astype(jnp.bfloat16)
    grad_output = cotangent.astype(jnp.float32)
    grad_scale_mlp = jnp.sum(grad_normed_mlp * hat_mlp, axis=1)
    grad_hidden = grad_output + normalize_back(grad_normed_mlp * scale_mlp, hat_mlp, inverse_mlp)
    grad_attn_all = lax.all_gather(grad_hidden.astype(jnp.bfloat16), "tp", axis=1, tiled=True)
    grad_mixed = jnp.einsum(
        "rtd,dc->rtc", grad_attn_all, out_all, preferred_element_type=jnp.float32
    ).astype(jnp.bfloat16)
    grad_proj = jnp.einsum(
        "rtd,rtc->dc", grad_attn_all, mixed_heads, preferred_element_type=jnp.float32
    )
    grad_mixed = grad_mixed.reshape(row_count, ctx_len, head_count, HEAD_DIM)
    inner_sums = jnp.einsum("rqhe,rqhe->rhq", grad_mixed.astype(jnp.float32), mixed_exact)
    query_grads = []
    key_grads = []
    value_grads = []
    for row_index in range(row_count):
        grad_query, grad_keys, grad_values = attend_backward(
            query_all[row_index],
            key_all[row_index],
            value_all[row_index],
            segment_ids[row_index],
            block_pairs[row_index, 0],
            pair_counts[row_index, 0],
            offset,
            log_list[row_index],
            grad_mixed[row_index],
            inner_sums[row_index],
        )
        query_grads.append(grad_query)
        key_grads.append(grad_keys)
        value_grads.append(grad_values)
    key_local, value_local = (
        lax.psum_scatter(
            jnp.stack(key_grads).astype(jnp.bfloat16), "ctx", scatter_dimension=1, tiled=True
        ).astype(jnp.float32),
        lax.psum_scatter(
            jnp.stack(value_grads).astype(jnp.bfloat16), "ctx", scatter_dimension=1, tiled=True
        ).astype(jnp.float32),
    )
    grad_projected = jnp.stack(
        [
            jnp.stack(query_grads).astype(jnp.bfloat16),
            key_local.astype(jnp.bfloat16),
            value_local.astype(jnp.bfloat16),
        ],
        axis=3,
    )
    grad_projected = grad_projected.reshape(row_count, ctx_len, head_count * 3 * HEAD_DIM)
    grad_qkv = jnp.einsum(
        "rtd,rtc->dc", normed_all, grad_projected, preferred_element_type=jnp.float32
    )
    first_part = jnp.einsum(
        "rtc,dc->rtd", grad_projected, qkv_all, preferred_element_type=jnp.float32
    )
    grad_normed = lax.psum_scatter(
        first_part.astype(jnp.bfloat16), "tp", scatter_dimension=1, tiled=True
    ).astype(jnp.float32)
    grad_scale_attn = jnp.sum(grad_normed * hat_attn, axis=1)
    grad_tokens = grad_hidden + normalize_back(grad_normed * scale_attn, hat_attn, inverse_attn)
    grad_scales = lax.psum(jnp.concatenate([grad_scale_attn, grad_scale_mlp], axis=1), "tp")
    grad_time = jnp.dot(time_embed.T, grad_scales, precision=highest)
    shared = (
        lax.psum_scatter(
            grad_time.astype(jnp.bfloat16), ("fsdp", "ctx"), scatter_dimension=0, tiled=True
        ).astype(jnp.float32),
        lax.psum_scatter(
            grad_qkv.astype(jnp.bfloat16), ("fsdp", "ctx"), scatter_dimension=0, tiled=True
        ).astype(jnp.float32),
        lax.psum_scatter(
            grad_proj.astype(jnp.bfloat16), ("fsdp", "ctx"), scatter_dimension=0, tiled=True
        ).astype(jnp.float32),
        lax.psum_scatter(
            grad_up.astype(jnp.bfloat16), ("fsdp", "ctx"), scatter_dimension=0, tiled=True
        ).astype(jnp.float32),
        lax.psum_scatter(
            grad_down.astype(jnp.bfloat16), ("fsdp", "ctx"), scatter_dimension=0, tiled=True
        ).astype(jnp.float32),
    )
    return (
        layer_out,
        grad_tokens.astype(jnp.bfloat16),
        shared[0],
        shared[1],
        shared[2],
        shared[3],
        shared[4],
    )


def params(limit=58):
    return pltpu.CompilerParams(vmem_limit_bytes=limit * 1024 * 1024)


def whole(shape):
    zeros = (0,) * len(shape)
    return pl.BlockSpec(shape, lambda *_: zeros, pipeline_mode=pl.Buffered(1))


def cost(flops, nbytes, exps=0):
    return pl.CostEstimate(flops=int(flops), bytes_accessed=int(nbytes), transcendentals=int(exps))


def dot_nn(left, right):
    return jnp.dot(left, right, preferred_element_type=jnp.float32)


def dot_nt(left, right):
    return lax.dot_general(left, right, (((1,), (1,)), ((), ())), preferred_element_type=jnp.float32)


def transposed(values):
    return values.astype(jnp.float32).T.astype(values.dtype)


def turned_apart(into_ref, values, core, chunks):
    turned = transposed(values)
    high = turned.shape[0] // chunks
    for chunk in range(chunks):
        inner = (chunk // 2 % 2) * (chunks // 4) + chunk // 4
        at = ((chunk % 2) ^ core) * (chunks // 2) + inner
        into_ref[pl.ds(pl.multiple_of(at * high, high), high), :] = turned[chunk * high : (chunk + 1) * high]


def put_apart(keep_ref, send_ref, grad):
    middle = grad.shape[0] // 2
    shape = (keep_ref.shape[0],) + keep_ref.shape[2:]
    keep_ref[:, 0] = grad[:middle].reshape(shape)
    send_ref[:, 0] = grad[middle:].reshape(shape)


def low_lanes(shape):
    return lax.broadcasted_iota(jnp.int32, shape, 1) < HEAD_DIM


def pair_apart(stored):
    first, second, third = stored[:, :128], stored[:, 128:256], stored[:, 256:]
    low = low_lanes(first.shape)
    keys = pltpu.roll(jnp.where(low, third, first), HEAD_DIM, 1)
    return jnp.concatenate(
        [jnp.where(low, first, second), keys, jnp.where(low, second, third)], axis=1
    )


def pair_together(query, keys, values):
    low = low_lanes(query.shape)
    turned = pltpu.roll(keys, HEAD_DIM, 1)
    return jnp.concatenate(
        [jnp.where(low, query, turned), jnp.where(low, values, query), jnp.where(low, turned, values)],
        axis=1,
    )


def project_kernel(place_ref, scales_ref, *refs, row, pieces, parts):
    weight_refs, token_refs = refs[:parts], refs[parts : parts + pieces]
    qkv_ref, normed_ref, held_ref, w_ref, sem_ref = refs[parts + pieces :]
    step = pl.program_id(0)

    def fetch(piece):
        source = token_refs[piece]
        source = source.at[row] if len(source.shape) == 3 else source
        return pltpu.make_async_copy(source, held_ref.at[piece], sem_ref.at[piece])

    @pl.when(step == 0)
    def _():
        for piece in range(pieces):
            fetch(piece).start()
        tall = weight_refs[0].shape[0]
        for apart, weight_ref in enumerate(weight_refs):
            at = pl.multiple_of((apart ^ place_ref[1]) * tall, tall)
            w_ref[pl.ds(at, tall), :] = pair_apart(weight_ref[...].astype(jnp.float32)).astype(jnp.bfloat16)
    pltpu.make_async_copy(held_ref.at[step], held_ref.at[step], sem_ref.at[step]).wait()
    values = held_ref[step].astype(jnp.float32)
    width = values.shape[1]
    hat, _ = normalize(values)
    normed = (hat * scales_ref[row : row + 1, :width]).astype(jnp.bfloat16)
    normed_ref[0] = normed
    qkv_ref[0] = dot_nn(normed, w_ref[...]).astype(jnp.bfloat16)


def project(row, place, scales, weights, tokens, others):
    _, length, width = tokens.shape
    pair = weights[0].shape[1]
    pieces = 1 + len(others)
    anywhere = pl.BlockSpec(memory_space=pl.ANY)
    return pl.pallas_call(
        functools.partial(project_kernel, row=row, pieces=pieces, parts=len(weights)),
        grid_spec=pltpu.PrefetchScalarGridSpec(
            num_scalar_prefetch=1,
            grid=(pieces,),
            in_specs=[whole(scales.shape)]
            + [whole(one.shape) for one in weights]
            + [anywhere] * pieces,
            out_specs=[
                pl.BlockSpec((1, length, pair), lambda i, place: (i ^ place[0], 0, 0)),
                pl.BlockSpec((1, length, width), lambda i, place: (i ^ place[0], 0, 0)),
            ],
            scratch_shapes=[
                pltpu.VMEM((pieces, length, width), jnp.bfloat16),
                pltpu.VMEM((width, pair), jnp.bfloat16),
                pltpu.SemaphoreType.DMA((pieces,)),
            ],
        ),
        out_shape=[
            jax.ShapeDtypeStruct((pieces, length, pair), jnp.bfloat16),
            jax.ShapeDtypeStruct((pieces, length, width), jnp.bfloat16),
        ],
        compiler_params=params(),
        cost_estimate=cost(2 * pieces * length * width * pair, 5 * pieces * length * width),
        name="project",
    )(place, scales, *weights, tokens, *others)


HALF = BLK // 2


def tile_mask(segc_ref, segr_ref, key_at, query_at, size):
    key_at, query_at = pl.multiple_of(key_at, size), pl.multiple_of(query_at, size)
    same = segc_ref[0, pl.ds(key_at, size), :] == segr_ref[0, :, pl.ds(query_at, size)]
    key_pos = key_at + lax.broadcasted_iota(jnp.int32, (size, size), 0)
    query_pos = query_at + lax.broadcasted_iota(jnp.int32, (size, size), 1)
    return same & (key_pos <= query_pos)


def split_heads(values):
    low = low_lanes(values.shape)
    zero = jnp.zeros_like(values)
    return jnp.concatenate([jnp.where(low, values, zero), jnp.where(low, zero, values)], axis=0)


def is_full(edge_ref, row, key_block, query_block):
    ends = edge_ref.shape[1] // 2
    same = edge_ref[row, 2 * key_block] == edge_ref[row, ends + 2 * query_block + 1]
    return same & (key_block < query_block)


def over_quarters(edge_ref, row, key_block, query_block, update):
    ends = edge_ref.shape[1] // 2

    def quarter(number, carried):
        key_half = 2 * key_block + number % 2
        query_half = 2 * query_block + number // 2
        shared = edge_ref[row, ends + key_half] >= edge_ref[row, query_half]

        @pl.when(shared & (key_half <= query_half))
        def _():
            update(pl.multiple_of(key_half * HALF, HALF), pl.multiple_of(query_half * HALF, HALF))

        return carried

    lax.fori_loop(0, 4, quarter, 0)


def largest(values, head):
    part = jnp.where(low_lanes(values.shape) == (head == 0), values, 0.0)
    return jnp.max(jnp.sum(part * part, axis=1, keepdims=True))


def attend_kernel(
    listed_ref, edge_ref, qkv_ref, segc_ref, segr_ref, mixed_ref, lse_ref,
    vt_ref, qz_ref, acc_ref, stat_ref, *, row,
):
    blocks = qkv_ref.shape[0]
    tall = HEAD_DIM + 16

    def turn(block, tops):
        at = pl.multiple_of(block * BLK, BLK)
        turned = transposed(qkv_ref[block, :, 256:384])
        ones = jnp.ones((16, BLK), jnp.bfloat16)
        for head in range(2):
            vt_ref[head * tall : head * tall + HEAD_DIM, pl.ds(at, BLK)] = turned[
                head * HEAD_DIM : (head + 1) * HEAD_DIM
            ]
            vt_ref[head * tall + HEAD_DIM : (head + 1) * tall, pl.ds(at, BLK)] = ones
        keys = qkv_ref[block, :, 128:256].astype(jnp.float32)
        return tuple(jnp.maximum(tops[head], largest(keys, head)) for head in range(2))

    key_tops = lax.fori_loop(0, blocks, turn, (0.0, 0.0))

    def one_query(query_block, carried):
        query = qkv_ref[query_block, :, :128].astype(jnp.float32) * HEAD_DIM ** (-0.5)
        qz_ref[...] = split_heads(query.astype(jnp.bfloat16))
        acc_ref[...] = jnp.zeros(acc_ref.shape, jnp.float32)
        shift = []
        for head in range(2):
            both = jnp.full((1, BLK), largest(query, head) * key_tops[head], jnp.float32)
            shift.append(jnp.sqrt(both) * 1.01)
        small = (jnp.max(shift[0]) < 40.0) & (jnp.max(shift[1]) < 40.0)

        def over_keys(full_update, part_update):
            def one_key(key_block, carried):
                listed = listed_ref[row, query_block * blocks + key_block] != 0
                full = is_full(edge_ref, row, key_block, query_block)

                @pl.when(listed & full)
                def _():
                    full_update(key_block)

                @pl.when(listed & jnp.logical_not(full))
                def _():
                    part_update(key_block)

                return carried

            lax.fori_loop(0, query_block + 1, one_key, 0)

        @pl.when(small)
        def _():
            def update(key_block, mask):
                at = pl.multiple_of(key_block * BLK, BLK)
                keys = qkv_ref[key_block, :, 128:256]
                parts = [slice(head * BLK, (head + 1) * BLK) for head in range(2)]
                scores = [dot_nt(keys, qz_ref[part, :]) for part in parts]
                for head, part in enumerate(parts):
                    one = scores[head] - shift[head]
                    if mask is not None:
                        one = jnp.where(mask, one, masked_out)
                    value = vt_ref[head * tall : (head + 1) * tall, pl.ds(at, BLK)]
                    acc_ref[:, part] += dot_nn(value, jnp.exp(one).astype(jnp.bfloat16))

            def part_update(key_block):
                update(key_block, tile_mask(segc_ref, segr_ref, key_block * BLK, query_block * BLK, BLK))

            def full_update(key_block):
                update(key_block, None)

            over_keys(full_update, part_update)
            stat_ref[0:1, :] = jnp.concatenate(shift, axis=1)

        @pl.when(jnp.logical_not(small))
        def _():
            stat_ref[0:1, :] = jnp.full((1, 2 * BLK), masked_out, jnp.float32)

            def part_update(key_at, query_at):
                keys = qkv_ref[key_at // BLK, pl.ds(pl.multiple_of(key_at % BLK, HALF), HALF), 128:256]
                mask = tile_mask(segc_ref, segr_ref, key_at, query_at, HALF)
                for head in range(2):
                    part = pl.ds(pl.multiple_of(head * BLK + query_at % BLK, HALF), HALF)
                    scores = jnp.where(mask, dot_nt(keys, qz_ref[part, :]), masked_out)
                    old_max = stat_ref[0:1, part]
                    new_max = jnp.maximum(old_max, jnp.max(scores, axis=0, keepdims=True))
                    weights = jnp.where(mask, jnp.exp(scores - new_max), 0.0)
                    value = vt_ref[head * tall : (head + 1) * tall, pl.ds(key_at, HALF)]
                    shrink = jnp.exp(old_max - new_max)
                    acc_ref[:, part] = acc_ref[:, part] * shrink + dot_nn(value, weights.astype(jnp.bfloat16))
                    stat_ref[0:1, part] = new_max

            def full_update(key_block):
                over_quarters(edge_ref, row, key_block, query_block, part_update)

            over_keys(full_update, full_update)

        total = acc_ref[HEAD_DIM : HEAD_DIM + 1, :]
        mixed = acc_ref[:HEAD_DIM, :] / total
        mixed = jnp.concatenate([mixed[:, :BLK], mixed[:, BLK:]], axis=0).T
        mixed_ref[query_block] = mixed.astype(jnp.bfloat16)
        log_total = stat_ref[0:1, :] + jnp.log(total)
        at = pl.multiple_of(query_block * BLK, BLK)
        lse_ref[0:1, pl.ds(at, BLK)] = log_total[:, :BLK]
        lse_ref[1:2, pl.ds(at, BLK)] = log_total[:, BLK:]
        return carried

    lax.fori_loop(0, blocks, one_query, 0)


def attend(row, listed, edges, qkv, segc, segr):
    blocks, blk, width = qkv.shape
    length = blocks * blk
    pair = 2 * HEAD_DIM
    return pl.pallas_call(
        functools.partial(attend_kernel, row=row),
        grid_spec=pltpu.PrefetchScalarGridSpec(
            num_scalar_prefetch=2,
            grid=(1,),
            in_specs=[
                whole(qkv.shape),
                pl.BlockSpec((1, length, 1), lambda i, *_: (row, 0, 0)),
                pl.BlockSpec((1, 1, length), lambda i, *_: (row, 0, 0)),
            ],
            out_specs=[whole((blocks, blk, pair)), whole((2, length))],
            scratch_shapes=[
                pltpu.VMEM((pair + 32, length), jnp.bfloat16),
                pltpu.VMEM((2 * blk, pair), jnp.bfloat16),
                pltpu.VMEM((HEAD_DIM + 16, 2 * blk), jnp.float32),
                pltpu.VMEM((1, 2 * blk), jnp.float32),
            ],
        ),
        out_shape=[
            jax.ShapeDtypeStruct((blocks, blk, pair), jnp.bfloat16),
            jax.ShapeDtypeStruct((2, length), jnp.float32),
        ],
        compiler_params=params(),
        cost_estimate=cost(20e9, 6e6, 20e6),
        name="attend",
    )(listed, edges, qkv, segc, segr)


def attend_back_kernel(
    listed_ref, edge_ref, qkv_ref, grad_ref, mixed_ref, lse_ref, segc_ref, segr_ref, out_ref,
    kt_ref, qz_ref, gz_ref, inner_ref, dq_ref, dk_ref, dv_ref, *, row,
):
    blocks = qkv_ref.shape[0]
    scale = HEAD_DIM ** (-0.5)

    def prepare(block, carried):
        at = pl.multiple_of(block * BLK, BLK)
        kt_ref[:, pl.ds(at, BLK)] = transposed(qkv_ref[block, :, 128:256])
        query = qkv_ref[block, :, :128].astype(jnp.float32) * scale
        qz_ref[block] = split_heads(query.astype(jnp.bfloat16))
        grad = grad_ref[block]
        gz_ref[block] = split_heads(grad)
        product = (grad.astype(jnp.float32) * mixed_ref[block].astype(jnp.float32)).T
        for head in range(2):
            part = product[head * HEAD_DIM : (head + 1) * HEAD_DIM, :]
            inner_ref[head : head + 1, pl.ds(at, BLK)] = jnp.sum(part, axis=0, keepdims=True)
        return carried

    lax.fori_loop(0, blocks, prepare, 0)
    dq_ref[...] = jnp.zeros(dq_ref.shape, jnp.float32)

    def one_key(key_block, carried):
        dk_ref[...] = jnp.zeros(dk_ref.shape, jnp.float32)
        dv_ref[...] = jnp.zeros(dv_ref.shape, jnp.float32)
        key_at = pl.multiple_of(key_block * BLK, BLK)

        def accumulate(head, key_at, query_at, keys, values, query, grad, mask):
            keys_here = pl.ds(pl.multiple_of(key_at % BLK, HALF), keys.shape[0])
            queries_here = pl.ds(query_at, query.shape[0])
            scores = dot_nt(keys, query)
            probs = jnp.exp(scores - lse_ref[head : head + 1, queries_here])
            if mask is not None:
                probs = jnp.where(mask, probs, 0.0)
            grad_probs = dot_nt(values, grad)
            grad_scores = probs * (grad_probs - inner_ref[head : head + 1, queries_here])
            probs = probs.astype(jnp.bfloat16)
            grad_scores = grad_scores.astype(jnp.bfloat16)
            dv_ref[keys_here, :] += dot_nn(probs, grad)
            dk_ref[keys_here, :] += dot_nn(grad_scores, query)
            lanes = slice(head * HEAD_DIM, (head + 1) * HEAD_DIM)
            dq_ref[lanes, queries_here] += dot_nn(
                kt_ref[lanes, pl.ds(key_at, keys.shape[0])], grad_scores
            )

        def full_update(query_block, mask):
            query_at = pl.multiple_of(query_block * BLK, BLK)
            keys = qkv_ref[key_block, :, 128:256]
            values = qkv_ref[key_block, :, 256:384]
            for head in range(2):
                part = slice(head * BLK, (head + 1) * BLK)
                query, grad = qz_ref[query_block, part, :], gz_ref[query_block, part, :]
                accumulate(head, key_at, query_at, keys, values, query, grad, mask)

        def one_query(query_block, carried):
            listed = listed_ref[row, query_block * blocks + key_block] != 0
            full = is_full(edge_ref, row, key_block, query_block)

            @pl.when(listed & full)
            def _():
                full_update(query_block, None)

            @pl.when(listed & jnp.logical_not(full))
            def _():
                full_update(query_block, tile_mask(segc_ref, segr_ref, key_block * BLK, query_block * BLK, BLK))

            return carried

        lax.fori_loop(key_block, blocks, one_query, 0)
        grad_query = dq_ref[:, pl.ds(key_at, BLK)].T * scale
        out_ref[key_block] = pair_together(grad_query, dk_ref[...], dv_ref[...]).astype(jnp.bfloat16)
        return carried

    lax.fori_loop(0, blocks, one_key, 0)


def attend_back(row, listed, edges, qkv, grad, mixed, lse, segc, segr):
    blocks, blk, width = qkv.shape
    length = blocks * blk
    pair = 2 * HEAD_DIM
    return pl.pallas_call(
        functools.partial(attend_back_kernel, row=row),
        grid_spec=pltpu.PrefetchScalarGridSpec(
            num_scalar_prefetch=2,
            grid=(1,),
            in_specs=[
                whole(qkv.shape),
                whole(grad.shape),
                whole(mixed.shape),
                whole(lse.shape),
                pl.BlockSpec((1, length, 1), lambda i, *_: (row, 0, 0)),
                pl.BlockSpec((1, 1, length), lambda i, *_: (row, 0, 0)),
            ],
            out_specs=whole(qkv.shape),
            scratch_shapes=[
                pltpu.VMEM((pair, length), jnp.bfloat16),
                pltpu.VMEM((blocks, 2 * blk, pair), jnp.bfloat16),
                pltpu.VMEM((blocks, 2 * blk, pair), jnp.bfloat16),
                pltpu.VMEM((2, length), jnp.float32),
                pltpu.VMEM((pair, length), jnp.float32),
                pltpu.VMEM((blk, pair), jnp.float32),
                pltpu.VMEM((blk, pair), jnp.float32),
            ],
        ),
        out_shape=jax.ShapeDtypeStruct(qkv.shape, jnp.bfloat16),
        compiler_params=params(),
        cost_estimate=cost(50e9, 10e6, 20e6),
        name="attend_back",
    )(listed, edges, qkv, grad, mixed, lse, segc, segr)


def joined(ref, half, halves):
    return jnp.concatenate([ref[i * halves + half] for i in range(ref.shape[0] // halves)], axis=1)


def outward_kernel(mixed_ref, tok_ref, w_ref, scales_ref, hidden_ref, normed_ref, *, row):
    halves = w_ref.shape[1]
    hidden = tok_ref[0].astype(jnp.float32)
    width = hidden.shape[1]
    for half in range(halves):
        hidden += dot_nt(joined(mixed_ref, half, halves), w_ref[:, half].reshape(width, -1))
    hidden_ref[...] = hidden
    hat, _ = normalize(hidden)
    normed_ref[...] = (hat * scales_ref[row : row + 1, width:]).astype(jnp.bfloat16)


def outward(row, mixed, tokens, w_all, scales, columns):
    rows, length, width = tokens.shape
    groups, _, pair = mixed.shape
    chunks, halves, high, _ = w_all.shape
    tile = 256
    one = pl.BlockSpec((tile, width), lambda i: (i, 0))
    return pl.pallas_call(
        functools.partial(outward_kernel, row=row),
        grid=(length // tile,),
        in_specs=[
            pl.BlockSpec((groups, tile, pair), lambda i: (0, i, 0)),
            pl.BlockSpec((1, tile, width), lambda i: (row, i, 0)),
            whole((chunks, halves, high, columns)),
            whole(scales.shape),
        ],
        out_specs=[one, one],
        out_shape=[
            jax.ShapeDtypeStruct((length, width), jnp.float32),
            jax.ShapeDtypeStruct((length, width), jnp.bfloat16),
        ],
        compiler_params=params(),
        cost_estimate=cost(2 * length * width * width, 12 * length * width),
        name="outward",
    )(mixed, tokens, w_all, scales)


def mlp_kernel(
    place_ref, nm0_ref, nm1_ref, cot_ref, hidden0_ref, hidden1_ref, scales_ref, up_ref, down_ref,
    keep_ref, send_ref, layer_ref, grad_hidden_ref, grad_attn_ref, gscale_ref,
    nmt_ref, cott_ref, out_ref, gn_ref, act_ref, gpre_ref,
):
    tile = pl.program_id(0)
    phase = pl.program_id(1)
    length, width = nm0_ref.shape
    count = 2 * length
    root = 0.7978845608028654
    cube = 0.044715

    @pl.when((tile == 0) & (phase == 0))
    def _():
        chunks = up_ref.shape[0]
        turned_apart(nmt_ref.at[:, :length], nm0_ref[...], place_ref[2], chunks)
        turned_apart(nmt_ref.at[:, length:], nm1_ref[...], place_ref[2], chunks)
        turned_apart(cott_ref, cot_ref[...], place_ref[2], chunks)
        out_ref[...] = jnp.zeros(out_ref.shape, jnp.float32)
        gn_ref[...] = jnp.zeros(gn_ref.shape, jnp.float32)

    @pl.when(phase == 0)
    def _():
        up = up_ref[:, 0].reshape(width, -1)
        down = down_ref[:, 0].reshape(width, -1)
        for row, nm_ref in enumerate((nm0_ref, nm1_ref)):
            part = slice(row * length, (row + 1) * length)
            pre = dot_nn(nm_ref[...], up)
            grad_act = dot_nn(cot_ref[part, :], down)
            square = pre * pre
            bent = jnp.tanh(root * (pre + cube * pre * square))
            half = 0.5 * (1.0 + bent)
            act_ref[part, :] = (pre * half).astype(jnp.bfloat16)
            slope = half + (0.5 * root) * pre * (1.0 - bent * bent) * (1.0 + (3.0 * cube) * square)
            gpre_ref[part, :] = (grad_act * slope).astype(jnp.bfloat16)
        put_apart(keep_ref, send_ref, dot_nn(nmt_ref[...], gpre_ref[...]).astype(jnp.bfloat16))

    @pl.when(phase == 1)
    def _():
        up = up_ref[:, 0].reshape(width, -1)
        down = down_ref[:, 0].reshape(width, -1)
        out_ref[...] += dot_nt(act_ref[...], down)
        gn_ref[...] += dot_nt(gpre_ref[...], up)
        put_apart(keep_ref, send_ref, dot_nn(cott_ref[...], act_ref[...]).astype(jnp.bfloat16))

    @pl.when((tile == pl.num_programs(0) - 1) & (phase == 1))
    def _():
        chunk = 256
        for row, hidden_ref in enumerate((hidden0_ref, hidden1_ref)):
            scale = scales_ref[row : row + 1, width:]
            total = jnp.zeros((1, width), jnp.float32)
            for at in range(0, length, chunk):
                part = slice(row * length + at, row * length + at + chunk)
                hidden = hidden_ref[at : at + chunk, :]
                layer_ref[part, :] = (hidden + out_ref[part, :]).astype(jnp.bfloat16)
                hat, inverse = normalize(hidden)
                grad = gn_ref[part, :]
                total += jnp.sum(grad * hat, axis=0, keepdims=True)
                back = cot_ref[part, :].astype(jnp.float32) + normalize_back(grad * scale, hat, inverse)
                grad_hidden_ref[part, :] = back
                grad_attn_ref[part, :] = back.astype(jnp.bfloat16)
            gscale_ref[row : row + 1, :] = total


def mlp(place, normed, cotangent, hidden, scales, w_all, room):
    rows, length, width = cotangent.shape
    count = rows * length
    chunks, halves, high, columns = w_all.shape
    tile = 512
    hidden_cols = (columns - room) // 2
    per_half = hidden_cols // tile
    first = room // tile
    flat = (count, width)
    one = (length, width)
    block = (chunks, 1, high, tile)
    apart = pl.BlockSpec(
        (2, 1, chunks // 4, high, tile),
        lambda f, s, at: (0, f // per_half, 0, 0, first + s * per_half + f % per_half),
    )
    grads = jax.ShapeDtypeStruct((2, halves, chunks // 4, high, columns), jnp.bfloat16)
    return pl.pallas_call(
        mlp_kernel,
        grid_spec=pltpu.PrefetchScalarGridSpec(
            num_scalar_prefetch=1,
            grid=(halves * per_half, 2),
            in_specs=[
                whole(one),
                whole(one),
                whole(flat),
                whole(one),
                whole(one),
                whole(scales.shape),
                pl.BlockSpec(block, lambda f, s, at: (0, f // per_half, 0, first + f % per_half)),
                pl.BlockSpec(block, lambda f, s, at: (0, f // per_half, 0, first + per_half + f % per_half)),
            ],
            out_specs=[
                apart,
                apart,
                whole(flat),
                whole(flat),
                whole(flat),
                whole((rows, width)),
            ],
            scratch_shapes=[
                pltpu.VMEM((width, count), jnp.bfloat16),
                pltpu.VMEM((width, count), jnp.bfloat16),
                pltpu.VMEM(flat, jnp.float32),
                pltpu.VMEM(flat, jnp.float32),
                pltpu.VMEM((count, tile), jnp.bfloat16),
                pltpu.VMEM((count, tile), jnp.bfloat16),
            ],
        ),
        out_shape=[
            grads,
            grads,
            jax.ShapeDtypeStruct(flat, jnp.bfloat16),
            jax.ShapeDtypeStruct(flat, jnp.float32),
            jax.ShapeDtypeStruct(flat, jnp.bfloat16),
            jax.ShapeDtypeStruct((rows, width), jnp.float32),
        ],
        compiler_params=params(60),
        cost_estimate=cost(12 * count * width * halves * hidden_cols, 4 * w_all.size + 16 * count * width),
        name="mlp",
    )(place, *normed, cotangent.reshape(flat), *hidden, scales, w_all, w_all)


def grad_mixed_kernel(grad_ref, w_ref, out_ref):
    halves = w_ref.shape[1]
    per_half = out_ref.shape[0] // halves
    grad = grad_ref[...]
    pair = out_ref.shape[2]
    for half in range(halves):
        out = dot_nn(grad, w_ref[:, half].reshape(grad.shape[1], -1)).astype(jnp.bfloat16)
        for group in range(per_half):
            out_ref[group * halves + half] = out[:, group * pair : (group + 1) * pair]


def grad_mixed_of(row, grad_attn, w_all, mixed_shape, columns):
    groups, length, pair = mixed_shape
    chunks, halves, high, _ = w_all.shape
    width = grad_attn.shape[1]
    tile = 256
    tiles = length // tile
    return pl.pallas_call(
        grad_mixed_kernel,
        grid=(tiles,),
        in_specs=[
            pl.BlockSpec((tile, width), lambda i: (row * tiles + i, 0)),
            whole((chunks, halves, high, columns)),
        ],
        out_specs=pl.BlockSpec((groups, tile, pair), lambda i: (0, i, 0)),
        out_shape=jax.ShapeDtypeStruct(mixed_shape, jnp.bfloat16),
        compiler_params=params(),
        cost_estimate=cost(2 * length * width * width, 8 * length * width),
        name="grad_mixed",
    )(grad_attn, w_all)


def grad_proj_kernel(place_ref, grad_ref, mixed0_ref, mixed1_ref, _k, _s, keep_ref, send_ref, turned_ref):
    half = pl.program_id(0)
    halves = pl.num_programs(0)

    @pl.when(half == 0)
    def _():
        turned_apart(turned_ref, grad_ref[...], place_ref[2], 4 * keep_ref.shape[2])

    groups, length, pair = mixed0_ref.shape
    count = keep_ref.shape[4] // pair
    grad = 0.0
    for row, mixed_ref in enumerate((mixed0_ref, mixed1_ref)):
        mixed = jnp.concatenate([mixed_ref[i * halves + half] for i in range(count)], axis=1)
        grad += dot_nn(turned_ref[:, row * length : (row + 1) * length], mixed)
    put_apart(keep_ref, send_ref, grad.astype(jnp.bfloat16))


def grad_proj_into(place, keep, send, grad_attn, mixed, columns):
    count, width = grad_attn.shape
    given = whole(mixed[0].shape)
    anywhere = pl.BlockSpec(memory_space=pl.ANY)
    out = pl.BlockSpec((2, 1) + keep.shape[2:4] + (columns,), lambda h, at: (0, h, 0, 0, 0))
    return pl.pallas_call(
        grad_proj_kernel,
        grid_spec=pltpu.PrefetchScalarGridSpec(
            num_scalar_prefetch=1,
            grid=(keep.shape[1],),
            in_specs=[whole(grad_attn.shape), given, given, anywhere, anywhere],
            out_specs=[out, out],
            scratch_shapes=[pltpu.VMEM((width, count), jnp.bfloat16)],
        ),
        out_shape=[jax.ShapeDtypeStruct(keep.shape, jnp.bfloat16)] * 2,
        input_output_aliases={4: 0, 5: 1},
        compiler_params=params(),
        cost_estimate=cost(2 * count * width * width, 6 * count * width),
        name="grad_proj",
    )(place, grad_attn, *mixed, keep, send)


def first_norm_kernel(gq_ref, tok_ref, grad_hidden_ref, w_ref, scales_ref, out_ref, gscale_ref, *, row, q_cols):
    step = pl.program_id(0)
    halves = w_ref.shape[1]
    values = tok_ref[0].astype(jnp.float32)
    width = values.shape[1]
    grad = jnp.zeros(values.shape, jnp.float32)
    for half in range(halves):
        weights = w_ref[:, half, :, :q_cols].reshape(width, q_cols)
        grad += dot_nt(joined(gq_ref, half, halves), weights)
    hat, inverse = normalize(values)
    total = jnp.sum(grad * hat, axis=0, keepdims=True)

    @pl.when(step == 0)
    def _():
        gscale_ref[...] = total

    @pl.when(step != 0)
    def _():
        gscale_ref[...] += total

    back = normalize_back(grad * scales_ref[row : row + 1, :width], hat, inverse)
    out_ref[...] = (grad_hidden_ref[...] + back).astype(jnp.bfloat16)


def first_norm_back(row, grad_qkv, tokens, grad_hidden, w_all, scales, q_cols):
    rows, length, width = tokens.shape
    groups, _, pair = grad_qkv.shape
    tile = 256
    tiles = length // tile
    return pl.pallas_call(
        functools.partial(first_norm_kernel, row=row, q_cols=q_cols),
        grid=(tiles,),
        in_specs=[
            pl.BlockSpec((groups, tile, pair), lambda i: (0, i, 0)),
            pl.BlockSpec((1, tile, width), lambda i: (row, i, 0)),
            pl.BlockSpec((tile, width), lambda i: (row * tiles + i, 0)),
            whole(w_all.shape),
            whole(scales.shape),
        ],
        out_specs=[pl.BlockSpec((tile, width), lambda i: (i, 0)), whole((1, width))],
        out_shape=[
            jax.ShapeDtypeStruct((length, width), jnp.bfloat16),
            jax.ShapeDtypeStruct((1, width), jnp.float32),
        ],
        compiler_params=params(),
        cost_estimate=cost(2 * length * width * groups * pair, 2 * w_all.size + 20 * length * width),
        name="first_norm_back",
    )(grad_qkv, tokens, grad_hidden, w_all, scales)


def grad_qkv_kernel(place_ref, normed_ref, gq_ref, *refs):
    step = pl.program_id(0)
    base_refs, out_refs, total_ref = refs[:-2], refs[-2:-1], refs[-1]
    if len(refs) > 3:
        base_refs, out_refs, (total_ref, turned_ref) = refs[:1], refs[1:-2], refs[-2:]

    @pl.when(step == 0)
    def _():
        total_ref[...] = base_refs[0][...] if base_refs else jnp.zeros(total_ref.shape, jnp.float32)

    total_ref[...] += dot_nn(transposed(gq_ref[0]), normed_ref[0])

    @pl.when(step == pl.num_programs(0) - 1)
    def _():
        if base_refs:
            turned_ref[...] = total_ref[...].T
            tall = out_refs[0].shape[0]
            for apart, out_ref in enumerate(out_refs):
                at = pl.multiple_of((apart ^ place_ref[1]) * tall, tall)
                out_ref[...] = turned_ref[pl.ds(at, tall), :].astype(jnp.bfloat16)
        else:
            out_refs[0][...] = total_ref[...]


def grad_qkv_of(place, normed, grad_qkv, parts, base=()):
    blocks, length, width = normed.shape
    pair = grad_qkv.shape[2]
    turned = (pair, width)
    if base:
        shapes = [jax.ShapeDtypeStruct((width // parts, pair), jnp.bfloat16)] * parts
    else:
        shapes = [jax.ShapeDtypeStruct(turned, jnp.float32)]
    return pl.pallas_call(
        grad_qkv_kernel,
        grid_spec=pltpu.PrefetchScalarGridSpec(
            num_scalar_prefetch=1,
            grid=(blocks,),
            in_specs=[
                pl.BlockSpec((1, length, width), lambda i, place: (i, 0, 0)),
                pl.BlockSpec((1, length, pair), lambda i, place: (i, 0, 0)),
            ]
            + [whole(turned)] * len(base),
            out_specs=[whole(one.shape) for one in shapes],
            scratch_shapes=[pltpu.VMEM(turned, jnp.float32)]
            + [pltpu.VMEM((width, pair), jnp.float32)] * len(base),
        ),
        out_shape=shapes,
        compiler_params=params(),
        cost_estimate=cost(2 * blocks * length * width * pair, 3 * blocks * length * width),
        name="grad_qkv",
    )(place, normed, grad_qkv, *base)


CTX = ("x", "core")
GROUP = ("x", "core", "tp")
EVERY = ("fsdp", "x", "core", "tp")


def size_of(axis):
    names = (axis,) if isinstance(axis, str) else axis
    return functools.reduce(lambda size, name: size * lax.axis_size(name), names, 1)


def across(values, axis, apart):
    size = size_of(axis)
    return lax.ppermute(values, axis, [(i, i ^ apart) for i in range(size)])


def summed(parts):
    return sum(part.astype(jnp.float32) for part in parts)


def exchange(values, axes):
    return lax.all_to_all(values, axes, 0, 0, tiled=True)


HOPS = {1: "tp", 2: "core", 4: "x"}


def widened(found, apart):
    return {**found, **{held ^ apart: across(one, HOPS[apart], 1) for held, one in found.items()}}


def listed_table(block_pairs, pair_counts, row_blocks, ctx_size):
    rows, _, slots, _ = block_pairs.shape
    packed = jnp.concatenate([block_pairs.reshape(rows, 1, slots * 2), pair_counts[:, :, None]], axis=2)
    packed = jnp.concatenate(
        [packed] + [across(packed, CTX, apart) for apart in range(1, ctx_size)], axis=1
    )
    pairs = packed[:, :, : slots * 2].reshape(rows, ctx_size, slots, 2)
    live = jnp.arange(slots, dtype=jnp.int32)[None, None, :] < packed[:, :, slots * 2 :]
    owner = lax.axis_index(CTX) ^ jnp.arange(ctx_size, dtype=jnp.int32)[None, :, None]
    base = owner * (row_blocks // ctx_size)
    code = jnp.where(live, (base + pairs[..., 0]) * row_blocks + pairs[..., 1], -1)
    code = code.reshape(rows, ctx_size * slots)
    cells = jnp.arange(row_blocks * row_blocks, dtype=jnp.int32)
    return jnp.any(code[:, :, None] == cells[None, None, :], axis=1).astype(jnp.int32)


def spread_body(
    tokens, time_embed, segment_ids, block_pairs, pair_counts,
    w_time, w_qkv, w_out, w_up, w_down, cotangent,
):
    rows, length, width = tokens.shape
    chunks = width // w_qkv.shape[0]
    halves = lax.axis_size("tp")
    high = w_qkv.shape[0]
    q_cols, o_cols, f_cols = w_qkv.shape[1], w_out.shape[1], w_up.shape[1]
    k_rows = w_time.shape[0]
    mine = lax.axis_index("tp")
    ctx, fsdp = lax.axis_index(CTX), lax.axis_index("fsdp")
    n_ctx, n_fsdp = size_of(CTX), lax.axis_size("fsdp")
    bf16, f32 = jnp.bfloat16, jnp.float32
    chunk = fsdp * n_ctx + ctx
    place = jnp.stack([ctx * halves + mine, fsdp, lax.axis_index("core")])

    found = [{0: tokens[row]} for row in range(rows)]
    orders = [(4, 1, 2) if row % 2 == 0 else (1, 4, 2) for row in range(rows)]
    found = [widened(one, order[0]) for one, order in zip(found, orders)]
    w_qkv = w_qkv.astype(bf16)
    columns = exchange(w_qkv.reshape(high, n_ctx, -1).transpose(1, 0, 2), CTX)
    embeds = [time_embed] + [across(time_embed, "fsdp", apart) for apart in range(1, n_fsdp)]
    w_time = w_time.astype(bf16)
    times = [w_time] + [across(w_time, CTX, apart) for apart in range(1, n_ctx)]
    row_blocks = segment_ids.shape[1] // BLK
    listed = listed_table(block_pairs, pair_counts, row_blocks, n_ctx)
    edges = jnp.concatenate([segment_ids[:, ::HALF], segment_ids[:, HALF - 1 :: HALF]], axis=1)
    segc = segment_ids[:, :, None]
    segr = segment_ids[:, None, :]
    second = jnp.concatenate([w_out, w_up, w_down], axis=1).astype(bf16)
    found, columns, embeds, times, second = lax.optimization_barrier((found, columns, embeds, times, second))
    second = lax.all_gather(second, EVERY, axis=0, tiled=True)
    found = [widened(one, order[1]) for one, order in zip(found, orders)]
    columns = columns.reshape(n_ctx * high, -1)
    columns = [columns] + [across(columns, "fsdp", apart) for apart in range(1, n_fsdp)]
    rows_of = [(chunk ^ apart) * k_rows for apart in range(n_ctx)]
    some = [
        jnp.concatenate([lax.dynamic_slice_in_dim(one, at, k_rows, 1) for at in rows_of], axis=1)
        for one in embeds
    ]
    mine_of = [one[:, :k_rows] for one in some]
    given = jnp.dot(jnp.concatenate(some, axis=0), jnp.concatenate(times, axis=0).astype(f32), precision=highest)
    given = given.reshape(n_fsdp, rows, -1)
    scales = 1.0 + given[0] + sum(across(given[apart], "fsdp", apart) for apart in range(1, n_fsdp))
    found, scales, columns, listed, edges, segc, segr = lax.optimization_barrier(
        (found, scales, columns, listed, edges, segc, segr)
    )
    found = [widened(one, order[2]) for one, order in zip(found, orders)]
    others = [[one[apart] for apart in range(1, len(one))] for one in found]

    qkv, normed = [], []
    for row in range(rows):
        out, one = project(row, place, scales, columns, tokens, others[row])
        qkv.append(out)
        normed.append(one)
    mixed_own, lse, mixed = [], [], []
    for row in range(rows):
        out, one = attend(row, listed, edges, qkv[row], segc, segr)
        mixed_own.append(out)
        lse.append(one)
        mixed.append(exchange(out, GROUP))
    mixed[0], mixed_own = lax.optimization_barrier((mixed[0], mixed_own))
    second = second.reshape(chunks, halves, high, -1)
    hidden, normed_mlp = [], []
    for row in range(rows):
        if row:
            mixed[row], hidden[row - 1] = lax.optimization_barrier((mixed[row], hidden[row - 1]))
        out, one = outward(row, mixed[row], tokens, second, scales, o_cols)
        hidden.append(out)
        normed_mlp.append(one)
    w_qkv, normed_mlp = lax.optimization_barrier((w_qkv, normed_mlp))
    third = lax.all_gather(w_qkv, EVERY, axis=0, tiled=True).reshape(chunks, halves, high, -1)
    keep, send, layer_out, grad_hidden, grad_attn, gscale_mlp = mlp(
        place, normed_mlp, cotangent, hidden, scales, second, o_cols
    )
    keep, send = grad_proj_into(place, keep, send, grad_attn, mixed, o_cols)
    grad_attn, keep, send, third = lax.optimization_barrier((grad_attn, keep, send, third))
    sent = across(send, "core", 1)
    grad_mixed = {}
    for row in reversed(range(rows)):
        out = grad_mixed_of(row, grad_attn, second, mixed[row].shape, o_cols)
        grad_mixed[row] = exchange(out, GROUP)
    last = rows - 1
    grads = summed([keep, sent]).astype(bf16)
    grad_mixed[last], grads = lax.optimization_barrier((grad_mixed[last], grads))
    grads = lax.psum_scatter(
        grads.reshape(-1, grads.shape[4]), ("x", "tp"), scatter_dimension=0, tiled=True
    )
    own, grad_qkv = {}, {}
    for row in reversed(range(rows)):
        if row < last:
            grad_mixed[row], own[row + 1] = lax.optimization_barrier((grad_mixed[row], own[row + 1]))
        own[row] = attend_back(row, listed, edges, qkv[row], grad_mixed[row], mixed_own[row], lse[row], segc, segr)
        if row < last:
            grad_qkv[row + 1] = exchange(own[row + 1], GROUP)
    grad_qkv[0] = exchange(own[0], GROUP)
    held, _ = lax.optimization_barrier((own[last], own[0]))
    base = grad_qkv_of(place, normed[last], held, n_fsdp)
    cut = list(grad_qkv_of(place, normed[0], own[0], n_fsdp, base))
    grad_tokens, gscale_attn = {}, {}
    held, _ = lax.optimization_barrier((grad_qkv[last], cut[0]))
    grad_tokens[last], gscale_attn[last] = first_norm_back(
        last, held, tokens, grad_hidden, third, scales, q_cols
    )
    cut[0], gscale_attn[last] = lax.optimization_barrier((cut[0], gscale_attn[last]))
    total = summed([cut[0]] + [across(cut[apart], "fsdp", apart) for apart in range(1, n_fsdp)])
    grads, gscale_attn[last], total = lax.optimization_barrier(
        (grads, gscale_attn[last], total.astype(bf16))
    )
    grads = lax.psum_scatter(grads, "fsdp", scatter_dimension=0, tiled=True)
    total = exchange(total.reshape(n_ctx, high, -1), CTX)
    grad_tokens[0], gscale_attn[0] = first_norm_back(
        0, grad_qkv[0], tokens, grad_hidden, third, scales, q_cols
    )
    devices = n_fsdp * n_ctx * halves
    both = jnp.concatenate([gscale_mlp, gscale_attn[last], gscale_attn[0]], axis=0)
    both = exchange(jnp.broadcast_to(both.astype(bf16)[None], (devices,) + both.shape), EVERY).astype(f32)
    both, total = lax.optimization_barrier((both, total))
    grad_w_qkv = total.transpose(1, 0, 2).reshape(high, q_cols).astype(f32)
    both = jnp.sum(both.reshape(n_fsdp, n_ctx * halves, 2 * rows, width), axis=1)
    both = jnp.concatenate([both[:, 3], both[:, 0], both[:, 2], both[:, 1]], axis=1)
    both = both.reshape(n_fsdp * rows, 2 * width)
    mine_of = [lax.dynamic_index_in_dim(jnp.stack(mine_of), i ^ fsdp, 0, False) for i in range(n_fsdp)]
    grad_time = jnp.dot(jnp.concatenate(mine_of, axis=0).T, both, precision=highest)
    return (
        layer_out.reshape(tokens.shape),
        jnp.stack([grad_tokens[row] for row in range(rows)]),
        grad_time,
        grad_w_qkv,
        grads[:, :o_cols].astype(f32),
        grads[:, o_cols : o_cols + f_cols].astype(f32),
        grads[:, o_cols + f_cols :].astype(f32),
    )


def specs_of(ctx):
    flat = ctx if isinstance(ctx, tuple) else (ctx,)
    tokens, weights = P("fsdp", (*flat, "tp"), None), P(("fsdp", *flat), "tp")
    placed = (tokens, P("fsdp", None), P("fsdp", None), P("fsdp", ctx, None, None), P("fsdp", ctx))
    placed += (P(("fsdp", *flat), None), weights, weights, weights, weights, tokens)
    return placed, (tokens, tokens, P(("fsdp", *flat), None), weights, weights, weights, weights)


def solution(mesh):
    sizes = tuple(mesh.shape[name] for name in ("fsdp", "ctx", "tp"))

    def run(*args):
        tokens, w_qkv, w_out, w_up = args[0], args[6], args[7], args[8]
        group = sizes[1] * sizes[2]
        fits = (
            sizes == (4, 4, 2)
            and tokens.shape[:2] == (8, group * BLK)
            and w_qkv.shape[1] == group * 6 * HEAD_DIM
            and w_out.shape[1] % (512 * sizes[2]) == 0
            and w_up.shape[1] % (512 * sizes[2]) == 0
        )
        if fits:
            devices = mesh.devices.reshape(sizes[0], 2, 2, sizes[2])
            parted = Mesh(devices, ("fsdp", "x", "core", "tp"))
            placed, given = specs_of(CTX)
            return jax.shard_map(
                spread_body, mesh=parted, in_specs=placed, out_specs=given, check_vma=False
            )(*args)
        placed, given = specs_of("ctx")
        return jax.shard_map(body, mesh=mesh, in_specs=placed, out_specs=given, check_vma=False)(*args)

    return run
```

```python
import functools

import jax
import jax.numpy as jnp
from jax import lax
from jax.experimental import pallas as pl
from jax.experimental.pallas import tpu as pltpu
from jax.sharding import Mesh
from jax.sharding import PartitionSpec as P

HEAD_DIM = 64
BLK = 512


epsilon = 1e-05
highest = lax.Precision.HIGHEST
masked_out = -1e30


def normalize(values):
    mean_value = jnp.mean(values, axis=-1, keepdims=True)
    centred = values - mean_value
    variance = jnp.mean(centred * centred, axis=-1, keepdims=True)
    inverse = lax.rsqrt(variance + epsilon)
    return (centred * inverse, inverse)


def normalize_back(grad_hat, normal_hat, inverse):
    first_mean = jnp.mean(grad_hat, axis=-1, keepdims=True)
    second_mean = jnp.mean(grad_hat * normal_hat, axis=-1, keepdims=True)
    return inverse * (grad_hat - first_mean - normal_hat * second_mean)


def smooth_gate(values):
    return jax.nn.gelu(values, approximate=True)


def block_scores(pair_entry, query_rows, key_rows, seg_row, offset):
    query_start = pair_entry[0] * BLK
    key_start = pair_entry[1] * BLK
    query_block = lax.dynamic_slice_in_dim(query_rows, query_start, BLK, 0)
    key_block = lax.dynamic_slice_in_dim(key_rows, key_start, BLK, 0)
    seg_query = lax.dynamic_slice_in_dim(seg_row, offset + query_start, BLK, 0)
    seg_keys = lax.dynamic_slice_in_dim(seg_row, key_start, BLK, 0)
    steps_in = jnp.arange(BLK, dtype=jnp.int32)
    allowed = (seg_query[:, None] == seg_keys[None, :]) & (
        key_start + steps_in[None, :] <= offset + query_start + steps_in[:, None]
    )
    scores = jnp.einsum(
        "qhe,khe->hqk", query_block, key_block, preferred_element_type=jnp.float32
    ) * HEAD_DIM ** (-0.5)
    return (query_block, key_block, query_start, key_start, allowed, scores)


def attend_forward(query_rows, key_rows, value_rows, seg_row, pair_rows, pair_total, offset):
    length_here, head_count, _ = query_rows.shape

    def statistic_step(pair_index, carried):
        running_max, running_sum = carried
        _, _, query_start, _, allowed, scores = block_scores(
            pair_rows[pair_index], query_rows, key_rows, seg_row, offset
        )
        scores = jnp.where(allowed[None], scores, masked_out)
        old_max = lax.dynamic_slice_in_dim(running_max, query_start, BLK, 1)
        old_sum = lax.dynamic_slice_in_dim(running_sum, query_start, BLK, 1)
        new_max = jnp.maximum(old_max, jnp.max(scores, axis=-1))
        weights = jnp.where(allowed[None], jnp.exp(scores - new_max[:, :, None]), 0.0)
        new_sum = old_sum * jnp.exp(old_max - new_max) + jnp.sum(weights, axis=-1)
        return (
            lax.dynamic_update_slice_in_dim(running_max, new_max, query_start, 1),
            lax.dynamic_update_slice_in_dim(running_sum, new_sum, query_start, 1),
        )

    start_max = jnp.full((head_count, length_here), masked_out, jnp.float32)
    start_sum = jnp.zeros((head_count, length_here), jnp.float32)
    running_max, running_sum = lax.fori_loop(0, pair_total, statistic_step, (start_max, start_sum))
    log_total = running_max + jnp.log(running_sum)

    def output_step(pair_index, accumulated):
        _, _, query_start, key_start, allowed, scores = block_scores(
            pair_rows[pair_index], query_rows, key_rows, seg_row, offset
        )
        block_log = lax.dynamic_slice_in_dim(log_total, query_start, BLK, 1)
        probabilities = jnp.where(
            allowed[None], jnp.exp(scores - block_log[:, :, None]), 0.0
        ).astype(jnp.bfloat16)
        value_block = lax.dynamic_slice_in_dim(value_rows, key_start, BLK, 0)
        addition = jnp.einsum(
            "hqk,khe->qhe", probabilities, value_block, preferred_element_type=jnp.float32
        )
        previous = lax.dynamic_slice_in_dim(accumulated, query_start, BLK, 0)
        return lax.dynamic_update_slice_in_dim(accumulated, previous + addition, query_start, 0)

    mixed_rows = lax.fori_loop(0, pair_total, output_step, jnp.zeros(query_rows.shape, jnp.float32))
    return (mixed_rows, log_total)


def attend_backward(
    query_rows,
    key_rows,
    value_rows,
    seg_row,
    pair_rows,
    pair_total,
    offset,
    log_total,
    grad_mixed,
    inner_sums,
):
    scale_factor = HEAD_DIM ** (-0.5)

    def add_block(whole, start_at, addition):
        previous = lax.dynamic_slice_in_dim(whole, start_at, BLK, 0)
        return lax.dynamic_update_slice_in_dim(whole, previous + addition, start_at, 0)

    def gradient_step(pair_index, carried):
        grad_query, grad_keys, grad_values = carried
        query_block, key_block, query_start, key_start, allowed, scores = block_scores(
            pair_rows[pair_index], query_rows, key_rows, seg_row, offset
        )
        block_log = lax.dynamic_slice_in_dim(log_total, query_start, BLK, 1)
        probabilities = jnp.where(allowed[None], jnp.exp(scores - block_log[:, :, None]), 0.0)
        grad_block = lax.dynamic_slice_in_dim(grad_mixed, query_start, BLK, 0)
        value_block = lax.dynamic_slice_in_dim(value_rows, key_start, BLK, 0)
        grad_probs = jnp.einsum(
            "qhe,khe->hqk", grad_block, value_block, preferred_element_type=jnp.float32
        )
        inner_block = lax.dynamic_slice_in_dim(inner_sums, query_start, BLK, 1)
        grad_scores = (probabilities * (grad_probs - inner_block[:, :, None])).astype(jnp.bfloat16)
        query_add = (
            jnp.einsum("hqk,khe->qhe", grad_scores, key_block, preferred_element_type=jnp.float32)
            * scale_factor
        )
        key_add = (
            jnp.einsum("hqk,qhe->khe", grad_scores, query_block, preferred_element_type=jnp.float32)
            * scale_factor
        )
        value_add = jnp.einsum(
            "hqk,qhe->khe",
            probabilities.astype(jnp.bfloat16),
            grad_block,
            preferred_element_type=jnp.float32,
        )
        return (
            add_block(grad_query, query_start, query_add),
            add_block(grad_keys, key_start, key_add),
            add_block(grad_values, key_start, value_add),
        )

    start_state = (
        jnp.zeros(query_rows.shape, jnp.float32),
        jnp.zeros(key_rows.shape, jnp.float32),
        jnp.zeros(value_rows.shape, jnp.float32),
    )
    return lax.fori_loop(0, pair_total, gradient_step, start_state)


def body(
    tokens,
    time_embed,
    segment_ids,
    block_pairs,
    pair_counts,
    w_time,
    w_qkv,
    w_out,
    w_up,
    w_down,
    cotangent,
):
    row_count, local_len, model_width = tokens.shape
    time_all, qkv_all, out_all, up_all, down_all = (
        lax.all_gather(w_time.astype(jnp.bfloat16), ("fsdp", "ctx"), axis=0, tiled=True),
        lax.all_gather(w_qkv.astype(jnp.bfloat16), ("fsdp", "ctx"), axis=0, tiled=True),
        lax.all_gather(w_out.astype(jnp.bfloat16), ("fsdp", "ctx"), axis=0, tiled=True),
        lax.all_gather(w_up.astype(jnp.bfloat16), ("fsdp", "ctx"), axis=0, tiled=True),
        lax.all_gather(w_down.astype(jnp.bfloat16), ("fsdp", "ctx"), axis=0, tiled=True),
    )
    scales = 1.0 + jnp.dot(time_embed, time_all.astype(jnp.float32), precision=highest)
    scale_attn = scales[:, None, :model_width]
    scale_mlp = scales[:, None, model_width:]
    x_input = tokens.astype(jnp.float32)
    hat_attn, inverse_attn = normalize(x_input)
    normed = (hat_attn * scale_attn).astype(jnp.bfloat16)
    normed_all = lax.all_gather(normed, "tp", axis=1, tiled=True)
    ctx_len = normed_all.shape[1]
    head_count = qkv_all.shape[1] // (3 * HEAD_DIM)
    projected = jnp.einsum("rtd,dc->rtc", normed_all, qkv_all, preferred_element_type=jnp.float32)
    projected = projected.astype(jnp.bfloat16).reshape(row_count, ctx_len, head_count, 3, HEAD_DIM)
    query_all = projected[:, :, :, 0]
    key_part = projected[:, :, :, 1]
    value_part = projected[:, :, :, 2]
    key_all, value_all = (
        lax.all_gather(key_part, "ctx", axis=1, tiled=True),
        lax.all_gather(value_part, "ctx", axis=1, tiled=True),
    )
    offset = lax.axis_index("ctx") * ctx_len
    mixed_list = []
    log_list = []
    for row_index in range(row_count):
        mixed_rows, log_total = attend_forward(
            query_all[row_index],
            key_all[row_index],
            value_all[row_index],
            segment_ids[row_index],
            block_pairs[row_index, 0],
            pair_counts[row_index, 0],
            offset,
        )
        mixed_list.append(mixed_rows)
        log_list.append(log_total)
    mixed_exact = jnp.stack(mixed_list)
    mixed_heads = mixed_exact.astype(jnp.bfloat16).reshape(
        row_count, ctx_len, head_count * HEAD_DIM
    )
    attn_part = jnp.einsum("rtc,dc->rtd", mixed_heads, out_all, preferred_element_type=jnp.float32)
    attn_local = lax.psum_scatter(
        attn_part.astype(jnp.bfloat16), "tp", scatter_dimension=1, tiled=True
    ).astype(jnp.float32)
    hidden = x_input + attn_local
    hat_mlp, inverse_mlp = normalize(hidden)
    normed_mlp = (hat_mlp * scale_mlp).astype(jnp.bfloat16)
    mlp_all = lax.all_gather(normed_mlp, "tp", axis=1, tiled=True)
    pre_act = jnp.einsum("rtd,df->rtf", mlp_all, up_all, preferred_element_type=jnp.float32)
    activated = smooth_gate(pre_act).astype(jnp.bfloat16)
    mlp_part = jnp.einsum("rtf,df->rtd", activated, down_all, preferred_element_type=jnp.float32)
    mlp_local = lax.psum_scatter(
        mlp_part.astype(jnp.bfloat16), "tp", scatter_dimension=1, tiled=True
    ).astype(jnp.float32)
    grad_all = lax.all_gather(cotangent, "tp", axis=1, tiled=True)
    grad_act = jnp.einsum("rtd,df->rtf", grad_all, down_all, preferred_element_type=jnp.float32)
    _, gate_back = jax.vjp(smooth_gate, pre_act)
    grad_pre = gate_back(grad_act)[0].astype(jnp.bfloat16)
    grad_down = jnp.einsum("rtd,rtf->df", grad_all, activated, preferred_element_type=jnp.float32)
    grad_up = jnp.einsum("rtd,rtf->df", mlp_all, grad_pre, preferred_element_type=jnp.float32)
    norm_part = jnp.einsum("rtf,df->rtd", grad_pre, up_all, preferred_element_type=jnp.float32)
    grad_normed_mlp = lax.psum_scatter(
        norm_part.astype(jnp.bfloat16), "tp", scatter_dimension=1, tiled=True
    ).astype(jnp.float32)
    layer_out = (hidden + mlp_local).astype(jnp.bfloat16)
    grad_output = cotangent.astype(jnp.float32)
    grad_scale_mlp = jnp.sum(grad_normed_mlp * hat_mlp, axis=1)
    grad_hidden = grad_output + normalize_back(grad_normed_mlp * scale_mlp, hat_mlp, inverse_mlp)
    grad_attn_all = lax.all_gather(grad_hidden.astype(jnp.bfloat16), "tp", axis=1, tiled=True)
    grad_mixed = jnp.einsum(
        "rtd,dc->rtc", grad_attn_all, out_all, preferred_element_type=jnp.float32
    ).astype(jnp.bfloat16)
    grad_proj = jnp.einsum(
        "rtd,rtc->dc", grad_attn_all, mixed_heads, preferred_element_type=jnp.float32
    )
    grad_mixed = grad_mixed.reshape(row_count, ctx_len, head_count, HEAD_DIM)
    inner_sums = jnp.einsum("rqhe,rqhe->rhq", grad_mixed.astype(jnp.float32), mixed_exact)
    query_grads = []
    key_grads = []
    value_grads = []
    for row_index in range(row_count):
        grad_query, grad_keys, grad_values = attend_backward(
            query_all[row_index],
            key_all[row_index],
            value_all[row_index],
            segment_ids[row_index],
            block_pairs[row_index, 0],
            pair_counts[row_index, 0],
            offset,
            log_list[row_index],
            grad_mixed[row_index],
            inner_sums[row_index],
        )
        query_grads.append(grad_query)
        key_grads.append(grad_keys)
        value_grads.append(grad_values)
    key_local, value_local = (
        lax.psum_scatter(
            jnp.stack(key_grads).astype(jnp.bfloat16), "ctx", scatter_dimension=1, tiled=True
        ).astype(jnp.float32),
        lax.psum_scatter(
            jnp.stack(value_grads).astype(jnp.bfloat16), "ctx", scatter_dimension=1, tiled=True
        ).astype(jnp.float32),
    )
    grad_projected = jnp.stack(
        [
            jnp.stack(query_grads).astype(jnp.bfloat16),
            key_local.astype(jnp.bfloat16),
            value_local.astype(jnp.bfloat16),
        ],
        axis=3,
    )
    grad_projected = grad_projected.reshape(row_count, ctx_len, head_count * 3 * HEAD_DIM)
    grad_qkv = jnp.einsum(
        "rtd,rtc->dc", normed_all, grad_projected, preferred_element_type=jnp.float32
    )
    first_part = jnp.einsum(
        "rtc,dc->rtd", grad_projected, qkv_all, preferred_element_type=jnp.float32
    )
    grad_normed = lax.psum_scatter(
        first_part.astype(jnp.bfloat16), "tp", scatter_dimension=1, tiled=True
    ).astype(jnp.float32)
    grad_scale_attn = jnp.sum(grad_normed * hat_attn, axis=1)
    grad_tokens = grad_hidden + normalize_back(grad_normed * scale_attn, hat_attn, inverse_attn)
    grad_scales = lax.psum(jnp.concatenate([grad_scale_attn, grad_scale_mlp], axis=1), "tp")
    grad_time = jnp.dot(time_embed.T, grad_scales, precision=highest)
    shared = (
        lax.psum_scatter(
            grad_time.astype(jnp.bfloat16), ("fsdp", "ctx"), scatter_dimension=0, tiled=True
        ).astype(jnp.float32),
        lax.psum_scatter(
            grad_qkv.astype(jnp.bfloat16), ("fsdp", "ctx"), scatter_dimension=0, tiled=True
        ).astype(jnp.float32),
        lax.psum_scatter(
            grad_proj.astype(jnp.bfloat16), ("fsdp", "ctx"), scatter_dimension=0, tiled=True
        ).astype(jnp.float32),
        lax.psum_scatter(
            grad_up.astype(jnp.bfloat16), ("fsdp", "ctx"), scatter_dimension=0, tiled=True
        ).astype(jnp.float32),
        lax.psum_scatter(
            grad_down.astype(jnp.bfloat16), ("fsdp", "ctx"), scatter_dimension=0, tiled=True
        ).astype(jnp.float32),
    )
    return (
        layer_out,
        grad_tokens.astype(jnp.bfloat16),
        shared[0],
        shared[1],
        shared[2],
        shared[3],
        shared[4],
    )


def params(limit=58):
    return pltpu.CompilerParams(vmem_limit_bytes=limit * 1024 * 1024)


def whole(shape):
    zeros = (0,) * len(shape)
    return pl.BlockSpec(shape, lambda *_: zeros, pipeline_mode=pl.Buffered(1))


def cost(flops, nbytes, exps=0):
    return pl.CostEstimate(flops=int(flops), bytes_accessed=int(nbytes), transcendentals=int(exps))


def dot_nn(left, right):
    return jnp.dot(left, right, preferred_element_type=jnp.float32)


def dot_nt(left, right):
    return lax.dot_general(left, right, (((1,), (1,)), ((), ())), preferred_element_type=jnp.float32)


def transposed(values):
    return values.T


def turned_apart(into_ref, values, core, chunks):
    turned = transposed(values)
    high = turned.shape[0] // chunks
    for chunk in range(chunks):
        inner = (chunk // 2 % 2) * (chunks // 4) + chunk // 4
        at = ((chunk % 2) ^ core) * (chunks // 2) + inner
        into_ref[pl.ds(pl.multiple_of(at * high, high), high), :] = turned[chunk * high : (chunk + 1) * high]


def put_apart(keep_ref, send_ref, grad):
    middle = grad.shape[0] // 2
    shape = (keep_ref.shape[0],) + keep_ref.shape[2:]
    keep_ref[:, 0] = grad[:middle].reshape(shape)
    send_ref[:, 0] = grad[middle:].reshape(shape)


def low_lanes(shape):
    return lax.broadcasted_iota(jnp.int32, shape, 1) < HEAD_DIM


def pair_apart(stored):
    first, second, third = stored[:, :128], stored[:, 128:256], stored[:, 256:]
    low = low_lanes(first.shape)
    keys = pltpu.roll(jnp.where(low, third, first), HEAD_DIM, 1)
    return jnp.concatenate(
        [jnp.where(low, first, second), keys, jnp.where(low, second, third)], axis=1
    )


def pair_together(query, keys, values):
    low = low_lanes(query.shape)
    turned = pltpu.roll(keys, HEAD_DIM, 1)
    return jnp.concatenate(
        [jnp.where(low, query, turned), jnp.where(low, values, query), jnp.where(low, turned, values)],
        axis=1,
    )


def project_kernel(place_ref, scales_ref, *refs, row, pieces, parts):
    weight_refs, token_refs = refs[:parts], refs[parts : parts + pieces]
    qkv_ref, normed_ref, held_ref, w_ref, sem_ref = refs[parts + pieces :]
    step = pl.program_id(0)

    def fetch(piece):
        source = token_refs[piece]
        source = source.at[row] if len(source.shape) == 3 else source
        return pltpu.make_async_copy(source, held_ref.at[piece], sem_ref.at[piece])

    @pl.when(step == 0)
    def _():
        for piece in range(pieces):
            fetch(piece).start()
        tall = weight_refs[0].shape[0]
        for apart, weight_ref in enumerate(weight_refs):
            at = pl.multiple_of((apart ^ place_ref[1]) * tall, tall)
            w_ref[pl.ds(at, tall), :] = pair_apart(weight_ref[...].astype(jnp.float32)).astype(jnp.bfloat16)
    pltpu.make_async_copy(held_ref.at[step], held_ref.at[step], sem_ref.at[step]).wait()
    values = held_ref[step].astype(jnp.float32)
    width = values.shape[1]
    hat, _ = normalize(values)
    normed = (hat * scales_ref[row : row + 1, :width]).astype(jnp.bfloat16)
    normed_ref[0] = normed
    qkv_ref[0] = dot_nn(normed, w_ref[...]).astype(jnp.bfloat16)


def project(row, place, scales, weights, tokens, others):
    _, length, width = tokens.shape
    pair = weights[0].shape[1]
    pieces = 1 + len(others)
    anywhere = pl.BlockSpec(memory_space=pl.ANY)
    return pl.pallas_call(
        functools.partial(project_kernel, row=row, pieces=pieces, parts=len(weights)),
        grid_spec=pltpu.PrefetchScalarGridSpec(
            num_scalar_prefetch=1,
            grid=(pieces,),
            in_specs=[whole(scales.shape)]
            + [whole(one.shape) for one in weights]
            + [anywhere] * pieces,
            out_specs=[
                pl.BlockSpec((1, length, pair), lambda i, place: (i ^ place[0], 0, 0)),
                pl.BlockSpec((1, length, width), lambda i, place: (i ^ place[0], 0, 0)),
            ],
            scratch_shapes=[
                pltpu.VMEM((pieces, length, width), jnp.bfloat16),
                pltpu.VMEM((width, pair), jnp.bfloat16),
                pltpu.SemaphoreType.DMA((pieces,)),
            ],
        ),
        out_shape=[
            jax.ShapeDtypeStruct((pieces, length, pair), jnp.bfloat16),
            jax.ShapeDtypeStruct((pieces, length, width), jnp.bfloat16),
        ],
        compiler_params=params(),
        cost_estimate=cost(2 * pieces * length * width * pair, 5 * pieces * length * width),
        name="project",
    )(place, scales, *weights, tokens, *others)


HALF = BLK // 2


def tile_mask(segc_ref, segr_ref, key_at, query_at, size):
    key_at, query_at = pl.multiple_of(key_at, size), pl.multiple_of(query_at, size)
    same = segc_ref[0, pl.ds(key_at, size), :] == segr_ref[0, :, pl.ds(query_at, size)]
    key_pos = key_at + lax.broadcasted_iota(jnp.int32, (size, size), 0)
    query_pos = query_at + lax.broadcasted_iota(jnp.int32, (size, size), 1)
    return same & (key_pos <= query_pos)


def split_heads(values):
    low = low_lanes(values.shape)
    zero = jnp.zeros_like(values)
    return jnp.concatenate([jnp.where(low, values, zero), jnp.where(low, zero, values)], axis=0)


def is_full(edge_ref, row, key_block, query_block):
    ends = edge_ref.shape[1] // 2
    same = edge_ref[row, 2 * key_block] == edge_ref[row, ends + 2 * query_block + 1]
    return same & (key_block < query_block)


def over_quarters(edge_ref, row, key_block, query_block, update):
    ends = edge_ref.shape[1] // 2

    def quarter(number, carried):
        key_half = 2 * key_block + number % 2
        query_half = 2 * query_block + number // 2
        shared = edge_ref[row, ends + key_half] >= edge_ref[row, query_half]

        @pl.when(shared & (key_half <= query_half))
        def _():
            update(pl.multiple_of(key_half * HALF, HALF), pl.multiple_of(query_half * HALF, HALF))

        return carried

    lax.fori_loop(0, 4, quarter, 0)


def largest(values, head):
    part = jnp.where(low_lanes(values.shape) == (head == 0), values, 0.0)
    return jnp.max(jnp.sum(part * part, axis=1, keepdims=True))


def attend_kernel(
    listed_ref, edge_ref, qkv_ref, segc_ref, segr_ref, mixed_ref, lse_ref,
    vt_ref, qz_ref, acc_ref, stat_ref, *, row,
):
    blocks = qkv_ref.shape[0]
    tall = HEAD_DIM + 16

    def turn(block, tops):
        at = pl.multiple_of(block * BLK, BLK)
        turned = transposed(qkv_ref[block, :, 256:384])
        ones = jnp.ones((16, BLK), jnp.bfloat16)
        for head in range(2):
            vt_ref[head * tall : head * tall + HEAD_DIM, pl.ds(at, BLK)] = turned[
                head * HEAD_DIM : (head + 1) * HEAD_DIM
            ]
            vt_ref[head * tall + HEAD_DIM : (head + 1) * tall, pl.ds(at, BLK)] = ones
        keys = qkv_ref[block, :, 128:256].astype(jnp.float32)
        return tuple(jnp.maximum(tops[head], largest(keys, head)) for head in range(2))

    key_tops = lax.fori_loop(0, blocks, turn, (0.0, 0.0))

    def one_query(query_block, carried):
        query = qkv_ref[query_block, :, :128].astype(jnp.float32) * HEAD_DIM ** (-0.5)
        qz_ref[...] = split_heads(query.astype(jnp.bfloat16))
        acc_ref[...] = jnp.zeros(acc_ref.shape, jnp.float32)
        shift = []
        for head in range(2):
            both = jnp.full((1, BLK), largest(query, head) * key_tops[head], jnp.float32)
            shift.append(jnp.sqrt(both) * 1.01)
        small = (jnp.max(shift[0]) < 40.0) & (jnp.max(shift[1]) < 40.0)

        def over_keys(full_update, part_update):
            def one_key(key_block, carried):
                listed = listed_ref[row, query_block * blocks + key_block] != 0
                full = is_full(edge_ref, row, key_block, query_block)

                @pl.when(listed & full)
                def _():
                    full_update(key_block)

                @pl.when(listed & jnp.logical_not(full))
                def _():
                    part_update(key_block)

                return carried

            lax.fori_loop(0, query_block + 1, one_key, 0)

        @pl.when(small)
        def _():
            def update(key_block, mask):
                at = pl.multiple_of(key_block * BLK, BLK)
                keys = qkv_ref[key_block, :, 128:256]
                parts = [slice(head * BLK, (head + 1) * BLK) for head in range(2)]
                scores = [dot_nt(keys, qz_ref[part, :]) for part in parts]
                for head, part in enumerate(parts):
                    one = scores[head] - shift[head]
                    if mask is not None:
                        one = jnp.where(mask, one, masked_out)
                    value = vt_ref[head * tall : (head + 1) * tall, pl.ds(at, BLK)]
                    acc_ref[:, part] += dot_nn(value, jnp.exp(one).astype(jnp.bfloat16))

            def part_update(key_block):
                update(key_block, tile_mask(segc_ref, segr_ref, key_block * BLK, query_block * BLK, BLK))

            def full_update(key_block):
                update(key_block, None)

            over_keys(full_update, part_update)
            stat_ref[0:1, :] = jnp.concatenate(shift, axis=1)

        @pl.when(jnp.logical_not(small))
        def _():
            stat_ref[0:1, :] = jnp.full((1, 2 * BLK), masked_out, jnp.float32)

            def part_update(key_at, query_at):
                keys = qkv_ref[key_at // BLK, pl.ds(pl.multiple_of(key_at % BLK, HALF), HALF), 128:256]
                mask = tile_mask(segc_ref, segr_ref, key_at, query_at, HALF)
                for head in range(2):
                    part = pl.ds(pl.multiple_of(head * BLK + query_at % BLK, HALF), HALF)
                    scores = jnp.where(mask, dot_nt(keys, qz_ref[part, :]), masked_out)
                    old_max = stat_ref[0:1, part]
                    new_max = jnp.maximum(old_max, jnp.max(scores, axis=0, keepdims=True))
                    weights = jnp.where(mask, jnp.exp(scores - new_max), 0.0)
                    value = vt_ref[head * tall : (head + 1) * tall, pl.ds(key_at, HALF)]
                    shrink = jnp.exp(old_max - new_max)
                    acc_ref[:, part] = acc_ref[:, part] * shrink + dot_nn(value, weights.astype(jnp.bfloat16))
                    stat_ref[0:1, part] = new_max

            def full_update(key_block):
                over_quarters(edge_ref, row, key_block, query_block, part_update)

            over_keys(full_update, full_update)

        total = acc_ref[HEAD_DIM : HEAD_DIM + 1, :]
        mixed = acc_ref[:HEAD_DIM, :] / total
        mixed = jnp.concatenate([mixed[:, :BLK], mixed[:, BLK:]], axis=0).T
        mixed_ref[query_block] = mixed.astype(jnp.bfloat16)
        log_total = stat_ref[0:1, :] + jnp.log(total)
        at = pl.multiple_of(query_block * BLK, BLK)
        lse_ref[0:1, pl.ds(at, BLK)] = log_total[:, :BLK]
        lse_ref[1:2, pl.ds(at, BLK)] = log_total[:, BLK:]
        return carried

    lax.fori_loop(0, blocks, one_query, 0)


def attend(row, listed, edges, qkv, segc, segr):
    blocks, blk, width = qkv.shape
    length = blocks * blk
    pair = 2 * HEAD_DIM
    return pl.pallas_call(
        functools.partial(attend_kernel, row=row),
        grid_spec=pltpu.PrefetchScalarGridSpec(
            num_scalar_prefetch=2,
            grid=(1,),
            in_specs=[
                whole(qkv.shape),
                pl.BlockSpec((1, length, 1), lambda i, *_: (row, 0, 0)),
                pl.BlockSpec((1, 1, length), lambda i, *_: (row, 0, 0)),
            ],
            out_specs=[whole((blocks, blk, pair)), whole((2, length))],
            scratch_shapes=[
                pltpu.VMEM((pair + 32, length), jnp.bfloat16),
                pltpu.VMEM((2 * blk, pair), jnp.bfloat16),
                pltpu.VMEM((HEAD_DIM + 16, 2 * blk), jnp.float32),
                pltpu.VMEM((1, 2 * blk), jnp.float32),
            ],
        ),
        out_shape=[
            jax.ShapeDtypeStruct((blocks, blk, pair), jnp.bfloat16),
            jax.ShapeDtypeStruct((2, length), jnp.float32),
        ],
        compiler_params=params(),
        cost_estimate=cost(20e9, 6e6, 20e6),
        name="attend",
    )(listed, edges, qkv, segc, segr)


def attend_back_kernel(
    listed_ref, edge_ref, qkv_ref, grad_ref, mixed_ref, lse_ref, segc_ref, segr_ref, out_ref,
    kt_ref, qz_ref, gz_ref, inner_ref, dq_ref, dk_ref, dv_ref, *, row,
):
    blocks = qkv_ref.shape[0]
    scale = HEAD_DIM ** (-0.5)

    def prepare(block, carried):
        at = pl.multiple_of(block * BLK, BLK)
        kt_ref[:, pl.ds(at, BLK)] = transposed(qkv_ref[block, :, 128:256])
        query = qkv_ref[block, :, :128].astype(jnp.float32) * scale
        qz_ref[block] = split_heads(query.astype(jnp.bfloat16))
        grad = grad_ref[block]
        gz_ref[block] = split_heads(grad)
        product = (grad.astype(jnp.float32) * mixed_ref[block].astype(jnp.float32)).T
        for head in range(2):
            part = product[head * HEAD_DIM : (head + 1) * HEAD_DIM, :]
            inner_ref[head : head + 1, pl.ds(at, BLK)] = jnp.sum(part, axis=0, keepdims=True)
        return carried

    lax.fori_loop(0, blocks, prepare, 0)
    dq_ref[...] = jnp.zeros(dq_ref.shape, jnp.float32)

    def one_key(key_block, carried):
        dk_ref[...] = jnp.zeros(dk_ref.shape, jnp.float32)
        dv_ref[...] = jnp.zeros(dv_ref.shape, jnp.float32)
        key_at = pl.multiple_of(key_block * BLK, BLK)

        def accumulate(head, key_at, query_at, keys, values, query, grad, mask):
            keys_here = pl.ds(pl.multiple_of(key_at % BLK, HALF), keys.shape[0])
            queries_here = pl.ds(query_at, query.shape[0])
            scores = dot_nt(keys, query)
            probs = jnp.exp(scores - lse_ref[head : head + 1, queries_here])
            if mask is not None:
                probs = jnp.where(mask, probs, 0.0)
            grad_probs = dot_nt(values, grad)
            grad_scores = probs * (grad_probs - inner_ref[head : head + 1, queries_here])
            probs = probs.astype(jnp.bfloat16)
            grad_scores = grad_scores.astype(jnp.bfloat16)
            dv_ref[keys_here, :] += dot_nn(probs, grad)
            dk_ref[keys_here, :] += dot_nn(grad_scores, query)
            lanes = slice(head * HEAD_DIM, (head + 1) * HEAD_DIM)
            dq_ref[lanes, queries_here] += dot_nn(
                kt_ref[lanes, pl.ds(key_at, keys.shape[0])], grad_scores
            )

        def full_update(query_block, mask):
            query_at = pl.multiple_of(query_block * BLK, BLK)
            keys = qkv_ref[key_block, :, 128:256]
            values = qkv_ref[key_block, :, 256:384]
            for head in range(2):
                part = slice(head * BLK, (head + 1) * BLK)
                query, grad = qz_ref[query_block, part, :], gz_ref[query_block, part, :]
                accumulate(head, key_at, query_at, keys, values, query, grad, mask)

        def one_query(query_block, carried):
            listed = listed_ref[row, query_block * blocks + key_block] != 0
            full = is_full(edge_ref, row, key_block, query_block)

            @pl.when(listed & full)
            def _():
                full_update(query_block, None)

            @pl.when(listed & jnp.logical_not(full))
            def _():
                full_update(query_block, tile_mask(segc_ref, segr_ref, key_block * BLK, query_block * BLK, BLK))

            return carried

        lax.fori_loop(key_block, blocks, one_query, 0)
        grad_query = dq_ref[:, pl.ds(key_at, BLK)].T * scale
        out_ref[key_block] = pair_together(grad_query, dk_ref[...], dv_ref[...]).astype(jnp.bfloat16)
        return carried

    lax.fori_loop(0, blocks, one_key, 0)


def attend_back(row, listed, edges, qkv, grad, mixed, lse, segc, segr):
    blocks, blk, width = qkv.shape
    length = blocks * blk
    pair = 2 * HEAD_DIM
    return pl.pallas_call(
        functools.partial(attend_back_kernel, row=row),
        grid_spec=pltpu.PrefetchScalarGridSpec(
            num_scalar_prefetch=2,
            grid=(1,),
            in_specs=[
                whole(qkv.shape),
                whole(grad.shape),
                whole(mixed.shape),
                whole(lse.shape),
                pl.BlockSpec((1, length, 1), lambda i, *_: (row, 0, 0)),
                pl.BlockSpec((1, 1, length), lambda i, *_: (row, 0, 0)),
            ],
            out_specs=whole(qkv.shape),
            scratch_shapes=[
                pltpu.VMEM((pair, length), jnp.bfloat16),
                pltpu.VMEM((blocks, 2 * blk, pair), jnp.bfloat16),
                pltpu.VMEM((blocks, 2 * blk, pair), jnp.bfloat16),
                pltpu.VMEM((2, length), jnp.float32),
                pltpu.VMEM((pair, length), jnp.float32),
                pltpu.VMEM((blk, pair), jnp.float32),
                pltpu.VMEM((blk, pair), jnp.float32),
            ],
        ),
        out_shape=jax.ShapeDtypeStruct(qkv.shape, jnp.bfloat16),
        compiler_params=params(),
        cost_estimate=cost(50e9, 10e6, 20e6),
        name="attend_back",
    )(listed, edges, qkv, grad, mixed, lse, segc, segr)


def joined(ref, half, halves):
    return jnp.concatenate([ref[i * halves + half] for i in range(ref.shape[0] // halves)], axis=1)


def outward_kernel(mixed_ref, tok_ref, w_ref, scales_ref, hidden_ref, normed_ref, *, row):
    halves = w_ref.shape[1]
    hidden = tok_ref[0].astype(jnp.float32)
    width = hidden.shape[1]
    for half in range(halves):
        hidden += dot_nt(joined(mixed_ref, half, halves), w_ref[:, half].reshape(width, -1))
    hidden_ref[...] = hidden
    hat, _ = normalize(hidden)
    normed_ref[...] = (hat * scales_ref[row : row + 1, width:]).astype(jnp.bfloat16)


def outward(row, mixed, tokens, w_all, scales, columns):
    rows, length, width = tokens.shape
    groups, _, pair = mixed.shape
    chunks, halves, high, _ = w_all.shape
    tile = 256
    one = pl.BlockSpec((tile, width), lambda i: (i, 0))
    return pl.pallas_call(
        functools.partial(outward_kernel, row=row),
        grid=(length // tile,),
        in_specs=[
            pl.BlockSpec((groups, tile, pair), lambda i: (0, i, 0)),
            pl.BlockSpec((1, tile, width), lambda i: (row, i, 0)),
            whole((chunks, halves, high, columns)),
            whole(scales.shape),
        ],
        out_specs=[one, one],
        out_shape=[
            jax.ShapeDtypeStruct((length, width), jnp.float32),
            jax.ShapeDtypeStruct((length, width), jnp.bfloat16),
        ],
        compiler_params=params(),
        cost_estimate=cost(2 * length * width * width, 12 * length * width),
        name="outward",
    )(mixed, tokens, w_all, scales)


def mlp_kernel(
    place_ref, nm0_ref, nm1_ref, cot_ref, hidden0_ref, hidden1_ref, scales_ref, up_ref, down_ref,
    keep_ref, send_ref, layer_ref, grad_hidden_ref, grad_attn_ref, gscale_ref,
    nmt_ref, cott_ref, out_ref, gn_ref, act_ref, gpre_ref,
):
    tile = pl.program_id(0)
    phase = pl.program_id(1)
    length, width = nm0_ref.shape
    count = 2 * length
    root = 0.7978845608028654
    cube = 0.044715

    @pl.when((tile == 0) & (phase == 0))
    def _():
        chunks = up_ref.shape[0]
        turned_apart(nmt_ref.at[:, :length], nm0_ref[...], place_ref[2], chunks)
        turned_apart(nmt_ref.at[:, length:], nm1_ref[...], place_ref[2], chunks)
        turned_apart(cott_ref, cot_ref[...], place_ref[2], chunks)
        out_ref[...] = jnp.zeros(out_ref.shape, jnp.float32)
        gn_ref[...] = jnp.zeros(gn_ref.shape, jnp.float32)

    @pl.when(phase == 0)
    def _():
        up = up_ref[:, 0].reshape(width, -1)
        down = down_ref[:, 0].reshape(width, -1)
        for row, nm_ref in enumerate((nm0_ref, nm1_ref)):
            part = slice(row * length, (row + 1) * length)
            pre = dot_nn(nm_ref[...], up)
            grad_act = dot_nn(cot_ref[part, :], down)
            square = pre * pre
            bent = jnp.tanh(root * (pre + cube * pre * square))
            half = 0.5 * (1.0 + bent)
            act_ref[part, :] = (pre * half).astype(jnp.bfloat16)
            slope = half + (0.5 * root) * pre * (1.0 - bent * bent) * (1.0 + (3.0 * cube) * square)
            gpre_ref[part, :] = (grad_act * slope).astype(jnp.bfloat16)
        put_apart(keep_ref, send_ref, dot_nn(nmt_ref[...], gpre_ref[...]).astype(jnp.bfloat16))

    @pl.when(phase == 1)
    def _():
        up = up_ref[:, 0].reshape(width, -1)
        down = down_ref[:, 0].reshape(width, -1)
        out_ref[...] += dot_nt(act_ref[...], down)
        gn_ref[...] += dot_nt(gpre_ref[...], up)
        put_apart(keep_ref, send_ref, dot_nn(cott_ref[...], act_ref[...]).astype(jnp.bfloat16))

    @pl.when((tile == pl.num_programs(0) - 1) & (phase == 1))
    def _():
        chunk = 256
        for row, hidden_ref in enumerate((hidden0_ref, hidden1_ref)):
            scale = scales_ref[row : row + 1, width:]
            total = jnp.zeros((1, width), jnp.float32)
            for at in range(0, length, chunk):
                part = slice(row * length + at, row * length + at + chunk)
                hidden = hidden_ref[at : at + chunk, :]
                layer_ref[part, :] = (hidden + out_ref[part, :]).astype(jnp.bfloat16)
                hat, inverse = normalize(hidden)
                grad = gn_ref[part, :]
                total += jnp.sum(grad * hat, axis=0, keepdims=True)
                back = cot_ref[part, :].astype(jnp.float32) + normalize_back(grad * scale, hat, inverse)
                grad_hidden_ref[part, :] = back
                grad_attn_ref[part, :] = back.astype(jnp.bfloat16)
            gscale_ref[row : row + 1, :] = total


def mlp(place, normed, cotangent, hidden, scales, w_all, room):
    rows, length, width = cotangent.shape
    count = rows * length
    chunks, halves, high, columns = w_all.shape
    tile = 512
    hidden_cols = (columns - room) // 2
    per_half = hidden_cols // tile
    first = room // tile
    flat = (count, width)
    one = (length, width)
    block = (chunks, 1, high, tile)
    apart = pl.BlockSpec(
        (2, 1, chunks // 4, high, tile),
        lambda f, s, at: (0, f // per_half, 0, 0, first + s * per_half + f % per_half),
    )
    grads = jax.ShapeDtypeStruct((2, halves, chunks // 4, high, columns), jnp.bfloat16)
    return pl.pallas_call(
        mlp_kernel,
        grid_spec=pltpu.PrefetchScalarGridSpec(
            num_scalar_prefetch=1,
            grid=(halves * per_half, 2),
            in_specs=[
                whole(one),
                whole(one),
                whole(flat),
                whole(one),
                whole(one),
                whole(scales.shape),
                pl.BlockSpec(block, lambda f, s, at: (0, f // per_half, 0, first + f % per_half)),
                pl.BlockSpec(block, lambda f, s, at: (0, f // per_half, 0, first + per_half + f % per_half)),
            ],
            out_specs=[
                apart,
                apart,
                whole(flat),
                whole(flat),
                whole(flat),
                whole((rows, width)),
            ],
            scratch_shapes=[
                pltpu.VMEM((width, count), jnp.bfloat16),
                pltpu.VMEM((width, count), jnp.bfloat16),
                pltpu.VMEM(flat, jnp.float32),
                pltpu.VMEM(flat, jnp.float32),
                pltpu.VMEM((count, tile), jnp.bfloat16),
                pltpu.VMEM((count, tile), jnp.bfloat16),
            ],
        ),
        out_shape=[
            grads,
            grads,
            jax.ShapeDtypeStruct(flat, jnp.bfloat16),
            jax.ShapeDtypeStruct(flat, jnp.float32),
            jax.ShapeDtypeStruct(flat, jnp.bfloat16),
            jax.ShapeDtypeStruct((rows, width), jnp.float32),
        ],
        compiler_params=params(60),
        cost_estimate=cost(12 * count * width * halves * hidden_cols, 4 * w_all.size + 16 * count * width),
        name="mlp",
    )(place, *normed, cotangent.reshape(flat), *hidden, scales, w_all, w_all)


def grad_mixed_kernel(grad_ref, w_ref, out_ref):
    halves = w_ref.shape[1]
    per_half = out_ref.shape[0] // halves
    grad = grad_ref[...]
    pair = out_ref.shape[2]
    for half in range(halves):
        out = dot_nn(grad, w_ref[:, half].reshape(grad.shape[1], -1)).astype(jnp.bfloat16)
        for group in range(per_half):
            out_ref[group * halves + half] = out[:, group * pair : (group + 1) * pair]


def grad_mixed_of(row, grad_attn, w_all, mixed_shape, columns):
    groups, length, pair = mixed_shape
    chunks, halves, high, _ = w_all.shape
    width = grad_attn.shape[1]
    tile = 256
    tiles = length // tile
    return pl.pallas_call(
        grad_mixed_kernel,
        grid=(tiles,),
        in_specs=[
            pl.BlockSpec((tile, width), lambda i: (row * tiles + i, 0)),
            whole((chunks, halves, high, columns)),
        ],
        out_specs=pl.BlockSpec((groups, tile, pair), lambda i: (0, i, 0)),
        out_shape=jax.ShapeDtypeStruct(mixed_shape, jnp.bfloat16),
        compiler_params=params(),
        cost_estimate=cost(2 * length * width * width, 8 * length * width),
        name="grad_mixed",
    )(grad_attn, w_all)


def grad_proj_kernel(place_ref, grad_ref, mixed0_ref, mixed1_ref, _k, _s, keep_ref, send_ref, turned_ref):
    half = pl.program_id(0)
    halves = pl.num_programs(0)

    @pl.when(half == 0)
    def _():
        turned_apart(turned_ref, grad_ref[...], place_ref[2], 4 * keep_ref.shape[2])

    groups, length, pair = mixed0_ref.shape
    count = keep_ref.shape[4] // pair
    grad = 0.0
    for row, mixed_ref in enumerate((mixed0_ref, mixed1_ref)):
        mixed = jnp.concatenate([mixed_ref[i * halves + half] for i in range(count)], axis=1)
        grad += dot_nn(turned_ref[:, row * length : (row + 1) * length], mixed)
    put_apart(keep_ref, send_ref, grad.astype(jnp.bfloat16))


def grad_proj_into(place, keep, send, grad_attn, mixed, columns):
    count, width = grad_attn.shape
    given = whole(mixed[0].shape)
    anywhere = pl.BlockSpec(memory_space=pl.ANY)
    out = pl.BlockSpec((2, 1) + keep.shape[2:4] + (columns,), lambda h, at: (0, h, 0, 0, 0))
    return pl.pallas_call(
        grad_proj_kernel,
        grid_spec=pltpu.PrefetchScalarGridSpec(
            num_scalar_prefetch=1,
            grid=(keep.shape[1],),
            in_specs=[whole(grad_attn.shape), given, given, anywhere, anywhere],
            out_specs=[out, out],
            scratch_shapes=[pltpu.VMEM((width, count), jnp.bfloat16)],
        ),
        out_shape=[jax.ShapeDtypeStruct(keep.shape, jnp.bfloat16)] * 2,
        input_output_aliases={4: 0, 5: 1},
        compiler_params=params(),
        cost_estimate=cost(2 * count * width * width, 6 * count * width),
        name="grad_proj",
    )(place, grad_attn, *mixed, keep, send)


def first_norm_kernel(gq_ref, tok_ref, grad_hidden_ref, w_ref, scales_ref, out_ref, gscale_ref, *, row, q_cols):
    step = pl.program_id(0)
    halves = w_ref.shape[1]
    values = tok_ref[0].astype(jnp.float32)
    width = values.shape[1]
    grad = jnp.zeros(values.shape, jnp.float32)
    for half in range(halves):
        weights = w_ref[:, half, :, :q_cols].reshape(width, q_cols)
        grad += dot_nt(joined(gq_ref, half, halves), weights)
    hat, inverse = normalize(values)
    total = jnp.sum(grad * hat, axis=0, keepdims=True)

    @pl.when(step == 0)
    def _():
        gscale_ref[...] = total

    @pl.when(step != 0)
    def _():
        gscale_ref[...] += total

    back = normalize_back(grad * scales_ref[row : row + 1, :width], hat, inverse)
    out_ref[...] = (grad_hidden_ref[...] + back).astype(jnp.bfloat16)


def first_norm_back(row, grad_qkv, tokens, grad_hidden, w_all, scales, q_cols):
    rows, length, width = tokens.shape
    groups, _, pair = grad_qkv.shape
    tile = 256
    tiles = length // tile
    return pl.pallas_call(
        functools.partial(first_norm_kernel, row=row, q_cols=q_cols),
        grid=(tiles,),
        in_specs=[
            pl.BlockSpec((groups, tile, pair), lambda i: (0, i, 0)),
            pl.BlockSpec((1, tile, width), lambda i: (row, i, 0)),
            pl.BlockSpec((tile, width), lambda i: (row * tiles + i, 0)),
            whole(w_all.shape),
            whole(scales.shape),
        ],
        out_specs=[pl.BlockSpec((tile, width), lambda i: (i, 0)), whole((1, width))],
        out_shape=[
            jax.ShapeDtypeStruct((length, width), jnp.bfloat16),
            jax.ShapeDtypeStruct((1, width), jnp.float32),
        ],
        compiler_params=params(),
        cost_estimate=cost(2 * length * width * groups * pair, 2 * w_all.size + 20 * length * width),
        name="first_norm_back",
    )(grad_qkv, tokens, grad_hidden, w_all, scales)


def grad_qkv_kernel(place_ref, normed_ref, gq_ref, *refs):
    step = pl.program_id(0)
    base_refs, out_refs, total_ref = refs[:-2], refs[-2:-1], refs[-1]
    if len(refs) > 3:
        base_refs, out_refs, (total_ref, turned_ref) = refs[:1], refs[1:-2], refs[-2:]

    @pl.when(step == 0)
    def _():
        total_ref[...] = base_refs[0][...] if base_refs else jnp.zeros(total_ref.shape, jnp.float32)

    total_ref[...] += dot_nn(transposed(gq_ref[0]), normed_ref[0])

    @pl.when(step == pl.num_programs(0) - 1)
    def _():
        if base_refs:
            turned_ref[...] = total_ref[...].T
            tall = out_refs[0].shape[0]
            for apart, out_ref in enumerate(out_refs):
                at = pl.multiple_of((apart ^ place_ref[1]) * tall, tall)
                out_ref[...] = turned_ref[pl.ds(at, tall), :].astype(jnp.bfloat16)
        else:
            out_refs[0][...] = total_ref[...]


def grad_qkv_of(place, normed, grad_qkv, parts, base=()):
    blocks, length, width = normed.shape
    pair = grad_qkv.shape[2]
    turned = (pair, width)
    if base:
        shapes = [jax.ShapeDtypeStruct((width // parts, pair), jnp.bfloat16)] * parts
    else:
        shapes = [jax.ShapeDtypeStruct(turned, jnp.float32)]
    return pl.pallas_call(
        grad_qkv_kernel,
        grid_spec=pltpu.PrefetchScalarGridSpec(
            num_scalar_prefetch=1,
            grid=(blocks,),
            in_specs=[
                pl.BlockSpec((1, length, width), lambda i, place: (i, 0, 0)),
                pl.BlockSpec((1, length, pair), lambda i, place: (i, 0, 0)),
            ]
            + [whole(turned)] * len(base),
            out_specs=[whole(one.shape) for one in shapes],
            scratch_shapes=[pltpu.VMEM(turned, jnp.float32)]
            + [pltpu.VMEM((width, pair), jnp.float32)] * len(base),
        ),
        out_shape=shapes,
        compiler_params=params(),
        cost_estimate=cost(2 * blocks * length * width * pair, 3 * blocks * length * width),
        name="grad_qkv",
    )(place, normed, grad_qkv, *base)


CTX = ("x", "core")
GROUP = ("x", "core", "tp")
EVERY = ("fsdp", "x", "core", "tp")


def size_of(axis):
    names = (axis,) if isinstance(axis, str) else axis
    return functools.reduce(lambda size, name: size * lax.axis_size(name), names, 1)


def across(values, axis, apart):
    size = size_of(axis)
    return lax.ppermute(values, axis, [(i, i ^ apart) for i in range(size)])


def summed(parts):
    return sum(part.astype(jnp.float32) for part in parts)


def exchange(values, axes):
    return lax.all_to_all(values, axes, 0, 0, tiled=True)


HOPS = {1: "tp", 2: "core", 4: "x"}


def widened(found, apart):
    return {**found, **{held ^ apart: across(one, HOPS[apart], 1) for held, one in found.items()}}


def listed_table(block_pairs, pair_counts, row_blocks, ctx_size):
    rows, _, slots, _ = block_pairs.shape
    packed = jnp.concatenate([block_pairs.reshape(rows, 1, slots * 2), pair_counts[:, :, None]], axis=2)
    packed = jnp.concatenate(
        [packed] + [across(packed, CTX, apart) for apart in range(1, ctx_size)], axis=1
    )
    pairs = packed[:, :, : slots * 2].reshape(rows, ctx_size, slots, 2)
    live = jnp.arange(slots, dtype=jnp.int32)[None, None, :] < packed[:, :, slots * 2 :]
    owner = lax.axis_index(CTX) ^ jnp.arange(ctx_size, dtype=jnp.int32)[None, :, None]
    base = owner * (row_blocks // ctx_size)
    code = jnp.where(live, (base + pairs[..., 0]) * row_blocks + pairs[..., 1], -1)
    code = code.reshape(rows, ctx_size * slots)
    cells = jnp.arange(row_blocks * row_blocks, dtype=jnp.int32)
    return jnp.any(code[:, :, None] == cells[None, None, :], axis=1).astype(jnp.int32)


def spread_body(
    tokens, time_embed, segment_ids, block_pairs, pair_counts,
    w_time, w_qkv, w_out, w_up, w_down, cotangent,
):
    rows, length, width = tokens.shape
    chunks = width // w_qkv.shape[0]
    halves = lax.axis_size("tp")
    high = w_qkv.shape[0]
    q_cols, o_cols, f_cols = w_qkv.shape[1], w_out.shape[1], w_up.shape[1]
    k_rows = w_time.shape[0]
    mine = lax.axis_index("tp")
    ctx, fsdp = lax.axis_index(CTX), lax.axis_index("fsdp")
    n_ctx, n_fsdp = size_of(CTX), lax.axis_size("fsdp")
    bf16, f32 = jnp.bfloat16, jnp.float32
    chunk = fsdp * n_ctx + ctx
    place = jnp.stack([ctx * halves + mine, fsdp, lax.axis_index("core")])

    found = [{0: tokens[row]} for row in range(rows)]
    orders = [(4, 1, 2) if row % 2 == 0 else (1, 4, 2) for row in range(rows)]
    found = [widened(one, order[0]) for one, order in zip(found, orders)]
    w_qkv = w_qkv.astype(bf16)
    columns = exchange(w_qkv.reshape(high, n_ctx, -1).transpose(1, 0, 2), CTX)
    embeds = [time_embed] + [across(time_embed, "fsdp", apart) for apart in range(1, n_fsdp)]
    w_time = w_time.astype(bf16)
    times = [w_time] + [across(w_time, CTX, apart) for apart in range(1, n_ctx)]
    row_blocks = segment_ids.shape[1] // BLK
    listed = listed_table(block_pairs, pair_counts, row_blocks, n_ctx)
    edges = jnp.concatenate([segment_ids[:, ::HALF], segment_ids[:, HALF - 1 :: HALF]], axis=1)
    segc = segment_ids[:, :, None]
    segr = segment_ids[:, None, :]
    second = jnp.concatenate([w_out, w_up, w_down], axis=1).astype(bf16)
    found, columns, embeds, times, second = lax.optimization_barrier((found, columns, embeds, times, second))
    second = lax.all_gather(second, EVERY, axis=0, tiled=True)
    found = [widened(one, order[1]) for one, order in zip(found, orders)]
    columns = columns.reshape(n_ctx * high, -1)
    columns = [columns] + [across(columns, "fsdp", apart) for apart in range(1, n_fsdp)]
    rows_of = [(chunk ^ apart) * k_rows for apart in range(n_ctx)]
    some = [
        jnp.concatenate([lax.dynamic_slice_in_dim(one, at, k_rows, 1) for at in rows_of], axis=1)
        for one in embeds
    ]
    mine_of = [one[:, :k_rows] for one in some]
    given = jnp.dot(jnp.concatenate(some, axis=0), jnp.concatenate(times, axis=0).astype(f32), precision=highest)
    given = given.reshape(n_fsdp, rows, -1)
    scales = 1.0 + given[0] + sum(across(given[apart], "fsdp", apart) for apart in range(1, n_fsdp))
    found, scales, columns, listed, edges, segc, segr = lax.optimization_barrier(
        (found, scales, columns, listed, edges, segc, segr)
    )
    found = [widened(one, order[2]) for one, order in zip(found, orders)]
    others = [[one[apart] for apart in range(1, len(one))] for one in found]

    qkv, normed = [], []
    for row in range(rows):
        out, one = project(row, place, scales, columns, tokens, others[row])
        qkv.append(out)
        normed.append(one)
    mixed_own, lse, mixed = [], [], []
    for row in range(rows):
        out, one = attend(row, listed, edges, qkv[row], segc, segr)
        mixed_own.append(out)
        lse.append(one)
        mixed.append(exchange(out, GROUP))
    mixed[0], mixed_own = lax.optimization_barrier((mixed[0], mixed_own))
    second = second.reshape(chunks, halves, high, -1)
    hidden, normed_mlp = [], []
    for row in range(rows):
        if row:
            mixed[row], hidden[row - 1] = lax.optimization_barrier((mixed[row], hidden[row - 1]))
        out, one = outward(row, mixed[row], tokens, second, scales, o_cols)
        hidden.append(out)
        normed_mlp.append(one)
    w_qkv, normed_mlp = lax.optimization_barrier((w_qkv, normed_mlp))
    third = lax.all_gather(w_qkv, EVERY, axis=0, tiled=True).reshape(chunks, halves, high, -1)
    keep, send, layer_out, grad_hidden, grad_attn, gscale_mlp = mlp(
        place, normed_mlp, cotangent, hidden, scales, second, o_cols
    )
    keep, send = grad_proj_into(place, keep, send, grad_attn, mixed, o_cols)
    grad_attn, keep, send, third = lax.optimization_barrier((grad_attn, keep, send, third))
    sent = across(send, "core", 1)
    grad_mixed = {}
    for row in reversed(range(rows)):
        out = grad_mixed_of(row, grad_attn, second, mixed[row].shape, o_cols)
        grad_mixed[row] = exchange(out, GROUP)
    last = rows - 1
    grads = summed([keep, sent]).astype(bf16)
    grad_mixed[last], grads = lax.optimization_barrier((grad_mixed[last], grads))
    grads = lax.psum_scatter(
        grads.reshape(-1, grads.shape[4]), ("x", "tp"), scatter_dimension=0, tiled=True
    )
    own, grad_qkv = {}, {}
    for row in reversed(range(rows)):
        if row < last:
            grad_mixed[row], own[row + 1] = lax.optimization_barrier((grad_mixed[row], own[row + 1]))
        own[row] = attend_back(row, listed, edges, qkv[row], grad_mixed[row], mixed_own[row], lse[row], segc, segr)
        if row < last:
            grad_qkv[row + 1] = exchange(own[row + 1], GROUP)
    grad_qkv[0] = exchange(own[0], GROUP)
    held, _ = lax.optimization_barrier((own[last], own[0]))
    base = grad_qkv_of(place, normed[last], held, n_fsdp)
    cut = list(grad_qkv_of(place, normed[0], own[0], n_fsdp, base))
    grad_tokens, gscale_attn = {}, {}
    held, _ = lax.optimization_barrier((grad_qkv[last], cut[0]))
    grad_tokens[last], gscale_attn[last] = first_norm_back(
        last, held, tokens, grad_hidden, third, scales, q_cols
    )
    cut[0], gscale_attn[last] = lax.optimization_barrier((cut[0], gscale_attn[last]))
    total = summed([cut[0]] + [across(cut[apart], "fsdp", apart) for apart in range(1, n_fsdp)])
    grads, gscale_attn[last], total = lax.optimization_barrier(
        (grads, gscale_attn[last], total.astype(bf16))
    )
    grads = lax.psum_scatter(grads, "fsdp", scatter_dimension=0, tiled=True)
    total = exchange(total.reshape(n_ctx, high, -1), CTX)
    grad_tokens[0], gscale_attn[0] = first_norm_back(
        0, grad_qkv[0], tokens, grad_hidden, third, scales, q_cols
    )
    devices = n_fsdp * n_ctx * halves
    both = jnp.concatenate([gscale_mlp, gscale_attn[last], gscale_attn[0]], axis=0)
    both = exchange(jnp.broadcast_to(both.astype(bf16)[None], (devices,) + both.shape), EVERY).astype(f32)
    both, total = lax.optimization_barrier((both, total))
    grad_w_qkv = total.transpose(1, 0, 2).reshape(high, q_cols).astype(f32)
    both = jnp.sum(both.reshape(n_fsdp, n_ctx * halves, 2 * rows, width), axis=1)
    both = jnp.concatenate([both[:, 3], both[:, 0], both[:, 2], both[:, 1]], axis=1)
    both = both.reshape(n_fsdp * rows, 2 * width)
    mine_of = [lax.dynamic_index_in_dim(jnp.stack(mine_of), i ^ fsdp, 0, False) for i in range(n_fsdp)]
    grad_time = jnp.dot(jnp.concatenate(mine_of, axis=0).T, both, precision=highest)
    return (
        layer_out.reshape(tokens.shape),
        jnp.stack([grad_tokens[row] for row in range(rows)]),
        grad_time,
        grad_w_qkv,
        grads[:, :o_cols].astype(f32),
        grads[:, o_cols : o_cols + f_cols].astype(f32),
        grads[:, o_cols + f_cols :].astype(f32),
    )


def specs_of(ctx):
    flat = ctx if isinstance(ctx, tuple) else (ctx,)
    tokens, weights = P("fsdp", (*flat, "tp"), None), P(("fsdp", *flat), "tp")
    placed = (tokens, P("fsdp", None), P("fsdp", None), P("fsdp", ctx, None, None), P("fsdp", ctx))
    placed += (P(("fsdp", *flat), None), weights, weights, weights, weights, tokens)
    return placed, (tokens, tokens, P(("fsdp", *flat), None), weights, weights, weights, weights)


def solution(mesh):
    sizes = tuple(mesh.shape[name] for name in ("fsdp", "ctx", "tp"))

    def run(*args):
        tokens, w_qkv, w_out, w_up = args[0], args[6], args[7], args[8]
        group = sizes[1] * sizes[2]
        fits = (
            sizes == (4, 4, 2)
            and tokens.shape[:2] == (8, group * BLK)
            and w_qkv.shape[1] == group * 6 * HEAD_DIM
            and w_out.shape[1] % (512 * sizes[2]) == 0
            and w_up.shape[1] % (512 * sizes[2]) == 0
        )
        if fits:
            devices = mesh.devices.reshape(sizes[0], 2, 2, sizes[2])
            parted = Mesh(devices, ("fsdp", "x", "core", "tp"))
            placed, given = specs_of(CTX)
            return jax.shard_map(
                spread_body, mesh=parted, in_specs=placed, out_specs=given, check_vma=False
            )(*args)
        placed, given = specs_of("ctx")
        return jax.shard_map(body, mesh=mesh, in_specs=placed, out_specs=given, check_vma=False)(*args)

    return run
```
